32 devices in a mesh: fsdp: 2 (over y), ctx: 4 (over x, core), tp: 4 (over z).
Axes of the slice: x: 2, y: 2, z: 4, core: 2. Of those that a mesh axis runs over, the one named last changes fastest.
Arguments:
- hidden: bfloat16 [8192, 768], P(('fsdp', 'ctx', 'tp')), may hold values from -6 to 6
- cotangent: bfloat16 [8192, 768], P(('fsdp', 'ctx', 'tp')), may hold values from -6 to 6
- mem_pos: int32 [2, 4, 20], P('fsdp', 'ctx'), may hold values from 0 to 1023, as said below
- parents: int32 [2, 4], P('fsdp'), may hold values from 0 to 2, as said below
- memory: float32 [20, 768], replicated, may hold values from -6 to 6
- wq: bfloat16 [2, 768, 768], P(None, 'fsdp', 'tp'), may hold values from -0.5 to 0.5
- wk: bfloat16 [2, 768, 768], P(None, 'fsdp', 'tp'), may hold values from -0.21875 to 0.21875
- wv: bfloat16 [2, 768, 768], P(None, 'fsdp', 'tp'), may hold values from -0.21875 to 0.21875
- wo: bfloat16 [2, 768, 768], P(None, 'tp', 'fsdp'), may hold values from -0.625 to 0.625
- w1: bfloat16 [2, 768, 3072], P(None, 'fsdp', 'tp'), may hold values from -0.21875 to 0.21875
- w2: bfloat16 [2, 3072, 768], P(None, 'tp', 'fsdp'), may hold values from -0.109375 to 0.109375
- head_bias: float32 [2, 2, 768], P(None, None, 'tp'), may hold values from -3 to 3
- ffn_bias: float32 [2, 3072], P(None, 'tp'), may hold values from -3 to 3
- out_bias: float32 [2, 2, 768], replicated, may hold values from -3 to 3
- norm_gains: float32 [2, 2, 768], replicated, may hold values from 0.5 to 1.5
- norm_shifts: float32 [2, 2, 768], replicated, may hold values from -2 to 2
Outputs:
- output: bfloat16 [8192, 768], P(('fsdp', 'ctx', 'tp'))
- hidden_grad: bfloat16 [8192, 768], P(('fsdp', 'ctx', 'tp'))
- memory_grad: float32 [20, 768], replicated
- wq_grad: float32 [2, 768, 768], P(None, 'fsdp', 'tp')
- wk_grad: float32 [2, 768, 768], P(None, 'fsdp', 'tp')
- wv_grad: float32 [2, 768, 768], P(None, 'fsdp', 'tp')
- wo_grad: float32 [2, 768, 768], P(None, 'tp', 'fsdp')
- w1_grad: float32 [2, 768, 3072], P(None, 'fsdp', 'tp')
- w2_grad: float32 [2, 3072, 768], P(None, 'tp', 'fsdp')
- head_bias_grad: float32 [2, 2, 768], P(None, None, 'tp')
- ffn_bias_grad: float32 [2, 3072], P(None, 'tp')
- out_bias_grad: float32 [2, 2, 768], replicated
- norm_gains_grad: float32 [2, 2, 768], replicated
- norm_shifts_grad: float32 [2, 2, 768], replicated
The draws below stay inside these ranges and needn't reach their ends.
Inputs may be any that keep to these rules, and one draw needn't show every extreme that they name: `mem_pos`: in each segment the 10 read rows and 10 write rows sit at distinct positions; every segment has one memory row at position 0 and one at 1023. parents[t, 0] = 0 and every other segment's parent is an earlier segment; in one tree each segment's parent is the one before it.
All inputs are finite; a program needn't handle non-finite values.
Results may differ from the reference program's by a relative error of at most 0.035.
Values may be sent and summed in bfloat16 or wider, within the bound.
A program may use at most 192 MiB of HBM per device.

```python
import jax
import jax.numpy as jnp
from jax import lax

D = 768
HEADS = 12
HEAD = 64
FF = 3072
LAYERS = 2
MEM = 10
SEG = 1024
TREES = 2
TOKENS = 8192
N_CTX = 4


def draw_parents(key, part):
    raw_picks = jax.random.randint(jax.random.fold_in(key, 11), (TREES, N_CTX), 0, 1 << 20)
    segment_ids = jnp.arange(N_CTX, dtype=jnp.int32)
    parent_any = raw_picks % jnp.maximum(segment_ids, 1)[None, :]
    chain_tree = jax.random.randint(jax.random.fold_in(key, 12), (), 0, TREES)
    chain_row = jnp.maximum(segment_ids - 1, 0)
    chosen = jnp.arange(TREES, dtype=jnp.int32)[:, None] == chain_tree
    return jnp.where(chosen, chain_row[None, :], parent_any).astype(jnp.int32)


def draw_mem_pos(key, part):
    seg_keys = jax.random.split(jax.random.fold_in(key, 21), TREES * N_CTX)

    def one_segment(seg_key):
        first_key, second_key = jax.random.split(seg_key)
        interior = jax.random.permutation(first_key, SEG - 2)[:2 * MEM - 2].astype(jnp.int32) + 1
        chosen = jnp.concatenate([jnp.array([0, SEG - 1], jnp.int32), interior])
        return jax.random.permutation(second_key, chosen)
    return jax.vmap(one_segment)(seg_keys).reshape(TREES, N_CTX, 2 * MEM).astype(jnp.int32)


def block_scale(key, dims, shards, smallest, top_value):
    def one(axis_at, blocks):
        draws = jax.random.uniform(jax.random.fold_in(jax.random.fold_in(key, 6), axis_at), (blocks,), jnp.float32, smallest / len(shards), top_value / len(shards))
        return jnp.repeat(jnp.exp(draws), dims[axis_at] // blocks).reshape((-1,) + (1,) * (len(dims) - axis_at - 1))

    level = one(*shards[0])
    for cut in shards[1:]:
        level = level * one(*cut)
    return level


def centred(stream_key, extent, width, most, cuts=(), kind=jnp.bfloat16):
    values = jax.random.normal(stream_key, extent, jnp.float32) * width
    if len(cuts) > 0:
        values = block_scale(stream_key, extent, cuts, -0.22, 0.18) * values
    return jnp.clip(values, min=-most, max=most).astype(kind)


def setup_inputs(seed: int = 0) -> dict:
    splits = jax.random.split(jax.random.key(seed), 17)
    return {
        "hidden": centred(splits[0], (TOKENS, D), 1.0, 6.0, ((0, 32),)),
        "cotangent": centred(splits[1], (TOKENS, D), 1.0, 6.0, ((0, 32),)),
        "mem_pos": draw_mem_pos(jax.random.fold_in(splits[16], 71), 0),
        "parents": draw_parents(jax.random.fold_in(splits[16], 71), 0),
        "memory": centred(splits[4], (2 * MEM, D), 1.0, 6.0, (), jnp.float32),
        "wq": centred(splits[5], (LAYERS, D, D), (D // 6) ** -0.5, 0.5, ((1, 2), (2, 4))),
        "wk": centred(splits[6], (LAYERS, D, D), D ** -0.5, 0.21875, ((1, 2), (2, 4))),
        "wv": centred(splits[7], (LAYERS, D, D), D ** -0.5, 0.21875, ((1, 2), (2, 4))),
        "wo": centred(splits[8], (LAYERS, D, D), (D // 8) ** -0.5, 0.625, ((1, 4), (2, 2))),
        "w1": centred(splits[9], (LAYERS, D, FF), D ** -0.5, 0.21875, ((1, 2), (2, 4))),
        "w2": centred(splits[10], (LAYERS, FF, D), FF ** -0.5, 0.109375, ((1, 4), (2, 2))),
        "head_bias": centred(splits[11], (LAYERS, 2, D), 0.5, 3.0, ((2, 4),), jnp.float32),
        "ffn_bias": centred(splits[12], (LAYERS, FF), 0.5, 3.0, ((1, 4),), jnp.float32),
        "out_bias": centred(splits[13], (LAYERS, 2, D), 0.5, 3.0, (), jnp.float32),
        "norm_gains": jnp.clip(1.0 + 0.1 * jax.random.normal(splits[14], (LAYERS, 2, D), jnp.float32), 0.5, 1.5),
        "norm_shifts": centred(splits[15], (LAYERS, 2, D), 0.3, 2.0, (), jnp.float32),
    }


HIGHEST = lax.Precision.HIGHEST
EPSILON = 1e-05
MASKED = -1000000000.0

@jax.custom_vjp
def low(v):
    return lax.optimization_barrier(v.astype(jnp.bfloat16)).astype(jnp.float32)

@jax.custom_vjp
def low_back(v):
    return v

def low_keep(v):
    return (low(v), None)

def low_pass(kept, grad):
    return (grad,)

def back_keep(v):
    return (v, None)

def back_low(kept, grad):
    return (low(grad),)
low.defvjp(low_keep, low_pass)
low_back.defvjp(back_keep, back_low)

def matmul(left_side, right_side):
    return jnp.dot(left_side, right_side, precision=HIGHEST, preferred_element_type=jnp.float32)

def norm_rows(summed, gain_row, shift_row):
    row_mean = lax.optimization_barrier(jnp.mean(summed, axis=-1, keepdims=True))
    centered = summed - row_mean
    variance = lax.optimization_barrier(jnp.mean(centered * centered, axis=-1, keepdims=True))
    return centered * lax.rsqrt(variance + EPSILON) * gain_row + shift_row

def ancestry(parent_row):
    seg_count = parent_row.shape[0]
    segment_ids = jnp.arange(seg_count, dtype=jnp.int32)
    parent_hop = (parent_row[:, None] == segment_ids[None, :]).astype(jnp.int32)
    reached = (segment_ids[:, None] == segment_ids[None, :]).astype(jnp.int32)
    on_path = reached
    for hop_number in range(seg_count - 1):
        reached = jnp.dot(reached, parent_hop)
        on_path = jnp.maximum(on_path, reached)
    return on_path

def attend_block(queries, key_rows, value_rows, allowed):
    scores = jnp.einsum('qhe,khe->hqk', queries, key_rows, precision=HIGHEST)
    scores = jnp.where(allowed[None, None, :], low_back(scores), MASKED)
    biggest = lax.optimization_barrier(jnp.max(scores, axis=-1, keepdims=True))
    row_total = lax.optimization_barrier(jnp.sum(jnp.exp(scores - biggest), axis=-1, keepdims=True))
    log_total = biggest + jnp.log(row_total)
    probs = low(jnp.exp(scores - log_total))
    return jnp.einsum('hqk,khe->qhe', probs, value_rows, precision=HIGHEST)

def attention(queries, key_rows, value_rows, parents):
    tree_count = parents.shape[0]
    query_blocks = queries.reshape(tree_count * N_CTX, SEG, HEADS, HEAD)
    key_trees = key_rows.reshape(tree_count, N_CTX * SEG, HEADS, HEAD)
    value_trees = value_rows.reshape(tree_count, N_CTX * SEG, HEADS, HEAD)
    ancestors = jax.vmap(ancestry)(parents)
    allowed = jnp.repeat(ancestors, SEG, axis=2).reshape(tree_count * N_CTX, N_CTX * SEG) > 0
    owners = jnp.repeat(jnp.arange(tree_count, dtype=jnp.int32), N_CTX)

    def one_block(operands):
        block_query, block_allowed, tree_no = operands
        return attend_block(block_query, key_trees[tree_no], value_trees[tree_no], block_allowed)
    result = lax.map(jax.checkpoint(one_block), (query_blocks, allowed, owners))
    return result.reshape(tree_count * N_CTX * SEG, D)

def forward(hidden, memory, wq, wk, wv, wo, w1, w2, head_bias, ffn_bias, out_bias, norm_gains, norm_shifts, mem_pos, parents):
    positions = jnp.arange(SEG, dtype=jnp.int32)
    mem_marks = (mem_pos[:, :, None, :] == positions[None, None, :, None]).astype(jnp.float32)
    embedding = jnp.einsum('tcsm,md->tcsd', mem_marks, memory, precision=HIGHEST).reshape(-1, D)
    stream = hidden + embedding
    for layer_no in range(LAYERS):
        rounded = low(stream)
        queries = low(low_back((matmul(rounded, wq[layer_no]) + head_bias[layer_no, 0]) * 0.125))
        key_rows = low(low_back(matmul(rounded, wk[layer_no])))
        value_rows = low(low_back(matmul(rounded, wv[layer_no]) + head_bias[layer_no, 1]))
        attended = low(low_back(attention(queries, key_rows, value_rows, parents)))
        branch = low_back(matmul(attended, wo[layer_no]) + out_bias[layer_no, 0])
        stream = norm_rows(stream + branch, norm_gains[layer_no, 0], norm_shifts[layer_no, 0])
        rounded = low(stream)
        hidden_pre = low_back(matmul(rounded, w1[layer_no]) + ffn_bias[layer_no])
        active = low(jax.nn.gelu(hidden_pre, approximate=False))
        branch = low_back(matmul(active, w2[layer_no]) + out_bias[layer_no, 1])
        stream = norm_rows(stream + branch, norm_gains[layer_no, 1], norm_shifts[layer_no, 1])
    return stream

def reference(hidden, cotangent, mem_pos, parents, memory, wq, wk, wv, wo, w1, w2, head_bias, ffn_bias, out_bias, norm_gains, norm_shifts):
    floats = tuple((item.astype(jnp.float32) for item in (hidden, memory, wq, wk, wv, wo, w1, w2, head_bias, ffn_bias, out_bias, norm_gains, norm_shifts)))

    def wrapped(hidden_f, memory_f, wq_f, wk_f, wv_f, wo_f, w1_f, w2_f, head_f, ffn_f, out_f, gains_f, shifts_f):
        return forward(hidden_f, memory_f, wq_f, wk_f, wv_f, wo_f, w1_f, w2_f, head_f, ffn_f, out_f, gains_f, shifts_f, mem_pos, parents)
    result, pullback = jax.vjp(wrapped, *floats)
    grads = pullback(cotangent.astype(jnp.float32))
    return (result.astype(jnp.bfloat16), grads[0].astype(jnp.bfloat16), grads[1], grads[2], grads[3], grads[4], grads[5], grads[6], grads[7], grads[8], grads[9], grads[10], grads[11], grads[12])
```

```python
import functools

import jax
import jax.numpy as jnp
from jax import lax
from jax.experimental import pallas as pl
from jax.experimental.pallas import tpu as pltpu
from jax.sharding import PartitionSpec as P

HEAD = 64
EPSILON = 1e-05
MASKED = -1000000000.0
MESH = pl.DeviceIdType.MESH
F32 = jnp.float32
BF16 = jnp.bfloat16
NEAR = (0, 1)
ORDER = ((0, 1), (1, 0), (2, 2), (3, 3))


def mm(left, right):
    return jnp.dot(left, right, preferred_element_type=F32)


def mm_nt(left, right):
    return lax.dot_general(left, right, (((1,), (1,)), ((), ())), preferred_element_type=F32)


def mm_tn(left, right):
    return lax.dot_general(left, right, (((0,), (0,)), ((), ())), preferred_element_type=F32)


def rcopy(src, dst, send_sem, recv_sem, device):
    return pltpu.make_async_remote_copy(
        src_ref=src,
        dst_ref=dst,
        send_sem=send_sem,
        recv_sem=recv_sem,
        device_id=device,
        device_id_type=MESH,
    )


def mate_of(c):
    return c + 1 - 2 * (c % 2)


def across_of(c):
    return (c + 2) % 4


def signal(sem, device):
    pl.semaphore_signal(sem, inc=1, device_id=device, device_id_type=MESH)


def ordered(place, step):
    half = place // 2
    inner = place + half * (3 - 2 * place)
    first, second = ORDER[step]
    chunk = first + inner * (second - first)
    return chunk + half * (3 - 2 * chunk)


def dma(*shape):
    return pltpu.SemaphoreType.DMA(shape)


def call(kernel, out_shapes, scratch, collective_id, name, n_in, cost, vmem=None, smem=()):
    params = dict(vmem_limit_bytes=56 * 1024 * 1024)
    if collective_id is not None:
        params.update(collective_id=collective_id, has_side_effects=True)
    return pl.pallas_call(
        kernel,
        out_shape=out_shapes,
        in_specs=[
            pl.BlockSpec(memory_space=pltpu.SMEM if i in smem else pltpu.VMEM) for i in range(n_in)
        ],
        out_specs=[pl.BlockSpec(memory_space=pltpu.VMEM)] * len(out_shapes),
        scratch_shapes=scratch,
        compiler_params=pltpu.CompilerParams(**params),
        cost_estimate=pl.CostEstimate(flops=cost[0], bytes_accessed=cost[1], transcendentals=cost[2]),
        name=name,
    )


def sds(*shape, dtype=BF16):
    return jax.ShapeDtypeStruct(shape, dtype)


def project_kernel(
    x_ref, w_ref, b_ref, xg_ref, qw_ref, kv_ref,
    qbuf, x_recv, x_right, x_left, k1_send, k1_recv, k2_send, k2_recv, kf_send, kf_recv, q_send, q_recv,
):
    c = lax.axis_index("ctx")
    t = lax.axis_index("tp")
    barrier = pltpu.get_barrier_semaphore()
    for device in (mate_of(c), across_of(c), 3 - c):
        signal(barrier, {"ctx": device})

    @pl.when(t > 0)
    def _():
        signal(barrier, {"tp": t - 1})

    @pl.when(t < 3)
    def _():
        signal(barrier, {"tp": t + 1})

    ends = (t // 3) + (3 - t) // 3
    pl.semaphore_wait(barrier, 5 - ends)

    def right(src, chunk, step):
        return rcopy(src, xg_ref.at[chunk], x_right.at[step], x_recv.at[chunk], {"tp": t + 1})

    def left(src, chunk, step):
        return rcopy(src, xg_ref.at[chunk], x_left.at[step], x_recv.at[chunk], {"tp": t - 1})

    def arrived(chunk):
        rcopy(xg_ref.at[chunk], xg_ref.at[chunk], x_right.at[0], x_recv.at[chunk], {"tp": t}).wait_recv()

    @pl.when(t < 3)
    def _():
        right(x_ref, t, 0).start()

    @pl.when(t > 0)
    def _():
        left(x_ref, t, 0).start()

    def mate(chunk):
        return rcopy(kv_ref.at[c, chunk], kv_ref.at[c, chunk], k1_send.at[chunk], k1_recv.at[chunk], {"ctx": mate_of(c)})

    def across(chunk):
        return rcopy(kv_ref.at[c, chunk], kv_ref.at[c, chunk], k2_send.at[chunk], k2_recv.at[chunk], {"ctx": across_of(c)})

    def onward(chunk):
        return rcopy(
            kv_ref.at[across_of(c), chunk], kv_ref.at[across_of(c), chunk], kf_send.at[chunk], kf_recv.at[chunk], {"ctx": mate_of(c)}
        )

    def partner(slot):
        return rcopy(qbuf.at[slot], qw_ref.at[slot + 2], q_send.at[slot], q_recv.at[slot], {"ctx": 3 - c})

    for step in range(4):
        if step == 0:
            xg_ref[t] = x_ref[...]
        else:

            @pl.when(t - step >= 0)
            def _():
                arrived(t - step)

                @pl.when(t < 3)
                def _():
                    right(xg_ref.at[t - step], t - step, step).start()

            @pl.when(t + step <= 3)
            def _():
                arrived(t + step)

                @pl.when(t > 0)
                def _():
                    left(xg_ref.at[t + step], t + step, step).start()

        chunk = ordered(t, step)
        made = mm(xg_ref[chunk], w_ref[...]) + b_ref[...]
        kv_ref[c, chunk] = made[:, 256:].astype(BF16)
        mate(chunk).start()
        across(chunk).start()
        query = (made[:, :256] * 0.125).astype(BF16)

        @pl.when(chunk < 2)
        def _():
            qw_ref[chunk] = query

        @pl.when(chunk >= 2)
        def _():
            qbuf[chunk - 2] = query
            partner(chunk - 2).start()

        if step >= 1:
            before = ordered(t, step - 1)
            across(before).wait_recv()
            onward(before).start()
    last = ordered(t, 3)
    across(last).wait_recv()
    onward(last).start()
    for chunk in range(4):
        mate(chunk).wait()
        across(chunk).wait_send()
        onward(chunk).wait()
    for slot in range(2):
        partner(slot).wait()

    @pl.when(t < 3)
    def _():
        right(x_ref, t, 0).wait_send()

    @pl.when(t > 0)
    def _():
        left(x_ref, t, 0).wait_send()

    for step in (1, 2):

        @pl.when((t - step >= 0) & (t < 3))
        def _():
            right(xg_ref.at[t - step], t - step, step).wait_send()

        @pl.when((t + step <= 3) & (t > 0))
        def _():
            left(xg_ref.at[t + step], t + step, step).wait_send()


def project(x, w, b, cid):
    outs = [sds(4, 256, 768), sds(4, 256, 256), sds(4, 4, 256, 384)]
    scratch = [
        pltpu.VMEM((2, 256, 256), BF16),
        dma(4), dma(3), dma(3),
        dma(4), dma(4), dma(4), dma(4), dma(4), dma(4), dma(2), dma(2),
    ]
    xg, qw, kv = call(project_kernel, outs, scratch, cid, "project", 3, (2 * 1024 * 768 * 640, 8 << 20, 0))(x, w, b)
    return xg.reshape(1024, 768), qw.reshape(1024, 256), kv.reshape(4, 1024, 384)


def norm_stats(summed):
    row_mean = jnp.mean(summed, axis=-1, keepdims=True)
    centered = summed - row_mean
    variance = jnp.mean(centered * centered, axis=-1, keepdims=True)
    scale = lax.rsqrt(variance + EPSILON)
    return centered * scale, scale


def norm_back(grad, xhat, scale, gain):
    scaled = grad * gain
    first = jnp.mean(scaled, axis=-1, keepdims=True)
    second = jnp.mean(scaled * xhat, axis=-1, keepdims=True)
    return scale * (scaled - first - xhat * second)


def gelu_both(up):
    phi = 0.5 * (1.0 + lax.erf(up * 0.7071067811865476))
    slope = phi + up * jnp.exp(-0.5 * up * up) * 0.3989422804014327
    return (up * phi).astype(BF16), slope.astype(BF16)


Q_TILE = 256
K_TILE = 256


def attend_kernel(flag_ref, qw_ref, kv_ref, o_ref, lse_ref, qm_ref, m_ref, l_ref, acc_ref):
    c = lax.axis_index("ctx")
    low = lax.broadcasted_iota(jnp.int32, (Q_TILE, 128), 1) < 64
    per_half = 512 // Q_TILE

    @pl.loop(0, 1024 // Q_TILE)
    def _(tile):
        half = tile // per_half
        segment = c + half * (3 - 2 * c)
        rows = pl.ds(pl.multiple_of(tile * Q_TILE, Q_TILE), Q_TILE)
        pair = qw_ref[rows, 0:128]
        qm_ref[0] = jnp.where(low, pair, jnp.zeros_like(pair))
        qm_ref[1] = jnp.where(low, jnp.zeros_like(pair), pair)
        qm_ref[2] = qw_ref[rows, 128:256]
        m_ref[...] = jnp.full_like(m_ref, MASKED)
        l_ref[...] = jnp.zeros_like(l_ref)
        acc_ref[...] = jnp.zeros_like(acc_ref)

        @pl.loop(0, segment + 1)
        def _(block):
            @pl.when(flag_ref[half, block] > 0)
            def _():
                keys = pl.ds(pl.multiple_of(block * 1024, 1024), 1024)
                for head in range(3):
                    k_at = 0 if head < 2 else 128
                    v_at = 256 if head < 2 else 128
                    scores = mm_nt(qm_ref[head], kv_ref[keys, k_at : k_at + 128])
                    old = m_ref[head]
                    new = jnp.maximum(old, jnp.max(scores, axis=-1, keepdims=True))
                    probs = jnp.exp(scores - new)
                    keep = jnp.exp(old - new)
                    m_ref[head] = new
                    l_ref[head] = l_ref[head] * keep + jnp.sum(probs, axis=-1, keepdims=True)
                    acc_ref[head] = acc_ref[head] * keep + mm(
                        probs.astype(BF16), kv_ref[keys, v_at : v_at + 128]
                    )

        first = acc_ref[0] / l_ref[0]
        second = acc_ref[1] / l_ref[1]
        o_ref[rows, 0:128] = jnp.where(low, first, second).astype(BF16)
        o_ref[rows, 128:192] = (acc_ref[2] / l_ref[2])[:, :64].astype(BF16)
        lane = lax.broadcasted_iota(jnp.int32, (Q_TILE, 128), 1)
        totals = [m_ref[head] + jnp.log(l_ref[head]) for head in range(3)]
        lse_ref[rows, :] = jnp.where(lane == 0, totals[0], jnp.where(lane == 1, totals[1], totals[2]))


def attend(qw, kv, flags):
    outs = [sds(1024, 192), sds(1024, 128, dtype=F32)]
    scratch = [
        pltpu.VMEM((3, Q_TILE, 128), BF16),
        pltpu.VMEM((3, Q_TILE, 1), F32),
        pltpu.VMEM((3, Q_TILE, 1), F32),
        pltpu.VMEM((3, Q_TILE, 128), F32),
    ]
    cost = (5 * 512 * 1024 * 64 * 4 * 3, 6 << 20, 5 * 512 * 1024 * 3)
    return call(attend_kernel, outs, scratch, None, "attend", 3, cost, smem=(0,))(
        flags, qw, kv.reshape(4096, 384)
    )


def attend_back_kernel(
    flag_ref, qw_ref, kv_ref, do_ref, o_ref, lse_ref, dq_ref, dkv_ref,
    qm_ref, dm_ref, row_ref, acc_ref, key_ref,
):
    c = lax.axis_index("ctx")
    low = lax.broadcasted_iota(jnp.int32, (1024, 128), 1) < 64
    pair = qw_ref[:, 0:128]
    none = jnp.zeros_like(pair)
    qm_ref[0] = jnp.where(low, pair, none)
    qm_ref[1] = jnp.where(low, none, pair)
    qm_ref[2] = qw_ref[:, 128:256]
    pair = do_ref[:, 0:128]
    dm_ref[0] = jnp.where(low, pair, none)
    dm_ref[1] = jnp.where(low, none, pair)
    dm_ref[2] = jnp.concatenate([do_ref[:, 128:192], none[:, :64]], axis=1)
    turned = jnp.transpose(lse_ref[...], (1, 0))
    row_ref[0:8] = turned[0:8]
    product = do_ref[...].astype(F32) * o_ref[...].astype(F32)
    head_row = lax.broadcasted_iota(jnp.int32, (8, 192), 0)
    head_of = lax.broadcasted_iota(jnp.int32, (8, 192), 1) // 64
    marks = (head_row == head_of).astype(F32)
    row_ref[8:16] = lax.dot_general(
        marks, product, (((1,), (1,)), ((), ())),
        precision=lax.Precision.HIGHEST, preferred_element_type=F32,
    )
    acc_ref[...] = jnp.zeros_like(acc_ref)
    low_keys = lax.broadcasted_iota(jnp.int32, (K_TILE, 128), 1) < 64

    @pl.loop(0, 4)
    def _(block):
        @pl.loop(0, 1024 // K_TILE)
        def _(tile):
            keys = pl.ds(pl.multiple_of(block * 1024 + tile * K_TILE, K_TILE), K_TILE)
            key_ref[...] = jnp.zeros_like(key_ref)
            key_pair = kv_ref[keys, 0:128]
            nothing = jnp.zeros_like(key_pair)
            key_parts = (
                jnp.where(low_keys, key_pair, nothing),
                jnp.where(low_keys, nothing, key_pair),
                jnp.where(low_keys, nothing, kv_ref[keys, 128:256]),
            )
            for half in range(2):
                segment = c if half == 0 else 3 - c

                @pl.when((block <= segment) & (flag_ref[half, block] > 0))
                def _():
                    rows = pl.ds(half * 512, 512)
                    for head in range(3):
                        k_at = 0 if head < 2 else 128
                        v_at = 256 if head < 2 else 128
                        query = qm_ref[head, rows]
                        grads = dm_ref[head, rows]
                        scores = mm_nt(kv_ref[keys, k_at : k_at + 128], query)
                        probs = jnp.exp(scores - row_ref[head : head + 1, rows])
                        grad_probs = mm_nt(kv_ref[keys, v_at : v_at + 128], grads)
                        grad_scores = (probs * (grad_probs - row_ref[8 + head : 9 + head, rows])).astype(BF16)
                        key_ref[:, v_at : v_at + 128] += mm(probs.astype(BF16), grads)
                        key_ref[:, k_at : k_at + 128] += mm(grad_scores, query)
                        q_at = 0 if head < 2 else 128
                        acc_ref[rows, q_at : q_at + 128] += mm_tn(grad_scores, key_parts[head])

            dkv_ref[keys, :] = key_ref[...].astype(BF16)

    dq_ref[...] = (acc_ref[...].astype(BF16).astype(F32) * 0.125).astype(BF16)


def attend_back(qw, kv, do, o, lse, flags):
    outs = [sds(1024, 256), sds(4096, 384)]
    scratch = [
        pltpu.VMEM((3, 1024, 128), BF16),
        pltpu.VMEM((3, 1024, 128), BF16),
        pltpu.VMEM((16, 1024), F32),
        pltpu.VMEM((1024, 256), F32),
        pltpu.VMEM((K_TILE, 384), F32),
    ]
    cost = (5 * 512 * 1024 * 64 * 10 * 3, 12 << 20, 5 * 512 * 1024 * 3)
    dq, dkv = call(attend_back_kernel, outs, scratch, None, "attend_back", 6, cost, smem=(0,))(
        flags, qw, kv.reshape(4096, 384), do, o, lse
    )
    return dq, dkv.reshape(4, 1024, 384)


def block_kernel(
    o_ref, wo_ref, w1_ref, w2_ref, b1_ref, vec_ref, stream_ref,
    out_ref, low_ref, xhat1_ref, r1_ref, xhat2_ref, r2_ref, xg_ref, act_ref, slope_ref, rows_ref,
    mine_ref, send_ref, got_ref, o_send, o_recv, a_send, a_recv, s_send, s_recv,
):
    c = lax.axis_index("ctx")
    t = lax.axis_index("tp")
    barrier = pltpu.get_barrier_semaphore()
    for place in range(4):

        @pl.when((t < 2) & (t != place))
        def _():
            signal(barrier, {"tp": place})

        @pl.when(t >= 2)
        def _():
            signal(barrier, {"ctx": 3 - c, "tp": place})

    signal(barrier, {"ctx": mate_of(c)})
    signal(barrier, {"ctx": across_of(c)})
    pl.semaphore_wait(barrier, 5 + t // 2)

    def give(quarter):
        device = {"tp": quarter} if quarter < 2 else {"ctx": 3 - c, "tp": quarter}
        return rcopy(o_ref.at[quarter], rows_ref.at[t], o_send.at[quarter], o_recv.at[t], device)

    def given(group):
        rcopy(rows_ref.at[group], rows_ref.at[group], o_send.at[0], o_recv.at[group], {"tp": t}).wait_recv()

    for quarter in (3, 2, 1, 0):
        if quarter < 2:

            @pl.when(t != quarter)
            def _():
                give(quarter).start()

            @pl.when(t == quarter)
            def _():
                rows_ref[quarter] = o_ref[quarter]

        else:
            give(quarter).start()
    branch = stream_ref[...] + vec_ref[0:1]
    for group in range(4):

        @pl.when((t >= 2) | (t != group))
        def _():
            given(group)

        branch += mm(rows_ref[group], wo_ref[group * 192 : (group + 1) * 192])
    xhat, scale = norm_stats(branch)
    xhat1_ref[...] = xhat
    r1_ref[...] = jnp.broadcast_to(scale, r1_ref.shape)
    normed = xhat * vec_ref[2:3] + vec_ref[3:4]
    xg_ref[c] = normed.astype(BF16)
    mate, across, far = mate_of(c), across_of(c), 3 - c

    def gather(slot, index, device):
        return rcopy(xg_ref.at[slot], xg_ref.at[slot], a_send.at[index], a_recv.at[index], {"ctx": device})

    gather(c, 1, across).start()
    gather(c, 0, mate).start()

    def feed(segment):
        up = mm(xg_ref[segment], w1_ref[...]) + b1_ref[...]
        act, slope = gelu_both(up)
        act_ref[segment] = act
        slope_ref[segment] = slope
        return mm(act, w2_ref[...])

    mine_ref[...] = feed(c) + normed + vec_ref[1:2]
    gather(mate, 0, mate).wait_recv()

    def scatter(index, device):
        return rcopy(send_ref.at[index], got_ref.at[index], s_send.at[index], s_recv.at[index], {"ctx": device})

    send_ref[0] = feed(mate).astype(BF16)
    scatter(0, mate).start()
    gather(across, 1, across).wait_recv()
    gather(across, 2, mate).start()
    own_across = feed(across)
    gather(far, 2, mate).wait_recv()
    send_ref[1] = feed(far).astype(BF16)
    scatter(1, mate).start()
    scatter(1, mate).wait_recv()
    send_ref[2] = (own_across + got_ref[1].astype(F32)).astype(BF16)
    scatter(2, across).start()
    scatter(0, mate).wait_recv()
    scatter(2, across).wait_recv()
    summed = mine_ref[...] + got_ref[0].astype(F32) + got_ref[2].astype(F32)
    xhat, scale = norm_stats(summed)
    xhat2_ref[...] = xhat
    r2_ref[...] = jnp.broadcast_to(scale, r2_ref.shape)
    out = xhat * vec_ref[4:5] + vec_ref[5:6]
    out_ref[...] = out
    low_ref[...] = out.astype(BF16)
    for quarter in range(4):
        if quarter < 2:

            @pl.when(t != quarter)
            def _():
                give(quarter).wait_send()

        else:
            give(quarter).wait_send()
    gather(c, 0, mate).wait_send()
    gather(c, 1, across).wait_send()
    gather(across, 2, mate).wait_send()
    for index in range(3):
        scatter(index, mate).wait_send()


def block(o, wo, w1, w2, b1, vecs, stream, cid):
    f = functools.partial(sds, dtype=F32)
    outs = [
        f(256, 768), sds(256, 768), f(256, 768), f(256, 128), f(256, 768), f(256, 128),
        sds(4, 256, 768), sds(4, 256, 768), sds(4, 256, 768), sds(4, 256, 192),
    ]
    scratch = [
        pltpu.VMEM((256, 768), F32),
        pltpu.VMEM((3, 256, 768), BF16),
        pltpu.VMEM((3, 256, 768), BF16),
        dma(4), dma(4), dma(3), dma(3), dma(3), dma(3),
    ]
    cost = (2 * 256 * 768 * 768 + 4 * 1024 * 768 * 768, 16 << 20, 1 << 20)
    res = call(block_kernel, outs, scratch, cid, "block", 7, cost)(
        o.reshape(4, 256, 192), wo, w1, w2, b1, vecs, stream
    )
    flat = lambda a: a.reshape(1024, 768)
    return tuple(res[:6]) + (flat(res[6]), flat(res[7]), flat(res[8]), res[9])


def block_back_kernel(
    grad_ref, xhat2_ref, r2_ref, xhat1_ref, r1_ref, vec_ref, slope_ref, w1_ref, w2_ref, wo_ref,
    gg_ref, gu_ref, back_ref, g1_ref, do_ref, stat_ref,
    mine_ref, send_ref, got_ref, dsend_ref, d_send, d_recv, a_send, a_recv, s_send, s_recv,
):
    c = lax.axis_index("ctx")
    t = lax.axis_index("tp")
    barrier = pltpu.get_barrier_semaphore()
    for place in range(4):
        if place < 2:

            @pl.when(t != place)
            def _():
                signal(barrier, {"tp": place})

        else:
            signal(barrier, {"ctx": 3 - c, "tp": place})
    signal(barrier, {"ctx": mate_of(c)})
    signal(barrier, {"ctx": across_of(c)})
    pl.semaphore_wait(barrier, 5 + t // 2)
    mate, across, far = mate_of(c), across_of(c), 3 - c

    def row(values):
        return jnp.sum(values, axis=0, keepdims=True)

    grad = grad_ref[...]
    back_two = norm_back(grad, xhat2_ref[...], r2_ref[:, 0:1], vec_ref[4:5])
    g2 = back_two.astype(BF16)
    gg_ref[c] = g2

    def gather(slot, index, device):
        return rcopy(gg_ref.at[slot], gg_ref.at[slot], a_send.at[index], a_recv.at[index], {"ctx": device})

    gather(c, 1, across).start()
    gather(c, 0, mate).start()
    stat_ref[1:2] = row(grad * xhat2_ref[...])
    stat_ref[3:4] = row(grad)
    stat_ref[5:6] = row(g2.astype(F32))
    stat_ref[7:8] = jnp.zeros((1, 768), F32)

    def feed(segment):
        gu = (mm_nt(gg_ref[segment], w2_ref[...]) * slope_ref[segment].astype(F32)).astype(BF16)
        gu_ref[segment] = gu
        return mm_nt(gu, w1_ref[...]), row(gu.astype(F32))

    part, bias = feed(c)
    mine_ref[...] = part + back_two
    gather(mate, 0, mate).wait_recv()

    def scatter(index, device):
        return rcopy(send_ref.at[index], got_ref.at[index], s_send.at[index], s_recv.at[index], {"ctx": device})

    part, more = feed(mate)
    bias += more
    send_ref[0] = part.astype(BF16)
    scatter(0, mate).start()
    gather(across, 1, across).wait_recv()
    gather(across, 2, mate).start()
    own_across, more = feed(across)
    bias += more
    gather(far, 2, mate).wait_recv()
    part, more = feed(far)
    bias += more
    stat_ref[6:7] = bias
    send_ref[1] = part.astype(BF16)
    scatter(1, mate).start()
    scatter(1, mate).wait_recv()
    send_ref[2] = (own_across + got_ref[1].astype(F32)).astype(BF16)
    scatter(2, across).start()
    scatter(0, mate).wait_recv()
    scatter(2, across).wait_recv()
    grad_normed = mine_ref[...] + got_ref[0].astype(F32) + got_ref[2].astype(F32)
    back_one = norm_back(grad_normed, xhat1_ref[...], r1_ref[:, 0:1], vec_ref[2:3])
    back_ref[...] = back_one
    g1 = back_one.astype(BF16)
    g1_ref[...] = g1

    def give_near(group):
        return rcopy(dsend_ref.at[group], do_ref.at[t], d_send.at[group], d_recv.at[t], {"tp": group})

    def give_far(group):
        return rcopy(dsend_ref.at[group], do_ref.at[t], d_send.at[group], d_recv.at[t], {"ctx": 3 - c, "tp": group})

    for group in range(4):
        dsend_ref[group] = mm_nt(g1, wo_ref[group * 192 : (group + 1) * 192]).astype(BF16)

        @pl.when((t < 2) & (t == group))
        def _():
            do_ref[t] = dsend_ref[group]

        @pl.when((t < 2) & (t != group))
        def _():
            give_near(group).start()

        @pl.when(t >= 2)
        def _():
            give_far(group).start()

    stat_ref[0:1] = row(grad_normed * xhat1_ref[...])
    stat_ref[2:3] = row(grad_normed)
    stat_ref[4:5] = row(g1.astype(F32))
    for quarter in range(4):

        def taken():
            rcopy(do_ref.at[quarter], do_ref.at[quarter], d_send.at[0], d_recv.at[quarter], {"tp": t}).wait_recv()

        if quarter < 2:
            pl.when(t != quarter)(taken)
        else:
            taken()
    for group in range(4):

        @pl.when((t >= 2) | (t != group))
        def _():
            give_near(group).wait_send()

    gather(c, 0, mate).wait_send()
    gather(c, 1, across).wait_send()
    gather(across, 2, mate).wait_send()
    for index in range(3):
        scatter(index, mate).wait_send()


def block_back(grad, xhat2, r2, xhat1, r1, vecs, slope, w1, w2, wo, cid):
    f = functools.partial(sds, dtype=F32)
    outs = [sds(4, 256, 768), sds(4, 256, 768), f(256, 768), sds(256, 768), sds(4, 256, 192), f(8, 768)]
    scratch = [
        pltpu.VMEM((256, 768), F32),
        pltpu.VMEM((3, 256, 768), BF16),
        pltpu.VMEM((3, 256, 768), BF16),
        pltpu.VMEM((4, 256, 192), BF16),
        dma(4), dma(4), dma(3), dma(3), dma(3), dma(3),
    ]
    cost = (2 * 256 * 768 * 768 + 4 * 1024 * 768 * 768, 16 << 20, 1 << 10)
    gg, gu, back, g1, do, stats = call(block_back_kernel, outs, scratch, cid, "block_back", 10, cost)(
        grad, xhat2, r2, xhat1, r1, vecs, slope.reshape(4, 256, 768), w1, w2, wo
    )
    return gg.reshape(1024, 768), gu.reshape(1024, 768), back, g1, do.reshape(1024, 192), stats


def project_back_kernel(
    dqw_ref, dkv_ref, w_ref, back_ref, dq_ref, own_ref, grad_ref,
    part_ref, near_ref, join_ref, sum_ref, far_ref, pass_ref, take_ref,
    q_send, q_recv, n_send, n_recv, j_send, j_recv, f_send, f_recv, p_send, p_recv,
):
    c = lax.axis_index("ctx")
    t = lax.axis_index("tp")
    barrier = pltpu.get_barrier_semaphore()
    for device in (mate_of(c), across_of(c), 3 - c):
        signal(barrier, {"ctx": device})

    @pl.when(t > 0)
    def _():
        signal(barrier, {"tp": t - 1})

    @pl.when(t < 3)
    def _():
        signal(barrier, {"tp": t + 1})

    ends = (t // 3) + (3 - t) // 3
    pl.semaphore_wait(barrier, 5 - ends)
    mate, across, far = mate_of(c), across_of(c), 3 - c

    def partner(slot):
        return rcopy(dqw_ref.at[slot + 2], dq_ref.at[slot + 2], q_send.at[slot], q_recv.at[slot], {"ctx": far})

    def near(chunk):
        return rcopy(dkv_ref.at[mate, chunk], near_ref.at[chunk], n_send.at[chunk], n_recv.at[chunk], {"ctx": mate})

    def join(chunk):
        return rcopy(dkv_ref.at[far, chunk], join_ref.at[chunk], j_send.at[chunk], j_recv.at[chunk], {"ctx": mate})

    def cross(chunk):
        return rcopy(sum_ref.at[chunk], far_ref.at[chunk], f_send.at[chunk], f_recv.at[chunk], {"ctx": across})

    chunks = [ordered(t, 3 - k) for k in range(4)]
    for chunk in chunks:
        join(chunk).start()
    for slot in range(2):
        partner(slot).start()
    for chunk in chunks:
        near(chunk).start()
    for quarter in range(2):
        dq_ref[quarter] = dqw_ref[quarter]
    for chunk in chunks:
        join(chunk).wait_recv()
        sum_ref[chunk] = (dkv_ref[across, chunk].astype(F32) + join_ref[chunk].astype(F32)).astype(BF16)
        cross(chunk).start()

    def lower(chunk):
        return rcopy(pass_ref.at[chunk], take_ref.at[0, chunk], p_send.at[chunk], p_recv.at[0, chunk], {"tp": t - 1})

    def upper(chunk):
        return rcopy(pass_ref.at[chunk], take_ref.at[1, chunk], p_send.at[chunk], p_recv.at[1, chunk], {"tp": t + 1})

    def passed(side, chunk):
        rcopy(
            take_ref.at[side, chunk], take_ref.at[side, chunk], p_send.at[0], p_recv.at[side, chunk], {"tp": t}
        ).wait_recv()

    def relay(chunk):
        @pl.when(chunk < t)
        def _():
            @pl.when(t < 3)
            def _():
                passed(0, chunk)
                pass_ref[chunk] = (part_ref[chunk] + take_ref[0, chunk].astype(F32)).astype(BF16)

            @pl.when(t == 3)
            def _():
                pass_ref[chunk] = part_ref[chunk].astype(BF16)

            lower(chunk).start()

        @pl.when(chunk > t)
        def _():
            @pl.when(t > 0)
            def _():
                passed(1, chunk)
                pass_ref[chunk] = (part_ref[chunk] + take_ref[1, chunk].astype(F32)).astype(BF16)

            @pl.when(t == 0)
            def _():
                pass_ref[chunk] = part_ref[chunk].astype(BF16)

            upper(chunk).start()

    at_end = (t == 0) | (t == 3)
    for step, chunk in enumerate(chunks):

        @pl.when(chunk >= 2)
        def _():
            partner(chunk - 2).wait_recv()

        near(chunk).wait_recv()
        cross(chunk).wait_recv()
        own = (
            dkv_ref[c, chunk].astype(F32) + near_ref[chunk].astype(F32) + far_ref[chunk].astype(F32)
        ).astype(BF16)
        own_ref[chunk] = own
        part_ref[chunk] = mm_nt(dq_ref[chunk], w_ref[:, 0:256]) + mm_nt(own, w_ref[:, 256:640])
        if step < 3:

            @pl.when(at_end)
            def _():
                relay(chunk)

    for chunk in chunks[:3]:

        @pl.when(jnp.logical_not(at_end))
        def _():
            relay(chunk)

    grad_ref[...] = part_ref[t] + back_ref[...]

    @pl.when(t < 3)
    def _():
        passed(0, t)
        grad_ref[...] += take_ref[0, t].astype(F32)

    @pl.when(t > 0)
    def _():
        passed(1, t)
        grad_ref[...] += take_ref[1, t].astype(F32)

    for chunk in range(4):
        join(chunk).wait_send()
        near(chunk).wait_send()
        cross(chunk).wait_send()

        @pl.when(t != chunk)
        def _():
            upper(chunk).wait_send()

    for slot in range(2):
        partner(slot).wait_send()


def project_back(dqw, dkv, w, back_one, cid):
    outs = [sds(4, 256, 256), sds(4, 256, 384), sds(256, 768, dtype=F32)]
    scratch = [
        pltpu.VMEM((4, 256, 768), F32),
        pltpu.VMEM((4, 256, 384), BF16), pltpu.VMEM((4, 256, 384), BF16),
        pltpu.VMEM((4, 256, 384), BF16), pltpu.VMEM((4, 256, 384), BF16),
        pltpu.VMEM((4, 256, 768), BF16), pltpu.VMEM((2, 4, 256, 768), BF16),
        dma(2), dma(2), dma(4), dma(4), dma(4), dma(4), dma(4), dma(4), dma(4), dma(2, 4),
    ]
    cost = (2 * 1024 * 768 * 640, 8 << 20, 0)
    dq, own, grad = call(project_back_kernel, outs, scratch, cid, "project_back", 4, cost)(
        dqw.reshape(4, 256, 256), dkv.reshape(4, 4, 256, 384), w, back_one
    )
    return dq.reshape(1024, 256), own.reshape(1024, 384), grad


FLIP = (0, 2, 1, 3)


def ancestry(parent_row):
    seg_count = parent_row.shape[0]
    segment_ids = jnp.arange(seg_count, dtype=jnp.int32)
    parent_hop = (parent_row[:, None] == segment_ids[None, :]).astype(jnp.int32)
    reached = (segment_ids[:, None] == segment_ids[None, :]).astype(jnp.int32)
    on_path = reached
    for hop_number in range(seg_count - 1):
        reached = jnp.dot(reached, parent_hop)
        on_path = jnp.maximum(on_path, reached)
    return on_path


def flip_units(values):
    pairs = [(c * 4 + t, c * 4 + (t ^ FLIP[c])) for c in range(4) for t in range(4)]
    return lax.ppermute(values, ("ctx", "tp"), pairs)


def joined(query, key, value, gap):
    return jnp.concatenate(
        [
            query[..., :128], gap, query[..., 128:],
            key[..., :128], value[..., 128:], key[..., 128:], value[..., :128],
        ],
        axis=-1,
    )


def parted(grads):
    query = jnp.concatenate([grads[..., :128], grads[..., 192:256]], axis=-1)
    key = jnp.concatenate([grads[..., 256:384], grads[..., 448:512]], axis=-1)
    value = jnp.concatenate([grads[..., 512:640], grads[..., 384:448]], axis=-1)
    return query, key, value


def shards(
    hidden, cotangent, mem_pos, parents, memory, wq, wk, wv, wo, w1, w2,
    head_bias, ffn_bias, out_bias, norm_gains, norm_shifts,
):
    c = lax.axis_index("ctx")
    t = lax.axis_index("tp")
    layers = wq.shape[0]
    share_rows = hidden.shape[0]
    positions = t * share_rows + jnp.arange(share_rows, dtype=jnp.int32)
    marks = (mem_pos[0, 0][None, :] == positions[:, None]).astype(F32)
    stream = hidden.astype(F32) + jnp.dot(
        marks, memory, precision=lax.Precision.HIGHEST, preferred_element_type=F32
    )
    on_path = ancestry(parents[0])
    ids = jnp.arange(4, dtype=jnp.int32)
    pick = lambda seg: jnp.sum(on_path * (ids == seg).astype(jnp.int32)[:, None], axis=0)
    flags = jnp.stack([pick(c), pick(3 - c)])

    gap = jnp.zeros(wq.shape[:2] + (64,), BF16)
    local_in = joined(wq, wk, wv, gap)
    zeros = jnp.zeros((layers, 64), F32)
    none = jnp.zeros((layers, 192), F32)
    in_bias = joined(head_bias[:, 0], none, head_bias[:, 1], zeros)
    w1_flip = flip_units(w1)
    w2_flip = flip_units(w2)
    ffn_flip = flip_units(ffn_bias)
    piece = wo.shape[1] // 4
    wo_piece = lax.dynamic_slice_in_dim(wo, c * piece, piece, axis=1)
    weights = []
    for n in range(layers):
        w_in = lax.all_gather(local_in[n], "fsdp", axis=0, tiled=True)
        w_up = lax.all_gather(w1_flip[n], "fsdp", axis=0, tiled=True)
        w_down = lax.all_gather(w2_flip[n], "fsdp", axis=1, tiled=True)
        w_out = lax.all_gather(wo_piece[n], "fsdp", axis=1, tiled=True)
        w_out = lax.all_gather(w_out[None], "tp", axis=0, tiled=True)
        w_out = lax.all_gather(w_out, "ctx", axis=1, tiled=True).reshape(768, 768)
        vecs = jnp.concatenate(
            [
                out_bias[n],
                jnp.stack([norm_gains[n, 0], norm_shifts[n, 0], norm_gains[n, 1], norm_shifts[n, 1]]),
                jnp.zeros((2, 768), F32),
            ]
        )
        weights.append((w_in, w_up, w_down, w_out, vecs))
    saved = []
    rounded = stream.astype(BF16)
    for n in range(layers):
        w_in, w_up, w_down, w_out, vecs = weights[n]
        xg, qw, kv = project(rounded, w_in, in_bias[n][None], 8 * n)
        o, lse = attend(qw, kv, flags)
        stream, rounded, xhat1, r1, xhat2, r2, xg2, act, slope, rows = block(
            o, w_out, w_up, w_down, ffn_flip[n][None], vecs, stream, 8 * n + 1
        )
        saved.append((xg, qw, kv, o, lse, xhat1, r1, xhat2, r2, xg2, act, slope, rows))
    output = rounded
    grad = cotangent.astype(F32)
    matrix = [None] * layers
    small = [None] * layers
    heads = [None] * layers
    for n in reversed(range(layers)):
        w_in, w_up, w_down, w_out, vecs = weights[n]
        xg, qw, kv, o, lse, xhat1, r1, xhat2, r2, xg2, act, slope, rows = saved[n]
        gg, gu, back_one, g1, do, stats = block_back(
            grad, xhat2, r2, xhat1, r1, vecs, slope, w_up, w_down, w_out, 8 * n + 2
        )
        small[n] = stats
        d_up = mm_tn(xg2, gu).astype(BF16)
        d_down = mm_tn(act, gg).astype(BF16)
        d_out = jnp.stack([mm_tn(rows[g], g1) for g in range(4)]).astype(BF16)
        d_up = lax.psum_scatter(d_up, "fsdp", scatter_dimension=0, tiled=True)
        d_down = lax.psum_scatter(d_down, "fsdp", scatter_dimension=1, tiled=True)
        d_up = lax.psum(flip_units(d_up), "ctx").astype(F32)
        d_down = lax.psum(flip_units(d_down), "ctx").astype(F32)
        d_out = lax.psum_scatter(d_out, "ctx", scatter_dimension=1, tiled=True)
        d_out = lax.psum_scatter(d_out, "tp", scatter_dimension=0, tiled=True)
        d_out = lax.psum_scatter(d_out, "fsdp", scatter_dimension=2, tiled=True)
        d_out = lax.all_gather(d_out[0], "ctx", axis=0, tiled=True).astype(F32)
        dqw, dkv = attend_back(qw, kv, do, o, lse, flags)
        dq, own, grad = project_back(dqw, dkv, w_in, back_one, 8 * n + 3)
        both = jnp.concatenate([dq, own], axis=1)
        d_in = mm_tn(xg, both).astype(BF16)
        d_in = lax.psum_scatter(d_in, "fsdp", scatter_dimension=0, tiled=True)
        d_in = lax.psum(d_in, "ctx").astype(F32)
        sums = jnp.sum(both.astype(F32), axis=0)
        d_query_bias, _, d_value_bias = parted(sums)
        heads[n] = jnp.stack([d_query_bias, d_value_bias])
        matrix[n] = parted(d_in) + (d_out, d_up, d_down)
    hidden_grad = grad.astype(BF16)
    memory_part = lax.dot_general(
        marks, grad, (((0,), (0,)), ((), ())),
        precision=lax.Precision.HIGHEST, preferred_element_type=F32,
    )
    small = jnp.stack(small)
    heads = jnp.stack(heads)
    tp_mark = (ids == t).astype(F32)
    flipped = sum(((c == n) * (t ^ FLIP[n]) for n in range(4)), 0)
    unit_mark = (ids == flipped).astype(F32)
    padded_head = (heads[:, :, None, :] * tp_mark[None, None, :, None]).reshape(layers, 2, -1)
    padded_ffn = (small[:, 6][:, None, :] * unit_mark[None, :, None]).reshape(layers, -1)
    totals = lax.psum((padded_head, padded_ffn, small[:, :6], memory_part), ("fsdp", "ctx", "tp"))
    head_grad = jnp.sum(totals[0].reshape(layers, 2, 4, -1) * tp_mark[None, None, :, None], axis=2)
    ffn_grad = jnp.sum(totals[1].reshape(layers, 4, -1) * tp_mark[None, :, None], axis=1)
    stack = lambda k: jnp.stack([matrix[n][k] for n in range(layers)])
    return (
        output, hidden_grad, totals[3],
        stack(0), stack(1), stack(2), stack(3), stack(4), stack(5),
        head_grad, ffn_grad, totals[2][:, 4:6], totals[2][:, 0:2], totals[2][:, 2:4],
    )


def solution(mesh):
    rows = P(("fsdp", "ctx", "tp"), None)
    inner = P(None, "fsdp", "tp")
    outer = P(None, "tp", "fsdp")
    weights = (inner, inner, inner, outer, inner, outer)
    biases = (P(None, None, "tp"), P(None, "tp"), P(), P(), P())
    return jax.shard_map(
        shards,
        mesh=mesh,
        in_specs=(rows, rows, P("fsdp", "ctx", None), P("fsdp", None), P()) + weights + biases,
        out_specs=(rows, rows, P()) + weights + biases,
        check_vma=False,
    )
```

```python
import functools

import jax
import jax.numpy as jnp
from jax import lax
from jax.experimental import pallas as pl
from jax.experimental.pallas import tpu as pltpu
from jax.sharding import PartitionSpec as P

EPSILON = 1e-05
MASKED = -1000000000.0
MESH = pl.DeviceIdType.MESH
F32 = jnp.float32
BF16 = jnp.bfloat16
ORDER = ((0, 1), (1, 0), (2, 2), (3, 3))


def mm(left, right):
    return jnp.dot(left, right, preferred_element_type=F32)


def mm_nt(left, right):
    return lax.dot_general(left, right, (((1,), (1,)), ((), ())), preferred_element_type=F32)


def mm_tn(left, right):
    return lax.dot_general(left, right, (((0,), (0,)), ((), ())), preferred_element_type=F32)


def rcopy(src, dst, send_sem, recv_sem, device):
    return pltpu.make_async_remote_copy(
        src_ref=src,
        dst_ref=dst,
        send_sem=send_sem,
        recv_sem=recv_sem,
        device_id=device,
        device_id_type=MESH,
    )


def mate_of(c):
    return c + 1 - 2 * (c % 2)


def across_of(c):
    return (c + 2) % 4


def signal(sem, device):
    pl.semaphore_signal(sem, inc=1, device_id=device, device_id_type=MESH)


def ordered(place, step):
    half = place // 2
    inner = place + half * (3 - 2 * place)
    first, second = ORDER[step]
    chunk = first + inner * (second - first)
    return chunk + half * (3 - 2 * chunk)


def dma(*shape):
    return pltpu.SemaphoreType.DMA(shape)


class Rider:
    def __init__(self, array, out, make, scratch, chunks=0):
        self.array, self.out, self.make, self.scratch, self.chunks = array, out, make, scratch, chunks


class Copies:
    def __init__(self, steps, here, scratch):
        self.steps, self.here = steps, here
        self.send, self.recv, self.leg, self.stage = scratch
        self.turned = False

    def greetings(self):
        return [(origin, when, weight) for _, origin, _, _, when, weight in self.steps]

    def copies(self):
        for number, (to, _, source, target, when, _) in enumerate(self.steps):
            yield rcopy(source, target, self.send.at[number], self.recv.at[number], to), when

    def inward(self):
        return pltpu.make_async_copy(self.here[0], self.stage, self.leg.at[0])

    def outward(self):
        return pltpu.make_async_copy(self.stage, self.here[1], self.leg.at[1])

    def start(self):
        for copy, when in self.copies():
            guarded(when, copy.start)
        guarded(self.here[2], self.inward().start)

    def turn(self):
        guarded(self.here[2], self.inward().wait)
        guarded(self.here[2], self.outward().start)

    def finish(self):
        for copy, when in self.copies():
            guarded(when, copy.wait)
        guarded(self.here[2], self.outward().wait)


class FlipGather:
    def __init__(self, source, target, place, scratch):
        self.source, self.target = source, target
        self.f, self.c, self.t = place
        self.size = target.shape[0]
        self.send, self.recv, self.on_send, self.on_recv, self.leg, self.stage = scratch
        self.moves = self.c > 0

    def greetings(self):
        there = {"tp": flipped_place(self.c, self.t)}
        ring = [({"fsdp": (self.f + self.size - k) % self.size}, None, 1) for k in range(1, self.size)]
        return [(there, self.moves, (self.c + 3) // 4)] + ring

    def first(self, chunk):
        there = {"tp": flipped_place(self.c, self.t)}
        return rcopy(
            self.source.at[chunk], self.target.at[self.f, chunk], self.send.at[chunk], self.recv.at[chunk], there
        )

    def second(self, chunk, k, moved):
        source = self.target.at[self.f, chunk] if moved else self.source.at[chunk]
        device = {"fsdp": (self.f + k) % self.size}
        return rcopy(
            source, self.target.at[self.f, chunk], self.on_send.at[k - 1, chunk], self.on_recv.at[k - 1, chunk], device
        )

    def inward(self):
        return pltpu.make_async_copy(self.source, self.stage, self.leg.at[0])

    def outward(self):
        return pltpu.make_async_copy(self.stage, self.target.at[self.f], self.leg.at[1])

    def start(self):
        @pl.when(self.moves)
        def _():
            for chunk in range(self.source.shape[0]):
                self.first(chunk).start()

        @pl.when(self.c == 0)
        def _():
            self.inward().start()

    def hop(self, chunk):
        @pl.when(self.moves)
        def _():
            self.first(chunk).wait_recv()
            for k in range(1, self.size):
                self.second(chunk, k, True).start()

        @pl.when(self.c == 0)
        def _():
            for k in range(1, self.size):
                self.second(chunk, k, False).start()

    def turn(self):
        @pl.when(self.c == 0)
        def _():
            self.inward().wait()
            self.outward().start()

    def finish(self):
        @pl.when(self.moves)
        def _():
            for chunk in range(self.source.shape[0]):
                self.first(chunk).wait_send()

        for chunk in range(self.source.shape[0]):
            for k in range(1, self.size):
                self.second(chunk, k, False).wait()

        @pl.when(self.c == 0)
        def _():
            self.outward().wait()


class ScatterFlip:
    def __init__(self, source, target, place, scratch):
        self.source, self.target = source, target
        self.f, self.c, self.t = place
        self.size = source.shape[1]
        self.send, self.recv, self.on_send, self.on_recv, self.leg, self.got, self.out = scratch
        self.moves = self.c > 0

    def greetings(self):
        there = {"tp": flipped_place(self.c, self.t)}
        ring = [({"fsdp": (self.f + self.size - k) % self.size}, None, 1) for k in range(1, self.size)]
        return [(there, self.moves, (self.c + 3) // 4)] + ring

    def first(self, chunk, k):
        to = (self.f + k) % self.size
        return rcopy(
            self.source.at[chunk // 2, to, chunk % 2], self.got.at[k, chunk],
            self.send.at[k - 1, chunk], self.recv.at[k - 1, chunk], {"fsdp": to},
        )

    def own(self, chunk):
        return pltpu.make_async_copy(
            self.source.at[chunk // 2, self.f, chunk % 2], self.got.at[0, chunk], self.leg.at[chunk]
        )

    def second(self, chunk):
        there = {"tp": flipped_place(self.c, self.t)}
        return rcopy(self.out.at[chunk], self.target.at[chunk], self.on_send.at[chunk], self.on_recv.at[chunk], there)

    def stays(self, chunk):
        return pltpu.make_async_copy(self.out.at[chunk], self.target.at[chunk], self.on_send.at[chunk])

    def start(self):
        for chunk in range(self.target.shape[0]):
            for k in range(1, self.size):
                self.first(chunk, k).start()
            self.own(chunk).start()

    def hop(self, chunk):
        self.own(chunk).wait()
        total = self.got[0, chunk].astype(F32)
        for k in range(1, self.size):
            self.first(chunk, k).wait_recv()
            total += self.got[k, chunk].astype(F32)
        self.out[chunk] = total.astype(BF16)

        @pl.when(self.moves)
        def _():
            self.second(chunk).start()

        @pl.when(self.c == 0)
        def _():
            self.stays(chunk).start()

    def turn(self):
        pass

    def finish(self):
        for chunk in range(self.target.shape[0]):
            for k in range(1, self.size):
                self.first(chunk, k).wait_send()

            @pl.when(self.moves)
            def _():
                self.second(chunk).wait()

            @pl.when(self.c == 0)
            def _():
                self.stays(chunk).wait()


class CtxGather:
    def __init__(self, source, target, place, scratch):
        self.source, self.target = source, target
        self.c = place[1]
        self.send, self.recv, self.leg, self.stage = scratch

    def greetings(self):
        return [({"ctx": mate_of(self.c)}, None, 1), ({"ctx": across_of(self.c)}, None, 1)]

    def copy(self, number):
        c = self.c
        device = across_of(c) if number == 0 else mate_of(c)
        source = self.target.at[across_of(c)] if number == 2 else self.source
        slot = across_of(c) if number == 2 else c
        return rcopy(source, self.target.at[slot], self.send.at[number], self.recv.at[number], {"ctx": device})

    def inward(self):
        return pltpu.make_async_copy(self.source, self.stage, self.leg.at[0])

    def outward(self):
        return pltpu.make_async_copy(self.stage, self.target.at[self.c], self.leg.at[1])

    def start(self):
        self.copy(0).start()
        self.copy(1).start()
        self.inward().start()

    def turn(self):
        self.inward().wait()
        self.outward().start()
        self.copy(0).wait_recv()
        self.copy(2).start()

    def finish(self):
        self.copy(0).wait_send()
        self.copy(1).wait()
        self.copy(2).wait()
        self.outward().wait()


class CtxScatter:
    def __init__(self, pick, source, target, place, scratch):
        self.source, self.target, self.pick = source, target, pick
        self.c = place[1]
        self.send, self.recv, self.leg, self.stage, self.cross, self.far, self.total = scratch

    def greetings(self):
        return [({"ctx": mate_of(self.c)}, None, 1), ({"ctx": across_of(self.c)}, None, 1)]

    def copy(self, number):
        c = self.c
        device = across_of(c) if number == 2 else mate_of(c)
        source = (self.pick(self.source, 3 - c), self.pick(self.source, mate_of(c)), self.total)[number]
        target = (self.far, self.target.at[1], self.target.at[2])[number]
        return rcopy(source, target, self.send.at[number], self.recv.at[number], {"ctx": device})

    def inward(self):
        return pltpu.make_async_copy(self.pick(self.source, self.c), self.stage, self.leg.at[0])

    def outward(self):
        return pltpu.make_async_copy(self.stage, self.target.at[0], self.leg.at[1])

    def beside(self):
        return pltpu.make_async_copy(self.pick(self.source, across_of(self.c)), self.cross, self.leg.at[2])

    def start(self):
        self.copy(0).start()
        self.beside().start()
        self.copy(1).start()
        self.inward().start()

    def turn(self):
        self.copy(0).wait_recv()
        self.beside().wait()
        self.total[...] = (self.cross[...].astype(F32) + self.far[...].astype(F32)).astype(self.total.dtype)
        self.copy(2).start()
        self.inward().wait()
        self.outward().start()

    def finish(self):
        self.copy(0).wait_send()
        self.copy(1).wait()
        self.copy(2).wait()
        self.outward().wait()


class Riding:
    def __init__(self, riders, sources, targets, scratch):
        place = tuple(lax.axis_index(axis) for axis in ("fsdp", "ctx", "tp"))
        scratch = list(scratch)
        self.rides, self.hops = [], []
        self.turned = False
        for rider, source, target in zip(riders, sources, targets):
            own = [scratch.pop(0) for _ in rider.scratch]
            ride = rider.make(source, target, place, own)
            self.rides.append(ride)
            self.hops += [(ride, chunk) for chunk in range(rider.chunks)]

    def greet(self, barrier):
        count = 0
        for ride in self.rides:
            for origin, when, weight in ride.greetings():
                guarded(when, functools.partial(signal, barrier, origin))
                count = count + weight
        return count

    def start(self):
        for ride in self.rides:
            ride.start()

    def hop(self, number):
        if isinstance(number, int):
            if number < len(self.hops):
                ride, chunk = self.hops[number]
                ride.hop(chunk)
            return
        for at, (ride, chunk) in enumerate(self.hops):
            pl.when(number == at)(functools.partial(ride.hop, chunk))

    def turn(self):
        self.turned = True
        for ride in self.rides:
            ride.turn()

    def finish(self):
        if not self.turned:
            self.turn()
        for ride in self.rides:
            ride.finish()


def guarded(when, action):
    if when is None:
        action()
    else:
        pl.when(when)(action)


def call(kernel, operands, out_shapes, scratch, collective_id, name, cost, riders=(), smem=(), any_in=(), any_out=()):
    n_in, n_out, n_scratch, n_ride = len(operands), len(out_shapes), len(scratch), len(riders)

    def body(*refs):
        refs = list(refs)
        take = lambda n: [refs.pop(0) for _ in range(n)]
        ins, sources, outs, targets, own = take(n_in), take(n_ride), take(n_out), take(n_ride), take(n_scratch)
        kernel(Riding(riders, sources, targets, refs), *ins, *outs, *own)

    params = dict(vmem_limit_bytes=56 * 1024 * 1024)
    if collective_id is not None:
        params.update(collective_id=collective_id, has_side_effects=True)
    extra = [item for rider in riders for item in rider.scratch]
    anywhere = pl.BlockSpec(memory_space=pl.ANY)
    whole = pl.BlockSpec(memory_space=pltpu.VMEM)
    results = pl.pallas_call(
        body,
        out_shape=list(out_shapes) + [rider.out for rider in riders],
        in_specs=[
            pl.BlockSpec(memory_space=pltpu.SMEM) if i in smem else anywhere if i in any_in else whole
            for i in range(n_in)
        ]
        + [anywhere] * n_ride,
        out_specs=[anywhere if i in any_out else whole for i in range(n_out)] + [anywhere] * n_ride,
        scratch_shapes=list(scratch) + extra,
        compiler_params=pltpu.CompilerParams(**params),
        cost_estimate=pl.CostEstimate(flops=cost[0], bytes_accessed=cost[1], transcendentals=cost[2]),
        name=name,
    )(*operands, *[rider.array for rider in riders])
    return results[:n_out], results[n_out:]


def copies_rider(array, out, steps, stage, plan):
    def make(source, target, place, scratch):
        return Copies(*plan(source, target, *place), scratch)

    scratch = [dma(steps), dma(steps), dma(2), pltpu.VMEM(stage, array.dtype)]
    return Rider(array, out, make, scratch)


def flip_gather(own, size):
    own = own.reshape(2, own.shape[0] // 2, own.shape[1])
    scratch = [dma(2), dma(2), dma(size - 1, 2), dma(size - 1, 2), dma(2), pltpu.VMEM(own.shape, own.dtype)]
    return Rider(own, sds(size, *own.shape), FlipGather, scratch, chunks=2)


def scatter_flip(parts):
    n, size = parts.shape[0], parts.shape[1]
    shape = (2 * n, *parts.shape[3:])
    scratch = [
        dma(size - 1, 2 * n), dma(size - 1, 2 * n), dma(2 * n), dma(2 * n), dma(2 * n),
        pltpu.VMEM((size, *shape), BF16), pltpu.VMEM(shape, BF16),
    ]
    return Rider(parts, sds(*shape), ScatterFlip, scratch, chunks=2 * n)


def fsdp_gather(own, size):
    def make(source, target, f, c, t):
        steps = [
            ({"fsdp": (f + k) % size}, {"fsdp": (f + size - k) % size}, source, target.at[f], None, 1)
            for k in range(1, size)
        ]
        return steps, (source, target.at[f], None)

    return copies_rider(own, sds(size, *own.shape, dtype=own.dtype), size - 1, own.shape, make)


def fsdp_scatter(parts, size):
    out = sds(size, parts.shape[0], *parts.shape[2:], dtype=parts.dtype)

    def make(source, target, f, c, t):
        steps = [
            (
                {"fsdp": (f + k) % size}, {"fsdp": (f + size - k) % size},
                source.at[:, (f + k) % size], target.at[k], None, 1,
            )
            for k in range(1, size)
        ]
        return steps, (source.at[:, f], target.at[0], None)

    return copies_rider(parts, out, size - 1, out.shape[1:], make)


def ctx_gather(own):
    scratch = [dma(3), dma(3), dma(2), pltpu.VMEM(own.shape, own.dtype)]
    return Rider(own, sds(4, *own.shape, dtype=own.dtype), CtxGather, scratch)


def ctx_scatter(parts, axis=0):
    shape = parts.shape[:axis] + parts.shape[axis + 1 :]

    def pick(ref, slot):
        return ref.at[slot] if axis == 0 else ref.at[:, :, slot]

    buffer = pltpu.VMEM(shape, parts.dtype)
    scratch = [dma(3), dma(3), dma(3), buffer, buffer, buffer, buffer]
    return Rider(parts, sds(3, *shape, dtype=parts.dtype), functools.partial(CtxScatter, pick), scratch)


def flipped_place(c, t):
    return 2 * ((t // 2 + c % 2) % 2) + (t % 2 + c // 2) % 2


def tp_flip(own):
    def make(source, target, f, c, t):
        other = {"tp": flipped_place(c, t)}
        return [(other, other, source, target, c > 0, (c + 3) // 4)], (source, target, c == 0)

    return copies_rider(own, sds(*own.shape, dtype=own.dtype), 1, own.shape, make)


def plane(size):
    return [(kt, kf) for kt in (2, 3, 1, 0) for kf in range(size) if kt + kf > 0]


def plane_gather(own, size):
    def make(source, target, f, c, t):
        steps = [
            (
                {"fsdp": (f + kf) % size, "tp": (t + kt) % 4},
                {"fsdp": (f + size - kf) % size, "tp": (t + 4 - kt) % 4},
                source, target.at[t, f], None, 1,
            )
            for kt, kf in plane(size)
        ]
        return steps, (source, target.at[t, f], None)

    return copies_rider(own, sds(4, size, *own.shape, dtype=own.dtype), 4 * size - 1, own.shape, make)


def plane_scatter(parts, size):
    def make(source, target, f, c, t):
        steps = [
            (
                {"fsdp": (f + kf) % size, "tp": (t + kt) % 4},
                {"fsdp": (f + size - kf) % size, "tp": (t + 4 - kt) % 4},
                source.at[(t + kt) % 4, (f + kf) % size], target.at[kt, kf], None, 1,
            )
            for kt, kf in plane(size)
        ]
        return steps, (source.at[t, f], target.at[0, 0], None)

    return copies_rider(parts, sds(*parts.shape, dtype=parts.dtype), 4 * size - 1, parts.shape[2:], make)


def carry_kernel(ride):
    barrier = pltpu.get_barrier_semaphore()
    pl.semaphore_wait(barrier, ride.greet(barrier))
    ride.start()
    for number in range(len(ride.hops)):
        ride.hop(number)
    ride.finish()


def carry(riders, cid):
    return call(carry_kernel, (), (), (), cid, "carry", (1 << 20, 1 << 20, 0), riders)[1]


def sds(*shape, dtype=BF16):
    return jax.ShapeDtypeStruct(shape, dtype)


def project_kernel(
    fetch, ride, x_ref, w_ref, b_ref, xg_ref, qw_ref, kv_ref, *rest
):
    if fetch:
        full_ref, w_send, w_recv, *rest = rest
    (
        qbuf, x_recv, x_right, x_left, k1_send, k1_recv, k2_send, k2_recv, kf_send, kf_recv, q_send, q_recv,
    ) = rest
    c = lax.axis_index("ctx")
    t = lax.axis_index("tp")
    barrier = pltpu.get_barrier_semaphore()
    for device in (mate_of(c), across_of(c), 3 - c):
        signal(barrier, {"ctx": device})

    @pl.when(t > 0)
    def _():
        signal(barrier, {"tp": t - 1})

    @pl.when(t < 3)
    def _():
        signal(barrier, {"tp": t + 1})

    f, size = lax.axis_index("fsdp"), lax.axis_size("fsdp")
    if fetch:
        for k in range(1, size):
            signal(barrier, {"fsdp": (f + size - k) % size})
    ends = (t // 3) + (3 - t) // 3
    pl.semaphore_wait(barrier, 5 - ends + ride.greet(barrier) + (size - 1 if fetch else 0))

    def right(src, chunk, step):
        return rcopy(src, xg_ref.at[chunk], x_right.at[step], x_recv.at[chunk], {"tp": t + 1})

    def left(src, chunk, step):
        return rcopy(src, xg_ref.at[chunk], x_left.at[step], x_recv.at[chunk], {"tp": t - 1})

    def arrived(chunk):
        rcopy(xg_ref.at[chunk], xg_ref.at[chunk], x_right.at[0], x_recv.at[chunk], {"tp": t}).wait_recv()

    @pl.when(t < 3)
    def _():
        right(x_ref, t, 0).start()

    @pl.when(t > 0)
    def _():
        left(x_ref, t, 0).start()

    def weight(k):
        device = {"fsdp": (f + k) % size}
        return rcopy(w_ref, full_ref.at[f], w_send.at[k - 1], w_recv.at[k - 1], device)

    if fetch:
        for k in range(1, size):
            weight(k).start()
        full_ref[f] = w_ref[...]
        for k in range(1, size):
            weight(k).wait_recv()
    ride.start()

    def mate(chunk):
        return rcopy(kv_ref.at[c, chunk], kv_ref.at[c, chunk], k1_send.at[chunk], k1_recv.at[chunk], {"ctx": mate_of(c)})

    def across(chunk):
        return rcopy(kv_ref.at[c, chunk], kv_ref.at[c, chunk], k2_send.at[chunk], k2_recv.at[chunk], {"ctx": across_of(c)})

    def onward(chunk):
        return rcopy(
            kv_ref.at[across_of(c), chunk], kv_ref.at[across_of(c), chunk], kf_send.at[chunk], kf_recv.at[chunk], {"ctx": mate_of(c)}
        )

    def partner(slot):
        return rcopy(qbuf.at[slot], qw_ref.at[slot + 2], q_send.at[slot], q_recv.at[slot], {"ctx": 3 - c})

    for step in range(4):
        if step == 0:
            xg_ref[t] = x_ref[...]
        else:

            @pl.when(t - step >= 0)
            def _():
                arrived(t - step)

                @pl.when(t < 3)
                def _():
                    right(xg_ref.at[t - step], t - step, step).start()

            @pl.when(t + step <= 3)
            def _():
                arrived(t + step)

                @pl.when(t > 0)
                def _():
                    left(xg_ref.at[t + step], t + step, step).start()

        chunk = ordered(t, step)
        w = full_ref[...].reshape(768, 640) if fetch else w_ref[...]
        made = mm(xg_ref[chunk], w) + b_ref[...]
        kv_ref[c, chunk] = made[:, 256:].astype(BF16)
        mate(chunk).start()
        across(chunk).start()
        query = (made[:, :256] * 0.125).astype(BF16)

        @pl.when(chunk < 2)
        def _():
            qw_ref[chunk] = query

        @pl.when(chunk >= 2)
        def _():
            qbuf[chunk - 2] = query
            partner(chunk - 2).start()

        if step >= 1:
            before = ordered(t, step - 1)
            across(before).wait_recv()
            onward(before).start()
    last = ordered(t, 3)
    across(last).wait_recv()
    onward(last).start()
    for chunk in range(4):
        mate(chunk).wait()
        across(chunk).wait_send()
        onward(chunk).wait()
    for slot in range(2):
        partner(slot).wait()

    @pl.when(t < 3)
    def _():
        right(x_ref, t, 0).wait_send()

    @pl.when(t > 0)
    def _():
        left(x_ref, t, 0).wait_send()

    for step in (1, 2):

        @pl.when((t - step >= 0) & (t < 3))
        def _():
            right(xg_ref.at[t - step], t - step, step).wait_send()

        @pl.when((t + step <= 3) & (t > 0))
        def _():
            left(xg_ref.at[t + step], t + step, step).wait_send()

    if fetch:
        for k in range(1, size):
            weight(k).wait_send()
    ride.finish()


def project(x, w, b, cid, riders=(), fetch=False):
    outs = [sds(4, 256, 768), sds(4, 256, 256), sds(4, 4, 256, 384)]
    scratch = [
        pltpu.VMEM((2, 256, 256), BF16),
        dma(4), dma(3), dma(3),
        dma(4), dma(4), dma(4), dma(4), dma(4), dma(4), dma(2), dma(2),
    ]
    if fetch:
        size = lax.axis_size("fsdp")
        outs.append(sds(size, *w.shape))
        scratch = [dma(size - 1), dma(size - 1)] + scratch
    cost = (2 * 1024 * 768 * 640, 8 << 20, 0)
    kernel = functools.partial(project_kernel, fetch)
    res, ridden = call(kernel, (x, w, b), outs, scratch, cid, "project", cost, riders)
    xg, qw, kv = res[:3]
    full = res[3].reshape(768, 640) if fetch else w
    return xg.reshape(1024, 768), qw.reshape(1024, 256), kv.reshape(4, 1024, 384), full, ridden


def norm_stats(summed):
    row_mean = jnp.mean(summed, axis=-1, keepdims=True)
    centered = summed - row_mean
    variance = jnp.mean(centered * centered, axis=-1, keepdims=True)
    scale = lax.rsqrt(variance + EPSILON)
    return centered * scale, scale


def norm_back(grad, xhat, scale, gain):
    scaled = grad * gain
    first = jnp.mean(scaled, axis=-1, keepdims=True)
    second = jnp.mean(scaled * xhat, axis=-1, keepdims=True)
    return scale * (scaled - first - xhat * second)


def gelu_both(up):
    phi = 0.5 * (1.0 + lax.erf(up * 0.7071067811865476))
    slope = phi + up * jnp.exp(-0.5 * up * up) * 0.3989422804014327
    return (up * phi).astype(BF16), slope.astype(BF16)


Q_TILE = 256
K_TILE = 256


def open_up(ride):
    if ride.rides:
        barrier = pltpu.get_barrier_semaphore()
        pl.semaphore_wait(barrier, ride.greet(barrier))
        ride.start()


def attend_kernel(ride, flag_ref, qw_ref, kv_ref, o_ref, lse_ref, qm_ref, m_ref, l_ref, acc_ref):
    c = lax.axis_index("ctx")
    open_up(ride)
    low = lax.broadcasted_iota(jnp.int32, (Q_TILE, 128), 1) < 64
    per_half = 512 // Q_TILE

    @pl.loop(0, 1024 // Q_TILE)
    def _(tile):
        half = tile // per_half
        segment = c + half * (3 - 2 * c)
        rows = pl.ds(pl.multiple_of(tile * Q_TILE, Q_TILE), Q_TILE)
        pair = qw_ref[rows, 0:128]
        qm_ref[0] = jnp.where(low, pair, jnp.zeros_like(pair))
        qm_ref[1] = jnp.where(low, jnp.zeros_like(pair), pair)
        qm_ref[2] = qw_ref[rows, 128:256]
        m_ref[...] = jnp.full_like(m_ref, MASKED)
        l_ref[...] = jnp.zeros_like(l_ref)
        acc_ref[...] = jnp.zeros_like(acc_ref)

        @pl.loop(0, segment + 1)
        def _(block):
            seen = flag_ref[half, block] > 0
            keys = pl.ds(pl.multiple_of(block * 1024, 1024), 1024)
            for head in range(3):
                k_at = 0 if head < 2 else 128
                v_at = 256 if head < 2 else 128
                scores = mm_nt(qm_ref[head], kv_ref[keys, k_at : k_at + 128])
                scores = jnp.where(seen, scores, MASKED)
                old = m_ref[head]
                new = jnp.maximum(old, jnp.max(scores, axis=-1, keepdims=True))
                probs = jnp.exp(scores - new)
                keep = jnp.exp(old - new)
                m_ref[head] = new
                l_ref[head] = l_ref[head] * keep + jnp.sum(probs, axis=-1, keepdims=True)
                acc_ref[head] = acc_ref[head] * keep + mm(
                    probs.astype(BF16), kv_ref[keys, v_at : v_at + 128]
                )

        first = acc_ref[0] / l_ref[0]
        second = acc_ref[1] / l_ref[1]
        o_ref[rows, 0:128] = jnp.where(low, first, second).astype(BF16)
        o_ref[rows, 128:192] = (acc_ref[2] / l_ref[2])[:, :64].astype(BF16)
        lane = lax.broadcasted_iota(jnp.int32, (Q_TILE, 128), 1)
        totals = [m_ref[head] + jnp.log(l_ref[head]) for head in range(3)]
        lse_ref[rows, :] = jnp.where(lane == 0, totals[0], jnp.where(lane == 1, totals[1], totals[2]))
        ride.hop(tile)

    ride.finish()


def attend(qw, kv, flags, cid, riders=()):
    outs = [sds(1024, 192), sds(1024, 128, dtype=F32)]
    scratch = [
        pltpu.VMEM((3, Q_TILE, 128), BF16),
        pltpu.VMEM((3, Q_TILE, 1), F32),
        pltpu.VMEM((3, Q_TILE, 1), F32),
        pltpu.VMEM((3, Q_TILE, 128), F32),
    ]
    cost = (5 * 512 * 1024 * 64 * 4 * 3, 6 << 20, 5 * 512 * 1024 * 3)
    operands = (flags, qw, kv.reshape(4096, 384))
    cid = cid if riders else None
    res, ridden = call(attend_kernel, operands, outs, scratch, cid, "attend", cost, riders, smem=(0,))
    return res[0], res[1], ridden


def attend_back_kernel(
    ride, flag_ref, qw_ref, kv_ref, do_ref, o_ref, lse_ref, dq_ref, dkv_ref,
    qm_ref, dm_ref, row_ref, acc_ref, key_ref,
):
    c = lax.axis_index("ctx")
    open_up(ride)
    low = lax.broadcasted_iota(jnp.int32, (1024, 128), 1) < 64
    pair = qw_ref[:, 0:128]
    none = jnp.zeros_like(pair)
    qm_ref[0] = jnp.where(low, pair, none)
    qm_ref[1] = jnp.where(low, none, pair)
    qm_ref[2] = qw_ref[:, 128:256]
    pair = do_ref[:, 0:128]
    dm_ref[0] = jnp.where(low, pair, none)
    dm_ref[1] = jnp.where(low, none, pair)
    dm_ref[2] = jnp.concatenate([do_ref[:, 128:192], none[:, :64]], axis=1)
    turned = jnp.transpose(lse_ref[...], (1, 0))
    row_ref[0:8] = turned[0:8]
    product = do_ref[...].astype(F32) * o_ref[...].astype(F32)
    head_row = lax.broadcasted_iota(jnp.int32, (8, 192), 0)
    head_of = lax.broadcasted_iota(jnp.int32, (8, 192), 1) // 64
    marks = (head_row == head_of).astype(F32)
    row_ref[8:16] = lax.dot_general(
        marks, product, (((1,), (1,)), ((), ())),
        precision=lax.Precision.HIGHEST, preferred_element_type=F32,
    )
    acc_ref[...] = jnp.zeros_like(acc_ref)
    low_keys = lax.broadcasted_iota(jnp.int32, (K_TILE, 128), 1) < 64

    @pl.loop(0, 4)
    def _(block):
        @pl.loop(0, 1024 // K_TILE)
        def _(tile):
            keys = pl.ds(pl.multiple_of(block * 1024 + tile * K_TILE, K_TILE), K_TILE)
            key_ref[...] = jnp.zeros_like(key_ref)
            key_pair = kv_ref[keys, 0:128]
            nothing = jnp.zeros_like(key_pair)
            key_parts = (
                jnp.where(low_keys, key_pair, nothing),
                jnp.where(low_keys, nothing, key_pair),
                jnp.where(low_keys, nothing, kv_ref[keys, 128:256]),
            )
            for half in range(2):
                segment = c if half == 0 else 3 - c

                @pl.when(block <= segment)
                def _():
                    seen = flag_ref[half, block] > 0
                    rows = pl.ds(half * 512, 512)
                    for head in range(3):
                        k_at = 0 if head < 2 else 128
                        v_at = 256 if head < 2 else 128
                        query = qm_ref[head, rows]
                        grads = dm_ref[head, rows]
                        scores = mm_nt(kv_ref[keys, k_at : k_at + 128], query)
                        scores = jnp.where(seen, scores, MASKED)
                        probs = jnp.exp(scores - row_ref[head : head + 1, rows])
                        grad_probs = mm_nt(kv_ref[keys, v_at : v_at + 128], grads)
                        grad_scores = (probs * (grad_probs - row_ref[8 + head : 9 + head, rows])).astype(BF16)
                        key_ref[:, v_at : v_at + 128] += mm(probs.astype(BF16), grads)
                        key_ref[:, k_at : k_at + 128] += mm(grad_scores, query)
                        q_at = 0 if head < 2 else 128
                        acc_ref[rows, q_at : q_at + 128] += mm_tn(grad_scores, key_parts[head])

            dkv_ref[keys, :] = key_ref[...].astype(BF16)

        ride.hop(block)

    dq_ref[...] = (acc_ref[...].astype(BF16).astype(F32) * 0.125).astype(BF16)
    ride.finish()


def attend_back(qw, kv, do, o, lse, flags, cid, riders=()):
    outs = [sds(1024, 256), sds(4096, 384)]
    scratch = [
        pltpu.VMEM((3, 1024, 128), BF16),
        pltpu.VMEM((3, 1024, 128), BF16),
        pltpu.VMEM((16, 1024), F32),
        pltpu.VMEM((1024, 256), F32),
        pltpu.VMEM((K_TILE, 384), F32),
    ]
    cost = (5 * 512 * 1024 * 64 * 10 * 3, 12 << 20, 5 * 512 * 1024 * 3)
    operands = (flags, qw, kv.reshape(4096, 384), do, o, lse)
    cid = cid if riders else None
    res, ridden = call(attend_back_kernel, operands, outs, scratch, cid, "attend_back", cost, riders, smem=(0,))
    return res[0], res[1].reshape(4, 1024, 384), ridden


def block_kernel(
    ride, o_ref, wo_ref, w1_ref, w2_ref, b1_ref, vec_ref, stream_ref,
    out_ref, low_ref, xhat1_ref, r1_ref, xhat2_ref, r2_ref, xg_ref, act_ref, slope_ref, rows_ref,
    mine_ref, send_ref, got_ref, o_send, o_recv, a_send, a_recv, s_send, s_recv,
):
    c = lax.axis_index("ctx")
    t = lax.axis_index("tp")
    barrier = pltpu.get_barrier_semaphore()
    for place in range(4):

        @pl.when((t < 2) & (t != place))
        def _():
            signal(barrier, {"tp": place})

        @pl.when(t >= 2)
        def _():
            signal(barrier, {"ctx": 3 - c, "tp": place})

    signal(barrier, {"ctx": mate_of(c)})
    signal(barrier, {"ctx": across_of(c)})
    pl.semaphore_wait(barrier, 5 + t // 2 + ride.greet(barrier))

    def give(quarter):
        device = {"tp": quarter} if quarter < 2 else {"ctx": 3 - c, "tp": quarter}
        return rcopy(o_ref.at[quarter], rows_ref.at[t], o_send.at[quarter], o_recv.at[t], device)

    def given(group):
        rcopy(rows_ref.at[group], rows_ref.at[group], o_send.at[0], o_recv.at[group], {"tp": t}).wait_recv()

    for quarter in (3, 2, 1, 0):
        if quarter < 2:

            @pl.when(t != quarter)
            def _():
                give(quarter).start()

            @pl.when(t == quarter)
            def _():
                rows_ref[quarter] = o_ref[quarter]

        else:
            give(quarter).start()
    branch = stream_ref[...] + vec_ref[0:1]
    for group in range(4):

        @pl.when((t >= 2) | (t != group))
        def _():
            given(group)

        branch += mm_nt(rows_ref[group], wo_ref[group])
    ride.start()
    xhat, scale = norm_stats(branch)
    xhat1_ref[...] = xhat
    r1_ref[...] = jnp.broadcast_to(scale, r1_ref.shape)
    normed = xhat * vec_ref[2:3] + vec_ref[3:4]
    xg_ref[c] = normed.astype(BF16)
    mate, across, far = mate_of(c), across_of(c), 3 - c

    def gather(slot, index, device):
        return rcopy(xg_ref.at[slot], xg_ref.at[slot], a_send.at[index], a_recv.at[index], {"ctx": device})

    gather(c, 1, across).start()
    gather(c, 0, mate).start()

    def feed(segment):
        up = mm(xg_ref[segment], w1_ref[...]) + b1_ref[...]
        act, slope = gelu_both(up)
        act_ref[segment] = act
        slope_ref[segment] = slope
        return mm_nt(act, w2_ref[...])

    mine_ref[...] = feed(c) + normed + vec_ref[1:2]
    gather(mate, 0, mate).wait_recv()

    def scatter(index, device):
        return rcopy(send_ref.at[index], got_ref.at[index], s_send.at[index], s_recv.at[index], {"ctx": device})

    send_ref[0] = feed(mate).astype(BF16)
    scatter(0, mate).start()
    gather(across, 1, across).wait_recv()
    gather(across, 2, mate).start()
    own_across = feed(across)
    gather(far, 2, mate).wait_recv()
    send_ref[1] = feed(far).astype(BF16)
    scatter(1, mate).start()
    scatter(1, mate).wait_recv()
    send_ref[2] = (own_across + got_ref[1].astype(F32)).astype(BF16)
    scatter(2, across).start()
    ride.turn()
    scatter(0, mate).wait_recv()
    scatter(2, across).wait_recv()
    summed = mine_ref[...] + got_ref[0].astype(F32) + got_ref[2].astype(F32)
    xhat, scale = norm_stats(summed)
    xhat2_ref[...] = xhat
    r2_ref[...] = jnp.broadcast_to(scale, r2_ref.shape)
    out = xhat * vec_ref[4:5] + vec_ref[5:6]
    out_ref[...] = out
    low_ref[...] = out.astype(BF16)
    for quarter in range(4):
        if quarter < 2:

            @pl.when(t != quarter)
            def _():
                give(quarter).wait_send()

        else:
            give(quarter).wait_send()
    gather(c, 0, mate).wait_send()
    gather(c, 1, across).wait_send()
    gather(across, 2, mate).wait_send()
    for index in range(3):
        scatter(index, mate).wait_send()
    ride.finish()


def block(o, wo, w1, w2, b1, vecs, stream, cid, riders=()):
    f = functools.partial(sds, dtype=F32)
    outs = [
        f(256, 768), sds(256, 768), f(256, 768), f(256, 128), f(256, 768), f(256, 128),
        sds(4, 256, 768), sds(4, 256, 768), sds(4, 256, 768), sds(4, 256, 192),
    ]
    scratch = [
        pltpu.VMEM((256, 768), F32),
        pltpu.VMEM((3, 256, 768), BF16),
        pltpu.VMEM((3, 256, 768), BF16),
        dma(4), dma(4), dma(3), dma(3), dma(3), dma(3),
    ]
    cost = (2 * 256 * 768 * 768 + 4 * 1024 * 768 * 768, 16 << 20, 1 << 20)
    operands = (o.reshape(4, 256, 192), wo, w1, w2, b1, vecs, stream)
    res, ridden = call(block_kernel, operands, outs, scratch, cid, "block", cost, riders)
    flat = lambda a: a.reshape(1024, 768)
    return tuple(res[:6]) + (flat(res[6]), flat(res[7]), flat(res[8]), res[9], ridden)


def block_back_kernel(
    ride, grad_ref, xhat2_ref, r2_ref, xhat1_ref, r1_ref, vec_ref, slope_ref, w1_ref, w2_ref, wo_ref,
    xg_ref, act_ref, rows_ref, back_ref, do_ref, stat_ref, dffn_ref, dout_ref,
    gg_ref, gu_ref, mine_ref, send_ref, got_ref, dsend_ref, d_send, d_recv, a_send, a_recv, s_send, s_recv,
):
    c = lax.axis_index("ctx")
    t = lax.axis_index("tp")
    barrier = pltpu.get_barrier_semaphore()
    for place in range(4):
        if place < 2:

            @pl.when(t != place)
            def _():
                signal(barrier, {"tp": place})

        else:
            signal(barrier, {"ctx": 3 - c, "tp": place})
    signal(barrier, {"ctx": mate_of(c)})
    signal(barrier, {"ctx": across_of(c)})
    pl.semaphore_wait(barrier, 5 + t // 2 + ride.greet(barrier))
    mate, across, far = mate_of(c), across_of(c), 3 - c

    def row(values):
        return jnp.sum(values, axis=0, keepdims=True)

    grad = grad_ref[...]
    back_two = norm_back(grad, xhat2_ref[...], r2_ref[:, 0:1], vec_ref[4:5])
    g2 = back_two.astype(BF16)
    gg_ref[c] = g2

    def gather(slot, index, device):
        return rcopy(gg_ref.at[slot], gg_ref.at[slot], a_send.at[index], a_recv.at[index], {"ctx": device})

    gather(c, 1, across).start()
    gather(c, 0, mate).start()
    ride.start()
    stat_ref[1:2] = row(grad * xhat2_ref[...])
    stat_ref[3:4] = row(grad)
    stat_ref[5:6] = row(g2.astype(F32))
    stat_ref[7:8] = jnp.zeros((1, 768), F32)

    def feed(segment):
        gu = (mm(gg_ref[segment], w2_ref[...]) * slope_ref[segment].astype(F32)).astype(BF16)
        gu_ref[segment] = gu
        return mm_nt(gu, w1_ref[...]), row(gu.astype(F32))

    part, bias = feed(c)
    mine_ref[...] = part + back_two
    gather(mate, 0, mate).wait_recv()

    def scatter(index, device):
        return rcopy(send_ref.at[index], got_ref.at[index], s_send.at[index], s_recv.at[index], {"ctx": device})

    part, more = feed(mate)
    bias += more
    send_ref[0] = part.astype(BF16)
    scatter(0, mate).start()
    gather(across, 1, across).wait_recv()
    gather(across, 2, mate).start()
    own_across, more = feed(across)
    bias += more
    gather(far, 2, mate).wait_recv()
    part, more = feed(far)
    bias += more
    stat_ref[6:7] = bias
    send_ref[1] = part.astype(BF16)
    scatter(1, mate).start()
    scatter(1, mate).wait_recv()
    send_ref[2] = (own_across + got_ref[1].astype(F32)).astype(BF16)
    scatter(2, across).start()
    tall = lambda ref: ref[...].reshape(1024, 768)

    @pl.loop(0, 3)
    def _(tile):
        cols = pl.ds(pl.multiple_of(tile * 256, 256), 256)
        dffn_ref[0, cols] = mm_tn(xg_ref[:, cols], tall(gu_ref)).astype(BF16)
        dffn_ref[1, cols] = mm_tn(gg_ref[:, :, cols].reshape(1024, 256), act_ref[...]).astype(BF16)

    scatter(0, mate).wait_recv()
    scatter(2, across).wait_recv()
    grad_normed = mine_ref[...] + got_ref[0].astype(F32) + got_ref[2].astype(F32)
    back_one = norm_back(grad_normed, xhat1_ref[...], r1_ref[:, 0:1], vec_ref[2:3])
    back_ref[...] = back_one
    g1 = back_one.astype(BF16)

    def give_near(group):
        return rcopy(dsend_ref.at[group], do_ref.at[t], d_send.at[group], d_recv.at[t], {"tp": group})

    def give_far(group):
        return rcopy(dsend_ref.at[group], do_ref.at[t], d_send.at[group], d_recv.at[t], {"ctx": 3 - c, "tp": group})

    for group in range(4):
        dsend_ref[group] = mm(g1, wo_ref[group]).astype(BF16)

        @pl.when((t < 2) & (t == group))
        def _():
            do_ref[t] = dsend_ref[group]

        @pl.when((t < 2) & (t != group))
        def _():
            give_near(group).start()

        @pl.when(t >= 2)
        def _():
            give_far(group).start()

    stat_ref[0:1] = row(grad_normed * xhat1_ref[...])
    stat_ref[2:3] = row(grad_normed)
    stat_ref[4:5] = row(g1.astype(F32))
    for group in range(4):
        dout_ref[group] = mm_tn(g1, rows_ref[group]).astype(BF16)
    for quarter in range(4):

        def taken():
            rcopy(do_ref.at[quarter], do_ref.at[quarter], d_send.at[0], d_recv.at[quarter], {"tp": t}).wait_recv()

        if quarter < 2:
            pl.when(t != quarter)(taken)
        else:
            taken()
    for group in range(4):

        @pl.when((t >= 2) | (t != group))
        def _():
            give_near(group).wait_send()

    gather(c, 0, mate).wait_send()
    gather(c, 1, across).wait_send()
    gather(across, 2, mate).wait_send()
    for index in range(3):
        scatter(index, mate).wait_send()
    ride.finish()


def block_back(grad, xhat2, r2, xhat1, r1, vecs, slope, w1, w2, wo, xg, act, rows, cid, riders=()):
    f = functools.partial(sds, dtype=F32)
    outs = [f(256, 768), sds(4, 256, 192), f(8, 768), sds(2, 768, 768), sds(4, 768, 192)]
    scratch = [
        pltpu.VMEM((4, 256, 768), BF16),
        pltpu.VMEM((4, 256, 768), BF16),
        pltpu.VMEM((256, 768), F32),
        pltpu.VMEM((3, 256, 768), BF16),
        pltpu.VMEM((3, 256, 768), BF16),
        pltpu.VMEM((4, 256, 192), BF16),
        dma(4), dma(4), dma(3), dma(3), dma(3), dma(3),
    ]
    cost = (4 * 256 * 768 * 768 + 8 * 1024 * 768 * 768, 20 << 20, 1 << 10)
    operands = (grad, xhat2, r2, xhat1, r1, vecs, slope.reshape(4, 256, 768), w1, w2, wo, xg, act, rows)
    res, ridden = call(block_back_kernel, operands, outs, scratch, cid, "block_back", cost, riders)
    back, do, stats, d_ffn, d_out = res
    return back, do.reshape(1024, 192), stats, d_ffn, d_out, ridden


def project_back_kernel(
    ride, dqw_ref, dkv_ref, w_ref, back_ref, xg_ref, grad_ref, din_ref, sum_out_ref,
    dq_ref, own_ref, part_ref, near_ref, join_ref, sum_ref, far_ref, pass_ref, take_ref,
    q_send, q_recv, n_send, n_recv, j_send, j_recv, f_send, f_recv, p_send, p_recv,
):
    c = lax.axis_index("ctx")
    t = lax.axis_index("tp")
    barrier = pltpu.get_barrier_semaphore()
    for device in (mate_of(c), across_of(c), 3 - c):
        signal(barrier, {"ctx": device})

    @pl.when(t > 0)
    def _():
        signal(barrier, {"tp": t - 1})

    @pl.when(t < 3)
    def _():
        signal(barrier, {"tp": t + 1})

    ends = (t // 3) + (3 - t) // 3
    pl.semaphore_wait(barrier, 5 - ends + ride.greet(barrier))
    mate, across, far = mate_of(c), across_of(c), 3 - c

    def partner(slot):
        return rcopy(dqw_ref.at[slot + 2], dq_ref.at[slot + 2], q_send.at[slot], q_recv.at[slot], {"ctx": far})

    def near(chunk):
        return rcopy(dkv_ref.at[mate, chunk], near_ref.at[chunk], n_send.at[chunk], n_recv.at[chunk], {"ctx": mate})

    def join(chunk):
        return rcopy(dkv_ref.at[far, chunk], join_ref.at[chunk], j_send.at[chunk], j_recv.at[chunk], {"ctx": mate})

    def cross(chunk):
        return rcopy(sum_ref.at[chunk], far_ref.at[chunk], f_send.at[chunk], f_recv.at[chunk], {"ctx": across})

    chunks = [ordered(t, 3 - k) for k in range(4)]
    for chunk in chunks:
        join(chunk).start()
    for slot in range(2):
        partner(slot).start()
    for chunk in chunks:
        near(chunk).start()
    for quarter in range(2):
        dq_ref[quarter] = dqw_ref[quarter]
    for chunk in chunks:
        join(chunk).wait_recv()
        sum_ref[chunk] = (dkv_ref[across, chunk].astype(F32) + join_ref[chunk].astype(F32)).astype(BF16)
        cross(chunk).start()

    def lower(chunk):
        return rcopy(pass_ref.at[chunk], take_ref.at[0, chunk], p_send.at[chunk], p_recv.at[0, chunk], {"tp": t - 1})

    def upper(chunk):
        return rcopy(pass_ref.at[chunk], take_ref.at[1, chunk], p_send.at[chunk], p_recv.at[1, chunk], {"tp": t + 1})

    def passed(side, chunk):
        rcopy(
            take_ref.at[side, chunk], take_ref.at[side, chunk], p_send.at[0], p_recv.at[side, chunk], {"tp": t}
        ).wait_recv()

    def relay(chunk):
        @pl.when(chunk < t)
        def _():
            @pl.when(t < 3)
            def _():
                passed(0, chunk)
                pass_ref[chunk] = (part_ref[chunk] + take_ref[0, chunk].astype(F32)).astype(BF16)

            @pl.when(t == 3)
            def _():
                pass_ref[chunk] = part_ref[chunk].astype(BF16)

            lower(chunk).start()

        @pl.when(chunk > t)
        def _():
            @pl.when(t > 0)
            def _():
                passed(1, chunk)
                pass_ref[chunk] = (part_ref[chunk] + take_ref[1, chunk].astype(F32)).astype(BF16)

            @pl.when(t == 0)
            def _():
                pass_ref[chunk] = part_ref[chunk].astype(BF16)

            upper(chunk).start()

    at_end = (t == 0) | (t == 3)
    for step, chunk in enumerate(chunks):

        @pl.when(chunk >= 2)
        def _():
            partner(chunk - 2).wait_recv()

        near(chunk).wait_recv()
        cross(chunk).wait_recv()
        own = (
            dkv_ref[c, chunk].astype(F32) + near_ref[chunk].astype(F32) + far_ref[chunk].astype(F32)
        ).astype(BF16)
        own_ref[chunk] = own
        part_ref[chunk] = mm_nt(dq_ref[chunk], w_ref[:, 0:256]) + mm_nt(own, w_ref[:, 256:640])
        if step < 3:

            @pl.when(at_end)
            def _():
                relay(chunk)

    ride.start()
    for chunk in chunks[:3]:

        @pl.when(jnp.logical_not(at_end))
        def _():
            relay(chunk)

    query, own = dq_ref[...].reshape(1024, 256), own_ref[...].reshape(1024, 384)
    sum_out_ref[0:1, 0:256] = jnp.sum(query.astype(F32), axis=0, keepdims=True)
    sum_out_ref[0:1, 256:640] = jnp.sum(own.astype(F32), axis=0, keepdims=True)

    @pl.loop(0, 3)
    def _(tile):
        cols = pl.ds(pl.multiple_of(tile * 256, 256), 256)
        din_ref[cols, 0:256] = mm_tn(xg_ref[:, cols], dq_ref[...].reshape(1024, 256)).astype(BF16)
        din_ref[cols, 256:640] = mm_tn(xg_ref[:, cols], own_ref[...].reshape(1024, 384)).astype(BF16)

    ride.turn()
    grad_ref[...] = part_ref[t] + back_ref[...]

    @pl.when(t < 3)
    def _():
        passed(0, t)
        grad_ref[...] += take_ref[0, t].astype(F32)

    @pl.when(t > 0)
    def _():
        passed(1, t)
        grad_ref[...] += take_ref[1, t].astype(F32)

    for chunk in range(4):
        join(chunk).wait_send()
        near(chunk).wait_send()
        cross(chunk).wait_send()

        @pl.when(t != chunk)
        def _():
            upper(chunk).wait_send()

    for slot in range(2):
        partner(slot).wait_send()
    ride.finish()


def project_back(dqw, dkv, w, back_one, xg, cid, riders=()):
    outs = [sds(256, 768, dtype=F32), sds(768, 640), sds(8, 640, dtype=F32)]
    scratch = [
        pltpu.VMEM((4, 256, 256), BF16), pltpu.VMEM((4, 256, 384), BF16),
        pltpu.VMEM((4, 256, 768), F32),
        pltpu.VMEM((4, 256, 384), BF16), pltpu.VMEM((4, 256, 384), BF16),
        pltpu.VMEM((4, 256, 384), BF16), pltpu.VMEM((4, 256, 384), BF16),
        pltpu.VMEM((4, 256, 768), BF16), pltpu.VMEM((2, 4, 256, 768), BF16),
        dma(2), dma(2), dma(4), dma(4), dma(4), dma(4), dma(4), dma(4), dma(4), dma(2, 4),
    ]
    cost = (4 * 1024 * 768 * 640, 12 << 20, 0)
    operands = (dqw.reshape(4, 256, 256), dkv.reshape(4, 4, 256, 384), w, back_one, xg)
    res, ridden = call(project_back_kernel, operands, outs, scratch, cid, "project_back", cost, riders)
    return res[0], res[1], res[2][0], ridden


def ancestry(parent_row):
    seg_count = parent_row.shape[0]
    segment_ids = jnp.arange(seg_count, dtype=jnp.int32)
    parent_hop = (parent_row[:, None] == segment_ids[None, :]).astype(jnp.int32)
    reached = (segment_ids[:, None] == segment_ids[None, :]).astype(jnp.int32)
    on_path = reached
    for hop_number in range(seg_count - 1):
        reached = jnp.dot(reached, parent_hop)
        on_path = jnp.maximum(on_path, reached)
    return on_path


def joined(query, key, value, gap):
    return jnp.concatenate(
        [
            query[..., :128], gap, query[..., 128:],
            key[..., :128], value[..., 128:], key[..., 128:], value[..., :128],
        ],
        axis=-1,
    )


def parted(grads):
    query = jnp.concatenate([grads[..., :128], grads[..., 192:256]], axis=-1)
    key = jnp.concatenate([grads[..., 256:384], grads[..., 448:512]], axis=-1)
    value = jnp.concatenate([grads[..., 512:640], grads[..., 384:448]], axis=-1)
    return query, key, value


def added(terms, axes=(0,)):
    return jnp.sum(terms.astype(F32), axis=axes)


def low(values):
    return values.astype(BF16)


def shards(
    hidden, cotangent, mem_pos, parents, memory, wq, wk, wv, wo, w1, w2,
    head_bias, ffn_bias, out_bias, norm_gains, norm_shifts,
):
    c = lax.axis_index("ctx")
    t = lax.axis_index("tp")
    size = lax.axis_size("fsdp")
    layers = wq.shape[0]
    share = hidden.shape[0]
    depth = wq.shape[1]
    piece = depth // 4
    positions = t * share + jnp.arange(share, dtype=jnp.int32)
    marks = (mem_pos[0, 0][None, :] == positions[:, None]).astype(F32)
    stream = hidden.astype(F32) + jnp.dot(
        marks, memory, precision=lax.Precision.HIGHEST, preferred_element_type=F32
    )
    on_path = ancestry(parents[0])
    ids = jnp.arange(4, dtype=jnp.int32)
    pick = lambda seg: jnp.sum(on_path * (ids == seg).astype(jnp.int32)[:, None], axis=0)
    flags = jnp.stack([pick(c), pick(3 - c)])

    gap = jnp.zeros(wq.shape[:2] + (64,), BF16)
    own_in = joined(wq, wk, wv, gap)
    none = jnp.zeros((layers, 192), F32)
    in_bias = joined(head_bias[:, 0], none, head_bias[:, 1], jnp.zeros((layers, 64), F32))
    down_turned = jnp.swapaxes(w2, 1, 2)
    out_turned = jnp.swapaxes(wo, 1, 2).reshape(layers, 4, piece, 192)
    out_piece = lax.dynamic_index_in_dim(out_turned, c, axis=1, keepdims=False)

    def out_whole(gathered):
        return jnp.transpose(gathered, (1, 2, 0, 3, 4)).reshape(4, 768, 192)

    def vectors(n):
        norms = [norm_gains[n, 0], norm_shifts[n, 0], norm_gains[n, 1], norm_shifts[n, 1]]
        return jnp.concatenate([out_bias[n], jnp.stack(norms), jnp.zeros((2, 768), F32)])

    saved, weights = [], []
    rounded = low(stream)
    riders = [plane_gather(out_piece[0], size), tp_flip(ffn_bias)]
    xg, qw, kv, w_in, (out, units) = project(
        rounded, own_in[0], in_bias[0][None], 0, riders, fetch=True
    )
    for n in range(layers):
        last = n == layers - 1
        riders = [ctx_gather(out)]
        if n == 0:
            riders += [flip_gather(w1[0], size), flip_gather(down_turned[0], size)]
        else:
            riders += [fsdp_gather(up, size), fsdp_gather(down, size)]
        o, lse, got = attend(qw, kv, flags, 16 * n + 1, riders)
        w_out = out_whole(got[0])
        w_up, w_down = got[1:]
        w_up, w_down = w_up.reshape(768, 768), w_down.reshape(768, 768)
        vecs = vectors(n)
        weights.append((w_in, w_up, w_down, w_out, vecs))
        riders = []
        if not last:
            riders = [
                tp_flip(w1[n + 1]), tp_flip(down_turned[n + 1]),
                plane_gather(out_piece[n + 1], size), fsdp_gather(own_in[n + 1], size),
            ]
        stream, rounded, xhat1, r1, xhat2, r2, xg2, act, slope, rows, got = block(
            o, w_out, w_up, w_down, units[n][None], vecs, stream, 16 * n + 2, riders
        )
        saved.append((xg, qw, kv, o, lse, xhat1, r1, xhat2, r2, xg2, act, slope, rows))
        if not last:
            up, down, out, w_in = got
            xg, qw, kv, w_in, _ = project(rounded, w_in.reshape(768, 640), in_bias[n + 1][None], 16 * n + 16)
    output = rounded

    grad = cotangent.astype(F32)
    small, heads = [None] * layers, [None] * layers
    done = [None] * layers
    above = None
    for n in reversed(range(layers)):
        w_in, w_up, w_down, w_out, vecs = weights[n]
        xg, qw, kv, o, lse, xhat1, r1, xhat2, r2, xg2, act, slope, rows = saved[n]
        riders = []
        if above is not None:
            riders = [plane_scatter(above["out"], size), fsdp_scatter(above["in"], size)]
        back_one, do, small[n], d_ffn, d_out, got = block_back(
            grad, xhat2, r2, xhat1, r1, vecs, slope, w_up, w_down, w_out, xg2, act, rows, 16 * n + 3, riders
        )
        if above is not None:
            above["out"] = low(added(got[0], (0, 1)))
            above["in"] = low(added(got[1])).reshape(4, depth // 4, 640)
        d_ffn = d_ffn.reshape(2, size, 2, depth // 2, 768)
        riders = [scatter_flip(d_ffn), ctx_scatter(d_out.reshape(4, size, 4, piece, 192), axis=2)]
        if above is not None:
            riders += [ctx_scatter(above["ffn"]), ctx_scatter(above["in"]), ctx_gather(above["out"])]
        dqw, dkv, got = attend_back(qw, kv, do, o, lse, flags, 16 * n + 4, riders)
        d_ffn = got[0]
        d_out = low(added(got[1]))
        riders = []
        if above is not None:
            above["out"] = got[4]
            riders = [ctx_gather(low(added(got[2]))), ctx_gather(low(added(got[3])))]
        if n == 0:
            riders += [ctx_scatter(d_ffn), plane_scatter(d_out, size)]
        grad, d_in, sums, got = project_back(dqw, dkv, w_in, back_one, xg, 16 * n + 5, riders)
        if above is not None:
            done[n + 1] = (got[1], above["out"], got[0])
        d_in = d_in.reshape(1, size, depth, 640)
        d_query_bias, _, d_value_bias = parted(sums)
        heads[n] = jnp.stack([d_query_bias, d_value_bias])
        above = {"ffn": d_ffn, "out": d_out, "in": d_in}
    hidden_grad = low(grad)
    memory_part = lax.dot_general(
        marks, grad, (((0,), (0,)), ((), ())),
        precision=lax.Precision.HIGHEST, preferred_element_type=F32,
    )
    ffn0 = low(added(got[-2]))
    out0 = low(added(got[-1], (0, 1)))
    small = jnp.stack(small)
    place = (ids == t).astype(F32)
    unit = (ids == flipped_place(c, t)).astype(F32)
    head_rows = (jnp.stack(heads)[:, :, None, :] * place[None, None, :, None]).reshape(2 * layers, 768)
    unit_rows = (small[:, 6][:, None, :] * unit[None, :, None]).reshape(4 * layers, 768)
    stat_rows = small[:, :6].reshape(6 * layers, 768)
    short = 48 - 12 * layers - memory_part.shape[0]
    sums = jnp.concatenate([stat_rows, unit_rows, head_rows, memory_part, jnp.zeros((short, 768), F32)])
    got = carry(
        [fsdp_scatter(d_in, size), ctx_gather(ffn0), ctx_gather(out0), ctx_scatter(sums.reshape(4, 12, 768))], 6
    )
    d_in = low(added(got[0])).reshape(4, depth // 4, 640)
    ffn0, out0 = got[1:3]
    got = carry([ctx_scatter(d_in), plane_gather(added(got[3]), size)], 7)
    got = carry([ctx_gather(low(added(got[0]))), ctx_gather(added(got[1], (0, 1)))], 8)
    done[0] = (got[0], out0, ffn0)
    totals = got[1].reshape(48, 768)
    stats = totals[: 6 * layers].reshape(layers, 6, 768)
    at = 6 * layers
    ffn_rows = totals[at : at + 4 * layers].reshape(layers, 4, 768)
    ffn_grad = jnp.sum(ffn_rows * place[None, :, None], axis=1)
    at += 4 * layers
    head_sums = totals[at : at + 2 * layers].reshape(layers, 2, 4, 192)
    head_grad = jnp.sum(head_sums * place[None, None, :, None], axis=2)
    at += 2 * layers
    memory_grad = totals[at : at + memory_part.shape[0]]
    d_in = jnp.stack([part[0].reshape(depth, 640) for part in done]).astype(F32)
    d_out = jnp.stack([jnp.swapaxes(part[1].reshape(depth, 192), 0, 1) for part in done]).astype(F32)
    d_ffn = jnp.stack([part[2].reshape(2, depth, 768) for part in done]).astype(F32)
    return (
        output, hidden_grad, memory_grad, *parted(d_in), d_out, d_ffn[:, 0], jnp.swapaxes(d_ffn[:, 1], 1, 2),
        head_grad, ffn_grad, stats[:, 4:6], stats[:, 0:2], stats[:, 2:4],
    )


def solution(mesh):
    rows = P(("fsdp", "ctx", "tp"), None)
    inner = P(None, "fsdp", "tp")
    outer = P(None, "tp", "fsdp")
    weights = (inner, inner, inner, outer, inner, outer)
    biases = (P(None, None, "tp"), P(None, "tp"), P(), P(), P())
    return jax.shard_map(
        shards,
        mesh=mesh,
        in_specs=(rows, rows, P("fsdp", "ctx", None), P("fsdp", None), P()) + weights + biases,
        out_specs=(rows, rows, P()) + weights + biases,
        check_vma=False,
    )
```

```python
import functools

import jax
import jax.numpy as jnp
from jax import lax
from jax.experimental import pallas as pl
from jax.experimental.pallas import tpu as pltpu
from jax.sharding import PartitionSpec as P

EPSILON = 1e-05
MASKED = -1000000000.0
MESH = pl.DeviceIdType.MESH
F32 = jnp.float32
BF16 = jnp.bfloat16
ORDER = ((0, 1), (1, 0), (2, 2), (3, 3))


def mm(left, right):
    return jnp.dot(left, right, preferred_element_type=F32)


def mm_nt(left, right):
    return lax.dot_general(left, right, (((1,), (1,)), ((), ())), preferred_element_type=F32)


def mm_tn(left, right):
    return lax.dot_general(left, right, (((0,), (0,)), ((), ())), preferred_element_type=F32)


def rcopy(src, dst, send_sem, recv_sem, device):
    return pltpu.make_async_remote_copy(
        src_ref=src,
        dst_ref=dst,
        send_sem=send_sem,
        recv_sem=recv_sem,
        device_id=device,
        device_id_type=MESH,
    )


def mate_of(c):
    return c + 1 - 2 * (c % 2)


def across_of(c):
    return (c + 2) % 4


def signal(sem, device):
    pl.semaphore_signal(sem, inc=1, device_id=device, device_id_type=MESH)


def ordered(place, step):
    half = place // 2
    inner = place + half * (3 - 2 * place)
    first, second = ORDER[step]
    chunk = first + inner * (second - first)
    return chunk + half * (3 - 2 * chunk)


def dma(*shape):
    return pltpu.SemaphoreType.DMA(shape)


class Rider:
    def __init__(self, array, out, make, scratch, chunks=0):
        self.array, self.out, self.make, self.scratch, self.chunks = array, out, make, scratch, chunks
        self.late = False

    def after(self):
        self.late = True
        return self


class Copies:
    def __init__(self, steps, here, scratch):
        self.steps, self.here = steps, here
        self.send, self.recv, self.leg, self.stage = scratch
        self.turned = False

    def greetings(self):
        return [(origin, when, weight) for _, origin, _, _, when, weight in self.steps]

    def copies(self):
        for number, (to, _, source, target, when, _) in enumerate(self.steps):
            yield rcopy(source, target, self.send.at[number], self.recv.at[number], to), when

    def inward(self):
        return pltpu.make_async_copy(self.here[0], self.stage, self.leg.at[0])

    def outward(self):
        return pltpu.make_async_copy(self.stage, self.here[1], self.leg.at[1])

    def start(self):
        for copy, when in self.copies():
            guarded(when, copy.start)
        guarded(self.here[2], self.inward().start)

    def turn(self):
        guarded(self.here[2], self.inward().wait)
        guarded(self.here[2], self.outward().start)

    def finish(self):
        for copy, when in self.copies():
            guarded(when, copy.wait)
        guarded(self.here[2], self.outward().wait)


class FlipGather:
    def __init__(self, source, target, place, scratch):
        self.source, self.target = source, target
        self.f, self.c, self.t = place
        self.size = target.shape[0]
        self.send, self.recv, self.on_send, self.on_recv, self.leg, self.stage = scratch
        self.moves = self.c > 0

    def greetings(self):
        there = {"tp": flipped_place(self.c, self.t)}
        ring = [({"fsdp": (self.f + self.size - k) % self.size}, None, 1) for k in range(1, self.size)]
        return [(there, self.moves, (self.c + 3) // 4)] + ring

    def first(self, chunk):
        there = {"tp": flipped_place(self.c, self.t)}
        return rcopy(
            self.source.at[chunk], self.target.at[self.f, chunk], self.send.at[chunk], self.recv.at[chunk], there
        )

    def second(self, chunk, k, moved):
        source = self.target.at[self.f, chunk] if moved else self.source.at[chunk]
        device = {"fsdp": (self.f + k) % self.size}
        return rcopy(
            source, self.target.at[self.f, chunk], self.on_send.at[k - 1, chunk], self.on_recv.at[k - 1, chunk], device
        )

    def inward(self):
        return pltpu.make_async_copy(self.source, self.stage, self.leg.at[0])

    def outward(self):
        return pltpu.make_async_copy(self.stage, self.target.at[self.f], self.leg.at[1])

    def start(self):
        @pl.when(self.moves)
        def _():
            for chunk in range(self.source.shape[0]):
                self.first(chunk).start()

        @pl.when(self.c == 0)
        def _():
            self.inward().start()

    def hop(self, chunk):
        @pl.when(self.moves)
        def _():
            self.first(chunk).wait_recv()
            for k in range(1, self.size):
                self.second(chunk, k, True).start()

        @pl.when(self.c == 0)
        def _():
            for k in range(1, self.size):
                self.second(chunk, k, False).start()

    def turn(self):
        @pl.when(self.c == 0)
        def _():
            self.inward().wait()
            self.outward().start()

    def finish(self):
        @pl.when(self.moves)
        def _():
            for chunk in range(self.source.shape[0]):
                self.first(chunk).wait_send()

        for chunk in range(self.source.shape[0]):
            for k in range(1, self.size):
                self.second(chunk, k, False).wait()

        @pl.when(self.c == 0)
        def _():
            self.outward().wait()


class ScatterFlip:
    def __init__(self, source, target, place, scratch):
        self.source, self.target = source, target
        self.f, self.c, self.t = place
        self.size = source.shape[1]
        self.send, self.recv, self.on_send, self.on_recv, self.leg, self.got, self.out = scratch
        self.moves = self.c > 0

    def greetings(self):
        there = {"tp": flipped_place(self.c, self.t)}
        ring = [({"fsdp": (self.f + self.size - k) % self.size}, None, 1) for k in range(1, self.size)]
        return [(there, self.moves, (self.c + 3) // 4)] + ring

    def first(self, chunk, k):
        to = (self.f + k) % self.size
        return rcopy(
            self.source.at[chunk // 2, to, chunk % 2], self.got.at[k, chunk],
            self.send.at[k - 1, chunk], self.recv.at[k - 1, chunk], {"fsdp": to},
        )

    def own(self, chunk):
        return pltpu.make_async_copy(
            self.source.at[chunk // 2, self.f, chunk % 2], self.got.at[0, chunk], self.leg.at[chunk]
        )

    def second(self, chunk):
        there = {"tp": flipped_place(self.c, self.t)}
        return rcopy(self.out.at[chunk], self.target.at[chunk], self.on_send.at[chunk], self.on_recv.at[chunk], there)

    def stays(self, chunk):
        return pltpu.make_async_copy(self.out.at[chunk], self.target.at[chunk], self.on_send.at[chunk])

    def start(self):
        for chunk in range(self.target.shape[0]):
            for k in range(1, self.size):
                self.first(chunk, k).start()
            self.own(chunk).start()

    def hop(self, chunk):
        self.own(chunk).wait()
        total = self.got[0, chunk].astype(F32)
        for k in range(1, self.size):
            self.first(chunk, k).wait_recv()
            total += self.got[k, chunk].astype(F32)
        self.out[chunk] = total.astype(BF16)

        @pl.when(self.moves)
        def _():
            self.second(chunk).start()

        @pl.when(self.c == 0)
        def _():
            self.stays(chunk).start()

    def turn(self):
        pass

    def finish(self):
        for chunk in range(self.target.shape[0]):
            for k in range(1, self.size):
                self.first(chunk, k).wait_send()

            @pl.when(self.moves)
            def _():
                self.second(chunk).wait()

            @pl.when(self.c == 0)
            def _():
                self.stays(chunk).wait()


class CtxGather:
    def __init__(self, source, target, place, scratch):
        self.source, self.target = source, target
        self.c = place[1]
        self.send, self.recv, self.leg, self.stage = scratch

    def greetings(self):
        return [({"ctx": mate_of(self.c)}, None, 1), ({"ctx": across_of(self.c)}, None, 1)]

    def copy(self, number):
        c = self.c
        device = across_of(c) if number == 0 else mate_of(c)
        source = self.target.at[across_of(c)] if number == 2 else self.source
        slot = across_of(c) if number == 2 else c
        return rcopy(source, self.target.at[slot], self.send.at[number], self.recv.at[number], {"ctx": device})

    def inward(self):
        return pltpu.make_async_copy(self.source, self.stage, self.leg.at[0])

    def outward(self):
        return pltpu.make_async_copy(self.stage, self.target.at[self.c], self.leg.at[1])

    def start(self):
        self.copy(0).start()
        self.copy(1).start()
        self.inward().start()

    def turn(self):
        self.inward().wait()
        self.outward().start()
        self.copy(0).wait_recv()
        self.copy(2).start()

    def finish(self):
        self.copy(0).wait_send()
        self.copy(1).wait()
        self.copy(2).wait()
        self.outward().wait()


class CtxScatter:
    def __init__(self, pick, source, target, place, scratch):
        self.source, self.target, self.pick = source, target, pick
        self.c = place[1]
        self.send, self.recv, self.leg, self.stage, self.cross, self.far, self.total = scratch

    def greetings(self):
        return [({"ctx": mate_of(self.c)}, None, 1), ({"ctx": across_of(self.c)}, None, 1)]

    def copy(self, number):
        c = self.c
        device = across_of(c) if number == 2 else mate_of(c)
        source = (self.pick(self.source, 3 - c), self.pick(self.source, mate_of(c)), self.total)[number]
        target = (self.far, self.target.at[1], self.target.at[2])[number]
        return rcopy(source, target, self.send.at[number], self.recv.at[number], {"ctx": device})

    def inward(self):
        return pltpu.make_async_copy(self.pick(self.source, self.c), self.stage, self.leg.at[0])

    def outward(self):
        return pltpu.make_async_copy(self.stage, self.target.at[0], self.leg.at[1])

    def beside(self):
        return pltpu.make_async_copy(self.pick(self.source, across_of(self.c)), self.cross, self.leg.at[2])

    def start(self):
        self.copy(0).start()
        self.beside().start()
        self.copy(1).start()
        self.inward().start()

    def turn(self):
        self.copy(0).wait_recv()
        self.beside().wait()
        self.total[...] = (self.cross[...].astype(F32) + self.far[...].astype(F32)).astype(self.total.dtype)
        self.copy(2).start()
        self.inward().wait()
        self.outward().start()

    def finish(self):
        self.copy(0).wait_send()
        self.copy(1).wait()
        self.copy(2).wait()
        self.outward().wait()


class Riding:
    def __init__(self, riders, sources, targets, scratch, fetches, results, puts):
        self.fetches, self.results, self.puts = fetches, results, puts
        self.gone = [False] * len(puts)
        place = tuple(lax.axis_index(axis) for axis in ("fsdp", "ctx", "tp"))
        scratch = list(scratch)
        self.rides, self.hops, self.late = [], [], []
        self.turned = False
        for rider, source, target in zip(riders, sources, targets):
            own = [scratch.pop(0) for _ in rider.scratch]
            ride = rider.make(source, target, place, own)
            self.rides.append(ride)
            if rider.late:
                self.late.append(ride)
            self.hops += [(ride, chunk) for chunk in range(rider.chunks)]

    def ready(self):
        for fetch in self.fetches:
            fetch.wait()

    def put(self, *refs):
        for ref in refs:
            slot = [ref is result for result in self.results].index(True)
            self.gone[slot] = True
            self.puts[slot].start()

    def close(self):
        for slot, put in enumerate(self.puts):
            if not self.gone[slot]:
                put.start()
        for put in self.puts:
            put.wait()

    def greet(self, barrier):
        count = 0
        for ride in self.rides:
            for origin, when, weight in ride.greetings():
                guarded(when, functools.partial(signal, barrier, origin))
                count = count + weight
        return count

    def start(self):
        for ride in self.rides:
            if ride not in self.late:
                ride.start()

    def one_hop(self, at):
        ride, chunk = self.hops[at]
        ride.hop(chunk)
        if at == len(self.hops) - 1:
            for ride in self.late:
                ride.start()

    def hop(self, number):
        for at in range(len(self.hops)):
            pl.when(number == at)(functools.partial(self.one_hop, at))

    def turn_at(self, number, at):
        if self.rides:
            pl.when(number == at)(self.turn)

    def turn(self):
        self.turned = True
        for ride in self.rides:
            ride.turn()

    def finish(self):
        if not self.turned:
            self.turn()
        for ride in self.rides:
            ride.finish()


def guarded(when, action):
    if when is None:
        action()
    else:
        pl.when(when)(action)


def call(kernel, operands, out_shapes, scratch, collective_id, name, cost, riders=(), smem=()):
    n_in, n_out, n_scratch, n_ride = len(operands), len(out_shapes), len(scratch), len(riders)
    large = [i for i in range(n_in) if i not in smem]

    def body(*refs):
        refs = list(refs)
        take = lambda n: [refs.pop(0) for _ in range(n)]
        ins, sources, outs, targets = take(n_in), take(n_ride), take(n_out), take(n_ride)
        near_ins, near_outs, (in_sem, out_sem), own = take(len(large)), take(n_out), take(2), take(n_scratch)
        fetches = [
            pltpu.make_async_copy(ins[i], near, in_sem.at[slot]) for slot, (i, near) in enumerate(zip(large, near_ins))
        ]
        for fetch in fetches:
            fetch.start()
        for i, near in zip(large, near_ins):
            ins[i] = near
        puts = [pltpu.make_async_copy(near, far, out_sem.at[i]) for i, (near, far) in enumerate(zip(near_outs, outs))]
        ride = Riding(riders, sources, targets, refs, fetches, near_outs, puts)
        kernel(ride, *ins, *near_outs, *own)
        ride.close()

    params = dict(vmem_limit_bytes=60 * 1024 * 1024)
    if collective_id is not None:
        params.update(collective_id=collective_id, has_side_effects=True)
    extra = [item for rider in riders for item in rider.scratch]
    anywhere = pl.BlockSpec(memory_space=pl.ANY)
    near = [pltpu.VMEM(operands[i].shape, operands[i].dtype) for i in large]
    near += [pltpu.VMEM(out.shape, out.dtype) for out in out_shapes]
    results = pl.pallas_call(
        body,
        out_shape=list(out_shapes) + [rider.out for rider in riders],
        in_specs=[pl.BlockSpec(memory_space=pltpu.SMEM) if i in smem else anywhere for i in range(n_in)]
        + [anywhere] * n_ride,
        out_specs=[anywhere] * (n_out + n_ride),
        scratch_shapes=near + [dma(max(len(large), 1)), dma(max(n_out, 1))] + list(scratch) + extra,
        compiler_params=pltpu.CompilerParams(**params),
        cost_estimate=pl.CostEstimate(flops=cost[0], bytes_accessed=cost[1], transcendentals=cost[2]),
        name=name,
    )(*operands, *[rider.array for rider in riders])
    return results[:n_out], results[n_out:]


def copies_rider(array, out, steps, stage, plan):
    def make(source, target, place, scratch):
        return Copies(*plan(source, target, *place), scratch)

    scratch = [dma(steps), dma(steps), dma(2), pltpu.VMEM(stage, array.dtype)]
    return Rider(array, out, make, scratch)


def flip_gather(own, size):
    own = own.reshape(2, own.shape[0] // 2, own.shape[1])
    scratch = [dma(2), dma(2), dma(size - 1, 2), dma(size - 1, 2), dma(2), pltpu.VMEM(own.shape, own.dtype)]
    return Rider(own, sds(size, *own.shape), FlipGather, scratch, chunks=2)


def scatter_flip(parts):
    n, size = parts.shape[0], parts.shape[1]
    shape = (2 * n, *parts.shape[3:])
    scratch = [
        dma(size - 1, 2 * n), dma(size - 1, 2 * n), dma(2 * n), dma(2 * n), dma(2 * n),
        pltpu.VMEM((size, *shape), BF16), pltpu.VMEM(shape, BF16),
    ]
    return Rider(parts, sds(*shape), ScatterFlip, scratch, chunks=2 * n)


def fsdp_gather(own, size):
    def make(source, target, f, c, t):
        steps = [
            ({"fsdp": (f + k) % size}, {"fsdp": (f + size - k) % size}, source, target.at[f], None, 1)
            for k in range(1, size)
        ]
        return steps, (source, target.at[f], None)

    return copies_rider(own, sds(size, *own.shape, dtype=own.dtype), size - 1, own.shape, make)


def fsdp_scatter(parts, size):
    out = sds(size, parts.shape[0], *parts.shape[2:], dtype=parts.dtype)

    def make(source, target, f, c, t):
        steps = [
            (
                {"fsdp": (f + k) % size}, {"fsdp": (f + size - k) % size},
                source.at[:, (f + k) % size], target.at[k], None, 1,
            )
            for k in range(1, size)
        ]
        return steps, (source.at[:, f], target.at[0], None)

    return copies_rider(parts, out, size - 1, out.shape[1:], make)


def ctx_gather(own):
    scratch = [dma(3), dma(3), dma(2), pltpu.VMEM(own.shape, own.dtype)]
    return Rider(own, sds(4, *own.shape, dtype=own.dtype), CtxGather, scratch)


def ctx_scatter(parts, axis=0):
    shape = parts.shape[:axis] + parts.shape[axis + 1 :]

    def pick(ref, slot):
        return ref.at[slot] if axis == 0 else ref.at[:, :, slot]

    buffer = pltpu.VMEM(shape, parts.dtype)
    scratch = [dma(3), dma(3), dma(3), buffer, buffer, buffer, buffer]
    return Rider(parts, sds(3, *shape, dtype=parts.dtype), functools.partial(CtxScatter, pick), scratch)


def flipped_place(c, t):
    return 2 * ((t // 2 + c % 2) % 2) + (t % 2 + c // 2) % 2


def tp_flip(own):
    def make(source, target, f, c, t):
        other = {"tp": flipped_place(c, t)}
        return [(other, other, source, target, c > 0, (c + 3) // 4)], (source, target, c == 0)

    return copies_rider(own, sds(*own.shape, dtype=own.dtype), 1, own.shape, make)


def plane(size):
    return [(kt, kf) for kt in (2, 3, 1, 0) for kf in range(size) if kt + kf > 0]


def plane_gather(own, size):
    def make(source, target, f, c, t):
        steps = [
            (
                {"fsdp": (f + kf) % size, "tp": (t + kt) % 4},
                {"fsdp": (f + size - kf) % size, "tp": (t + 4 - kt) % 4},
                source, target.at[t, f], None, 1,
            )
            for kt, kf in plane(size)
        ]
        return steps, (source, target.at[t, f], None)

    return copies_rider(own, sds(4, size, *own.shape, dtype=own.dtype), 4 * size - 1, own.shape, make)


def plane_scatter(parts, size):
    def make(source, target, f, c, t):
        steps = [
            (
                {"fsdp": (f + kf) % size, "tp": (t + kt) % 4},
                {"fsdp": (f + size - kf) % size, "tp": (t + 4 - kt) % 4},
                source.at[(t + kt) % 4, (f + kf) % size], target.at[kt, kf], None, 1,
            )
            for kt, kf in plane(size)
        ]
        return steps, (source.at[t, f], target.at[0, 0], None)

    return copies_rider(parts, sds(*parts.shape, dtype=parts.dtype), 4 * size - 1, parts.shape[2:], make)


def all_gather(own, size):
    others = [(kt, kc, kf) for kt in (2, 3, 1, 0) for kc in (2, 3, 1, 0) for kf in range(size)][:-size] + [
        (0, 0, kf) for kf in range(1, size)
    ]

    def make(source, target, f, c, t):
        steps = [
            (
                {"fsdp": (f + kf) % size, "ctx": (c + kc) % 4, "tp": (t + kt) % 4},
                {"fsdp": (f + size - kf) % size, "ctx": (c + 4 - kc) % 4, "tp": (t + 4 - kt) % 4},
                source, target.at[c, t, f], None, 1,
            )
            for kt, kc, kf in others
        ]
        return steps, (source, target.at[c, t, f], None)

    return copies_rider(own, sds(4, 4, size, *own.shape, dtype=own.dtype), 16 * size - 1, own.shape, make)


def carry_kernel(ride):
    barrier = pltpu.get_barrier_semaphore()
    pl.semaphore_wait(barrier, ride.greet(barrier))
    ride.start()
    ride.finish()


def carry(riders, cid):
    return call(carry_kernel, (), (), (), cid, "carry", (1 << 20, 1 << 20, 0), riders)[1]


def sds(*shape, dtype=BF16):
    return jax.ShapeDtypeStruct(shape, dtype)


def project_kernel(
    fetch, ride, x_ref, w_ref, b_ref, xg_ref, qw_ref, kv_ref, *rest
):
    if fetch:
        full_ref, w_send, w_recv, *rest = rest
    (
        qbuf, x_recv, x_right, x_left, k1_send, k1_recv, k2_send, k2_recv, kf_send, kf_recv, q_send, q_recv,
    ) = rest
    c = lax.axis_index("ctx")
    t = lax.axis_index("tp")
    barrier = pltpu.get_barrier_semaphore()
    for device in (mate_of(c), across_of(c), 3 - c):
        signal(barrier, {"ctx": device})

    @pl.when(t > 0)
    def _():
        signal(barrier, {"tp": t - 1})

    @pl.when(t < 3)
    def _():
        signal(barrier, {"tp": t + 1})

    f, size = lax.axis_index("fsdp"), lax.axis_size("fsdp")
    if fetch:
        for k in range(1, size):
            signal(barrier, {"fsdp": (f + size - k) % size})
    ends = (t // 3) + (3 - t) // 3
    count = 5 - ends + ride.greet(barrier) + (size - 1 if fetch else 0)
    ride.ready()
    pl.semaphore_wait(barrier, count)

    def right(src, chunk, step):
        return rcopy(src, xg_ref.at[chunk], x_right.at[step], x_recv.at[chunk], {"tp": t + 1})

    def left(src, chunk, step):
        return rcopy(src, xg_ref.at[chunk], x_left.at[step], x_recv.at[chunk], {"tp": t - 1})

    def arrived(chunk):
        rcopy(xg_ref.at[chunk], xg_ref.at[chunk], x_right.at[0], x_recv.at[chunk], {"tp": t}).wait_recv()

    @pl.when(t < 3)
    def _():
        right(x_ref, t, 0).start()

    @pl.when(t > 0)
    def _():
        left(x_ref, t, 0).start()

    def weight(k):
        device = {"fsdp": (f + k) % size}
        return rcopy(w_ref, full_ref.at[f], w_send.at[k - 1], w_recv.at[k - 1], device)

    if fetch:
        for k in range(1, size):
            weight(k).start()
        full_ref[f] = w_ref[...]
        for k in range(1, size):
            weight(k).wait_recv()
    ride.start()

    def mate(chunk):
        return rcopy(kv_ref.at[c, chunk], kv_ref.at[c, chunk], k1_send.at[chunk], k1_recv.at[chunk], {"ctx": mate_of(c)})

    def across(chunk):
        return rcopy(kv_ref.at[c, chunk], kv_ref.at[c, chunk], k2_send.at[chunk], k2_recv.at[chunk], {"ctx": across_of(c)})

    def onward(chunk):
        return rcopy(
            kv_ref.at[across_of(c), chunk], kv_ref.at[across_of(c), chunk], kf_send.at[chunk], kf_recv.at[chunk], {"ctx": mate_of(c)}
        )

    def partner(slot):
        return rcopy(qbuf.at[slot], qw_ref.at[slot + 2], q_send.at[slot], q_recv.at[slot], {"ctx": 3 - c})

    for step in range(4):
        if step == 0:
            xg_ref[t] = x_ref[...]
        else:

            @pl.when(t - step >= 0)
            def _():
                arrived(t - step)

                @pl.when(t < 3)
                def _():
                    right(xg_ref.at[t - step], t - step, step).start()

            @pl.when(t + step <= 3)
            def _():
                arrived(t + step)

                @pl.when(t > 0)
                def _():
                    left(xg_ref.at[t + step], t + step, step).start()

        chunk = ordered(t, step)
        w = full_ref[...].reshape(768, 640) if fetch else w_ref[...]
        made = mm(xg_ref[chunk], w) + b_ref[...]
        kv_ref[c, chunk] = made[:, 256:].astype(BF16)
        mate(chunk).start()
        across(chunk).start()
        query = (made[:, :256] * 0.125).astype(BF16)

        @pl.when(chunk < 2)
        def _():
            qw_ref[chunk] = query

        @pl.when(chunk >= 2)
        def _():
            qbuf[chunk - 2] = query
            partner(chunk - 2).start()

        if step >= 1:
            before = ordered(t, step - 1)
            across(before).wait_recv()
            onward(before).start()
    ride.put(xg_ref)
    ride.turn()
    last = ordered(t, 3)
    across(last).wait_recv()
    onward(last).start()
    for chunk in range(4):
        mate(chunk).wait()
        across(chunk).wait_send()
        onward(chunk).wait()
    for slot in range(2):
        partner(slot).wait()

    @pl.when(t < 3)
    def _():
        right(x_ref, t, 0).wait_send()

    @pl.when(t > 0)
    def _():
        left(x_ref, t, 0).wait_send()

    for step in (1, 2):

        @pl.when((t - step >= 0) & (t < 3))
        def _():
            right(xg_ref.at[t - step], t - step, step).wait_send()

        @pl.when((t + step <= 3) & (t > 0))
        def _():
            left(xg_ref.at[t + step], t + step, step).wait_send()

    if fetch:
        for k in range(1, size):
            weight(k).wait_send()
    ride.finish()


def project(x, w, b, cid, riders=(), fetch=False):
    outs = [sds(4, 256, 768), sds(4, 256, 256), sds(4, 4, 256, 384)]
    scratch = [
        pltpu.VMEM((2, 256, 256), BF16),
        dma(4), dma(3), dma(3),
        dma(4), dma(4), dma(4), dma(4), dma(4), dma(4), dma(2), dma(2),
    ]
    if fetch:
        size = lax.axis_size("fsdp")
        outs.append(sds(size, *w.shape))
        scratch = [dma(size - 1), dma(size - 1)] + scratch
    cost = (2 * 1024 * 768 * 640, 8 << 20, 0)
    kernel = functools.partial(project_kernel, fetch)
    res, ridden = call(kernel, (x, w, b), outs, scratch, cid, "project", cost, riders)
    xg, qw, kv = res[:3]
    full = res[3].reshape(768, 640) if fetch else w
    return xg.reshape(1024, 768), qw.reshape(1024, 256), kv.reshape(4, 1024, 384), full, ridden


def norm_stats(summed):
    row_mean = jnp.mean(summed, axis=-1, keepdims=True)
    centered = summed - row_mean
    variance = jnp.mean(centered * centered, axis=-1, keepdims=True)
    scale = lax.rsqrt(variance + EPSILON)
    return centered * scale, scale


def norm_back(grad, xhat, scale, gain):
    scaled = grad * gain
    first = jnp.mean(scaled, axis=-1, keepdims=True)
    second = jnp.mean(scaled * xhat, axis=-1, keepdims=True)
    return scale * (scaled - first - xhat * second)


def gelu_both(up):
    phi = 0.5 * (1.0 + lax.erf(up * 0.7071067811865476))
    slope = phi + up * jnp.exp(-0.5 * up * up) * 0.3989422804014327
    return (up * phi).astype(BF16), slope.astype(BF16)


Q_TILE = 256
FAR = 1e30
K_TILE = 256


def open_up(ride):
    if ride.rides:
        barrier = pltpu.get_barrier_semaphore()
        count = ride.greet(barrier)
        pl.semaphore_wait(barrier, count)
        ride.start()
    ride.ready()


def attend_kernel(ride, flag_ref, qw_ref, kv_ref, o_ref, lse_ref, qm_ref, m_ref, acc_ref, vo_ref):
    c = lax.axis_index("ctx")
    open_up(ride)
    low = lax.broadcasted_iota(jnp.int32, (Q_TILE, 128), 1) < 64
    per_half = 512 // Q_TILE
    for side, at in enumerate((128, 256)):
        vo_ref[side, :, 0:128] = kv_ref[:, at : at + 128]
        vo_ref[side, :, 128:256] = jnp.ones((4096, 128), BF16)

    @pl.loop(0, 1024 // Q_TILE)
    def _(tile):
        half = tile // per_half
        segment = c + half * (3 - 2 * c)
        rows = pl.ds(pl.multiple_of(tile * Q_TILE, Q_TILE), Q_TILE)
        pair = qw_ref[rows, 0:128]
        qm_ref[0] = jnp.where(low, pair, jnp.zeros_like(pair))
        qm_ref[1] = jnp.where(low, jnp.zeros_like(pair), pair)
        qm_ref[2] = qw_ref[rows, 128:256]
        m_ref[...] = jnp.full_like(m_ref, MASKED)
        acc_ref[...] = jnp.zeros_like(acc_ref)

        @pl.loop(0, segment + 1)
        def _(block):
            seen = flag_ref[half, block] > 0
            penalty = jnp.where(seen, 0.0, FAR)
            keys = pl.ds(pl.multiple_of(block * 1024, 1024), 1024)
            for head in range(3):
                k_at = 0 if head < 2 else 128
                scores = mm_nt(qm_ref[head], kv_ref[keys, k_at : k_at + 128])
                old = m_ref[head]
                most = jnp.max(scores, axis=-1, keepdims=True)
                new = jnp.maximum(old, jnp.where(seen, most, MASKED))
                probs = jnp.exp(scores - (new + penalty)).astype(BF16)
                keep = jnp.exp(old - new)
                m_ref[head] = new
                acc_ref[head] = acc_ref[head] * keep + mm(probs, vo_ref[1 if head < 2 else 0, keys])

        whole = [acc_ref[head][:, 128:256] for head in range(3)]
        first = acc_ref[0][:, 0:128] / whole[0]
        second = acc_ref[1][:, 0:128] / whole[1]
        o_ref[rows, 0:128] = jnp.where(low, first, second).astype(BF16)
        o_ref[rows, 128:192] = (acc_ref[2][:, 0:128] / whole[2])[:, :64].astype(BF16)
        lane = lax.broadcasted_iota(jnp.int32, (Q_TILE, 128), 1)
        totals = [m_ref[head] + jnp.log(whole[head]) for head in range(3)]
        lse_ref[rows, :] = jnp.where(lane == 0, totals[0], jnp.where(lane == 1, totals[1], totals[2]))
        ride.hop(tile)
        ride.turn_at(tile, 2)

    ride.finish()


def attend(qw, kv, flags, cid, riders=()):
    outs = [sds(1024, 192), sds(1024, 128, dtype=F32)]
    scratch = [
        pltpu.VMEM((3, Q_TILE, 128), BF16),
        pltpu.VMEM((3, Q_TILE, 1), F32),
        pltpu.VMEM((3, Q_TILE, 256), F32),
        pltpu.VMEM((2, 4096, 256), BF16),
    ]
    cost = (5 * 512 * 1024 * 64 * 4 * 3, 6 << 20, 5 * 512 * 1024 * 3)
    operands = (flags, qw, kv.reshape(4096, 384))
    cid = cid if riders else None
    res, ridden = call(attend_kernel, operands, outs, scratch, cid, "attend", cost, riders, smem=(0,))
    return res[0], res[1], ridden


def attend_back_kernel(
    ride, flag_ref, qw_ref, kv_ref, do_ref, o_ref, lse_ref, dq_ref, dkv_ref,
    qm_ref, dm_ref, row_ref, acc_ref, key_ref,
):
    c = lax.axis_index("ctx")
    open_up(ride)
    low = lax.broadcasted_iota(jnp.int32, (1024, 128), 1) < 64
    pair = qw_ref[:, 0:128]
    none = jnp.zeros_like(pair)
    qm_ref[0] = jnp.where(low, pair, none)
    qm_ref[1] = jnp.where(low, none, pair)
    qm_ref[2] = qw_ref[:, 128:256]
    pair = do_ref[:, 0:128]
    dm_ref[0] = jnp.where(low, pair, none)
    dm_ref[1] = jnp.where(low, none, pair)
    dm_ref[2] = jnp.concatenate([do_ref[:, 128:192], none[:, :64]], axis=1)
    turned = jnp.transpose(lse_ref[...], (1, 0))
    row_ref[0:8] = turned[0:8]
    product = do_ref[...].astype(F32) * o_ref[...].astype(F32)
    head_row = lax.broadcasted_iota(jnp.int32, (8, 192), 0)
    head_of = lax.broadcasted_iota(jnp.int32, (8, 192), 1) // 64
    marks = (head_row == head_of).astype(F32)
    row_ref[8:16] = lax.dot_general(
        marks, product, (((1,), (1,)), ((), ())),
        precision=lax.Precision.HIGHEST, preferred_element_type=F32,
    )
    acc_ref[...] = jnp.zeros_like(acc_ref)
    low_keys = lax.broadcasted_iota(jnp.int32, (K_TILE, 128), 1) < 64

    @pl.loop(0, 4)
    def _(block):
        @pl.loop(0, 1024 // K_TILE)
        def _(tile):
            keys = pl.ds(pl.multiple_of(block * 1024 + tile * K_TILE, K_TILE), K_TILE)
            key_ref[...] = jnp.zeros_like(key_ref)
            key_pair = kv_ref[keys, 0:128]
            nothing = jnp.zeros_like(key_pair)
            key_parts = (
                jnp.where(low_keys, key_pair, nothing),
                jnp.where(low_keys, nothing, key_pair),
                jnp.where(low_keys, nothing, kv_ref[keys, 128:256]),
            )
            for half in range(2):
                segment = c if half == 0 else 3 - c

                @pl.when(block <= segment)
                def _():
                    penalty = jnp.where(flag_ref[half, block] > 0, 0.0, FAR)
                    rows = pl.ds(half * 512, 512)
                    for head in range(3):
                        k_at = 0 if head < 2 else 128
                        v_at = 256 if head < 2 else 128
                        query = qm_ref[head, rows]
                        grads = dm_ref[head, rows]
                        scores = mm_nt(kv_ref[keys, k_at : k_at + 128], query)
                        probs = jnp.exp(scores - (row_ref[head : head + 1, rows] + penalty))
                        grad_probs = mm_nt(kv_ref[keys, v_at : v_at + 128], grads)
                        grad_scores = (probs * (grad_probs - row_ref[8 + head : 9 + head, rows])).astype(BF16)
                        key_ref[:, v_at : v_at + 128] += mm(probs.astype(BF16), grads)
                        key_ref[:, k_at : k_at + 128] += mm(grad_scores, query)
                        q_at = 0 if head < 2 else 128
                        acc_ref[rows, q_at : q_at + 128] += mm_tn(grad_scores, key_parts[head])

            dkv_ref[keys, :] = key_ref[...].astype(BF16)

        ride.hop(block)
        ride.turn_at(block, 0)

    dq_ref[...] = (acc_ref[...].astype(BF16).astype(F32) * 0.125).astype(BF16)
    ride.finish()


def attend_back(qw, kv, do, o, lse, flags, cid, riders=()):
    outs = [sds(1024, 256), sds(4096, 384)]
    scratch = [
        pltpu.VMEM((3, 1024, 128), BF16),
        pltpu.VMEM((3, 1024, 128), BF16),
        pltpu.VMEM((16, 1024), F32),
        pltpu.VMEM((1024, 256), F32),
        pltpu.VMEM((K_TILE, 384), F32),
    ]
    cost = (5 * 512 * 1024 * 64 * 10 * 3, 12 << 20, 5 * 512 * 1024 * 3)
    operands = (flags, qw, kv.reshape(4096, 384), do, o, lse)
    cid = cid if riders else None
    res, ridden = call(attend_back_kernel, operands, outs, scratch, cid, "attend_back", cost, riders, smem=(0,))
    return res[0], res[1].reshape(4, 1024, 384), ridden


PIECE = 128


def exchange(c, ref, feed, mine_ref, part_ref, send_ref, got_ref, a_send, a_recv, s_send, s_recv, meanwhile):
    mate, across, far = mate_of(c), across_of(c), 3 - c
    pieces = (pl.ds(0, PIECE), pl.ds(PIECE, PIECE))

    def gather(slot, index, p, device):
        part = ref.at[slot, pieces[p]]
        return rcopy(part, part, a_send.at[index, p], a_recv.at[index, p], {"ctx": device})

    def scatter(index, p, device):
        source, target = send_ref.at[index, pieces[p]], got_ref.at[index, pieces[p]]
        return rcopy(source, target, s_send.at[index, p], s_recv.at[index, p], {"ctx": device})

    for p in range(2):
        gather(c, 1, p, across).start()
    for p in range(2):
        gather(c, 0, p, mate).start()
    mine_ref[...] += feed(c, pl.ds(0, 2 * PIECE))
    for p in range(2):
        gather(mate, 0, p, mate).wait_recv()
    send_ref[0] = feed(mate, pl.ds(0, 2 * PIECE)).astype(BF16)
    for p in range(2):
        scatter(0, p, mate).start()

    def take_across(p):
        gather(across, 1, p, across).wait_recv()
        gather(across, 2, p, mate).start()
        part_ref[pieces[p]] = feed(across, pieces[p])

    def take_far(p):
        gather(far, 2, p, mate).wait_recv()
        send_ref[1, pieces[p]] = feed(far, pieces[p]).astype(BF16)
        scatter(1, p, mate).start()

    def join(p):
        scatter(1, p, mate).wait_recv()
        send_ref[2, pieces[p]] = (part_ref[pieces[p]] + got_ref[1, pieces[p]].astype(F32)).astype(BF16)
        scatter(2, p, across).start()

    take_across(0)
    take_far(0)
    take_across(1)
    join(0)
    take_far(1)
    join(1)
    meanwhile()
    for p in range(2):
        scatter(0, p, mate).wait_recv()
        scatter(2, p, across).wait_recv()

    def settle():
        for p in range(2):
            for index in range(3):
                gather(c, index, p, mate).wait_send()
                scatter(index, p, mate).wait_send()

    return mine_ref[...] + got_ref[0].astype(F32) + got_ref[2].astype(F32), settle


def block_kernel(
    ride, o_ref, wo_ref, w1_ref, w2_ref, b1_ref, vec_ref, stream_ref,
    out_ref, low_ref, xhat1_ref, r1_ref, xhat2_ref, r2_ref, xg_ref, act_ref, slope_ref, rows_ref, down_ref,
    w_send, w_recv, mine_ref, part_ref, send_ref, got_ref, o_send, o_recv, a_send, a_recv, s_send, s_recv,
):
    c = lax.axis_index("ctx")
    t = lax.axis_index("tp")
    barrier = pltpu.get_barrier_semaphore()
    for place in range(4):

        @pl.when((t < 2) & (t != place))
        def _():
            signal(barrier, {"tp": place})

        @pl.when(t >= 2)
        def _():
            signal(barrier, {"ctx": 3 - c, "tp": place})

    signal(barrier, {"ctx": mate_of(c)})
    signal(barrier, {"ctx": across_of(c)})
    f, size = lax.axis_index("fsdp"), lax.axis_size("fsdp")
    for k in range(1, size):
        signal(barrier, {"fsdp": (f + size - k) % size})
    count = 5 + t // 2 + size - 1 + ride.greet(barrier)
    ride.ready()
    pl.semaphore_wait(barrier, count)

    def weight(k):
        device = {"fsdp": (f + k) % size}
        return rcopy(w2_ref, down_ref.at[f], w_send.at[k - 1], w_recv.at[k - 1], device)

    def give(quarter):
        device = {"tp": quarter} if quarter < 2 else {"ctx": 3 - c, "tp": quarter}
        return rcopy(o_ref.at[quarter], rows_ref.at[t], o_send.at[quarter], o_recv.at[t], device)

    def given(group):
        rcopy(rows_ref.at[group], rows_ref.at[group], o_send.at[0], o_recv.at[group], {"tp": t}).wait_recv()

    for quarter in (3, 2, 1, 0):
        if quarter < 2:

            @pl.when(t != quarter)
            def _():
                give(quarter).start()

            @pl.when(t == quarter)
            def _():
                rows_ref[quarter] = o_ref[quarter]

        else:
            give(quarter).start()
    for k in range(1, size):
        weight(k).start()
    down_ref[f] = w2_ref[...]
    branch = stream_ref[...] + vec_ref[0:1]
    for group in range(4):

        @pl.when((t >= 2) | (t != group))
        def _():
            given(group)

        branch += mm_nt(rows_ref[group], wo_ref[group])
    ride.start()
    xhat, scale = norm_stats(branch)
    xhat1_ref[...] = xhat
    r1_ref[...] = jnp.broadcast_to(scale, r1_ref.shape)
    normed = xhat * vec_ref[2:3] + vec_ref[3:4]
    xg_ref[c] = normed.astype(BF16)
    mine_ref[...] = normed + vec_ref[1:2]
    for k in range(1, size):
        weight(k).wait_recv()

    def feed(segment, rows):
        up = mm(xg_ref[segment, rows], w1_ref[...]) + b1_ref[...]
        act, slope = gelu_both(up)
        act_ref[segment, rows] = act
        slope_ref[segment, rows] = slope
        return mm_nt(act, down_ref[...].reshape(768, 768))

    def meanwhile():
        ride.turn()
        ride.put(xhat1_ref, r1_ref, xg_ref, act_ref, slope_ref, rows_ref, down_ref)

    summed, settle = exchange(
        c, xg_ref, feed, mine_ref, part_ref, send_ref, got_ref, a_send, a_recv, s_send, s_recv, meanwhile
    )
    xhat, scale = norm_stats(summed)
    xhat2_ref[...] = xhat
    r2_ref[...] = jnp.broadcast_to(scale, r2_ref.shape)
    out = xhat * vec_ref[4:5] + vec_ref[5:6]
    out_ref[...] = out
    low_ref[...] = out.astype(BF16)
    ride.put(out_ref, low_ref, xhat2_ref, r2_ref)
    for quarter in range(4):
        if quarter < 2:

            @pl.when(t != quarter)
            def _():
                give(quarter).wait_send()

        else:
            give(quarter).wait_send()
    for k in range(1, size):
        weight(k).wait_send()
    settle()
    ride.finish()


def block(o, wo, w1, w2, b1, vecs, stream, cid, riders=()):
    size = lax.axis_size("fsdp")
    f = functools.partial(sds, dtype=F32)
    outs = [
        f(256, 768), sds(256, 768), f(256, 768), f(256, 128), f(256, 768), f(256, 128),
        sds(4, 256, 768), sds(4, 256, 768), sds(4, 256, 768), sds(4, 256, 192), sds(size, *w2.shape),
    ]
    scratch = [
        dma(size - 1), dma(size - 1),
        pltpu.VMEM((256, 768), F32),
        pltpu.VMEM((256, 768), F32),
        pltpu.VMEM((3, 256, 768), BF16),
        pltpu.VMEM((3, 256, 768), BF16),
        dma(4), dma(4), dma(3, 2), dma(3, 2), dma(3, 2), dma(3, 2),
    ]
    cost = (2 * 256 * 768 * 768 + 4 * 1024 * 768 * 768, 16 << 20, 1 << 20)
    operands = (o.reshape(4, 256, 192), wo, w1, w2, b1, vecs, stream)
    res, ridden = call(block_kernel, operands, outs, scratch, cid, "block", cost, riders)
    flat = lambda a: a.reshape(1024, 768)
    return tuple(res[:6]) + (flat(res[6]), flat(res[7]), flat(res[8]), res[9], res[10].reshape(768, 768), ridden)


def block_back_kernel(
    ride, grad_ref, xhat2_ref, r2_ref, xhat1_ref, r1_ref, vec_ref, slope_ref, w1_ref, w2_ref, wo_ref,
    xg_ref, act_ref, rows_ref, back_ref, do_ref, stat_ref, dup_ref, ddown_ref, dout_ref,
    w_send, w_recv, term_ref, all_up_ref, gg_ref, gu_ref, mine_ref, part_ref, send_ref, got_ref, dsend_ref, d_send, d_recv, a_send, a_recv, s_send, s_recv,
):
    c = lax.axis_index("ctx")
    t = lax.axis_index("tp")
    barrier = pltpu.get_barrier_semaphore()
    for place in range(4):
        if place < 2:

            @pl.when(t != place)
            def _():
                signal(barrier, {"tp": place})

        else:
            signal(barrier, {"ctx": 3 - c, "tp": place})
    signal(barrier, {"ctx": mate_of(c)})
    signal(barrier, {"ctx": across_of(c)})
    f, size = lax.axis_index("fsdp"), lax.axis_size("fsdp")
    depth = dup_ref.shape[0]
    for k in range(1, size):
        signal(barrier, {"fsdp": (f + size - k) % size})
    count = 5 + t // 2 + size - 1 + ride.greet(barrier)
    ride.ready()
    pl.semaphore_wait(barrier, count)

    def row(values):
        return jnp.sum(values, axis=0, keepdims=True)

    grad = grad_ref[...]
    back_two = norm_back(grad, xhat2_ref[...], r2_ref[:, 0:1], vec_ref[4:5])
    g2 = back_two.astype(BF16)
    gg_ref[c] = g2
    mine_ref[...] = back_two
    ride.start()
    stat_ref[1:2] = row(grad * xhat2_ref[...])
    stat_ref[3:4] = row(grad)
    stat_ref[5:6] = row(g2.astype(F32))
    stat_ref[6:8] = jnp.zeros((2, 768), F32)

    def feed(segment, rows):
        gu = (mm(gg_ref[segment, rows], w2_ref[...]) * slope_ref[segment, rows].astype(F32)).astype(BF16)
        gu_ref[segment, rows] = gu
        stat_ref[6:7] += row(gu.astype(F32))
        return mm_nt(gu, w1_ref[...])

    tall = lambda ref: ref[...].reshape(1024, 768)

    def slice_of(place):
        return pl.ds(pl.multiple_of(place * depth, depth), depth)

    def term(k):
        to = (f + k) % size
        return rcopy(
            all_up_ref.at[slice_of(to)], term_ref.at[k - 1], w_send.at[k - 1], w_recv.at[k - 1], {"fsdp": to}
        )

    def meanwhile():
        @pl.loop(0, 3)
        def _(tile):
            cols = pl.ds(pl.multiple_of(tile * 256, 256), 256)
            all_up_ref[cols] = mm_tn(xg_ref[:, cols], tall(gu_ref)).astype(BF16)

        for k in range(1, size):
            term(k).start()

        @pl.loop(0, 3)
        def _(tile):
            cols = pl.ds(pl.multiple_of(tile * 256, 256), 256)
            ddown_ref[cols] = mm_tn(gg_ref[:, :, cols].reshape(1024, 256), act_ref[...]).astype(BF16)

        ride.put(ddown_ref)
        ride.turn()

    grad_normed, settle = exchange(
        c, gg_ref, feed, mine_ref, part_ref, send_ref, got_ref, a_send, a_recv, s_send, s_recv, meanwhile
    )
    back_one = norm_back(grad_normed, xhat1_ref[...], r1_ref[:, 0:1], vec_ref[2:3])
    back_ref[...] = back_one
    g1 = back_one.astype(BF16)

    def give_near(group):
        return rcopy(dsend_ref.at[group], do_ref.at[t], d_send.at[group], d_recv.at[t], {"tp": group})

    def give_far(group):
        return rcopy(dsend_ref.at[group], do_ref.at[t], d_send.at[group], d_recv.at[t], {"ctx": 3 - c, "tp": group})

    for group in range(4):
        dsend_ref[group] = mm(g1, wo_ref[group]).astype(BF16)

        @pl.when((t < 2) & (t == group))
        def _():
            do_ref[t] = dsend_ref[group]

        @pl.when((t < 2) & (t != group))
        def _():
            give_near(group).start()

        @pl.when(t >= 2)
        def _():
            give_far(group).start()

    stat_ref[0:1] = row(grad_normed * xhat1_ref[...])
    stat_ref[2:3] = row(grad_normed)
    stat_ref[4:5] = row(g1.astype(F32))
    for group in range(4):
        dout_ref[group] = mm_tn(g1, rows_ref[group]).astype(BF16)
    ride.put(back_ref, stat_ref, dout_ref)
    total = all_up_ref[slice_of(f)].astype(F32)
    for k in range(1, size):
        term(k).wait_recv()
        total += term_ref[k - 1].astype(F32)
    dup_ref[...] = total.astype(BF16)
    ride.put(dup_ref)
    for quarter in range(4):

        def taken():
            rcopy(do_ref.at[quarter], do_ref.at[quarter], d_send.at[0], d_recv.at[quarter], {"tp": t}).wait_recv()

        if quarter < 2:
            pl.when(t != quarter)(taken)
        else:
            taken()
    for group in range(4):

        @pl.when((t >= 2) | (t != group))
        def _():
            give_near(group).wait_send()

    for k in range(1, size):
        term(k).wait_send()
    settle()
    ride.finish()


def block_back(grad, xhat2, r2, xhat1, r1, vecs, slope, w1, w2, wo, xg, act, rows, cid, riders=()):
    f = functools.partial(sds, dtype=F32)
    size = lax.axis_size("fsdp")
    depth = 768 // size
    outs = [
        f(256, 768), sds(4, 256, 192), f(8, 768), sds(depth, 768), sds(768, 768), sds(4, 768, 192),
    ]
    scratch = [
        dma(size - 1), dma(size - 1), pltpu.VMEM((size - 1, depth, 768), BF16), pltpu.VMEM((768, 768), BF16),
        pltpu.VMEM((4, 256, 768), BF16),
        pltpu.VMEM((4, 256, 768), BF16),
        pltpu.VMEM((256, 768), F32),
        pltpu.VMEM((256, 768), F32),
        pltpu.VMEM((3, 256, 768), BF16),
        pltpu.VMEM((3, 256, 768), BF16),
        pltpu.VMEM((4, 256, 192), BF16),
        dma(4), dma(4), dma(3, 2), dma(3, 2), dma(3, 2), dma(3, 2),
    ]
    cost = (4 * 256 * 768 * 768 + 8 * 1024 * 768 * 768, 20 << 20, 1 << 10)
    operands = (grad, xhat2, r2, xhat1, r1, vecs, slope.reshape(4, 256, 768), w1, w2, wo, xg, act, rows)
    res, ridden = call(block_back_kernel, operands, outs, scratch, cid, "block_back", cost, riders)
    back, do, stats, d_up, d_down, d_out = res
    return back, do.reshape(1024, 192), stats, d_up, d_down, d_out, ridden


def project_back_kernel(
    ride, dqw_ref, dkv_ref, w_ref, back_ref, xg_ref, mark_ref, grad_ref, low_ref, din_ref, sum_out_ref, mem_ref,
    w_send, w_recv, term_ref, all_in_ref, dq_ref, own_ref, part_ref, near_ref, join_ref, sum_ref, far_ref, pass_ref, take_ref,
    q_send, q_recv, n_send, n_recv, j_send, j_recv, f_send, f_recv, p_send, p_recv,
):
    c = lax.axis_index("ctx")
    t = lax.axis_index("tp")
    barrier = pltpu.get_barrier_semaphore()
    for device in (mate_of(c), across_of(c), 3 - c):
        signal(barrier, {"ctx": device})

    @pl.when(t > 0)
    def _():
        signal(barrier, {"tp": t - 1})

    @pl.when(t < 3)
    def _():
        signal(barrier, {"tp": t + 1})

    ends = (t // 3) + (3 - t) // 3
    f, size = lax.axis_index("fsdp"), lax.axis_size("fsdp")
    depth = din_ref.shape[0]
    for k in range(1, size):
        signal(barrier, {"fsdp": (f + size - k) % size})
    count = 5 - ends + size - 1 + ride.greet(barrier)
    ride.ready()
    pl.semaphore_wait(barrier, count)
    mate, across, far = mate_of(c), across_of(c), 3 - c

    def partner(slot):
        return rcopy(dqw_ref.at[slot + 2], dq_ref.at[slot + 2], q_send.at[slot], q_recv.at[slot], {"ctx": far})

    def near(chunk):
        return rcopy(dkv_ref.at[mate, chunk], near_ref.at[chunk], n_send.at[chunk], n_recv.at[chunk], {"ctx": mate})

    def join(chunk):
        return rcopy(dkv_ref.at[far, chunk], join_ref.at[chunk], j_send.at[chunk], j_recv.at[chunk], {"ctx": mate})

    def cross(chunk):
        return rcopy(sum_ref.at[chunk], far_ref.at[chunk], f_send.at[chunk], f_recv.at[chunk], {"ctx": across})

    chunks = [ordered(t, 3 - k) for k in range(4)]
    for chunk in chunks:
        join(chunk).start()
    for slot in range(2):
        partner(slot).start()
    for chunk in chunks:
        near(chunk).start()
    for quarter in range(2):
        dq_ref[quarter] = dqw_ref[quarter]
    for chunk in chunks:
        join(chunk).wait_recv()
        sum_ref[chunk] = (dkv_ref[across, chunk].astype(F32) + join_ref[chunk].astype(F32)).astype(BF16)
        cross(chunk).start()

    def lower(chunk):
        return rcopy(pass_ref.at[chunk], take_ref.at[0, chunk], p_send.at[chunk], p_recv.at[0, chunk], {"tp": t - 1})

    def upper(chunk):
        return rcopy(pass_ref.at[chunk], take_ref.at[1, chunk], p_send.at[chunk], p_recv.at[1, chunk], {"tp": t + 1})

    def passed(side, chunk):
        rcopy(
            take_ref.at[side, chunk], take_ref.at[side, chunk], p_send.at[0], p_recv.at[side, chunk], {"tp": t}
        ).wait_recv()

    def relay(chunk):
        @pl.when(chunk < t)
        def _():
            @pl.when(t < 3)
            def _():
                passed(0, chunk)
                pass_ref[chunk] = (part_ref[chunk] + take_ref[0, chunk].astype(F32)).astype(BF16)

            @pl.when(t == 3)
            def _():
                pass_ref[chunk] = part_ref[chunk].astype(BF16)

            lower(chunk).start()

        @pl.when(chunk > t)
        def _():
            @pl.when(t > 0)
            def _():
                passed(1, chunk)
                pass_ref[chunk] = (part_ref[chunk] + take_ref[1, chunk].astype(F32)).astype(BF16)

            @pl.when(t == 0)
            def _():
                pass_ref[chunk] = part_ref[chunk].astype(BF16)

            upper(chunk).start()

    at_end = (t == 0) | (t == 3)
    for step, chunk in enumerate(chunks):

        @pl.when(chunk >= 2)
        def _():
            partner(chunk - 2).wait_recv()

        near(chunk).wait_recv()
        cross(chunk).wait_recv()
        own = (
            dkv_ref[c, chunk].astype(F32) + near_ref[chunk].astype(F32) + far_ref[chunk].astype(F32)
        ).astype(BF16)
        own_ref[chunk] = own
        part_ref[chunk] = mm_nt(dq_ref[chunk], w_ref[:, 0:256]) + mm_nt(own, w_ref[:, 256:640])
        if step < 3:

            @pl.when(at_end)
            def _():
                relay(chunk)

    ride.start()

    def slice_of(place):
        return pl.ds(pl.multiple_of(place * depth, depth), depth)

    spans = (pl.ds(0, 256), pl.ds(256, 256), pl.ds(512, 128))

    def term(k, span):
        to, cols = (f + k) % size, spans[span]
        return rcopy(
            all_in_ref.at[slice_of(to), cols], term_ref.at[k - 1, :, cols],
            w_send.at[k - 1, span], w_recv.at[k - 1, span], {"fsdp": to},
        )

    query, own = dq_ref[...].reshape(1024, 256), own_ref[...].reshape(1024, 384)
    made = (query, own[:, 0:256], own[:, 256:384])
    for span, chunk in enumerate(chunks[:3]):

        @pl.when(jnp.logical_not(at_end))
        def _():
            relay(chunk)

        all_in_ref[:, spans[span]] = mm_tn(xg_ref[...], made[span]).astype(BF16)
        for k in range(1, size):
            term(k, span).start()

    ride.turn()
    sum_out_ref[0:1, 0:256] = jnp.sum(query.astype(F32), axis=0, keepdims=True)
    sum_out_ref[0:1, 256:640] = jnp.sum(own.astype(F32), axis=0, keepdims=True)
    ride.put(sum_out_ref)
    grad_ref[...] = part_ref[t] + back_ref[...]

    @pl.when(t < 3)
    def _():
        passed(0, t)
        grad_ref[...] += take_ref[0, t].astype(F32)

    @pl.when(t > 0)
    def _():
        passed(1, t)
        grad_ref[...] += take_ref[1, t].astype(F32)

    low_ref[...] = grad_ref[...].astype(BF16)
    ride.put(grad_ref, low_ref)
    mem_ref[...] = lax.dot_general(
        mark_ref[...], grad_ref[...], (((0,), (0,)), ((), ())),
        precision=lax.Precision.HIGHEST, preferred_element_type=F32,
    )
    ride.put(mem_ref)
    total = all_in_ref[slice_of(f)].astype(F32)
    for k in range(1, size):
        for span in range(3):
            term(k, span).wait_recv()
        total += term_ref[k - 1].astype(F32)
    din_ref[...] = total.astype(BF16)
    ride.put(din_ref)
    for k in range(1, size):
        for span in range(3):
            term(k, span).wait_send()
    for chunk in range(4):
        join(chunk).wait_send()
        near(chunk).wait_send()
        cross(chunk).wait_send()

        @pl.when(t != chunk)
        def _():
            upper(chunk).wait_send()

    for slot in range(2):
        partner(slot).wait_send()
    ride.finish()


def project_back(dqw, dkv, w, back_one, xg, marks, cid, riders=()):
    size = lax.axis_size("fsdp")
    depth = 768 // size
    f = functools.partial(sds, dtype=F32)
    outs = [f(256, 768), sds(256, 768), sds(depth, 640), f(8, 640), f(marks.shape[1], 768)]
    scratch = [
        dma(size - 1, 3), dma(size - 1, 3), pltpu.VMEM((size - 1, depth, 640), BF16), pltpu.VMEM((768, 640), BF16),
        pltpu.VMEM((4, 256, 256), BF16), pltpu.VMEM((4, 256, 384), BF16),
        pltpu.VMEM((4, 256, 768), F32),
        pltpu.VMEM((4, 256, 384), BF16), pltpu.VMEM((4, 256, 384), BF16),
        pltpu.VMEM((4, 256, 384), BF16), pltpu.VMEM((4, 256, 384), BF16),
        pltpu.VMEM((4, 256, 768), BF16), pltpu.VMEM((2, 4, 256, 768), BF16),
        dma(2), dma(2), dma(4), dma(4), dma(4), dma(4), dma(4), dma(4), dma(4), dma(2, 4),
    ]
    cost = (4 * 1024 * 768 * 640, 12 << 20, 0)
    operands = (dqw.reshape(4, 256, 256), dkv.reshape(4, 4, 256, 384), w, back_one, xg, marks)
    res, ridden = call(project_back_kernel, operands, outs, scratch, cid, "project_back", cost, riders)
    return (*res[:3], res[3][0], res[4], ridden)


def ancestry(parent_row):
    seg_count = parent_row.shape[0]
    segment_ids = jnp.arange(seg_count, dtype=jnp.int32)
    parent_hop = (parent_row[:, None] == segment_ids[None, :]).astype(jnp.int32)
    reached = (segment_ids[:, None] == segment_ids[None, :]).astype(jnp.int32)
    on_path = reached
    for hop_number in range(seg_count - 1):
        reached = jnp.dot(reached, parent_hop)
        on_path = jnp.maximum(on_path, reached)
    return on_path


def joined(query, key, value, gap):
    return jnp.concatenate(
        [
            query[..., :128], gap, query[..., 128:],
            key[..., :128], value[..., 128:], key[..., 128:], value[..., :128],
        ],
        axis=-1,
    )


def parted(grads):
    query = jnp.concatenate([grads[..., :128], grads[..., 192:256]], axis=-1)
    key = jnp.concatenate([grads[..., 256:384], grads[..., 448:512]], axis=-1)
    value = jnp.concatenate([grads[..., 512:640], grads[..., 384:448]], axis=-1)
    return query, key, value


def added(terms, axes=(0,)):
    return jnp.sum(terms.astype(F32), axis=axes)


def low(values):
    return values.astype(BF16)


def shards(
    hidden, cotangent, mem_pos, parents, memory, wq, wk, wv, wo, w1, w2,
    head_bias, ffn_bias, out_bias, norm_gains, norm_shifts,
):
    c = lax.axis_index("ctx")
    t = lax.axis_index("tp")
    size = lax.axis_size("fsdp")
    layers = wq.shape[0]
    share = hidden.shape[0]
    depth = wq.shape[1]
    piece = depth // 4
    positions = t * share + jnp.arange(share, dtype=jnp.int32)
    marks = (mem_pos[0, 0][None, :] == positions[:, None]).astype(F32)
    stream = hidden.astype(F32) + jnp.dot(
        marks, memory, precision=lax.Precision.HIGHEST, preferred_element_type=F32
    )
    on_path = ancestry(parents[0])
    ids = jnp.arange(4, dtype=jnp.int32)
    pick = lambda seg: jnp.sum(on_path * (ids == seg).astype(jnp.int32)[:, None], axis=0)
    flags = jnp.stack([pick(c), pick(3 - c)])

    gap = jnp.zeros(wq.shape[:2] + (64,), BF16)
    own_in = joined(wq, wk, wv, gap)
    none = jnp.zeros((layers, 192), F32)
    in_bias = joined(head_bias[:, 0], none, head_bias[:, 1], jnp.zeros((layers, 64), F32))
    down_turned = jnp.swapaxes(w2, 1, 2)
    out_turned = jnp.swapaxes(wo, 1, 2).reshape(layers, 4, piece, 192)
    out_piece = lax.dynamic_index_in_dim(out_turned, c, axis=1, keepdims=False)

    def out_whole(gathered):
        return jnp.transpose(gathered, (1, 2, 0, 3, 4)).reshape(4, 768, 192)

    def vectors(n):
        norms = [norm_gains[n, 0], norm_shifts[n, 0], norm_gains[n, 1], norm_shifts[n, 1]]
        return jnp.concatenate([out_bias[n], jnp.stack(norms), jnp.zeros((2, 768), F32)])

    saved, weights = [], []
    rounded = low(stream)
    riders = [plane_gather(out_piece[0], size), tp_flip(ffn_bias)]
    xg, qw, kv, w_in, (out, units) = project(
        rounded, own_in[0], in_bias[0][None], 0, riders, fetch=True
    )
    for n in range(layers):
        last = n == layers - 1
        riders = [ctx_gather(out)]
        if n == 0:
            riders += [flip_gather(w1[0], size)]
        riders += [tp_flip(down_turned[n])]
        if n == 0:
            riders[-1].after()
        o, lse, got = attend(qw, kv, flags, 16 * n + 1, riders)
        w_out = out_whole(got[0])
        if n == 0:
            w_up = got[1]
        w_up, down = w_up.reshape(768, 768), got[-1]
        vecs = vectors(n)
        riders = []
        if not last:
            riders = [
                tp_flip(w1[n + 1]),
                plane_gather(out_piece[n + 1], size), fsdp_gather(own_in[n + 1], size),
            ]
        stream, rounded, xhat1, r1, xhat2, r2, xg2, act, slope, rows, w_down, got = block(
            o, w_out, w_up, down, units[n][None], vecs, stream, 16 * n + 2, riders
        )
        weights.append((w_in, w_up, w_down, w_out, vecs))
        saved.append((xg, qw, kv, o, lse, xhat1, r1, xhat2, r2, xg2, act, slope, rows))
        if not last:
            up, out, w_in = got
            xg, qw, kv, w_in, (w_up,) = project(
                rounded, w_in.reshape(768, 640), in_bias[n + 1][None], 16 * n + 16, [fsdp_gather(up, size)]
            )
    output = rounded

    grad = cotangent.astype(F32)
    small, heads = [None] * layers, [None] * layers
    done = [None] * layers
    above = None
    for n in reversed(range(layers)):
        w_in, w_up, w_down, w_out, vecs = weights[n]
        xg, qw, kv, o, lse, xhat1, r1, xhat2, r2, xg2, act, slope, rows = saved[n]
        riders = []
        if above is not None:
            riders = [plane_scatter(above["out"], size)]
        back_one, do, small[n], d_up, d_down, d_out, got = block_back(
            grad, xhat2, r2, xhat1, r1, vecs, slope, w_up, w_down, w_out, xg2, act, rows, 16 * n + 3, riders
        )
        if above is not None:
            above["out"] = low(added(got[0], (0, 1)))
        d_down = d_down.reshape(1, size, 2, depth // 2, 768)
        riders = [tp_flip(d_up), scatter_flip(d_down), ctx_scatter(d_out.reshape(4, size, 4, piece, 192), axis=2)]
        if above is not None:
            riders += [ctx_scatter(part) for part in above["ffn"]]
            riders += [ctx_scatter(above["in"]), ctx_gather(above["out"])]
        dqw, dkv, got = attend_back(qw, kv, do, o, lse, flags, 16 * n + 4, riders)
        d_ffn = [got[0].reshape(4, depth // 4, 768), got[1].reshape(4, depth // 4, 768)]
        d_out = low(added(got[2]))
        riders = []
        if above is not None:
            above["out"] = got[6]
            riders = [ctx_gather(low(added(part))) for part in got[3:6]]
        if n == 0:
            riders += [ctx_scatter(part) for part in d_ffn] + [plane_scatter(d_out, size)]
        grad, low_grad, d_in, sums, memory_part, got = project_back(
            dqw, dkv, w_in, back_one, xg, marks, 16 * n + 5, riders
        )
        if above is not None:
            done[n + 1] = (got[2], above["out"], got[0], got[1])
        d_in = d_in.reshape(4, depth // 4, 640)
        d_query_bias, _, d_value_bias = parted(sums)
        heads[n] = jnp.stack([d_query_bias, d_value_bias])
        above = {"ffn": d_ffn, "out": d_out, "in": d_in}
    hidden_grad = low_grad
    up0, down0 = (low(added(part)) for part in got[-3:-1])
    out0 = low(added(got[-1], (0, 1)))
    small = jnp.stack(small)
    place = (ids == t).astype(F32)
    unit = (ids == flipped_place(c, t)).astype(F32)
    head_rows = (jnp.stack(heads)[:, :, None, :] * place[None, None, :, None]).reshape(2 * layers, 768)
    unit_rows = (small[:, 6][:, None, :] * unit[None, :, None]).reshape(4 * layers, 768)
    stat_rows = small[:, :6].reshape(6 * layers, 768)
    filled = 12 * layers + memory_part.shape[0]
    slices = 4 * size
    width = -(-filled // slices)
    rest = jnp.zeros((width * slices - filled, 768), F32)
    sums = jnp.concatenate([stat_rows, unit_rows, head_rows, memory_part, rest])
    sums = sums.reshape(4, size, width, 768)
    got = carry(
        [ctx_scatter(d_in), plane_scatter(sums, size), ctx_gather(up0), ctx_gather(down0), ctx_gather(out0)], 6
    )
    up0, down0, out0 = got[2:]
    got = carry([ctx_gather(low(added(got[0]))), all_gather(added(got[1], (0, 1)), size)], 7)
    done[0] = (got[0], out0, up0, down0)
    totals = added(got[1]).reshape(width * slices, 768)
    stats = totals[: 6 * layers].reshape(layers, 6, 768)
    at = 6 * layers
    ffn_rows = totals[at : at + 4 * layers].reshape(layers, 4, 768)
    ffn_grad = jnp.sum(ffn_rows * place[None, :, None], axis=1)
    at += 4 * layers
    head_sums = totals[at : at + 2 * layers].reshape(layers, 2, 4, 192)
    head_grad = jnp.sum(head_sums * place[None, None, :, None], axis=2)
    at += 2 * layers
    memory_grad = totals[at : at + memory_part.shape[0]]
    d_in = jnp.stack([part[0].reshape(depth, 640) for part in done]).astype(F32)
    d_out = jnp.stack([jnp.swapaxes(part[1].reshape(depth, 192), 0, 1) for part in done]).astype(F32)
    d_up = jnp.stack([part[2].reshape(depth, 768) for part in done]).astype(F32)
    d_down = jnp.stack([jnp.swapaxes(part[3].reshape(depth, 768), 0, 1) for part in done]).astype(F32)
    return (
        output, hidden_grad, memory_grad, *parted(d_in), d_out, d_up, d_down,
        head_grad, ffn_grad, stats[:, 4:6], stats[:, 0:2], stats[:, 2:4],
    )


def solution(mesh):
    rows = P(("fsdp", "ctx", "tp"), None)
    inner = P(None, "fsdp", "tp")
    outer = P(None, "tp", "fsdp")
    weights = (inner, inner, inner, outer, inner, outer)
    biases = (P(None, None, "tp"), P(None, "tp"), P(), P(), P())
    return jax.shard_map(
        shards,
        mesh=mesh,
        in_specs=(rows, rows, P("fsdp", "ctx", None), P("fsdp", None), P()) + weights + biases,
        out_specs=(rows, rows, P()) + weights + biases,
        check_vma=False,
    )
```

```python
import functools

import jax
import jax.numpy as jnp
from jax import lax
from jax.experimental import pallas as pl
from jax.experimental.pallas import tpu as pltpu
from jax.sharding import PartitionSpec as P

EPSILON = 1e-05
MASKED = -1000000000.0
MESH = pl.DeviceIdType.MESH
F32 = jnp.float32
BF16 = jnp.bfloat16
ORDER = ((0, 1), (1, 0), (2, 2), (3, 3))


def mm(left, right):
    return jnp.dot(left, right, preferred_element_type=F32)


def mm_nt(left, right):
    return lax.dot_general(left, right, (((1,), (1,)), ((), ())), preferred_element_type=F32)


def mm_tn(left, right):
    return lax.dot_general(left, right, (((0,), (0,)), ((), ())), preferred_element_type=F32)


def rcopy(src, dst, send_sem, recv_sem, device):
    return pltpu.make_async_remote_copy(
        src_ref=src,
        dst_ref=dst,
        send_sem=send_sem,
        recv_sem=recv_sem,
        device_id=device,
        device_id_type=MESH,
    )


def mate_of(c):
    return c + 1 - 2 * (c % 2)


def across_of(c):
    return (c + 2) % 4


def signal(sem, device):
    pl.semaphore_signal(sem, inc=1, device_id=device, device_id_type=MESH)


def ordered(place, step):
    half = place // 2
    inner = place + half * (3 - 2 * place)
    first, second = ORDER[step]
    chunk = first + inner * (second - first)
    return chunk + half * (3 - 2 * chunk)


def dma(*shape):
    return pltpu.SemaphoreType.DMA(shape)


class Rider:
    def __init__(self, array, out, make, scratch, chunks=0):
        self.array, self.out, self.make, self.scratch, self.chunks = array, out, make, scratch, chunks
        self.late = False

    def after(self):
        self.late = True
        return self


class Copies:
    def __init__(self, steps, here, scratch):
        self.steps, self.here = steps, here
        self.send, self.recv, self.leg, self.stage = scratch
        self.turned = False

    def greetings(self):
        return [(origin, when, weight) for _, origin, _, _, when, weight in self.steps]

    def copies(self):
        for number, (to, _, source, target, when, _) in enumerate(self.steps):
            yield rcopy(source, target, self.send.at[number], self.recv.at[number], to), when

    def inward(self):
        return pltpu.make_async_copy(self.here[0], self.stage, self.leg.at[0])

    def outward(self):
        return pltpu.make_async_copy(self.stage, self.here[1], self.leg.at[1])

    def start(self):
        for copy, when in self.copies():
            guarded(when, copy.start)
        guarded(self.here[2], self.inward().start)

    def turn(self):
        guarded(self.here[2], self.inward().wait)
        guarded(self.here[2], self.outward().start)

    def finish(self):
        for copy, when in self.copies():
            guarded(when, copy.wait)
        guarded(self.here[2], self.outward().wait)


class FlipGather:
    def __init__(self, source, target, place, scratch):
        self.source, self.target = source, target
        self.f, self.c, self.t = place
        self.size = target.shape[0]
        self.send, self.recv, self.on_send, self.on_recv, self.leg, self.stage = scratch
        self.moves = self.c > 0

    def greetings(self):
        there = {"tp": flipped_place(self.c, self.t)}
        ring = [({"fsdp": (self.f + self.size - k) % self.size}, None, 1) for k in range(1, self.size)]
        return [(there, self.moves, (self.c + 3) // 4)] + ring

    def first(self, chunk):
        there = {"tp": flipped_place(self.c, self.t)}
        return rcopy(
            self.source.at[chunk], self.target.at[self.f, chunk], self.send.at[chunk], self.recv.at[chunk], there
        )

    def second(self, chunk, k, moved):
        source = self.target.at[self.f, chunk] if moved else self.source.at[chunk]
        device = {"fsdp": (self.f + k) % self.size}
        return rcopy(
            source, self.target.at[self.f, chunk], self.on_send.at[k - 1, chunk], self.on_recv.at[k - 1, chunk], device
        )

    def inward(self):
        return pltpu.make_async_copy(self.source, self.stage, self.leg.at[0])

    def outward(self):
        return pltpu.make_async_copy(self.stage, self.target.at[self.f], self.leg.at[1])

    def start(self):
        @pl.when(self.moves)
        def _():
            for chunk in range(self.source.shape[0]):
                self.first(chunk).start()

        @pl.when(self.c == 0)
        def _():
            self.inward().start()

    def hop(self, chunk):
        @pl.when(self.moves)
        def _():
            self.first(chunk).wait_recv()
            for k in range(1, self.size):
                self.second(chunk, k, True).start()

        @pl.when(self.c == 0)
        def _():
            for k in range(1, self.size):
                self.second(chunk, k, False).start()

    def turn(self):
        @pl.when(self.c == 0)
        def _():
            self.inward().wait()
            self.outward().start()

    def finish(self):
        @pl.when(self.moves)
        def _():
            for chunk in range(self.source.shape[0]):
                self.first(chunk).wait_send()

        for chunk in range(self.source.shape[0]):
            for k in range(1, self.size):
                self.second(chunk, k, False).wait()

        @pl.when(self.c == 0)
        def _():
            self.outward().wait()


class ScatterFlip:
    def __init__(self, source, target, place, scratch):
        self.source, self.target = source, target
        self.f, self.c, self.t = place
        self.size = source.shape[1]
        self.send, self.recv, self.on_send, self.on_recv, self.leg, self.got, self.out = scratch
        self.moves = self.c > 0

    def greetings(self):
        there = {"tp": flipped_place(self.c, self.t)}
        ring = [({"fsdp": (self.f + self.size - k) % self.size}, None, 1) for k in range(1, self.size)]
        return [(there, self.moves, (self.c + 3) // 4)] + ring

    def first(self, chunk, k):
        to = (self.f + k) % self.size
        return rcopy(
            self.source.at[chunk // 2, to, chunk % 2], self.got.at[k, chunk],
            self.send.at[k - 1, chunk], self.recv.at[k - 1, chunk], {"fsdp": to},
        )

    def own(self, chunk):
        return pltpu.make_async_copy(
            self.source.at[chunk // 2, self.f, chunk % 2], self.got.at[0, chunk], self.leg.at[chunk]
        )

    def second(self, chunk):
        there = {"tp": flipped_place(self.c, self.t)}
        return rcopy(self.out.at[chunk], self.target.at[chunk], self.on_send.at[chunk], self.on_recv.at[chunk], there)

    def stays(self, chunk):
        return pltpu.make_async_copy(self.out.at[chunk], self.target.at[chunk], self.on_send.at[chunk])

    def start(self):
        for chunk in range(self.target.shape[0]):
            for k in range(1, self.size):
                self.first(chunk, k).start()
            self.own(chunk).start()

    def hop(self, chunk):
        self.own(chunk).wait()
        total = self.got[0, chunk].astype(F32)
        for k in range(1, self.size):
            self.first(chunk, k).wait_recv()
            total += self.got[k, chunk].astype(F32)
        self.out[chunk] = total.astype(BF16)

        @pl.when(self.moves)
        def _():
            self.second(chunk).start()

        @pl.when(self.c == 0)
        def _():
            self.stays(chunk).start()

    def turn(self):
        pass

    def finish(self):
        for chunk in range(self.target.shape[0]):
            for k in range(1, self.size):
                self.first(chunk, k).wait_send()

            @pl.when(self.moves)
            def _():
                self.second(chunk).wait()

            @pl.when(self.c == 0)
            def _():
                self.stays(chunk).wait()


class CtxGather:
    def __init__(self, source, target, place, scratch):
        self.source, self.target = source, target
        self.c = place[1]
        self.send, self.recv, self.leg, self.stage = scratch

    def greetings(self):
        return [({"ctx": mate_of(self.c)}, None, 1), ({"ctx": across_of(self.c)}, None, 1)]

    def copy(self, number):
        c = self.c
        device = across_of(c) if number == 0 else mate_of(c)
        source = self.target.at[across_of(c)] if number == 2 else self.source
        slot = across_of(c) if number == 2 else c
        return rcopy(source, self.target.at[slot], self.send.at[number], self.recv.at[number], {"ctx": device})

    def inward(self):
        return pltpu.make_async_copy(self.source, self.stage, self.leg.at[0])

    def outward(self):
        return pltpu.make_async_copy(self.stage, self.target.at[self.c], self.leg.at[1])

    def start(self):
        self.copy(0).start()
        self.copy(1).start()
        self.inward().start()

    def turn(self):
        self.inward().wait()
        self.outward().start()
        self.copy(0).wait_recv()
        self.copy(2).start()

    def finish(self):
        self.copy(0).wait_send()
        self.copy(1).wait()
        self.copy(2).wait()
        self.outward().wait()


class CtxScatter:
    def __init__(self, pick, source, target, place, scratch):
        self.source, self.target, self.pick = source, target, pick
        self.c = place[1]
        self.send, self.recv, self.leg, self.stage, self.cross, self.far, self.total = scratch

    def greetings(self):
        return [({"ctx": mate_of(self.c)}, None, 1), ({"ctx": across_of(self.c)}, None, 1)]

    def copy(self, number):
        c = self.c
        device = across_of(c) if number == 2 else mate_of(c)
        source = (self.pick(self.source, 3 - c), self.pick(self.source, mate_of(c)), self.total)[number]
        target = (self.far, self.target.at[1], self.target.at[2])[number]
        return rcopy(source, target, self.send.at[number], self.recv.at[number], {"ctx": device})

    def inward(self):
        return pltpu.make_async_copy(self.pick(self.source, self.c), self.stage, self.leg.at[0])

    def outward(self):
        return pltpu.make_async_copy(self.stage, self.target.at[0], self.leg.at[1])

    def beside(self):
        return pltpu.make_async_copy(self.pick(self.source, across_of(self.c)), self.cross, self.leg.at[2])

    def start(self):
        self.copy(0).start()
        self.beside().start()
        self.copy(1).start()
        self.inward().start()

    def turn(self):
        self.copy(0).wait_recv()
        self.beside().wait()
        self.total[...] = (self.cross[...].astype(F32) + self.far[...].astype(F32)).astype(self.total.dtype)
        self.copy(2).start()
        self.inward().wait()
        self.outward().start()

    def finish(self):
        self.copy(0).wait_send()
        self.copy(1).wait()
        self.copy(2).wait()
        self.outward().wait()


class Riding:
    def __init__(self, riders, sources, targets, scratch, fetches, results, puts):
        self.fetches, self.results, self.puts = fetches, results, puts
        self.gone = [False] * len(puts)
        place = tuple(lax.axis_index(axis) for axis in ("fsdp", "ctx", "tp"))
        scratch = list(scratch)
        self.rides, self.hops, self.late = [], [], []
        self.turned = False
        for rider, source, target in zip(riders, sources, targets):
            own = [scratch.pop(0) for _ in rider.scratch]
            ride = rider.make(source, target, place, own)
            self.rides.append(ride)
            if rider.late:
                self.late.append(ride)
            self.hops += [(ride, chunk) for chunk in range(rider.chunks)]

    def ready(self):
        for fetch in self.fetches:
            fetch.wait()

    def put(self, *refs):
        for ref in refs:
            slot = [ref is result for result in self.results].index(True)
            self.gone[slot] = True
            self.puts[slot].start()

    def close(self):
        for slot, put in enumerate(self.puts):
            if not self.gone[slot]:
                put.start()
        for put in self.puts:
            put.wait()

    def greet(self, barrier):
        count = 0
        for ride in self.rides:
            for origin, when, weight in ride.greetings():
                guarded(when, functools.partial(signal, barrier, origin))
                count = count + weight
        return count

    def start(self):
        for ride in self.rides:
            if ride not in self.late:
                ride.start()

    def one_hop(self, at):
        ride, chunk = self.hops[at]
        ride.hop(chunk)
        if at == len(self.hops) - 1:
            for ride in self.late:
                ride.start()

    def hop(self, number):
        for at in range(len(self.hops)):
            pl.when(number == at)(functools.partial(self.one_hop, at))

    def turn_when(self, when):
        if self.rides:
            pl.when(when)(self.turn)

    def turn(self):
        self.turned = True
        for ride in self.rides:
            ride.turn()

    def finish(self):
        if not self.turned:
            self.turn()
        for ride in self.rides:
            ride.finish()


def guarded(when, action):
    if when is None:
        action()
    else:
        pl.when(when)(action)


def call(kernel, operands, out_shapes, scratch, collective_id, name, cost, riders=(), smem=()):
    n_in, n_out, n_scratch, n_ride = len(operands), len(out_shapes), len(scratch), len(riders)
    large = [i for i in range(n_in) if i not in smem]

    def body(*refs):
        refs = list(refs)
        take = lambda n: [refs.pop(0) for _ in range(n)]
        ins, sources, outs, targets = take(n_in), take(n_ride), take(n_out), take(n_ride)
        near_ins, near_outs, (in_sem, out_sem), own = take(len(large)), take(n_out), take(2), take(n_scratch)
        fetches = [
            pltpu.make_async_copy(ins[i], near, in_sem.at[slot]) for slot, (i, near) in enumerate(zip(large, near_ins))
        ]
        for fetch in fetches:
            fetch.start()
        for i, near in zip(large, near_ins):
            ins[i] = near
        puts = [pltpu.make_async_copy(near, far, out_sem.at[i]) for i, (near, far) in enumerate(zip(near_outs, outs))]
        ride = Riding(riders, sources, targets, refs, fetches, near_outs, puts)
        kernel(ride, *ins, *near_outs, *own)
        ride.close()

    params = dict(vmem_limit_bytes=60 * 1024 * 1024)
    if collective_id is not None:
        params.update(collective_id=collective_id, has_side_effects=True)
    extra = [item for rider in riders for item in rider.scratch]
    anywhere = pl.BlockSpec(memory_space=pl.ANY)
    near = [pltpu.VMEM(operands[i].shape, operands[i].dtype) for i in large]
    near += [pltpu.VMEM(out.shape, out.dtype) for out in out_shapes]
    results = pl.pallas_call(
        body,
        out_shape=list(out_shapes) + [rider.out for rider in riders],
        in_specs=[pl.BlockSpec(memory_space=pltpu.SMEM) if i in smem else anywhere for i in range(n_in)]
        + [anywhere] * n_ride,
        out_specs=[anywhere] * (n_out + n_ride),
        scratch_shapes=near + [dma(max(len(large), 1)), dma(max(n_out, 1))] + list(scratch) + extra,
        compiler_params=pltpu.CompilerParams(**params),
        cost_estimate=pl.CostEstimate(flops=cost[0], bytes_accessed=cost[1], transcendentals=cost[2]),
        name=name,
    )(*operands, *[rider.array for rider in riders])
    return results[:n_out], results[n_out:]


def copies_rider(array, out, steps, stage, plan):
    def make(source, target, place, scratch):
        return Copies(*plan(source, target, *place), scratch)

    scratch = [dma(steps), dma(steps), dma(2), pltpu.VMEM(stage, array.dtype)]
    return Rider(array, out, make, scratch)


def flip_gather(own, size):
    own = own.reshape(2, own.shape[0] // 2, own.shape[1])
    scratch = [dma(2), dma(2), dma(size - 1, 2), dma(size - 1, 2), dma(2), pltpu.VMEM(own.shape, own.dtype)]
    return Rider(own, sds(size, *own.shape), FlipGather, scratch, chunks=2)


def scatter_flip(parts):
    n, size = parts.shape[0], parts.shape[1]
    shape = (2 * n, *parts.shape[3:])
    scratch = [
        dma(size - 1, 2 * n), dma(size - 1, 2 * n), dma(2 * n), dma(2 * n), dma(2 * n),
        pltpu.VMEM((size, *shape), BF16), pltpu.VMEM(shape, BF16),
    ]
    return Rider(parts, sds(*shape), ScatterFlip, scratch, chunks=2 * n)


def fsdp_gather(own, size):
    def make(source, target, f, c, t):
        steps = [
            ({"fsdp": (f + k) % size}, {"fsdp": (f + size - k) % size}, source, target.at[f], None, 1)
            for k in range(1, size)
        ]
        return steps, (source, target.at[f], None)

    return copies_rider(own, sds(size, *own.shape, dtype=own.dtype), size - 1, own.shape, make)


def fsdp_scatter(parts, size):
    out = sds(size, parts.shape[0], *parts.shape[2:], dtype=parts.dtype)

    def make(source, target, f, c, t):
        steps = [
            (
                {"fsdp": (f + k) % size}, {"fsdp": (f + size - k) % size},
                source.at[:, (f + k) % size], target.at[k], None, 1,
            )
            for k in range(1, size)
        ]
        return steps, (source.at[:, f], target.at[0], None)

    return copies_rider(parts, out, size - 1, out.shape[1:], make)


def ctx_gather(own):
    scratch = [dma(3), dma(3), dma(2), pltpu.VMEM(own.shape, own.dtype)]
    return Rider(own, sds(4, *own.shape, dtype=own.dtype), CtxGather, scratch)


def ctx_scatter(parts, axis=0):
    shape = parts.shape[:axis] + parts.shape[axis + 1 :]

    def pick(ref, slot):
        return ref.at[slot] if axis == 0 else ref.at[:, :, slot]

    buffer = pltpu.VMEM(shape, parts.dtype)
    scratch = [dma(3), dma(3), dma(3), buffer, buffer, buffer, buffer]
    return Rider(parts, sds(3, *shape, dtype=parts.dtype), functools.partial(CtxScatter, pick), scratch)


def flipped_place(c, t):
    return 2 * ((t // 2 + c % 2) % 2) + (t % 2 + c // 2) % 2


def tp_flip(own):
    def make(source, target, f, c, t):
        other = {"tp": flipped_place(c, t)}
        return [(other, other, source, target, c > 0, (c + 3) // 4)], (source, target, c == 0)

    return copies_rider(own, sds(*own.shape, dtype=own.dtype), 1, own.shape, make)


def plane(size):
    return [(kt, kf) for kt in (2, 3, 1, 0) for kf in range(size) if kt + kf > 0]


def plane_gather(own, size):
    def make(source, target, f, c, t):
        steps = [
            (
                {"fsdp": (f + kf) % size, "tp": (t + kt) % 4},
                {"fsdp": (f + size - kf) % size, "tp": (t + 4 - kt) % 4},
                source, target.at[t, f], None, 1,
            )
            for kt, kf in plane(size)
        ]
        return steps, (source, target.at[t, f], None)

    return copies_rider(own, sds(4, size, *own.shape, dtype=own.dtype), 4 * size - 1, own.shape, make)


def plane_scatter(parts, size):
    def make(source, target, f, c, t):
        steps = [
            (
                {"fsdp": (f + kf) % size, "tp": (t + kt) % 4},
                {"fsdp": (f + size - kf) % size, "tp": (t + 4 - kt) % 4},
                source.at[(t + kt) % 4, (f + kf) % size], target.at[kt, kf], None, 1,
            )
            for kt, kf in plane(size)
        ]
        return steps, (source.at[t, f], target.at[0, 0], None)

    return copies_rider(parts, sds(*parts.shape, dtype=parts.dtype), 4 * size - 1, parts.shape[2:], make)


def all_gather(own, size):
    others = [(kt, kc, kf) for kt in (2, 3, 1, 0) for kc in (2, 3, 1, 0) for kf in range(size)][:-size] + [
        (0, 0, kf) for kf in range(1, size)
    ]

    def make(source, target, f, c, t):
        steps = [
            (
                {"fsdp": (f + kf) % size, "ctx": (c + kc) % 4, "tp": (t + kt) % 4},
                {"fsdp": (f + size - kf) % size, "ctx": (c + 4 - kc) % 4, "tp": (t + 4 - kt) % 4},
                source, target.at[c, t, f], None, 1,
            )
            for kt, kc, kf in others
        ]
        return steps, (source, target.at[c, t, f], None)

    return copies_rider(own, sds(4, 4, size, *own.shape, dtype=own.dtype), 16 * size - 1, own.shape, make)


def carry_kernel(ride):
    barrier = pltpu.get_barrier_semaphore()
    pl.semaphore_wait(barrier, ride.greet(barrier))
    ride.start()
    ride.finish()


def carry(riders, cid):
    return call(carry_kernel, (), (), (), cid, "carry", (1 << 20, 1 << 20, 0), riders)[1]


def sds(*shape, dtype=BF16):
    return jax.ShapeDtypeStruct(shape, dtype)


def project_kernel(
    fetch, ride, x_ref, w_ref, b_ref, xg_ref, qw_ref, kv_ref, *rest
):
    if fetch:
        full_ref, w_send, w_recv, *rest = rest
    (
        qbuf, x_recv, x_right, x_left, k1_send, k1_recv, k2_send, k2_recv, kf_send, kf_recv, q_send, q_recv,
    ) = rest
    c = lax.axis_index("ctx")
    t = lax.axis_index("tp")
    barrier = pltpu.get_barrier_semaphore()
    for device in (mate_of(c), across_of(c), 3 - c):
        signal(barrier, {"ctx": device})

    @pl.when(t > 0)
    def _():
        signal(barrier, {"tp": t - 1})

    @pl.when(t < 3)
    def _():
        signal(barrier, {"tp": t + 1})

    f, size = lax.axis_index("fsdp"), lax.axis_size("fsdp")
    if fetch:
        for k in range(1, size):
            signal(barrier, {"fsdp": (f + size - k) % size})
    ends = (t // 3) + (3 - t) // 3
    count = 5 - ends + ride.greet(barrier) + (size - 1 if fetch else 0)
    ride.ready()
    pl.semaphore_wait(barrier, count)

    def right(src, chunk, step):
        return rcopy(src, xg_ref.at[chunk], x_right.at[step], x_recv.at[chunk], {"tp": t + 1})

    def left(src, chunk, step):
        return rcopy(src, xg_ref.at[chunk], x_left.at[step], x_recv.at[chunk], {"tp": t - 1})

    def arrived(chunk):
        rcopy(xg_ref.at[chunk], xg_ref.at[chunk], x_right.at[0], x_recv.at[chunk], {"tp": t}).wait_recv()

    @pl.when(t < 3)
    def _():
        right(x_ref, t, 0).start()

    @pl.when(t > 0)
    def _():
        left(x_ref, t, 0).start()

    def weight(k):
        device = {"fsdp": (f + k) % size}
        return rcopy(w_ref, full_ref.at[f], w_send.at[k - 1], w_recv.at[k - 1], device)

    if fetch:
        for k in range(1, size):
            weight(k).start()
        full_ref[f] = w_ref[...]
        for k in range(1, size):
            weight(k).wait_recv()
    ride.start()

    def mate(chunk):
        return rcopy(kv_ref.at[c, chunk], kv_ref.at[c, chunk], k1_send.at[chunk], k1_recv.at[chunk], {"ctx": mate_of(c)})

    def across(chunk):
        return rcopy(kv_ref.at[c, chunk], kv_ref.at[c, chunk], k2_send.at[chunk], k2_recv.at[chunk], {"ctx": across_of(c)})

    def onward(chunk):
        return rcopy(
            kv_ref.at[across_of(c), chunk], kv_ref.at[across_of(c), chunk], kf_send.at[chunk], kf_recv.at[chunk], {"ctx": mate_of(c)}
        )

    def partner(slot):
        return rcopy(qbuf.at[slot], qw_ref.at[2 * slot + 1], q_send.at[slot], q_recv.at[slot], {"ctx": 3 - c})

    for step in range(4):
        if step == 0:
            xg_ref[t] = x_ref[...]
        else:

            @pl.when(t - step >= 0)
            def _():
                arrived(t - step)

                @pl.when(t < 3)
                def _():
                    right(xg_ref.at[t - step], t - step, step).start()

            @pl.when(t + step <= 3)
            def _():
                arrived(t + step)

                @pl.when(t > 0)
                def _():
                    left(xg_ref.at[t + step], t + step, step).start()

        chunk = ordered(t, step)
        w = full_ref[...].reshape(768, 640) if fetch else w_ref[...]
        made = mm(xg_ref[chunk], w) + b_ref[...]
        kv_ref[c, chunk] = made[:, 256:].astype(BF16)
        mate(chunk).start()
        across(chunk).start()
        query = (made[:, :256] * 0.125).astype(BF16)

        @pl.when(chunk % 2 == 0)
        def _():
            qw_ref[chunk] = query

        @pl.when(chunk % 2 == 1)
        def _():
            qbuf[chunk // 2] = query
            partner(chunk // 2).start()

        if step >= 1:
            before = ordered(t, step - 1)
            across(before).wait_recv()
            onward(before).start()
    ride.put(xg_ref)
    ride.turn()
    last = ordered(t, 3)
    across(last).wait_recv()
    onward(last).start()
    for chunk in range(4):
        mate(chunk).wait()
        across(chunk).wait_send()
        onward(chunk).wait()
    for slot in range(2):
        partner(slot).wait()

    @pl.when(t < 3)
    def _():
        right(x_ref, t, 0).wait_send()

    @pl.when(t > 0)
    def _():
        left(x_ref, t, 0).wait_send()

    for step in (1, 2):

        @pl.when((t - step >= 0) & (t < 3))
        def _():
            right(xg_ref.at[t - step], t - step, step).wait_send()

        @pl.when((t + step <= 3) & (t > 0))
        def _():
            left(xg_ref.at[t + step], t + step, step).wait_send()

    if fetch:
        for k in range(1, size):
            weight(k).wait_send()
    ride.finish()


def project(x, w, b, cid, riders=(), fetch=False):
    outs = [sds(4, 256, 768), sds(4, 256, 256), sds(4, 4, 256, 384)]
    scratch = [
        pltpu.VMEM((2, 256, 256), BF16),
        dma(4), dma(3), dma(3),
        dma(4), dma(4), dma(4), dma(4), dma(4), dma(4), dma(2), dma(2),
    ]
    if fetch:
        size = lax.axis_size("fsdp")
        outs.append(sds(size, *w.shape))
        scratch = [dma(size - 1), dma(size - 1)] + scratch
    cost = (2 * 1024 * 768 * 640, 8 << 20, 0)
    kernel = functools.partial(project_kernel, fetch)
    res, ridden = call(kernel, (x, w, b), outs, scratch, cid, "project", cost, riders)
    xg, qw, kv = res[:3]
    full = res[3].reshape(768, 640) if fetch else w
    return xg.reshape(1024, 768), qw.reshape(1024, 256), kv.reshape(4, 1024, 384), full, ridden


def norm_stats(summed):
    row_mean = jnp.mean(summed, axis=-1, keepdims=True)
    centered = summed - row_mean
    variance = jnp.mean(centered * centered, axis=-1, keepdims=True)
    scale = lax.rsqrt(variance + EPSILON)
    return centered * scale, scale


def norm_back(grad, xhat, scale, gain):
    scaled = grad * gain
    first = jnp.mean(scaled, axis=-1, keepdims=True)
    second = jnp.mean(scaled * xhat, axis=-1, keepdims=True)
    return scale * (scaled - first - xhat * second)


def gelu_both(up):
    phi = 0.5 * (1.0 + lax.erf(up * 0.7071067811865476))
    slope = phi + up * jnp.exp(-0.5 * up * up) * 0.3989422804014327
    return (up * phi).astype(BF16), slope.astype(BF16)


Q_TILE = 256
FAR = 1e30


def open_up(ride):
    if ride.rides:
        barrier = pltpu.get_barrier_semaphore()
        count = ride.greet(barrier)
        pl.semaphore_wait(barrier, count)
        ride.start()
    ride.ready()


def attend_kernel(ride, flag_ref, qw_ref, kv_ref, o_ref, lse_ref, qm_ref, m_ref, acc_ref, vo_ref):
    c = lax.axis_index("ctx")
    open_up(ride)
    low = lax.broadcasted_iota(jnp.int32, (Q_TILE, 128), 1) < 64
    for side, at in enumerate((128, 256)):
        vo_ref[side, :, 0:128] = kv_ref[:, at : at + 128]
        vo_ref[side, :, 128:256] = jnp.ones((4096, 128), BF16)

    @pl.loop(0, 1024 // Q_TILE)
    def _(tile):
        half = tile % 2
        segment = c + half * (3 - 2 * c)
        rows = pl.ds(pl.multiple_of(tile * Q_TILE, Q_TILE), Q_TILE)
        pair = qw_ref[rows, 0:128]
        qm_ref[0] = jnp.where(low, pair, jnp.zeros_like(pair))
        qm_ref[1] = jnp.where(low, jnp.zeros_like(pair), pair)
        qm_ref[2] = qw_ref[rows, 128:256]
        m_ref[...] = jnp.full_like(m_ref, MASKED)
        acc_ref[...] = jnp.zeros_like(acc_ref)

        @pl.loop(0, segment + 1)
        def _(block):
            seen = flag_ref[half, block] > 0
            penalty = jnp.where(seen, 0.0, FAR)
            keys = pl.ds(pl.multiple_of(block * 1024, 1024), 1024)
            for head in range(3):
                k_at = 0 if head < 2 else 128
                scores = mm_nt(qm_ref[head], kv_ref[keys, k_at : k_at + 128])
                old = m_ref[head]
                most = jnp.max(scores, axis=-1, keepdims=True)
                new = jnp.maximum(old, jnp.where(seen, most, MASKED))
                probs = jnp.exp(scores - (new + penalty)).astype(BF16)
                keep = jnp.exp(old - new)
                m_ref[head] = new
                acc_ref[head] = acc_ref[head] * keep + mm(probs, vo_ref[1 if head < 2 else 0, keys])

        whole = [acc_ref[head][:, 128:256] for head in range(3)]
        first = acc_ref[0][:, 0:128] / whole[0]
        second = acc_ref[1][:, 0:128] / whole[1]
        o_ref[rows, 0:128] = jnp.where(low, first, second).astype(BF16)
        o_ref[rows, 128:192] = (acc_ref[2][:, 0:128] / whole[2])[:, :64].astype(BF16)
        lane = lax.broadcasted_iota(jnp.int32, (Q_TILE, 128), 1)
        totals = [m_ref[head] + jnp.log(whole[head]) for head in range(3)]
        lse_ref[rows, :] = jnp.where(lane == 0, totals[0], jnp.where(lane == 1, totals[1], totals[2]))
        ride.hop(tile)
        ride.turn_when(tile == 2)

    ride.finish()


def attend(qw, kv, flags, cid, riders=()):
    outs = [sds(1024, 192), sds(1024, 128, dtype=F32)]
    scratch = [
        pltpu.VMEM((3, Q_TILE, 128), BF16),
        pltpu.VMEM((3, Q_TILE, 1), F32),
        pltpu.VMEM((3, Q_TILE, 256), F32),
        pltpu.VMEM((2, 4096, 256), BF16),
    ]
    cost = (5 * 512 * 1024 * 64 * 4 * 3, 6 << 20, 5 * 512 * 1024 * 3)
    operands = (flags, qw, kv.reshape(4096, 384))
    cid = cid if riders else None
    res, ridden = call(attend_kernel, operands, outs, scratch, cid, "attend", cost, riders, smem=(0,))
    return res[0], res[1], ridden


PIECE = 128


def exchange(c, ref, feed, mine_ref, part_ref, send_ref, got_ref, a_send, a_recv, s_send, s_recv, meanwhile):
    mate, across, far = mate_of(c), across_of(c), 3 - c
    pieces = (pl.ds(0, PIECE), pl.ds(PIECE, PIECE))

    def gather(slot, index, p, device):
        part = ref.at[slot, pieces[p]]
        return rcopy(part, part, a_send.at[index, p], a_recv.at[index, p], {"ctx": device})

    def scatter(index, p, device):
        source, target = send_ref.at[index, pieces[p]], got_ref.at[index, pieces[p]]
        return rcopy(source, target, s_send.at[index, p], s_recv.at[index, p], {"ctx": device})

    for p in range(2):
        gather(c, 1, p, across).start()
    for p in range(2):
        gather(c, 0, p, mate).start()
    mine_ref[...] += feed(c, pl.ds(0, 2 * PIECE))
    for p in range(2):
        gather(mate, 0, p, mate).wait_recv()
    send_ref[0] = feed(mate, pl.ds(0, 2 * PIECE)).astype(BF16)
    for p in range(2):
        scatter(0, p, mate).start()

    def take_across(p):
        gather(across, 1, p, across).wait_recv()
        gather(across, 2, p, mate).start()
        part_ref[pieces[p]] = feed(across, pieces[p])

    def take_far(p):
        gather(far, 2, p, mate).wait_recv()
        send_ref[1, pieces[p]] = feed(far, pieces[p]).astype(BF16)
        scatter(1, p, mate).start()

    def join(p):
        scatter(1, p, mate).wait_recv()
        send_ref[2, pieces[p]] = (part_ref[pieces[p]] + got_ref[1, pieces[p]].astype(F32)).astype(BF16)
        scatter(2, p, across).start()

    take_across(0)
    take_far(0)
    take_across(1)
    join(0)
    take_far(1)
    join(1)
    meanwhile()
    for p in range(2):
        scatter(0, p, mate).wait_recv()
        scatter(2, p, across).wait_recv()

    def settle():
        for p in range(2):
            for index in range(3):
                gather(c, index, p, mate).wait_send()
                scatter(index, p, mate).wait_send()

    return mine_ref[...] + got_ref[0].astype(F32) + got_ref[2].astype(F32), settle


def block_kernel(
    ride, o_ref, wo_ref, w1_ref, w2_ref, b1_ref, vec_ref, stream_ref,
    out_ref, low_ref, xhat1_ref, r1_ref, xhat2_ref, r2_ref, xg_ref, act_ref, slope_ref, rows_ref, down_ref,
    w_send, w_recv, mine_ref, part_ref, send_ref, got_ref, o_send, o_recv, a_send, a_recv, s_send, s_recv,
):
    c = lax.axis_index("ctx")
    t = lax.axis_index("tp")
    barrier = pltpu.get_barrier_semaphore()
    for place in range(4):

        @pl.when((t % 2 == 0) & (t != place))
        def _():
            signal(barrier, {"tp": place})

        @pl.when(t % 2 == 1)
        def _():
            signal(barrier, {"ctx": 3 - c, "tp": place})

    signal(barrier, {"ctx": mate_of(c)})
    signal(barrier, {"ctx": across_of(c)})
    f, size = lax.axis_index("fsdp"), lax.axis_size("fsdp")
    for k in range(1, size):
        signal(barrier, {"fsdp": (f + size - k) % size})
    count = 5 + t % 2 + size - 1 + ride.greet(barrier)
    ride.ready()
    pl.semaphore_wait(barrier, count)

    def weight(k):
        device = {"fsdp": (f + k) % size}
        return rcopy(w2_ref, down_ref.at[f], w_send.at[k - 1], w_recv.at[k - 1], device)

    def give(quarter):
        device = {"tp": quarter} if quarter % 2 == 0 else {"ctx": 3 - c, "tp": quarter}
        return rcopy(o_ref.at[quarter], rows_ref.at[t], o_send.at[quarter], o_recv.at[t], device)

    def given(group):
        rcopy(rows_ref.at[group], rows_ref.at[group], o_send.at[0], o_recv.at[group], {"tp": t}).wait_recv()

    for quarter in (3, 2, 1, 0):
        if quarter % 2 == 0:

            @pl.when(t != quarter)
            def _():
                give(quarter).start()

            @pl.when(t == quarter)
            def _():
                rows_ref[quarter] = o_ref[quarter]

        else:
            give(quarter).start()
    for k in range(1, size):
        weight(k).start()
    down_ref[f] = w2_ref[...]
    branch = stream_ref[...] + vec_ref[0:1]
    for group in range(4):

        @pl.when((t % 2 == 1) | (t != group))
        def _():
            given(group)

        branch += mm_nt(rows_ref[group], wo_ref[group])
    ride.start()
    xhat, scale = norm_stats(branch)
    xhat1_ref[...] = xhat
    r1_ref[...] = jnp.broadcast_to(scale, r1_ref.shape)
    normed = xhat * vec_ref[2:3] + vec_ref[3:4]
    xg_ref[c] = normed.astype(BF16)
    mine_ref[...] = normed + vec_ref[1:2]
    for k in range(1, size):
        weight(k).wait_recv()

    def feed(segment, rows):
        up = mm(xg_ref[segment, rows], w1_ref[...]) + b1_ref[...]
        act, slope = gelu_both(up)
        act_ref[segment, rows] = act
        slope_ref[segment, rows] = slope
        return mm_nt(act, down_ref[...].reshape(768, 768))

    def meanwhile():
        ride.turn()
        ride.put(xhat1_ref, r1_ref, xg_ref, act_ref, slope_ref, rows_ref, down_ref)

    summed, settle = exchange(
        c, xg_ref, feed, mine_ref, part_ref, send_ref, got_ref, a_send, a_recv, s_send, s_recv, meanwhile
    )
    xhat, scale = norm_stats(summed)
    xhat2_ref[...] = xhat
    r2_ref[...] = jnp.broadcast_to(scale, r2_ref.shape)
    out = xhat * vec_ref[4:5] + vec_ref[5:6]
    out_ref[...] = out
    low_ref[...] = out.astype(BF16)
    ride.put(out_ref, low_ref, xhat2_ref, r2_ref)
    for quarter in range(4):
        if quarter % 2 == 0:

            @pl.when(t != quarter)
            def _():
                give(quarter).wait_send()

        else:
            give(quarter).wait_send()
    for k in range(1, size):
        weight(k).wait_send()
    settle()
    ride.finish()


def block(o, wo, w1, w2, b1, vecs, stream, cid, riders=()):
    size = lax.axis_size("fsdp")
    f = functools.partial(sds, dtype=F32)
    outs = [
        f(256, 768), sds(256, 768), f(256, 768), f(256, 128), f(256, 768), f(256, 128),
        sds(4, 256, 768), sds(4, 256, 768), sds(4, 256, 768), sds(4, 256, 192), sds(size, *w2.shape),
    ]
    scratch = [
        dma(size - 1), dma(size - 1),
        pltpu.VMEM((256, 768), F32),
        pltpu.VMEM((256, 768), F32),
        pltpu.VMEM((3, 256, 768), BF16),
        pltpu.VMEM((3, 256, 768), BF16),
        dma(4), dma(4), dma(3, 2), dma(3, 2), dma(3, 2), dma(3, 2),
    ]
    cost = (2 * 256 * 768 * 768 + 4 * 1024 * 768 * 768, 16 << 20, 1 << 20)
    operands = (o.reshape(4, 256, 192), wo, w1, w2, b1, vecs, stream)
    res, ridden = call(block_kernel, operands, outs, scratch, cid, "block", cost, riders)
    flat = lambda a: a.reshape(1024, 768)
    return tuple(res[:6]) + (flat(res[6]), flat(res[7]), flat(res[8]), res[9], res[10].reshape(768, 768), ridden)


def block_back_kernel(
    ride, grad_ref, xhat2_ref, r2_ref, xhat1_ref, r1_ref, vec_ref, slope_ref, w1_ref, w2_ref, wo_ref,
    xg_ref, act_ref, rows_ref, back_ref, do_ref, stat_ref, dup_ref, ddown_ref, dout_ref,
    w_send, w_recv, term_ref, all_up_ref, gg_ref, gu_ref, mine_ref, part_ref, send_ref, got_ref, dsend_ref, d_send, d_recv, a_send, a_recv, s_send, s_recv,
):
    c = lax.axis_index("ctx")
    t = lax.axis_index("tp")
    barrier = pltpu.get_barrier_semaphore()
    for place in range(4):
        if place % 2 == 0:

            @pl.when(t != place)
            def _():
                signal(barrier, {"tp": place})

        else:
            signal(barrier, {"ctx": 3 - c, "tp": place})
    signal(barrier, {"ctx": mate_of(c)})
    signal(barrier, {"ctx": across_of(c)})
    f, size = lax.axis_index("fsdp"), lax.axis_size("fsdp")
    depth = dup_ref.shape[0]
    for k in range(1, size):
        signal(barrier, {"fsdp": (f + size - k) % size})
    count = 5 + t % 2 + size - 1 + ride.greet(barrier)
    ride.ready()
    pl.semaphore_wait(barrier, count)

    def row(values):
        return jnp.sum(values, axis=0, keepdims=True)

    grad = grad_ref[...]
    back_two = norm_back(grad, xhat2_ref[...], r2_ref[:, 0:1], vec_ref[4:5])
    g2 = back_two.astype(BF16)
    gg_ref[c] = g2
    mine_ref[...] = back_two
    ride.start()
    stat_ref[1:2] = row(grad * xhat2_ref[...])
    stat_ref[3:4] = row(grad)
    stat_ref[5:6] = row(g2.astype(F32))
    stat_ref[6:8] = jnp.zeros((2, 768), F32)

    def feed(segment, rows):
        gu = (mm(gg_ref[segment, rows], w2_ref[...]) * slope_ref[segment, rows].astype(F32)).astype(BF16)
        gu_ref[segment, rows] = gu
        stat_ref[6:7] += row(gu.astype(F32))
        return mm_nt(gu, w1_ref[...])

    tall = lambda ref: ref[...].reshape(1024, 768)

    def slice_of(place):
        return pl.ds(pl.multiple_of(place * depth, depth), depth)

    def term(k):
        to = (f + k) % size
        return rcopy(
            all_up_ref.at[slice_of(to)], term_ref.at[k - 1], w_send.at[k - 1], w_recv.at[k - 1], {"fsdp": to}
        )

    def meanwhile():
        @pl.loop(0, 3)
        def _(tile):
            cols = pl.ds(pl.multiple_of(tile * 256, 256), 256)
            all_up_ref[cols] = mm_tn(xg_ref[:, cols], tall(gu_ref)).astype(BF16)

        for k in range(1, size):
            term(k).start()

        @pl.loop(0, 3)
        def _(tile):
            cols = pl.ds(pl.multiple_of(tile * 256, 256), 256)
            ddown_ref[cols] = mm_tn(gg_ref[:, :, cols].reshape(1024, 256), act_ref[...]).astype(BF16)

        ride.put(ddown_ref)
        ride.turn()

    grad_normed, settle = exchange(
        c, gg_ref, feed, mine_ref, part_ref, send_ref, got_ref, a_send, a_recv, s_send, s_recv, meanwhile
    )
    back_one = norm_back(grad_normed, xhat1_ref[...], r1_ref[:, 0:1], vec_ref[2:3])
    back_ref[...] = back_one
    g1 = back_one.astype(BF16)

    def give_near(group):
        return rcopy(dsend_ref.at[group], do_ref.at[t], d_send.at[group], d_recv.at[t], {"tp": group})

    def give_far(group):
        return rcopy(dsend_ref.at[group], do_ref.at[t], d_send.at[group], d_recv.at[t], {"ctx": 3 - c, "tp": group})

    for group in range(4):
        dsend_ref[group] = mm(g1, wo_ref[group]).astype(BF16)

        @pl.when((t % 2 == 0) & (t == group))
        def _():
            do_ref[t] = dsend_ref[group]

        @pl.when((t % 2 == 0) & (t != group))
        def _():
            give_near(group).start()

        @pl.when(t % 2 == 1)
        def _():
            give_far(group).start()

    stat_ref[0:1] = row(grad_normed * xhat1_ref[...])
    stat_ref[2:3] = row(grad_normed)
    stat_ref[4:5] = row(g1.astype(F32))
    for group in range(4):
        dout_ref[group] = mm_tn(g1, rows_ref[group]).astype(BF16)
    ride.put(back_ref, stat_ref, dout_ref)
    total = all_up_ref[slice_of(f)].astype(F32)
    for k in range(1, size):
        term(k).wait_recv()
        total += term_ref[k - 1].astype(F32)
    dup_ref[...] = total.astype(BF16)
    ride.put(dup_ref)
    for quarter in range(4):

        def taken():
            rcopy(do_ref.at[quarter], do_ref.at[quarter], d_send.at[0], d_recv.at[quarter], {"tp": t}).wait_recv()

        if quarter % 2 == 0:
            pl.when(t != quarter)(taken)
        else:
            taken()
    for group in range(4):

        @pl.when((t % 2 == 1) | (t != group))
        def _():
            give_near(group).wait_send()

    for k in range(1, size):
        term(k).wait_send()
    settle()
    ride.finish()


def block_back(grad, xhat2, r2, xhat1, r1, vecs, slope, w1, w2, wo, xg, act, rows, cid, riders=()):
    f = functools.partial(sds, dtype=F32)
    size = lax.axis_size("fsdp")
    depth = 768 // size
    outs = [
        f(256, 768), sds(4, 256, 192), f(8, 768), sds(depth, 768), sds(768, 768), sds(4, 768, 192),
    ]
    scratch = [
        dma(size - 1), dma(size - 1), pltpu.VMEM((size - 1, depth, 768), BF16), pltpu.VMEM((768, 768), BF16),
        pltpu.VMEM((4, 256, 768), BF16),
        pltpu.VMEM((4, 256, 768), BF16),
        pltpu.VMEM((256, 768), F32),
        pltpu.VMEM((256, 768), F32),
        pltpu.VMEM((3, 256, 768), BF16),
        pltpu.VMEM((3, 256, 768), BF16),
        pltpu.VMEM((4, 256, 192), BF16),
        dma(4), dma(4), dma(3, 2), dma(3, 2), dma(3, 2), dma(3, 2),
    ]
    cost = (4 * 256 * 768 * 768 + 8 * 1024 * 768 * 768, 20 << 20, 1 << 10)
    operands = (grad, xhat2, r2, xhat1, r1, vecs, slope.reshape(4, 256, 768), w1, w2, wo, xg, act, rows)
    res, ridden = call(block_back_kernel, operands, outs, scratch, cid, "block_back", cost, riders)
    back, do, stats, d_up, d_down, d_out = res
    return back, do.reshape(1024, 192), stats, d_up, d_down, d_out, ridden


def ordered_by(place, step):
    half = place // 2
    inner = place + half * (3 - 2 * place)
    chunk = step + inner * (1 - 2 * step) * ((3 - step) // 2)
    return chunk + half * (3 - 2 * chunk)


def inner_back_kernel(
    ride, flag_ref, qw_ref, kv_ref, do_ref, o_ref, lse_ref, w_ref, back_ref, xg_ref, mark_ref,
    grad_ref, low_ref, din_ref, sum_out_ref, mem_ref,
    qm_ref, dm_ref, row_ref, acc_ref, wide_ref, dkv_ref, dqs_ref,
    w_send, w_recv, term_ref, all_in_ref, dq_ref, own_ref, part_ref,
    near_ref, join_ref, sum_ref, far_ref, pass_ref, take_ref,
    q_send, q_recv, n_send, n_recv, j_send, j_recv, f_send, f_recv, p_send, p_recv,
):
    c = lax.axis_index("ctx")
    t = lax.axis_index("tp")
    f, size = lax.axis_index("fsdp"), lax.axis_size("fsdp")
    depth = din_ref.shape[0]
    mate, across, far = mate_of(c), across_of(c), 3 - c
    barrier = pltpu.get_barrier_semaphore()
    for device in (mate, across, far):
        signal(barrier, {"ctx": device})

    @pl.when(t > 0)
    def _():
        signal(barrier, {"tp": t - 1})

    @pl.when(t < 3)
    def _():
        signal(barrier, {"tp": t + 1})

    for k in range(1, size):
        signal(barrier, {"fsdp": (f + size - k) % size})
    ends = (t // 3) + (3 - t) // 3
    count = 5 - ends + size - 1 + ride.greet(barrier)
    ride.ready()

    low = lax.broadcasted_iota(jnp.int32, (1024, 128), 1) < 64
    pair = qw_ref[:, 0:128]
    none = jnp.zeros_like(pair)
    qm_ref[0] = jnp.where(low, pair, none)
    qm_ref[1] = jnp.where(low, none, pair)
    qm_ref[2] = qw_ref[:, 128:256]
    pair = do_ref[:, 0:128]
    dm_ref[0] = jnp.where(low, pair, none)
    dm_ref[1] = jnp.where(low, none, pair)
    dm_ref[2] = jnp.concatenate([do_ref[:, 128:192], none[:, :64]], axis=1)
    turned = jnp.transpose(lse_ref[...], (1, 0))
    product = do_ref[...].astype(F32) * o_ref[...].astype(F32)
    head_row = lax.broadcasted_iota(jnp.int32, (8, 192), 0)
    head_of = lax.broadcasted_iota(jnp.int32, (8, 192), 1) // 64
    delta = lax.dot_general(
        (head_row == head_of).astype(F32), product, (((1,), (1,)), ((), ())),
        precision=lax.Precision.HIGHEST, preferred_element_type=F32,
    )
    for quarter in range(4):
        row_ref[quarter, 0:8] = turned[0:8, quarter * 256 : (quarter + 1) * 256]
        row_ref[quarter, 8:16] = delta[:, quarter * 256 : (quarter + 1) * 256]
    acc_ref[...] = jnp.zeros_like(acc_ref)
    wide_ref[...] = jnp.zeros_like(wide_ref)
    pl.semaphore_wait(barrier, count)
    ride.start()

    def partner(slot):
        return rcopy(dqs_ref.at[slot], dq_ref.at[2 * slot + 1], q_send.at[slot], q_recv.at[slot], {"ctx": far})

    def near(chunk):
        return rcopy(dkv_ref.at[mate, chunk], near_ref.at[chunk], n_send.at[chunk], n_recv.at[chunk], {"ctx": mate})

    def join(chunk):
        return rcopy(dkv_ref.at[far, chunk], join_ref.at[chunk], j_send.at[chunk], j_recv.at[chunk], {"ctx": mate})

    def cross(chunk):
        return rcopy(sum_ref.at[chunk], far_ref.at[chunk], f_send.at[chunk], f_recv.at[chunk], {"ctx": across})

    def lower(chunk):
        return rcopy(pass_ref.at[chunk], take_ref.at[0, chunk], p_send.at[chunk], p_recv.at[0, chunk], {"tp": t - 1})

    def upper(chunk):
        return rcopy(pass_ref.at[chunk], take_ref.at[1, chunk], p_send.at[chunk], p_recv.at[1, chunk], {"tp": t + 1})

    def passed(side, chunk):
        rcopy(
            take_ref.at[side, chunk], take_ref.at[side, chunk], p_send.at[0], p_recv.at[side, chunk], {"tp": t}
        ).wait_recv()

    chunks = [ordered(t, 3 - k) for k in range(4)]
    at_end = (t == 0) | (t == 3)

    def leave(k):
        chunk = chunks[k]
        dkv_ref[:, chunk] = wide_ref[:, chunk].astype(BF16)
        join(chunk).start()
        near(chunk).start()
        query = (acc_ref[chunk].astype(BF16).astype(F32) * 0.125).astype(BF16)

        @pl.when(chunk % 2 == 0)
        def _():
            dq_ref[chunk] = query

        @pl.when(chunk % 2 == 1)
        def _():
            dqs_ref[chunk // 2] = query
            partner(chunk // 2).start()

    def go_across(k):
        chunk = chunks[k]
        join(chunk).wait_recv()
        sum_ref[chunk] = (dkv_ref[across, chunk].astype(F32) + join_ref[chunk].astype(F32)).astype(BF16)
        cross(chunk).start()

    def gather_up(k):
        chunk = chunks[k]
        if k < 3:

            @pl.when(chunk % 2 == 1)
            def _():
                partner(chunk // 2).wait_recv()

        near(chunk).wait_recv()
        cross(chunk).wait_recv()
        own = (
            dkv_ref[c, chunk].astype(F32) + near_ref[chunk].astype(F32) + far_ref[chunk].astype(F32)
        ).astype(BF16)
        own_ref[chunk] = own
        part_ref[chunk] = mm_nt(dq_ref[chunk], w_ref[:, 0:256]) + mm_nt(own, w_ref[:, 256:640])

    def relay(k):
        chunk = chunks[k]

        @pl.when(chunk < t)
        def _():
            @pl.when(t < 3)
            def _():
                passed(0, chunk)
                pass_ref[chunk] = (part_ref[chunk] + take_ref[0, chunk].astype(F32)).astype(BF16)

            @pl.when(t == 3)
            def _():
                pass_ref[chunk] = part_ref[chunk].astype(BF16)

            lower(chunk).start()

        @pl.when(chunk > t)
        def _():
            @pl.when(t > 0)
            def _():
                passed(1, chunk)
                pass_ref[chunk] = (part_ref[chunk] + take_ref[1, chunk].astype(F32)).astype(BF16)

            @pl.when(t == 0)
            def _():
                pass_ref[chunk] = part_ref[chunk].astype(BF16)

            upper(chunk).start()

    def relay_ends(k):
        pl.when(at_end)(functools.partial(relay, k))

    def relay_inner(k):
        pl.when(jnp.logical_not(at_end))(functools.partial(relay, k))

    low_keys = lax.broadcasted_iota(jnp.int32, (256, 128), 1) < 64

    def one_item(item, done):
        phase = (item + 9) // 16 + (item + 4) // 16 + (item + 1) // 16
        number = item - phase * (8 - phase)
        second = number // (4 - phase)
        query_at = ordered_by(t, 3 - (phase + second * (number - 3 + phase)))
        key_at = ordered_by(t, 3 - (phase + (1 - second) * number))
        half = query_at % 2
        rows = pl.ds(pl.multiple_of(query_at * 256, 256), 256)

        def visit(segments):
            queries = [qm_ref[head, rows] for head in range(3)]
            grads = [dm_ref[head, rows] for head in range(3)]
            made = []
            for segment in segments:
                penalty = jnp.where(flag_ref[half, segment] > 0, 0.0, FAR)
                key_pair = kv_ref[segment, key_at, :, 0:128]
                mixed = kv_ref[segment, key_at, :, 128:256]
                value_pair = kv_ref[segment, key_at, :, 256:384]
                for head in range(3):
                    shift = row_ref[query_at, head : head + 1] + penalty
                    prob = jnp.exp(mm_nt(key_pair if head < 2 else mixed, queries[head]) - shift)
                    grad_prob = mm_nt(value_pair if head < 2 else mixed, grads[head])
                    grad_score = (prob * (grad_prob - row_ref[query_at, 8 + head : 9 + head])).astype(BF16)
                    made.append((prob.astype(BF16), grad_score))
            pair_sum, mixed_sum = 0.0, 0.0
            for number, segment in enumerate(segments):
                (p0, g0), (p1, g1), (p2, g2) = made[3 * number : 3 * number + 3]
                for_keys = mm(g0, queries[0]) + mm(g1, queries[1])
                for_mixed = mm(g2, queries[2]) + mm(p2, grads[2])
                for_values = mm(p0, grads[0]) + mm(p1, grads[1])
                wide_ref[segment, key_at] += jnp.concatenate([for_keys, for_mixed, for_values], axis=1)
                key_pair = kv_ref[segment, key_at, :, 0:128]
                nothing = jnp.zeros_like(key_pair)
                pair_sum += mm_tn(g0, jnp.where(low_keys, key_pair, nothing))
                pair_sum += mm_tn(g1, jnp.where(low_keys, nothing, key_pair))
                mixed_sum += mm_tn(g2, jnp.where(low_keys, nothing, kv_ref[segment, key_at, :, 128:256]))
            acc_ref[query_at] += jnp.concatenate([pair_sum, mixed_sum], axis=1)

        length = c + 1 + half * (3 - 2 * c)

        @pl.loop(0, length // 2)
        def _(two):
            visit((2 * two, 2 * two + 1))

        @pl.when(length % 2 == 1)
        def _():
            visit((length - 1,))

        now = done + length

        def at(place, action, k):
            pl.when(item == place)(functools.partial(action, k))

        def once(amount, action, k):
            pl.when((done < amount) & (now >= amount))(functools.partial(action, k))

        for n in range(len(ride.hops)):
            once(RIDE_HOPS[n], ride.one_hop, n)
        ride.turn_when((done < 16) & (now >= 16))
        for k, place in enumerate((6, 11, 14)):
            at(place, leave, k)
        once(24, go_across, 0)
        once(31, gather_up, 0)
        once(31, relay_ends, 0)
        once(32, go_across, 1)
        once(38, gather_up, 1)
        once(38, relay_ends, 1)
        return now

    lax.fori_loop(0, 16, one_item, 0)
    leave(3)
    go_across(2)
    relay_inner(0)
    go_across(3)
    gather_up(2)
    relay_ends(2)
    relay_inner(1)

    def slice_of(place):
        return pl.ds(pl.multiple_of(place * depth, depth), depth)

    spans = (pl.ds(0, 256), pl.ds(256, 256), pl.ds(512, 128))

    def term(k, span):
        to, cols = (f + k) % size, spans[span]
        return rcopy(
            all_in_ref.at[slice_of(to), cols], term_ref.at[k - 1, :, cols],
            w_send.at[k - 1, span], w_recv.at[k - 1, span], {"fsdp": to},
        )


    @pl.when(t % 2 == 1)
    def _():
        partner(t // 2).wait_recv()

    query = dq_ref[...].reshape(1024, 256)
    for span in range(3):
        if span == 1:
            gather_up(3)
        own = own_ref[...].reshape(1024, 384)
        made = (query, own[:, 0:256], own[:, 256:384])[span]
        all_in_ref[:, spans[span]] = mm_tn(xg_ref[...], made).astype(BF16)
        for k in range(1, size):
            term(k, span).start()

    relay_inner(2)
    sum_out_ref[0:1, 0:256] = jnp.sum(query.astype(F32), axis=0, keepdims=True)
    sum_out_ref[0:1, 256:640] = jnp.sum(own.astype(F32), axis=0, keepdims=True)
    ride.put(sum_out_ref)
    grad_ref[...] = part_ref[t] + back_ref[...]

    @pl.when(t < 3)
    def _():
        passed(0, t)
        grad_ref[...] += take_ref[0, t].astype(F32)

    @pl.when(t > 0)
    def _():
        passed(1, t)
        grad_ref[...] += take_ref[1, t].astype(F32)

    low_ref[...] = grad_ref[...].astype(BF16)
    ride.put(grad_ref, low_ref)
    mem_ref[...] = lax.dot_general(
        mark_ref[...], grad_ref[...], (((0,), (0,)), ((), ())),
        precision=lax.Precision.HIGHEST, preferred_element_type=F32,
    )
    ride.put(mem_ref)
    total = all_in_ref[slice_of(f)].astype(F32)
    for k in range(1, size):
        for span in range(3):
            term(k, span).wait_recv()
        total += term_ref[k - 1].astype(F32)
    din_ref[...] = total.astype(BF16)
    ride.put(din_ref)
    for k in range(1, size):
        for span in range(3):
            term(k, span).wait_send()
    for chunk in range(4):
        join(chunk).wait_send()
        near(chunk).wait_send()
        cross(chunk).wait_send()

        @pl.when(t != chunk)
        def _():
            upper(chunk).wait_send()

    for slot in range(2):
        partner(slot).wait_send()
    ride.finish()


RIDE_HOPS = (10, 14)


def inner_back(qw, kv, do, o, lse, flags, w, back_one, xg, marks, cid, riders=()):
    size = lax.axis_size("fsdp")
    depth = 768 // size
    f = functools.partial(sds, dtype=F32)
    outs = [f(256, 768), sds(256, 768), sds(depth, 640), f(8, 640), f(marks.shape[1], 768)]
    scratch = [
        pltpu.VMEM((3, 1024, 128), BF16), pltpu.VMEM((3, 1024, 128), BF16), pltpu.VMEM((4, 16, 256), F32),
        pltpu.VMEM((4, 256, 256), F32), pltpu.VMEM((4, 4, 256, 384), F32), pltpu.VMEM((4, 4, 256, 384), BF16),
        pltpu.VMEM((2, 256, 256), BF16),
        dma(size - 1, 3), dma(size - 1, 3), pltpu.VMEM((size - 1, depth, 640), BF16), pltpu.VMEM((768, 640), BF16),
        pltpu.VMEM((4, 256, 256), BF16), pltpu.VMEM((4, 256, 384), BF16),
        pltpu.VMEM((4, 256, 768), F32),
        pltpu.VMEM((4, 256, 384), BF16), pltpu.VMEM((4, 256, 384), BF16),
        pltpu.VMEM((4, 256, 384), BF16), pltpu.VMEM((4, 256, 384), BF16),
        pltpu.VMEM((4, 256, 768), BF16), pltpu.VMEM((2, 4, 256, 768), BF16),
        dma(2), dma(2), dma(4), dma(4), dma(4), dma(4), dma(4), dma(4), dma(4), dma(2, 4),
    ]
    cost = (5 * 512 * 1024 * 64 * 30 + 4 * 1024 * 768 * 640, 16 << 20, 5 * 512 * 1024 * 3)
    operands = (flags, qw, kv.reshape(4, 4, 256, 384), do, o, lse, w, back_one, xg, marks)
    res, ridden = call(inner_back_kernel, operands, outs, scratch, cid, "inner_back", cost, riders, smem=(0,))
    return (*res[:3], res[3][0], res[4], ridden)


def ancestry(parent_row):
    seg_count = parent_row.shape[0]
    segment_ids = jnp.arange(seg_count, dtype=jnp.int32)
    parent_hop = (parent_row[:, None] == segment_ids[None, :]).astype(jnp.int32)
    reached = (segment_ids[:, None] == segment_ids[None, :]).astype(jnp.int32)
    on_path = reached
    for hop_number in range(seg_count - 1):
        reached = jnp.dot(reached, parent_hop)
        on_path = jnp.maximum(on_path, reached)
    return on_path


def joined(query, key, value, gap):
    return jnp.concatenate(
        [
            query[..., :128], gap, query[..., 128:],
            key[..., :128], value[..., 128:], key[..., 128:], value[..., :128],
        ],
        axis=-1,
    )


def parted(grads):
    query = jnp.concatenate([grads[..., :128], grads[..., 192:256]], axis=-1)
    key = jnp.concatenate([grads[..., 256:384], grads[..., 448:512]], axis=-1)
    value = jnp.concatenate([grads[..., 512:640], grads[..., 384:448]], axis=-1)
    return query, key, value


def added(terms, axes=(0,)):
    return jnp.sum(terms.astype(F32), axis=axes)


def low(values):
    return values.astype(BF16)


def shards(
    hidden, cotangent, mem_pos, parents, memory, wq, wk, wv, wo, w1, w2,
    head_bias, ffn_bias, out_bias, norm_gains, norm_shifts,
):
    c = lax.axis_index("ctx")
    t = lax.axis_index("tp")
    size = lax.axis_size("fsdp")
    layers = wq.shape[0]
    share = hidden.shape[0]
    depth = wq.shape[1]
    piece = depth // 4
    positions = t * share + jnp.arange(share, dtype=jnp.int32)
    marks = (mem_pos[0, 0][None, :] == positions[:, None]).astype(F32)
    stream = hidden.astype(F32) + jnp.dot(
        marks, memory, precision=lax.Precision.HIGHEST, preferred_element_type=F32
    )
    on_path = ancestry(parents[0])
    ids = jnp.arange(4, dtype=jnp.int32)
    pick = lambda seg: jnp.sum(on_path * (ids == seg).astype(jnp.int32)[:, None], axis=0)
    flags = jnp.stack([pick(c), pick(3 - c)])

    gap = jnp.zeros(wq.shape[:2] + (64,), BF16)
    own_in = joined(wq, wk, wv, gap)
    none = jnp.zeros((layers, 192), F32)
    in_bias = joined(head_bias[:, 0], none, head_bias[:, 1], jnp.zeros((layers, 64), F32))
    down_turned = jnp.swapaxes(w2, 1, 2)
    out_turned = jnp.swapaxes(wo, 1, 2).reshape(layers, 4, piece, 192)
    out_piece = lax.dynamic_index_in_dim(out_turned, c, axis=1, keepdims=False)

    def out_whole(gathered):
        return jnp.transpose(gathered, (1, 2, 0, 3, 4)).reshape(4, 768, 192)

    def vectors(n):
        norms = [norm_gains[n, 0], norm_shifts[n, 0], norm_gains[n, 1], norm_shifts[n, 1]]
        return jnp.concatenate([out_bias[n], jnp.stack(norms), jnp.zeros((2, 768), F32)])

    saved, weights = [], []
    rounded = low(stream)
    riders = [plane_gather(out_piece[0], size), tp_flip(ffn_bias)]
    xg, qw, kv, w_in, (out, units) = project(
        rounded, own_in[0], in_bias[0][None], 0, riders, fetch=True
    )
    for n in range(layers):
        last = n == layers - 1
        riders = [ctx_gather(out)]
        if n == 0:
            riders += [flip_gather(w1[0], size)]
        riders += [tp_flip(down_turned[n])]
        if n == 0:
            riders[-1].after()
        o, lse, got = attend(qw, kv, flags, 16 * n + 1, riders)
        w_out = out_whole(got[0])
        if n == 0:
            w_up = got[1]
        w_up, down = w_up.reshape(768, 768), got[-1]
        vecs = vectors(n)
        riders = []
        if not last:
            riders = [
                tp_flip(w1[n + 1]),
                plane_gather(out_piece[n + 1], size), fsdp_gather(own_in[n + 1], size),
            ]
        stream, rounded, xhat1, r1, xhat2, r2, xg2, act, slope, rows, w_down, got = block(
            o, w_out, w_up, down, units[n][None], vecs, stream, 16 * n + 2, riders
        )
        weights.append((w_in, w_up, w_down, w_out, vecs))
        saved.append((xg, qw, kv, o, lse, xhat1, r1, xhat2, r2, xg2, act, slope, rows))
        if not last:
            up, out, w_in = got
            xg, qw, kv, w_in, (w_up,) = project(
                rounded, w_in.reshape(768, 640), in_bias[n + 1][None], 16 * n + 16, [fsdp_gather(up, size)]
            )
    output = rounded

    grad = cotangent.astype(F32)
    small, heads = [None] * layers, [None] * layers
    done = [None] * layers
    above = None
    for n in reversed(range(layers)):
        w_in, w_up, w_down, w_out, vecs = weights[n]
        xg, qw, kv, o, lse, xhat1, r1, xhat2, r2, xg2, act, slope, rows = saved[n]
        riders = []
        if above is not None:
            riders = [plane_scatter(above["out"], size)]
            riders += [ctx_scatter(above[part]) for part in ("up", "down", "in")]
        back_one, do, small[n], d_up, d_down, d_out, got = block_back(
            grad, xhat2, r2, xhat1, r1, vecs, slope, w_up, w_down, w_out, xg2, act, rows, 16 * n + 3, riders
        )
        d_down = d_down.reshape(1, size, 2, depth // 2, 768)
        riders = [tp_flip(d_up), scatter_flip(d_down), ctx_scatter(d_out.reshape(4, size, 4, piece, 192), axis=2)]
        if above is not None:
            riders += [ctx_gather(low(added(got[0], (0, 1))))] + [ctx_gather(low(added(part))) for part in got[1:]]
        grad, low_grad, d_in, sums, memory_part, got = inner_back(
            qw, kv, do, o, lse, flags, w_in, back_one, xg, marks, 16 * n + 4, riders
        )
        if above is not None:
            done[n + 1] = (got[6], got[3], got[4], got[5])
        d_query_bias, _, d_value_bias = parted(sums)
        heads[n] = jnp.stack([d_query_bias, d_value_bias])
        above = {
            "up": got[0].reshape(4, depth // 4, 768),
            "down": got[1].reshape(4, depth // 4, 768),
            "in": d_in.reshape(4, depth // 4, 640),
            "out": low(added(got[2])),
        }
    hidden_grad = low_grad
    small = jnp.stack(small)
    place = (ids == t).astype(F32)
    unit = (ids == flipped_place(c, t)).astype(F32)
    head_rows = (jnp.stack(heads)[:, :, None, :] * place[None, None, :, None]).reshape(2 * layers, 768)
    unit_rows = (small[:, 6][:, None, :] * unit[None, :, None]).reshape(4 * layers, 768)
    stat_rows = small[:, :6].reshape(6 * layers, 768)
    filled = 12 * layers + memory_part.shape[0]
    slices = 4 * size
    width = -(-filled // slices)
    rest = jnp.zeros((width * slices - filled, 768), F32)
    sums = jnp.concatenate([stat_rows, unit_rows, head_rows, memory_part, rest])
    sums = sums.reshape(4, size, width, 768)
    riders = [ctx_scatter(above[part]) for part in ("up", "down", "in")]
    got = carry(riders + [plane_scatter(above["out"], size), plane_scatter(sums, size)], 6)
    up0, down0, in0 = (ctx_gather(low(added(part))) for part in got[:3])
    out0 = ctx_gather(low(added(got[3], (0, 1))))
    got = carry([up0, down0, in0, out0, all_gather(added(got[4], (0, 1)), size)], 7)
    done[0] = (got[2], got[3], got[0], got[1])
    totals = added(got[4]).reshape(width * slices, 768)
    stats = totals[: 6 * layers].reshape(layers, 6, 768)
    at = 6 * layers
    ffn_rows = totals[at : at + 4 * layers].reshape(layers, 4, 768)
    ffn_grad = jnp.sum(ffn_rows * place[None, :, None], axis=1)
    at += 4 * layers
    head_sums = totals[at : at + 2 * layers].reshape(layers, 2, 4, 192)
    head_grad = jnp.sum(head_sums * place[None, None, :, None], axis=2)
    at += 2 * layers
    memory_grad = totals[at : at + memory_part.shape[0]]
    d_in = jnp.stack([part[0].reshape(depth, 640) for part in done]).astype(F32)
    d_out = jnp.stack([jnp.swapaxes(part[1].reshape(depth, 192), 0, 1) for part in done]).astype(F32)
    d_up = jnp.stack([part[2].reshape(depth, 768) for part in done]).astype(F32)
    d_down = jnp.stack([jnp.swapaxes(part[3].reshape(depth, 768), 0, 1) for part in done]).astype(F32)
    return (
        output, hidden_grad, memory_grad, *parted(d_in), d_out, d_up, d_down,
        head_grad, ffn_grad, stats[:, 4:6], stats[:, 0:2], stats[:, 2:4],
    )


def solution(mesh):
    rows = P(("fsdp", "ctx", "tp"), None)
    inner = P(None, "fsdp", "tp")
    outer = P(None, "tp", "fsdp")
    weights = (inner, inner, inner, outer, inner, outer)
    biases = (P(None, None, "tp"), P(None, "tp"), P(), P(), P())
    return jax.shard_map(
        shards,
        mesh=mesh,
        in_specs=(rows, rows, P("fsdp", "ctx", None), P("fsdp", None), P()) + weights + biases,
        out_specs=(rows, rows, P()) + weights + biases,
        check_vma=False,
    )
```

```python
import functools

import jax
import jax.numpy as jnp
from jax import lax
from jax.experimental import pallas as pl
from jax.experimental.pallas import tpu as pltpu
from jax.sharding import PartitionSpec as P

EPSILON = 1e-05
MASKED = -1000000000.0
MESH = pl.DeviceIdType.MESH
F32 = jnp.float32
BF16 = jnp.bfloat16
ORDER = ((0, 1), (1, 0), (2, 2), (3, 3))


def mm(left, right):
    return jnp.dot(left, right, preferred_element_type=F32)


def mm_nt(left, right):
    return lax.dot_general(left, right, (((1,), (1,)), ((), ())), preferred_element_type=F32)


def mm_tn(left, right):
    return lax.dot_general(left, right, (((0,), (0,)), ((), ())), preferred_element_type=F32)


def rcopy(src, dst, send_sem, recv_sem, device):
    return pltpu.make_async_remote_copy(
        src_ref=src,
        dst_ref=dst,
        send_sem=send_sem,
        recv_sem=recv_sem,
        device_id=device,
        device_id_type=MESH,
    )


def mate_of(c):
    return c + 1 - 2 * (c % 2)


def across_of(c):
    return (c + 2) % 4


def signal(sem, device):
    pl.semaphore_signal(sem, inc=1, device_id=device, device_id_type=MESH)


def ordered(place, step):
    half = place // 2
    inner = place + half * (3 - 2 * place)
    first, second = ORDER[step]
    chunk = first + inner * (second - first)
    return chunk + half * (3 - 2 * chunk)


def ordered_by(place, step):
    half = place // 2
    inner = place + half * (3 - 2 * place)
    chunk = step + inner * (1 - 2 * step) * ((3 - step) // 2)
    return chunk + half * (3 - 2 * chunk)


def dma(*shape):
    return pltpu.SemaphoreType.DMA(shape)


class Rider:
    def __init__(self, array, out, make, scratch, chunks=0):
        self.array, self.out, self.make, self.scratch, self.chunks = array, out, make, scratch, chunks
        self.late = self.hopped = False

    def later(self, hopped=False):
        self.late, self.hopped = True, hopped
        return self


class Copies:
    def __init__(self, steps, here, scratch):
        self.steps, self.here = steps, here
        self.send, self.recv, self.leg, self.stage = scratch
        self.came = False

    def greetings(self):
        return [(origin, when, weight) for _, origin, _, _, when, weight in self.steps]

    def copies(self):
        for number, (to, _, source, target, when, _) in enumerate(self.steps):
            yield rcopy(source, target, self.send.at[number], self.recv.at[number], to), when

    def inward(self):
        return pltpu.make_async_copy(self.here[0], self.stage, self.leg.at[0])

    def outward(self):
        return pltpu.make_async_copy(self.stage, self.here[1], self.leg.at[1])

    def start(self):
        for copy, when in self.copies():
            guarded(when, copy.start)
        guarded(self.here[2], self.inward().start)

    def turn(self):
        guarded(self.here[2], self.inward().wait)
        guarded(self.here[2], self.outward().start)

    def arrive(self):
        self.came = True
        for copy, when in self.copies():
            guarded(when, copy.wait_recv)
        guarded(self.here[2], self.outward().wait)

    def finish(self):
        if not self.came:
            self.arrive()
        for copy, when in self.copies():
            guarded(when, copy.wait_send)


class FlipGather:
    def __init__(self, source, target, place, scratch):
        self.source, self.target = source, target
        self.f, self.c, self.t = place
        self.size = target.shape[0]
        self.send, self.recv, self.on_send, self.on_recv, self.leg, self.stage = scratch
        self.moves = self.c > 0

    def greetings(self):
        there = {"tp": flipped_place(self.c, self.t)}
        ring = [({"fsdp": (self.f + self.size - k) % self.size}, None, 1) for k in range(1, self.size)]
        return [(there, self.moves, (self.c + 3) // 4)] + ring

    def first(self, chunk):
        there = {"tp": flipped_place(self.c, self.t)}
        return rcopy(
            self.source.at[chunk], self.target.at[self.f, chunk], self.send.at[chunk], self.recv.at[chunk], there
        )

    def second(self, chunk, k, moved):
        source = self.target.at[self.f, chunk] if moved else self.source.at[chunk]
        device = {"fsdp": (self.f + k) % self.size}
        return rcopy(
            source, self.target.at[self.f, chunk], self.on_send.at[k - 1, chunk], self.on_recv.at[k - 1, chunk], device
        )

    def inward(self):
        return pltpu.make_async_copy(self.source, self.stage, self.leg.at[0])

    def outward(self):
        return pltpu.make_async_copy(self.stage, self.target.at[self.f], self.leg.at[1])

    def start(self):
        @pl.when(self.moves)
        def _():
            for chunk in range(self.source.shape[0]):
                self.first(chunk).start()

        @pl.when(self.c == 0)
        def _():
            self.inward().start()

    def hop(self, chunk):
        @pl.when(self.moves)
        def _():
            self.first(chunk).wait_recv()
            for k in range(1, self.size):
                self.second(chunk, k, True).start()

        @pl.when(self.c == 0)
        def _():
            for k in range(1, self.size):
                self.second(chunk, k, False).start()

    def turn(self):
        @pl.when(self.c == 0)
        def _():
            self.inward().wait()
            self.outward().start()

    def finish(self):
        @pl.when(self.moves)
        def _():
            for chunk in range(self.source.shape[0]):
                self.first(chunk).wait_send()

        for chunk in range(self.source.shape[0]):
            for k in range(1, self.size):
                self.second(chunk, k, False).wait()

        @pl.when(self.c == 0)
        def _():
            self.outward().wait()


class ScatterFlip:
    def __init__(self, source, target, place, scratch):
        self.source, self.target = source, target
        self.f, self.c, self.t = place
        self.size = source.shape[0]
        self.here = False
        self.send, self.recv, self.on_send, self.on_recv, self.leg, self.got, self.out = scratch
        self.moves = self.c > 0

    def greetings(self):
        there = {"tp": flipped_place(self.c, self.t)}
        ring = [({"fsdp": (self.f + self.size - k) % self.size}, None, 1) for k in range(1, self.size)]
        return [(there, self.moves, (self.c + 3) // 4)] + ring

    def first(self, chunk, k):
        to = (self.f + k) % self.size
        return rcopy(
            self.source.at[to, chunk], self.got.at[k, chunk],
            self.send.at[k - 1, chunk], self.recv.at[k - 1, chunk], {"fsdp": to},
        )

    def own(self, chunk):
        return pltpu.make_async_copy(
            self.source.at[self.f, chunk], self.got.at[0, chunk], self.leg.at[chunk]
        )

    def second(self, chunk):
        there = {"tp": flipped_place(self.c, self.t)}
        return rcopy(self.out.at[chunk], self.target.at[chunk], self.on_send.at[chunk], self.on_recv.at[chunk], there)

    def stays(self, chunk):
        return pltpu.make_async_copy(self.out.at[chunk], self.target.at[chunk], self.on_send.at[chunk])

    def start(self):
        for chunk in range(self.target.shape[0]):
            for k in range(1, self.size):
                self.first(chunk, k).start()
            self.own(chunk).start()

    def hop(self, chunk):
        self.own(chunk).wait()
        total = self.got[0, chunk].astype(F32)
        for k in range(1, self.size):
            self.first(chunk, k).wait_recv()
            total += self.got[k, chunk].astype(F32)
        self.out[chunk] = total.astype(BF16)

        @pl.when(self.moves)
        def _():
            self.second(chunk).start()

        @pl.when(self.c == 0)
        def _():
            self.stays(chunk).start()

    def turn(self):
        pass

    def arrive(self):
        self.here = True
        for chunk in range(self.target.shape[0]):
            guarded(self.moves, self.second(chunk).wait_recv)
            guarded(self.c == 0, self.stays(chunk).wait)

    def finish(self):
        if not self.here:
            self.arrive()
        for chunk in range(self.target.shape[0]):
            for k in range(1, self.size):
                self.first(chunk, k).wait_send()
            guarded(self.moves, self.second(chunk).wait_send)


class CtxGather:
    def __init__(self, source, target, place, scratch):
        self.source, self.target = source, target
        self.c = place[1]
        self.send, self.recv, self.leg, self.stage = scratch

    def greetings(self):
        return [({"ctx": mate_of(self.c)}, None, 1), ({"ctx": across_of(self.c)}, None, 1)]

    def copy(self, number):
        c = self.c
        device = across_of(c) if number == 0 else mate_of(c)
        source = self.target.at[across_of(c)] if number == 2 else self.source
        slot = across_of(c) if number == 2 else c
        return rcopy(source, self.target.at[slot], self.send.at[number], self.recv.at[number], {"ctx": device})

    def inward(self):
        return pltpu.make_async_copy(self.source, self.stage, self.leg.at[0])

    def outward(self):
        return pltpu.make_async_copy(self.stage, self.target.at[self.c], self.leg.at[1])

    def start(self):
        self.copy(0).start()
        self.copy(1).start()
        self.inward().start()

    def turn(self):
        self.inward().wait()
        self.outward().start()
        self.copy(0).wait_recv()
        self.copy(2).start()

    def finish(self):
        self.copy(0).wait_send()
        self.copy(1).wait()
        self.copy(2).wait()
        self.outward().wait()


class CtxScatter:
    def __init__(self, pick, source, target, place, scratch):
        self.source, self.target, self.pick = source, target, pick
        self.c = place[1]
        self.send, self.recv, self.leg, self.stage, self.cross, self.far, self.total = scratch

    def greetings(self):
        return [({"ctx": mate_of(self.c)}, None, 1), ({"ctx": across_of(self.c)}, None, 1)]

    def copy(self, number):
        c = self.c
        device = across_of(c) if number == 2 else mate_of(c)
        source = (self.pick(self.source, 3 - c), self.pick(self.source, mate_of(c)), self.total)[number]
        target = (self.far, self.target.at[1], self.target.at[2])[number]
        return rcopy(source, target, self.send.at[number], self.recv.at[number], {"ctx": device})

    def inward(self):
        return pltpu.make_async_copy(self.pick(self.source, self.c), self.stage, self.leg.at[0])

    def outward(self):
        return pltpu.make_async_copy(self.stage, self.target.at[0], self.leg.at[1])

    def beside(self):
        return pltpu.make_async_copy(self.pick(self.source, across_of(self.c)), self.cross, self.leg.at[2])

    def start(self):
        self.copy(0).start()
        self.beside().start()
        self.copy(1).start()
        self.inward().start()

    def turn(self):
        self.copy(0).wait_recv()
        self.beside().wait()
        self.total[...] = (self.cross[...].astype(F32) + self.far[...].astype(F32)).astype(self.total.dtype)
        self.copy(2).start()
        self.inward().wait()
        self.outward().start()

    def finish(self):
        self.copy(0).wait_send()
        self.copy(1).wait()
        self.copy(2).wait()
        self.outward().wait()


class Riding:
    def __init__(self, riders, sources, targets, scratch, fetches, results, puts):
        self.fetches, self.results, self.puts = fetches, results, puts
        self.gone = [False] * len(puts)
        place = tuple(lax.axis_index(axis) for axis in ("fsdp", "ctx", "tp"))
        scratch = list(scratch)
        self.rides, self.hops, self.late, self.hopped = [], [], [], []
        self.firsts, self.seconds, self.begun, self.turned = [], [], [], []
        for rider, target in zip(riders, targets):
            own = [scratch.pop(0) for _ in rider.scratch]
            chained = isinstance(rider.array, int)
            ride = rider.make(targets[rider.array] if chained else sources.pop(0), target, place, own)
            self.rides.append(ride)
            if chained:
                self.firsts.append(self.rides[rider.array])
                self.seconds.append(ride)
                self.late.append(ride)
            if rider.late:
                self.late.append(ride)
            if rider.hopped:
                self.hopped.append(ride)
            self.hops += [(ride, chunk) for chunk in range(rider.chunks)]

    def ready(self):
        for fetch in self.fetches:
            fetch.wait()

    def put(self, *refs):
        for ref in refs:
            slot = [ref is result for result in self.results].index(True)
            self.gone[slot] = True
            self.puts[slot].start()

    def close(self):
        for slot, put in enumerate(self.puts):
            if not self.gone[slot]:
                put.start()
        for put in self.puts:
            put.wait()

    def greet(self, barrier):
        count = 0
        for ride in self.rides:
            for origin, when, weight in ride.greetings():
                guarded(when, functools.partial(signal, barrier, origin))
                count = count + weight
        return count

    def begin(self, ride):
        self.begun.append(ride)
        ride.start()

    def start(self):
        for ride in self.rides:
            if ride not in self.late:
                self.begin(ride)

    def start_late(self):
        for ride in self.late:
            if ride not in self.hopped + self.seconds:
                self.begin(ride)

    def one_hop(self, at):
        ride, chunk = self.hops[at]
        ride.hop(chunk)
        if at == len(self.hops) - 1:
            for ride in self.hopped:
                self.begin(ride)

    def turn(self):
        for ride in self.begun:
            if ride not in self.turned + self.seconds:
                self.turned.append(ride)
                ride.turn()

    def turn_when(self, when):
        if self.rides:
            pl.when(when)(self.turn)

    def chain(self):
        for first, second in zip(self.firsts, self.seconds):
            first.arrive()
            self.begin(second)

    def chain_turn(self):
        for second in self.seconds:
            self.turned.append(second)
            second.turn()

    def finish(self):
        for ride in self.rides:
            if ride not in self.turned:
                ride.turn()
        for ride in self.rides:
            ride.finish()


def guarded(when, action):
    if when is None:
        action()
    else:
        pl.when(when)(action)


def call(kernel, operands, out_shapes, scratch, collective_id, name, cost, riders=(), smem=()):
    n_in, n_out, n_scratch, n_ride = len(operands), len(out_shapes), len(scratch), len(riders)
    large = [i for i in range(n_in) if i not in smem]
    carried = [rider.array for rider in riders if not isinstance(rider.array, int)]

    def body(*refs):
        refs = list(refs)
        take = lambda n: [refs.pop(0) for _ in range(n)]
        ins, sources, outs, targets = take(n_in), take(len(carried)), take(n_out), take(n_ride)
        near_ins, near_outs, (in_sem, out_sem), own = take(len(large)), take(n_out), take(2), take(n_scratch)
        fetches = [
            pltpu.make_async_copy(ins[i], near, in_sem.at[slot]) for slot, (i, near) in enumerate(zip(large, near_ins))
        ]
        for fetch in fetches:
            fetch.start()
        for i, near in zip(large, near_ins):
            ins[i] = near
        puts = [pltpu.make_async_copy(near, far, out_sem.at[i]) for i, (near, far) in enumerate(zip(near_outs, outs))]
        ride = Riding(riders, sources, targets, refs, fetches, near_outs, puts)
        kernel(ride, *ins, *near_outs, *own)
        ride.close()

    params = dict(vmem_limit_bytes=60 * 1024 * 1024)
    if collective_id is not None:
        params.update(collective_id=collective_id, has_side_effects=True)
    extra = [item for rider in riders for item in rider.scratch]
    anywhere = pl.BlockSpec(memory_space=pl.ANY)
    near = [pltpu.VMEM(operands[i].shape, operands[i].dtype) for i in large]
    near += [pltpu.VMEM(out.shape, out.dtype) for out in out_shapes]
    results = pl.pallas_call(
        body,
        out_shape=list(out_shapes) + [rider.out for rider in riders],
        in_specs=[pl.BlockSpec(memory_space=pltpu.SMEM) if i in smem else anywhere for i in range(n_in)]
        + [anywhere] * len(carried),
        out_specs=[anywhere] * (n_out + n_ride),
        scratch_shapes=near + [dma(max(len(large), 1)), dma(max(n_out, 1))] + list(scratch) + extra,
        compiler_params=pltpu.CompilerParams(**params),
        cost_estimate=pl.CostEstimate(flops=cost[0], bytes_accessed=cost[1], transcendentals=cost[2]),
        name=name,
    )(*operands, *carried)
    return results[:n_out], results[n_out:]


def copies_rider(array, out, steps, stage, plan):
    def make(source, target, place, scratch):
        return Copies(*plan(source, target, *place), scratch)

    scratch = [dma(steps), dma(steps), dma(2), pltpu.VMEM(stage, array.dtype)]
    return Rider(array, out, make, scratch)


def flip_gather(own, size):
    own = own.reshape(2, own.shape[0] // 2, own.shape[1])
    scratch = [dma(2), dma(2), dma(size - 1, 2), dma(size - 1, 2), dma(2), pltpu.VMEM(own.shape, own.dtype)]
    return Rider(own, sds(size, *own.shape), FlipGather, scratch, chunks=2)


def scatter_flip(parts):
    size, n = parts.shape[0], parts.shape[1]
    shape = parts.shape[1:]
    scratch = [
        dma(size - 1, n), dma(size - 1, n), dma(n), dma(n), dma(n),
        pltpu.VMEM((size, *shape), BF16), pltpu.VMEM(shape, BF16),
    ]
    return Rider(parts, sds(*shape), ScatterFlip, scratch, chunks=n)


def fsdp_gather(own, size):
    def make(source, target, f, c, t):
        steps = [
            ({"fsdp": (f + k) % size}, {"fsdp": (f + size - k) % size}, source, target.at[f], None, 1)
            for k in range(1, size)
        ]
        return steps, (source, target.at[f], None)

    return copies_rider(own, sds(size, *own.shape, dtype=own.dtype), size - 1, own.shape, make)


def fsdp_scatter(parts, size):
    out = sds(size, parts.shape[0], *parts.shape[2:], dtype=parts.dtype)

    def make(source, target, f, c, t):
        steps = [
            (
                {"fsdp": (f + k) % size}, {"fsdp": (f + size - k) % size},
                source.at[:, (f + k) % size], target.at[k], None, 1,
            )
            for k in range(1, size)
        ]
        return steps, (source.at[:, f], target.at[0], None)

    return copies_rider(parts, out, size - 1, out.shape[1:], make)


def ctx_gather(own, first=None):
    scratch = [dma(3), dma(3), dma(2), pltpu.VMEM(own.shape, own.dtype)]
    array = own if first is None else first
    return Rider(array, sds(4, *own.shape, dtype=own.dtype), CtxGather, scratch)


def ctx_scatter(parts, axis=0, first=None):
    shape = parts.shape[:axis] + parts.shape[axis + 1 :]

    def pick(ref, slot):
        return ref.at[slot] if axis == 0 else ref.at[:, :, slot]

    buffer = pltpu.VMEM(shape, parts.dtype)
    scratch = [dma(3), dma(3), dma(3), buffer, buffer, buffer, buffer]
    array = parts if first is None else first
    return Rider(array, sds(3, *shape, dtype=parts.dtype), functools.partial(CtxScatter, pick), scratch)


def flipped_place(c, t):
    return 2 * ((t // 2 + c % 2) % 2) + (t % 2 + c // 2) % 2


def tp_flip(own):
    def make(source, target, f, c, t):
        other = {"tp": flipped_place(c, t)}
        return [(other, other, source, target, c > 0, (c + 3) // 4)], (source, target, c == 0)

    return copies_rider(own, sds(*own.shape, dtype=own.dtype), 1, own.shape, make)


def plane(size):
    return [(kt, kf) for kt in (2, 3, 1, 0) for kf in range(size) if kt + kf > 0]


def plane_gather(own, size):
    def make(source, target, f, c, t):
        steps = [
            (
                {"fsdp": (f + kf) % size, "tp": (t + kt) % 4},
                {"fsdp": (f + size - kf) % size, "tp": (t + 4 - kt) % 4},
                source, target.at[t, f], None, 1,
            )
            for kt, kf in plane(size)
        ]
        return steps, (source, target.at[t, f], None)

    return copies_rider(own, sds(4, size, *own.shape, dtype=own.dtype), 4 * size - 1, own.shape, make)


def plane_scatter(parts, size):
    def make(source, target, f, c, t):
        steps = [
            (
                {"fsdp": (f + kf) % size, "tp": (t + kt) % 4},
                {"fsdp": (f + size - kf) % size, "tp": (t + 4 - kt) % 4},
                source.at[(t + kt) % 4, (f + kf) % size], target.at[kt, kf], None, 1,
            )
            for kt, kf in plane(size)
        ]
        return steps, (source.at[t, f], target.at[0, 0], None)

    return copies_rider(parts, sds(*parts.shape, dtype=parts.dtype), 4 * size - 1, parts.shape[2:], make)


class SmallSum:
    def __init__(self, source, target, place, scratch):
        self.source, self.target = source, target
        self.f, self.c, self.t = place
        self.size = target.shape[1]
        self.send, self.recv, self.on_send, self.on_recv, self.leg, self.terms, self.total = scratch

    def greetings(self):
        around = [({"ctx": (self.c + 4 - k) % 4}, None, 1) for k in (1, 2, 3)]
        return around + [
            ({"fsdp": (self.f + self.size - kf) % self.size, "tp": (self.t + 4 - kt) % 4}, None, 1)
            for kt, kf in plane(self.size)
        ]

    def first(self, k):
        device = {"ctx": (self.c + k) % 4}
        return rcopy(self.source, self.terms.at[self.c], self.send.at[k - 1], self.recv.at[k - 1], device)

    def own(self):
        return pltpu.make_async_copy(self.source, self.terms.at[self.c], self.leg.at[0])

    def second(self, number):
        kt, kf = plane(self.size)[number]
        device = {"fsdp": (self.f + kf) % self.size, "tp": (self.t + kt) % 4}
        target = self.target.at[self.t, self.f]
        return rcopy(self.total, target, self.on_send.at[number], self.on_recv.at[number], device)

    def stays(self):
        return pltpu.make_async_copy(self.total, self.target.at[self.t, self.f], self.leg.at[1])

    def start(self):
        for k in (2, 3, 1):
            self.first(k).start()
        self.own().start()

    def turn(self):
        self.own().wait()
        for k in (1, 2, 3):
            self.first(k).wait_recv()
        self.total[...] = self.terms[0] + self.terms[1] + self.terms[2] + self.terms[3]
        for number in range(4 * self.size - 1):
            self.second(number).start()
        self.stays().start()

    def finish(self):
        for k in (1, 2, 3):
            self.first(k).wait_send()
        for number in range(4 * self.size - 1):
            self.second(number).wait()
        self.stays().wait()


def small_sum(own, size):
    many = 4 * size - 1
    scratch = [
        dma(3), dma(3), dma(many), dma(many), dma(2),
        pltpu.VMEM((4, *own.shape), own.dtype), pltpu.VMEM(own.shape, own.dtype),
    ]
    return Rider(own, sds(4, size, *own.shape, dtype=own.dtype), SmallSum, scratch)


def carry_kernel(ride):
    barrier = pltpu.get_barrier_semaphore()
    pl.semaphore_wait(barrier, ride.greet(barrier))
    ride.start()
    ride.finish()


def carry(riders, cid):
    return call(carry_kernel, (), (), (), cid, "carry", (1 << 20, 1 << 20, 0), riders)[1]


def sds(*shape, dtype=BF16):
    return jax.ShapeDtypeStruct(shape, dtype)


FAR = 1e30


def inner_kernel(
    fetch, ride, flag_ref, x_ref, w_ref, b_ref, xg_ref, qw_ref, kv_ref, o_ref, lse_ref, *rest
):
    if fetch:
        full_ref, w_send, w_recv, *rest = rest
    (
        qbuf, qm_ref, m_ref, acc_ref, vt_ref, x_recv, x_right, x_left,
        k1_send, k1_recv, k2_send, k2_recv, kf_send, kf_recv, q_send, q_recv,
    ) = rest
    c = lax.axis_index("ctx")
    t = lax.axis_index("tp")
    f, size = lax.axis_index("fsdp"), lax.axis_size("fsdp")
    barrier = pltpu.get_barrier_semaphore()
    for device in (mate_of(c), across_of(c), 3 - c):
        signal(barrier, {"ctx": device})

    @pl.when(t > 0)
    def _():
        signal(barrier, {"tp": t - 1})

    @pl.when(t < 3)
    def _():
        signal(barrier, {"tp": t + 1})

    if fetch:
        for k in range(1, size):
            signal(barrier, {"fsdp": (f + size - k) % size})
    ends = (t // 3) + (3 - t) // 3
    count = 5 - ends + ride.greet(barrier) + (size - 1 if fetch else 0)
    m_ref[...] = jnp.full_like(m_ref, MASKED)
    acc_ref[...] = jnp.zeros_like(acc_ref)
    vt_ref[:, :, :, 128:144] = jnp.ones((4, 4, 2, 16, 256), BF16)
    ride.ready()
    pl.semaphore_wait(barrier, count)

    def right(src, chunk, step):
        return rcopy(src, xg_ref.at[chunk], x_right.at[step], x_recv.at[chunk], {"tp": t + 1})

    def left(src, chunk, step):
        return rcopy(src, xg_ref.at[chunk], x_left.at[step], x_recv.at[chunk], {"tp": t - 1})

    def arrived(chunk):
        rcopy(xg_ref.at[chunk], xg_ref.at[chunk], x_right.at[0], x_recv.at[chunk], {"tp": t}).wait_recv()

    @pl.when(t < 3)
    def _():
        right(x_ref, t, 0).start()

    @pl.when(t > 0)
    def _():
        left(x_ref, t, 0).start()

    def weight(k):
        device = {"fsdp": (f + k) % size}
        return rcopy(w_ref, full_ref.at[f], w_send.at[k - 1], w_recv.at[k - 1], device)

    if fetch:
        for k in range(1, size):
            weight(k).start()
        full_ref[f] = w_ref[...]
    xg_ref[t] = x_ref[...]
    ride.start()
    if fetch:
        for k in range(1, size):
            weight(k).wait_recv()

    def mate(chunk):
        part = kv_ref.at[c, chunk]
        return rcopy(part, part, k1_send.at[chunk], k1_recv.at[chunk], {"ctx": mate_of(c)})

    def across(chunk):
        part = kv_ref.at[c, chunk]
        return rcopy(part, part, k2_send.at[chunk], k2_recv.at[chunk], {"ctx": across_of(c)})

    def onward(chunk):
        part = kv_ref.at[across_of(c), chunk]
        return rcopy(part, part, kf_send.at[chunk], kf_recv.at[chunk], {"ctx": mate_of(c)})

    def partner(slot):
        return rcopy(qbuf.at[slot], qw_ref.at[2 * slot + 1], q_send.at[slot], q_recv.at[slot], {"ctx": 3 - c})

    def project(step):
        chunk = ordered(t, step)
        w = full_ref[...].reshape(768, 640) if fetch else w_ref[...]
        made = mm(xg_ref[chunk], w) + b_ref[...]
        kv_ref[c, chunk] = made[:, 256:].astype(BF16)
        across(chunk).start()
        mate(chunk).start()
        query = (made[:, :256] * 0.125).astype(BF16)

        @pl.when(chunk % 2 == 0)
        def _():
            qw_ref[chunk] = query

        @pl.when(chunk % 2 == 1)
        def _():
            qbuf[chunk // 2] = query
            partner(chunk // 2).start()

    low = lax.broadcasted_iota(jnp.int32, (256, 128), 1) < 64

    def complete(step):
        chunk = ordered(t, step)
        across(chunk).wait_recv()
        onward(chunk).start()
        mate(chunk).wait_recv()

        @pl.when(chunk % 2 == 1)
        def _():
            partner(chunk // 2).wait_recv()

        pair = qw_ref[chunk, :, 0:128]
        none = jnp.zeros_like(pair)
        qm_ref[0, chunk] = jnp.where(low, pair, none)
        qm_ref[1, chunk] = jnp.where(low, none, pair)
        qm_ref[2, chunk] = qw_ref[chunk, :, 128:256]
        onward(chunk).wait_recv()
        for segment in range(4):
            vt_ref[segment, chunk, 0, 0:128] = jnp.transpose(kv_ref[segment, chunk, :, 256:384], (1, 0))
            vt_ref[segment, chunk, 1, 0:128] = jnp.transpose(kv_ref[segment, chunk, :, 128:256], (1, 0))

    def items(step):
        @pl.loop(step * step, (step + 1) * (step + 1))
        def _(item):
            number = item - step * step
            second = number // (step + 1)
            query_at = ordered_by(t, step + second * (number - 2 * step - 1))
            key_at = ordered_by(t, number + second * (step - number))
            half = query_at % 2

            def visit(segments):
                seen = [flag_ref[half, segment] > 0 for segment in segments]
                far = [jnp.where(one, 0.0, FAR) for one in seen]
                scores, most, made = [], [], []
                for head in range(3):
                    query, at = qm_ref[head, query_at], 128 * (head // 2)
                    rows = [mm_nt(kv_ref[segment, key_at, :, at : at + 128], query) for segment in segments]
                    new = m_ref[query_at, head : head + 1]
                    for one, row in zip(seen, rows):
                        new = jnp.maximum(new, jnp.where(one, jnp.max(row, axis=0, keepdims=True), MASKED))
                    scores.append(rows)
                    most.append(new)
                for head in range(3):
                    total = acc_ref[query_at, head] * jnp.exp(m_ref[query_at, head : head + 1] - most[head])
                    for segment, row, off in zip(segments, scores[head], far):
                        probs = jnp.exp(row - (most[head] + off)).astype(BF16)
                        total += mm(vt_ref[segment, key_at, head // 2], probs)
                    made.append(total)
                for head in range(3):
                    m_ref[query_at, head : head + 1] = most[head]
                    acc_ref[query_at, head] = made[head]

            length = c + 1 + half * (3 - 2 * c)

            @pl.loop(0, length // 2)
            def _(two):
                visit((2 * two, 2 * two + 1))

            @pl.when(length % 2 == 1)
            def _():
                visit((length - 1,))

            if step == 3:
                for n in range(1, len(ride.hops)):
                    pl.when(item == 9 + 2 * n)(functools.partial(ride.one_hop, n))

    project(0)
    for step in range(1, 4):

        @pl.when(t - step >= 0)
        def _():
            arrived(t - step)

            @pl.when(t < 3)
            def _():
                right(xg_ref.at[t - step], t - step, step).start()

        @pl.when(t + step <= 3)
        def _():
            arrived(t + step)

            @pl.when(t > 0)
            def _():
                left(xg_ref.at[t + step], t + step, step).start()

        project(step)
        if step == 2:
            ride.turn()
        if step == 3:
            ride.start_late()
            ride.chain()
            ride.put(xg_ref)
        complete(step - 1)
        items(step - 1)
    complete(3)
    if ride.hops:
        ride.one_hop(0)
    ride.turn()
    ride.chain_turn()
    ride.put(qw_ref, kv_ref)
    items(3)
    for quarter in range(4):
        whole = [acc_ref[quarter, head, 128:129] for head in range(3)]
        parts = [acc_ref[quarter, head, 0:128] / whole[head] for head in range(3)]
        pair = jnp.concatenate([parts[0][0:64], parts[1][64:128]], axis=0)
        o_ref[quarter, :, 0:128] = jnp.transpose(pair, (1, 0)).astype(BF16)
        o_ref[quarter, :, 128:192] = jnp.transpose(parts[2], (1, 0))[:, :64].astype(BF16)
        for head in range(3):
            lse_ref[quarter, head : head + 1] = m_ref[quarter, head : head + 1] + jnp.log(whole[head])
        lse_ref[quarter, 3:8] = jnp.zeros((5, 256), F32)
    ride.put(o_ref, lse_ref)
    for chunk in range(4):
        mate(chunk).wait_send()
        across(chunk).wait_send()
        onward(chunk).wait_send()
    for slot in range(2):
        partner(slot).wait_send()

    @pl.when(t < 3)
    def _():
        right(x_ref, t, 0).wait_send()

    @pl.when(t > 0)
    def _():
        left(x_ref, t, 0).wait_send()

    for step in (1, 2):

        @pl.when((t - step >= 0) & (t < 3))
        def _():
            right(xg_ref.at[t - step], t - step, step).wait_send()

        @pl.when((t + step <= 3) & (t > 0))
        def _():
            left(xg_ref.at[t + step], t + step, step).wait_send()

    if fetch:
        for k in range(1, size):
            weight(k).wait_send()
    ride.finish()


def inner(x, w, b, flags, cid, riders=(), fetch=False):
    outs = [
        sds(4, 256, 768), sds(4, 256, 256), sds(4, 4, 256, 384), sds(4, 256, 192), sds(4, 8, 256, dtype=F32),
    ]
    scratch = [
        pltpu.VMEM((2, 256, 256), BF16),
        pltpu.VMEM((3, 4, 256, 128), BF16), pltpu.VMEM((4, 8, 256), F32), pltpu.VMEM((4, 3, 144, 256), F32),
        pltpu.VMEM((4, 4, 2, 144, 256), BF16),
        dma(4), dma(3), dma(3),
        dma(4), dma(4), dma(4), dma(4), dma(4), dma(4), dma(2), dma(2),
    ]
    if fetch:
        size = lax.axis_size("fsdp")
        outs.append(sds(size, *w.shape))
        scratch = [dma(size - 1), dma(size - 1)] + scratch
    cost = (2 * 1024 * 768 * 640 + 5 * 512 * 1024 * 64 * 12, 14 << 20, 5 * 512 * 1024 * 3)
    kernel = functools.partial(inner_kernel, fetch)
    res, ridden = call(kernel, (flags, x, w, b), outs, scratch, cid, "inner", cost, riders, smem=(0,))
    full = res[5].reshape(768, 640) if fetch else w
    xg, qw, kv, o, lse = res[:5]
    return (
        xg.reshape(1024, 768), qw.reshape(1024, 256), kv.reshape(4, 1024, 384),
        o.reshape(1024, 192), lse, full, ridden,
    )


def norm_stats(summed):
    row_mean = jnp.mean(summed, axis=-1, keepdims=True)
    centered = summed - row_mean
    variance = jnp.mean(centered * centered, axis=-1, keepdims=True)
    scale = lax.rsqrt(variance + EPSILON)
    return centered * scale, scale


def norm_back(grad, xhat, scale, gain):
    scaled = grad * gain
    first = jnp.mean(scaled, axis=-1, keepdims=True)
    second = jnp.mean(scaled * xhat, axis=-1, keepdims=True)
    return scale * (scaled - first - xhat * second)


def gelu_both(up):
    phi = 0.5 * (1.0 + lax.erf(up * 0.7071067811865476))
    slope = phi + up * jnp.exp(-0.5 * up * up) * 0.3989422804014327
    return (up * phi).astype(BF16), slope.astype(BF16)


PIECE = 128


def exchange(c, ref, feed, mine_ref, part_ref, send_ref, got_ref, a_send, a_recv, s_send, s_recv, meanwhile):
    mate, across, far = mate_of(c), across_of(c), 3 - c
    pieces = (pl.ds(0, PIECE), pl.ds(PIECE, PIECE))

    def gather(slot, index, p, device):
        part = ref.at[slot, pieces[p]]
        return rcopy(part, part, a_send.at[index, p], a_recv.at[index, p], {"ctx": device})

    def scatter(index, p, device):
        source, target = send_ref.at[index, pieces[p]], got_ref.at[index, pieces[p]]
        return rcopy(source, target, s_send.at[index, p], s_recv.at[index, p], {"ctx": device})

    for p in range(2):
        gather(c, 1, p, across).start()
    for p in range(2):
        gather(c, 0, p, mate).start()
    mine_ref[...] += feed(c, pl.ds(0, 2 * PIECE))
    for p in range(2):
        gather(mate, 0, p, mate).wait_recv()
    send_ref[0] = feed(mate, pl.ds(0, 2 * PIECE)).astype(BF16)
    for p in range(2):
        scatter(0, p, mate).start()

    def take_across(p):
        gather(across, 1, p, across).wait_recv()
        gather(across, 2, p, mate).start()
        part_ref[pieces[p]] = feed(across, pieces[p])

    def take_far(p):
        gather(far, 2, p, mate).wait_recv()
        send_ref[1, pieces[p]] = feed(far, pieces[p]).astype(BF16)
        scatter(1, p, mate).start()

    def join(p):
        scatter(1, p, mate).wait_recv()
        send_ref[2, pieces[p]] = (part_ref[pieces[p]] + got_ref[1, pieces[p]].astype(F32)).astype(BF16)
        scatter(2, p, across).start()

    take_across(0)
    take_far(0)
    take_across(1)
    join(0)
    take_far(1)
    join(1)
    meanwhile()
    for p in range(2):
        scatter(0, p, mate).wait_recv()
        scatter(2, p, across).wait_recv()

    def settle():
        for p in range(2):
            for index in range(3):
                gather(c, index, p, mate).wait_send()
                scatter(index, p, mate).wait_send()

    return mine_ref[...] + got_ref[0].astype(F32) + got_ref[2].astype(F32), settle


def block_kernel(
    ride, o_ref, wo_ref, w1_ref, w2_ref, b1_ref, vec_ref, stream_ref,
    out_ref, low_ref, xhat1_ref, r1_ref, xhat2_ref, r2_ref, xg_ref, act_ref, slope_ref, rows_ref, down_ref,
    w_send, w_recv, mine_ref, part_ref, send_ref, got_ref, o_send, o_recv, a_send, a_recv, s_send, s_recv,
):
    c = lax.axis_index("ctx")
    t = lax.axis_index("tp")
    barrier = pltpu.get_barrier_semaphore()
    for place in range(4):

        @pl.when((t % 2 == 0) & (t != place))
        def _():
            signal(barrier, {"tp": place})

        @pl.when(t % 2 == 1)
        def _():
            signal(barrier, {"ctx": 3 - c, "tp": place})

    signal(barrier, {"ctx": mate_of(c)})
    signal(barrier, {"ctx": across_of(c)})
    f, size = lax.axis_index("fsdp"), lax.axis_size("fsdp")
    for k in range(1, size):
        signal(barrier, {"fsdp": (f + size - k) % size})
    count = 5 + t % 2 + size - 1 + ride.greet(barrier)
    ride.ready()
    pl.semaphore_wait(barrier, count)

    def weight(k):
        device = {"fsdp": (f + k) % size}
        return rcopy(w2_ref, down_ref.at[f], w_send.at[k - 1], w_recv.at[k - 1], device)

    def give(quarter):
        device = {"tp": quarter} if quarter % 2 == 0 else {"ctx": 3 - c, "tp": quarter}
        return rcopy(o_ref.at[quarter], rows_ref.at[t], o_send.at[quarter], o_recv.at[t], device)

    def given(group):
        rcopy(rows_ref.at[group], rows_ref.at[group], o_send.at[0], o_recv.at[group], {"tp": t}).wait_recv()

    for quarter in (3, 2, 1, 0):
        if quarter % 2 == 0:

            @pl.when(t != quarter)
            def _():
                give(quarter).start()

            @pl.when(t == quarter)
            def _():
                rows_ref[quarter] = o_ref[quarter]

        else:
            give(quarter).start()
    for k in range(1, size):
        weight(k).start()
    down_ref[f] = w2_ref[...]
    branch = stream_ref[...] + vec_ref[0:1]
    for group in range(4):

        @pl.when((t % 2 == 1) | (t != group))
        def _():
            given(group)

        branch += mm_nt(rows_ref[group], wo_ref[group])
    ride.start()
    xhat, scale = norm_stats(branch)
    xhat1_ref[...] = xhat
    r1_ref[...] = jnp.broadcast_to(scale, r1_ref.shape)
    normed = xhat * vec_ref[2:3] + vec_ref[3:4]
    xg_ref[c] = normed.astype(BF16)
    mine_ref[...] = normed + vec_ref[1:2]
    for k in range(1, size):
        weight(k).wait_recv()

    def feed(segment, rows):
        up = mm(xg_ref[segment, rows], w1_ref[...]) + b1_ref[...]
        act, slope = gelu_both(up)
        act_ref[segment, rows] = act
        slope_ref[segment, rows] = slope
        return mm_nt(act, down_ref[...].reshape(768, 768))

    def meanwhile():
        ride.turn()
        ride.put(xhat1_ref, r1_ref, xg_ref, act_ref, slope_ref, rows_ref, down_ref)

    summed, settle = exchange(
        c, xg_ref, feed, mine_ref, part_ref, send_ref, got_ref, a_send, a_recv, s_send, s_recv, meanwhile
    )
    xhat, scale = norm_stats(summed)
    xhat2_ref[...] = xhat
    r2_ref[...] = jnp.broadcast_to(scale, r2_ref.shape)
    out = xhat * vec_ref[4:5] + vec_ref[5:6]
    out_ref[...] = out
    low_ref[...] = out.astype(BF16)
    ride.put(out_ref, low_ref, xhat2_ref, r2_ref)
    for quarter in range(4):
        if quarter % 2 == 0:

            @pl.when(t != quarter)
            def _():
                give(quarter).wait_send()

        else:
            give(quarter).wait_send()
    for k in range(1, size):
        weight(k).wait_send()
    settle()
    ride.finish()


def block(o, wo, w1, w2, b1, vecs, stream, cid, riders=()):
    size = lax.axis_size("fsdp")
    f = functools.partial(sds, dtype=F32)
    outs = [
        f(256, 768), sds(256, 768), f(256, 768), f(256, 128), f(256, 768), f(256, 128),
        sds(4, 256, 768), sds(4, 256, 768), sds(4, 256, 768), sds(4, 256, 192), sds(size, *w2.shape),
    ]
    scratch = [
        dma(size - 1), dma(size - 1),
        pltpu.VMEM((256, 768), F32),
        pltpu.VMEM((256, 768), F32),
        pltpu.VMEM((3, 256, 768), BF16),
        pltpu.VMEM((3, 256, 768), BF16),
        dma(4), dma(4), dma(3, 2), dma(3, 2), dma(3, 2), dma(3, 2),
    ]
    cost = (2 * 256 * 768 * 768 + 4 * 1024 * 768 * 768, 16 << 20, 1 << 20)
    operands = (o.reshape(4, 256, 192), wo, w1, w2, b1, vecs, stream)
    res, ridden = call(block_kernel, operands, outs, scratch, cid, "block", cost, riders)
    flat = lambda a: a.reshape(1024, 768)
    return tuple(res[:6]) + (flat(res[6]), flat(res[7]), flat(res[8]), res[9], res[10].reshape(768, 768), ridden)


def block_back_kernel(
    ride, grad_ref, xhat2_ref, r2_ref, xhat1_ref, r1_ref, vec_ref, slope_ref, w1_ref, w2_ref, wo_ref,
    xg_ref, act_ref, rows_ref, back_ref, do_ref, stat_ref, dup_ref, ddown_ref, dout_ref,
    w_send, w_recv, term_ref, all_up_ref, gg_ref, gu_ref, mine_ref, part_ref, send_ref, got_ref, dsend_ref, d_send, d_recv, a_send, a_recv, s_send, s_recv,
):
    c = lax.axis_index("ctx")
    t = lax.axis_index("tp")
    barrier = pltpu.get_barrier_semaphore()
    for place in range(4):
        if place % 2 == 0:

            @pl.when(t != place)
            def _():
                signal(barrier, {"tp": place})

        else:
            signal(barrier, {"ctx": 3 - c, "tp": place})
    signal(barrier, {"ctx": mate_of(c)})
    signal(barrier, {"ctx": across_of(c)})
    f, size = lax.axis_index("fsdp"), lax.axis_size("fsdp")
    depth = dup_ref.shape[0]
    for k in range(1, size):
        signal(barrier, {"fsdp": (f + size - k) % size})
    count = 5 + t % 2 + size - 1 + ride.greet(barrier)
    ride.ready()
    pl.semaphore_wait(barrier, count)

    def row(values):
        return jnp.sum(values, axis=0, keepdims=True)

    grad = grad_ref[...]
    back_two = norm_back(grad, xhat2_ref[...], r2_ref[:, 0:1], vec_ref[4:5])
    g2 = back_two.astype(BF16)
    gg_ref[c] = g2
    mine_ref[...] = back_two
    ride.start()
    stat_ref[1:2] = row(grad * xhat2_ref[...])
    stat_ref[3:4] = row(grad)
    stat_ref[5:6] = row(g2.astype(F32))
    stat_ref[6:8] = jnp.zeros((2, 768), F32)

    def feed(segment, rows):
        gu = (mm(gg_ref[segment, rows], w2_ref[...]) * slope_ref[segment, rows].astype(F32)).astype(BF16)
        gu_ref[segment, rows] = gu
        stat_ref[6:7] += row(gu.astype(F32))
        return mm_nt(gu, w1_ref[...])

    tall = lambda ref: ref[...].reshape(1024, 768)

    def slice_of(place):
        return pl.ds(pl.multiple_of(place * depth, depth), depth)

    def term(k):
        to = (f + k) % size
        return rcopy(
            all_up_ref.at[slice_of(to)], term_ref.at[k - 1], w_send.at[k - 1], w_recv.at[k - 1], {"fsdp": to}
        )

    def meanwhile():
        @pl.loop(0, 3)
        def _(tile):
            cols = pl.ds(pl.multiple_of(tile * 256, 256), 256)
            all_up_ref[cols] = mm_tn(xg_ref[:, cols], tall(gu_ref)).astype(BF16)

        for k in range(1, size):
            term(k).start()

        @pl.loop(0, 3)
        def _(tile):
            cols = pl.ds(pl.multiple_of(tile * 256, 256), 256)
            ddown_ref[cols] = mm_tn(gg_ref[:, :, cols].reshape(1024, 256), act_ref[...]).astype(BF16)

        ride.put(ddown_ref)
        ride.turn()

    grad_normed, settle = exchange(
        c, gg_ref, feed, mine_ref, part_ref, send_ref, got_ref, a_send, a_recv, s_send, s_recv, meanwhile
    )
    back_one = norm_back(grad_normed, xhat1_ref[...], r1_ref[:, 0:1], vec_ref[2:3])
    back_ref[...] = back_one
    g1 = back_one.astype(BF16)

    def give_near(group):
        return rcopy(dsend_ref.at[group], do_ref.at[t], d_send.at[group], d_recv.at[t], {"tp": group})

    def give_far(group):
        return rcopy(dsend_ref.at[group], do_ref.at[t], d_send.at[group], d_recv.at[t], {"ctx": 3 - c, "tp": group})

    for group in range(4):
        dsend_ref[group] = mm(g1, wo_ref[group]).astype(BF16)

        @pl.when((t % 2 == 0) & (t == group))
        def _():
            do_ref[t] = dsend_ref[group]

        @pl.when((t % 2 == 0) & (t != group))
        def _():
            give_near(group).start()

        @pl.when(t % 2 == 1)
        def _():
            give_far(group).start()

    stat_ref[0:1] = row(grad_normed * xhat1_ref[...])
    stat_ref[2:3] = row(grad_normed)
    stat_ref[4:5] = row(g1.astype(F32))
    for group in range(4):
        dout_ref[group] = mm_tn(g1, rows_ref[group]).astype(BF16)
    ride.put(back_ref, stat_ref, dout_ref)
    total = all_up_ref[slice_of(f)].astype(F32)
    for k in range(1, size):
        term(k).wait_recv()
        total += term_ref[k - 1].astype(F32)
    dup_ref[...] = total.astype(BF16)
    ride.put(dup_ref)
    for quarter in range(4):

        def taken():
            rcopy(do_ref.at[quarter], do_ref.at[quarter], d_send.at[0], d_recv.at[quarter], {"tp": t}).wait_recv()

        if quarter % 2 == 0:
            pl.when(t != quarter)(taken)
        else:
            taken()
    for group in range(4):

        @pl.when((t % 2 == 1) | (t != group))
        def _():
            give_near(group).wait_send()

    for k in range(1, size):
        term(k).wait_send()
    settle()
    ride.finish()


def block_back(grad, xhat2, r2, xhat1, r1, vecs, slope, w1, w2, wo, xg, act, rows, cid, riders=()):
    f = functools.partial(sds, dtype=F32)
    size = lax.axis_size("fsdp")
    depth = 768 // size
    outs = [
        f(256, 768), sds(4, 256, 192), f(8, 768), sds(depth, 768), sds(768, 768), sds(4, 768, 192),
    ]
    scratch = [
        dma(size - 1), dma(size - 1), pltpu.VMEM((size - 1, depth, 768), BF16), pltpu.VMEM((768, 768), BF16),
        pltpu.VMEM((4, 256, 768), BF16),
        pltpu.VMEM((4, 256, 768), BF16),
        pltpu.VMEM((256, 768), F32),
        pltpu.VMEM((256, 768), F32),
        pltpu.VMEM((3, 256, 768), BF16),
        pltpu.VMEM((3, 256, 768), BF16),
        pltpu.VMEM((4, 256, 192), BF16),
        dma(4), dma(4), dma(3, 2), dma(3, 2), dma(3, 2), dma(3, 2),
    ]
    cost = (4 * 256 * 768 * 768 + 8 * 1024 * 768 * 768, 20 << 20, 1 << 10)
    operands = (grad, xhat2, r2, xhat1, r1, vecs, slope.reshape(4, 256, 768), w1, w2, wo, xg, act, rows)
    res, ridden = call(block_back_kernel, operands, outs, scratch, cid, "block_back", cost, riders)
    back, do, stats, d_up, d_down, d_out = res
    return back, do.reshape(1024, 192), stats, d_up, d_down, d_out, ridden


def inner_back_kernel(
    ride, flag_ref, qw_ref, kv_ref, do_ref, o_ref, lse_ref, w_ref, back_ref, xg_ref, mark_ref,
    grad_ref, low_ref, din_ref, sum_out_ref, mem_ref,
    qm_ref, dm_ref, row_ref, acc_ref, wide_ref, dkv_ref, dqs_ref,
    w_send, w_recv, term_ref, all_in_ref, dq_ref, own_ref, part_ref,
    near_ref, join_ref, sum_ref, far_ref, pass_ref, take_ref,
    q_send, q_recv, n_send, n_recv, j_send, j_recv, f_send, f_recv, p_send, p_recv,
):
    c = lax.axis_index("ctx")
    t = lax.axis_index("tp")
    f, size = lax.axis_index("fsdp"), lax.axis_size("fsdp")
    depth = din_ref.shape[0]
    mate, across, far = mate_of(c), across_of(c), 3 - c
    barrier = pltpu.get_barrier_semaphore()
    for device in (mate, across, far):
        signal(barrier, {"ctx": device})

    @pl.when(t > 0)
    def _():
        signal(barrier, {"tp": t - 1})

    @pl.when(t < 3)
    def _():
        signal(barrier, {"tp": t + 1})

    for k in range(1, size):
        signal(barrier, {"fsdp": (f + size - k) % size})
    ends = (t // 3) + (3 - t) // 3
    count = 5 - ends + size - 1 + ride.greet(barrier)
    ride.ready()

    low = lax.broadcasted_iota(jnp.int32, (1024, 128), 1) < 64
    pair = qw_ref[:, 0:128]
    none = jnp.zeros_like(pair)
    qm_ref[0] = jnp.where(low, pair, none)
    qm_ref[1] = jnp.where(low, none, pair)
    qm_ref[2] = qw_ref[:, 128:256]
    pair = do_ref[:, 0:128]
    dm_ref[0] = jnp.where(low, pair, none)
    dm_ref[1] = jnp.where(low, none, pair)
    dm_ref[2] = jnp.concatenate([do_ref[:, 128:192], none[:, :64]], axis=1)
    product = do_ref[...].astype(F32) * o_ref[...].astype(F32)
    head_row = lax.broadcasted_iota(jnp.int32, (8, 192), 0)
    head_of = lax.broadcasted_iota(jnp.int32, (8, 192), 1) // 64
    delta = lax.dot_general(
        (head_row == head_of).astype(F32), product, (((1,), (1,)), ((), ())),
        precision=lax.Precision.HIGHEST, preferred_element_type=F32,
    )
    for quarter in range(4):
        row_ref[quarter, 0:8] = lse_ref[quarter]
        row_ref[quarter, 8:16] = delta[:, quarter * 256 : (quarter + 1) * 256]
    acc_ref[...] = jnp.zeros_like(acc_ref)
    wide_ref[...] = jnp.zeros_like(wide_ref)
    pl.semaphore_wait(barrier, count)
    ride.start()

    def partner(slot):
        return rcopy(dqs_ref.at[slot], dq_ref.at[2 * slot + 1], q_send.at[slot], q_recv.at[slot], {"ctx": far})

    def near(chunk):
        return rcopy(dkv_ref.at[mate, chunk], near_ref.at[chunk], n_send.at[chunk], n_recv.at[chunk], {"ctx": mate})

    def join(chunk):
        return rcopy(dkv_ref.at[far, chunk], join_ref.at[chunk], j_send.at[chunk], j_recv.at[chunk], {"ctx": mate})

    def cross(chunk):
        return rcopy(sum_ref.at[chunk], far_ref.at[chunk], f_send.at[chunk], f_recv.at[chunk], {"ctx": across})

    def lower(chunk):
        return rcopy(pass_ref.at[chunk], take_ref.at[0, chunk], p_send.at[chunk], p_recv.at[0, chunk], {"tp": t - 1})

    def upper(chunk):
        return rcopy(pass_ref.at[chunk], take_ref.at[1, chunk], p_send.at[chunk], p_recv.at[1, chunk], {"tp": t + 1})

    def passed(side, chunk):
        rcopy(
            take_ref.at[side, chunk], take_ref.at[side, chunk], p_send.at[0], p_recv.at[side, chunk], {"tp": t}
        ).wait_recv()

    chunks = [ordered(t, 3 - k) for k in range(4)]
    at_end = (t == 0) | (t == 3)

    def leave(k):
        chunk = chunks[k]
        dkv_ref[:, chunk] = wide_ref[:, chunk].astype(BF16)
        join(chunk).start()
        near(chunk).start()
        query = (acc_ref[chunk].astype(BF16).astype(F32) * 0.125).astype(BF16)

        @pl.when(chunk % 2 == 0)
        def _():
            dq_ref[chunk] = query

        @pl.when(chunk % 2 == 1)
        def _():
            dqs_ref[chunk // 2] = query
            partner(chunk // 2).start()

    def go_across(k):
        chunk = chunks[k]
        join(chunk).wait_recv()
        sum_ref[chunk] = (dkv_ref[across, chunk].astype(F32) + join_ref[chunk].astype(F32)).astype(BF16)
        cross(chunk).start()

    def gather_up(k):
        chunk = chunks[k]
        if k < 3:

            @pl.when(chunk % 2 == 1)
            def _():
                partner(chunk // 2).wait_recv()

        near(chunk).wait_recv()
        cross(chunk).wait_recv()
        own = (
            dkv_ref[c, chunk].astype(F32) + near_ref[chunk].astype(F32) + far_ref[chunk].astype(F32)
        ).astype(BF16)
        own_ref[chunk] = own
        part_ref[chunk] = mm_nt(dq_ref[chunk], w_ref[:, 0:256]) + mm_nt(own, w_ref[:, 256:640])

    def relay(k):
        chunk = chunks[k]

        @pl.when(chunk < t)
        def _():
            @pl.when(t < 3)
            def _():
                passed(0, chunk)
                pass_ref[chunk] = (part_ref[chunk] + take_ref[0, chunk].astype(F32)).astype(BF16)

            @pl.when(t == 3)
            def _():
                pass_ref[chunk] = part_ref[chunk].astype(BF16)

            lower(chunk).start()

        @pl.when(chunk > t)
        def _():
            @pl.when(t > 0)
            def _():
                passed(1, chunk)
                pass_ref[chunk] = (part_ref[chunk] + take_ref[1, chunk].astype(F32)).astype(BF16)

            @pl.when(t == 0)
            def _():
                pass_ref[chunk] = part_ref[chunk].astype(BF16)

            upper(chunk).start()

    def relay_ends(k):
        pl.when(at_end)(functools.partial(relay, k))

    def relay_inner(k):
        pl.when(jnp.logical_not(at_end))(functools.partial(relay, k))

    low_keys = lax.broadcasted_iota(jnp.int32, (256, 128), 1) < 64

    def one_item(item, done):
        phase = (item + 9) // 16 + (item + 4) // 16 + (item + 1) // 16
        number = item - phase * (8 - phase)
        second = number // (4 - phase)
        query_at = ordered_by(t, 3 - (phase + second * (number - 3 + phase)))
        key_at = ordered_by(t, 3 - (phase + (1 - second) * number))
        half = query_at % 2
        rows = pl.ds(pl.multiple_of(query_at * 256, 256), 256)

        def visit(segments):
            queries = [qm_ref[head, rows] for head in range(3)]
            grads = [dm_ref[head, rows] for head in range(3)]
            made = []
            for segment in segments:
                penalty = jnp.where(flag_ref[half, segment] > 0, 0.0, FAR)
                key_pair = kv_ref[segment, key_at, :, 0:128]
                mixed = kv_ref[segment, key_at, :, 128:256]
                value_pair = kv_ref[segment, key_at, :, 256:384]
                for head in range(3):
                    shift = row_ref[query_at, head : head + 1] + penalty
                    prob = jnp.exp(mm_nt(key_pair if head < 2 else mixed, queries[head]) - shift)
                    grad_prob = mm_nt(value_pair if head < 2 else mixed, grads[head])
                    grad_score = (prob * (grad_prob - row_ref[query_at, 8 + head : 9 + head])).astype(BF16)
                    made.append((prob.astype(BF16), grad_score))
            pair_sum, mixed_sum = 0.0, 0.0
            for number, segment in enumerate(segments):
                (p0, g0), (p1, g1), (p2, g2) = made[3 * number : 3 * number + 3]
                for_keys = mm(g0, queries[0]) + mm(g1, queries[1])
                for_mixed = mm(g2, queries[2]) + mm(p2, grads[2])
                for_values = mm(p0, grads[0]) + mm(p1, grads[1])
                wide_ref[segment, key_at] += jnp.concatenate([for_keys, for_mixed, for_values], axis=1)
                key_pair = kv_ref[segment, key_at, :, 0:128]
                nothing = jnp.zeros_like(key_pair)
                pair_sum += mm_tn(g0, jnp.where(low_keys, key_pair, nothing))
                pair_sum += mm_tn(g1, jnp.where(low_keys, nothing, key_pair))
                mixed_sum += mm_tn(g2, jnp.where(low_keys, nothing, kv_ref[segment, key_at, :, 128:256]))
            acc_ref[query_at] += jnp.concatenate([pair_sum, mixed_sum], axis=1)

        length = c + 1 + half * (3 - 2 * c)

        @pl.loop(0, length // 2)
        def _(two):
            visit((2 * two, 2 * two + 1))

        @pl.when(length % 2 == 1)
        def _():
            visit((length - 1,))

        now = done + length

        def at(place, action, k):
            pl.when(item == place)(functools.partial(action, k))

        def once(amount, action, k):
            pl.when((done < amount) & (now >= amount))(functools.partial(action, k))

        for n in range(len(ride.hops)):
            once(RIDE_HOPS[n], ride.one_hop, n)
        ride.turn_when((done < 14) & (now >= 14))
        for k, place in enumerate((6, 11, 14)):
            at(place, leave, k)
        once(24, go_across, 0)
        once(31, gather_up, 0)
        once(31, relay_ends, 0)
        once(32, go_across, 1)
        once(38, gather_up, 1)
        once(38, relay_ends, 1)
        return now

    lax.fori_loop(0, 16, one_item, 0)
    leave(3)
    go_across(2)
    relay_inner(0)
    go_across(3)
    gather_up(2)
    relay_ends(2)
    relay_inner(1)

    def slice_of(place):
        return pl.ds(pl.multiple_of(place * depth, depth), depth)

    spans = (pl.ds(0, 256), pl.ds(256, 256), pl.ds(512, 128))

    def term(k, span):
        to, cols = (f + k) % size, spans[span]
        return rcopy(
            all_in_ref.at[slice_of(to), cols], term_ref.at[k - 1, :, cols],
            w_send.at[k - 1, span], w_recv.at[k - 1, span], {"fsdp": to},
        )


    @pl.when(t % 2 == 1)
    def _():
        partner(t // 2).wait_recv()

    query = dq_ref[...].reshape(1024, 256)
    for span in range(3):
        if span == 1:
            gather_up(3)
        own = own_ref[...].reshape(1024, 384)
        made = (query, own[:, 0:256], own[:, 256:384])[span]
        all_in_ref[:, spans[span]] = mm_tn(xg_ref[...], made).astype(BF16)
        for k in range(1, size):
            term(k, span).start()

    ride.chain()
    relay_inner(2)
    sum_out_ref[0:1, 0:256] = jnp.sum(query.astype(F32), axis=0, keepdims=True)
    sum_out_ref[0:1, 256:640] = jnp.sum(own.astype(F32), axis=0, keepdims=True)
    ride.put(sum_out_ref)
    ride.chain_turn()
    grad_ref[...] = part_ref[t] + back_ref[...]

    @pl.when(t < 3)
    def _():
        passed(0, t)
        grad_ref[...] += take_ref[0, t].astype(F32)

    @pl.when(t > 0)
    def _():
        passed(1, t)
        grad_ref[...] += take_ref[1, t].astype(F32)

    low_ref[...] = grad_ref[...].astype(BF16)
    ride.put(grad_ref, low_ref)
    mem_ref[...] = lax.dot_general(
        mark_ref[...], grad_ref[...], (((0,), (0,)), ((), ())),
        precision=lax.Precision.HIGHEST, preferred_element_type=F32,
    )
    ride.put(mem_ref)
    total = all_in_ref[slice_of(f)].astype(F32)
    for k in range(1, size):
        for span in range(3):
            term(k, span).wait_recv()
        total += term_ref[k - 1].astype(F32)
    din_ref[...] = total.astype(BF16)
    ride.put(din_ref)
    for k in range(1, size):
        for span in range(3):
            term(k, span).wait_send()
    for chunk in range(4):
        join(chunk).wait_send()
        near(chunk).wait_send()
        cross(chunk).wait_send()

        @pl.when(t != chunk)
        def _():
            upper(chunk).wait_send()

    for slot in range(2):
        partner(slot).wait_send()
    ride.finish()


RIDE_HOPS = (8, 11, 14, 17)


def inner_back(qw, kv, do, o, lse, flags, w, back_one, xg, marks, cid, riders=()):
    size = lax.axis_size("fsdp")
    depth = 768 // size
    f = functools.partial(sds, dtype=F32)
    outs = [f(256, 768), sds(256, 768), sds(depth, 640), f(8, 640), f(marks.shape[1], 768)]
    scratch = [
        pltpu.VMEM((3, 1024, 128), BF16), pltpu.VMEM((3, 1024, 128), BF16), pltpu.VMEM((4, 16, 256), F32),
        pltpu.VMEM((4, 256, 256), F32), pltpu.VMEM((4, 4, 256, 384), F32), pltpu.VMEM((4, 4, 256, 384), BF16),
        pltpu.VMEM((2, 256, 256), BF16),
        dma(size - 1, 3), dma(size - 1, 3), pltpu.VMEM((size - 1, depth, 640), BF16), pltpu.VMEM((768, 640), BF16),
        pltpu.VMEM((4, 256, 256), BF16), pltpu.VMEM((4, 256, 384), BF16),
        pltpu.VMEM((4, 256, 768), F32),
        pltpu.VMEM((4, 256, 384), BF16), pltpu.VMEM((4, 256, 384), BF16),
        pltpu.VMEM((4, 256, 384), BF16), pltpu.VMEM((4, 256, 384), BF16),
        pltpu.VMEM((4, 256, 768), BF16), pltpu.VMEM((2, 4, 256, 768), BF16),
        dma(2), dma(2), dma(4), dma(4), dma(4), dma(4), dma(4), dma(4), dma(4), dma(2, 4),
    ]
    cost = (5 * 512 * 1024 * 64 * 30 + 4 * 1024 * 768 * 640, 16 << 20, 5 * 512 * 1024 * 3)
    operands = (flags, qw, kv.reshape(4, 4, 256, 384), do, o, lse, w, back_one, xg, marks)
    res, ridden = call(inner_back_kernel, operands, outs, scratch, cid, "inner_back", cost, riders, smem=(0,))
    return (*res[:3], res[3][0], res[4], ridden)


def ancestry(parent_row):
    seg_count = parent_row.shape[0]
    segment_ids = jnp.arange(seg_count, dtype=jnp.int32)
    parent_hop = (parent_row[:, None] == segment_ids[None, :]).astype(jnp.int32)
    reached = (segment_ids[:, None] == segment_ids[None, :]).astype(jnp.int32)
    on_path = reached
    for hop_number in range(seg_count - 1):
        reached = jnp.dot(reached, parent_hop)
        on_path = jnp.maximum(on_path, reached)
    return on_path


def joined(query, key, value, gap):
    return jnp.concatenate(
        [
            query[..., :128], gap, query[..., 128:],
            key[..., :128], value[..., 128:], key[..., 128:], value[..., :128],
        ],
        axis=-1,
    )


def parted(grads):
    query = jnp.concatenate([grads[..., :128], grads[..., 192:256]], axis=-1)
    key = jnp.concatenate([grads[..., 256:384], grads[..., 448:512]], axis=-1)
    value = jnp.concatenate([grads[..., 512:640], grads[..., 384:448]], axis=-1)
    return query, key, value


def added(terms, axes=(0,)):
    return jnp.sum(terms.astype(F32), axis=axes)


def low(values):
    return values.astype(BF16)


def shards(
    hidden, cotangent, mem_pos, parents, memory, wq, wk, wv, wo, w1, w2,
    head_bias, ffn_bias, out_bias, norm_gains, norm_shifts,
):
    c = lax.axis_index("ctx")
    t = lax.axis_index("tp")
    size = lax.axis_size("fsdp")
    layers = wq.shape[0]
    share = hidden.shape[0]
    depth = wq.shape[1]
    piece = depth // 4
    positions = t * share + jnp.arange(share, dtype=jnp.int32)
    marks = (mem_pos[0, 0][None, :] == positions[:, None]).astype(F32)
    stream = hidden.astype(F32) + jnp.dot(
        marks, memory, precision=lax.Precision.HIGHEST, preferred_element_type=F32
    )
    on_path = ancestry(parents[0])
    ids = jnp.arange(4, dtype=jnp.int32)
    pick = lambda seg: jnp.sum(on_path * (ids == seg).astype(jnp.int32)[:, None], axis=0)
    flags = jnp.stack([pick(c), pick(3 - c)])

    gap = jnp.zeros(wq.shape[:2] + (64,), BF16)
    own_in = joined(wq, wk, wv, gap)
    none = jnp.zeros((layers, 192), F32)
    in_bias = joined(head_bias[:, 0], none, head_bias[:, 1], jnp.zeros((layers, 64), F32))
    down_turned = jnp.swapaxes(w2, 1, 2)
    out_turned = jnp.swapaxes(wo, 1, 2).reshape(layers, 4, piece, 192)
    out_piece = lax.dynamic_index_in_dim(out_turned, c, axis=1, keepdims=False)

    def out_whole(gathered):
        return jnp.transpose(gathered, (1, 2, 0, 3, 4)).reshape(4, 768, 192)

    def vectors(n):
        norms = [norm_gains[n, 0], norm_shifts[n, 0], norm_gains[n, 1], norm_shifts[n, 1]]
        return jnp.concatenate([out_bias[n], jnp.stack(norms), jnp.zeros((2, 768), F32)])

    saved, weights = [], []
    rounded = low(stream)
    riders = [plane_gather(out_piece[0], size), ctx_gather(sds(4, size, piece, 192), first=0)]
    riders += [flip_gather(w1[0], size).later(), tp_flip(down_turned[0]).later(hopped=True), tp_flip(ffn_bias)]
    xg, qw, kv, o, lse, w_in, got = inner(rounded, own_in[0], in_bias[0][None], flags, 0, riders, fetch=True)
    _, out, w_up, down, units = got
    for n in range(layers):
        last = n == layers - 1
        w_out = out_whole(out)
        w_up = w_up.reshape(768, 768)
        vecs = vectors(n)
        riders = []
        if not last:
            riders = [
                tp_flip(w1[n + 1]),
                plane_gather(out_piece[n + 1], size), fsdp_gather(own_in[n + 1], size),
            ]
        stream, rounded, xhat1, r1, xhat2, r2, xg2, act, slope, rows, w_down, got = block(
            o, w_out, w_up, down, units[n][None], vecs, stream, 16 * n + 2, riders
        )
        weights.append((w_in, w_up, w_down, w_out, vecs))
        saved.append((xg, qw, kv, o, lse, xhat1, r1, xhat2, r2, xg2, act, slope, rows))
        if not last:
            up, out, w_in = got
            riders = [ctx_gather(out), tp_flip(down_turned[n + 1]).later(), fsdp_gather(up, size)]
            xg, qw, kv, o, lse, w_in, (out, down, w_up) = inner(
                rounded, w_in.reshape(768, 640), in_bias[n + 1][None], flags, 16 * n + 16, riders
            )
    output = rounded

    grad = cotangent.astype(F32)
    small, heads = [None] * layers, [None] * layers
    done = [None] * layers
    above = None
    for n in reversed(range(layers)):
        w_in, w_up, w_down, w_out, vecs = weights[n]
        xg, qw, kv, o, lse, xhat1, r1, xhat2, r2, xg2, act, slope, rows = saved[n]
        riders = []
        if above is not None:
            riders = [plane_scatter(above["out"], size), ctx_scatter(above["in"])]
        back_one, do, small[n], d_up, d_down, d_out, got = block_back(
            grad, xhat2, r2, xhat1, r1, vecs, slope, w_up, w_down, w_out, xg2, act, rows, 16 * n + 3, riders
        )
        quarters = sds(4, depth // 4, 768)
        riders = [
            tp_flip(d_up.reshape(quarters.shape)), scatter_flip(d_down.reshape(size, *quarters.shape)),
            ctx_scatter(d_out.reshape(4, size, 4, piece, 192), axis=2),
            ctx_scatter(quarters, first=0), ctx_scatter(quarters, first=1),
        ]
        if above is not None:
            gathered = (added(got[0], (0, 1)), above["up"], above["down"], added(got[1]))
            riders += [ctx_gather(low(part)) for part in gathered]
        grad, low_grad, d_in, sums, memory_part, got = inner_back(
            qw, kv, do, o, lse, flags, w_in, back_one, xg, marks, 16 * n + 4, riders
        )
        if above is not None:
            done[n + 1] = (got[8], got[5], got[6], got[7])
        d_query_bias, _, d_value_bias = parted(sums)
        heads[n] = jnp.stack([d_query_bias, d_value_bias])
        above = {
            "up": low(added(got[3])),
            "down": low(added(got[4])),
            "in": d_in.reshape(4, depth // 4, 640),
            "out": low(added(got[2])),
        }
    hidden_grad = low_grad
    small = jnp.stack(small)
    place = (ids == t).astype(F32)
    unit = (ids == flipped_place(c, t)).astype(F32)
    head_rows = (jnp.stack(heads)[:, :, None, :] * place[None, None, :, None]).reshape(2 * layers, 768)
    unit_rows = (small[:, 6][:, None, :] * unit[None, :, None]).reshape(4 * layers, 768)
    stat_rows = small[:, :6].reshape(6 * layers, 768)
    filled = 12 * layers + memory_part.shape[0]
    slices = 4 * size
    width = -(-filled // slices)
    rest = jnp.zeros((width * slices - filled, 768), F32)
    sums = jnp.concatenate([stat_rows, unit_rows, head_rows, memory_part, rest])
    sums = sums.reshape(4, size, width, 768)
    riders = [ctx_scatter(above["in"]), plane_scatter(above["out"], size), plane_scatter(sums, size)]
    got = carry(riders, 6)
    parts = (low(added(got[0])), low(added(got[1], (0, 1))), above["up"], above["down"])
    got = carry([ctx_gather(part) for part in parts] + [small_sum(added(got[2], (0, 1)), size)], 7)
    done[0] = got[:4]
    totals = got[4].reshape(width * slices, 768)
    stats = totals[: 6 * layers].reshape(layers, 6, 768)
    at = 6 * layers
    ffn_rows = totals[at : at + 4 * layers].reshape(layers, 4, 768)
    ffn_grad = jnp.sum(ffn_rows * place[None, :, None], axis=1)
    at += 4 * layers
    head_sums = totals[at : at + 2 * layers].reshape(layers, 2, 4, 192)
    head_grad = jnp.sum(head_sums * place[None, None, :, None], axis=2)
    at += 2 * layers
    memory_grad = totals[at : at + memory_part.shape[0]]
    d_in = jnp.stack([part[0].reshape(depth, 640) for part in done]).astype(F32)
    d_out = jnp.stack([jnp.swapaxes(part[1].reshape(depth, 192), 0, 1) for part in done]).astype(F32)
    d_up = jnp.stack([part[2].reshape(depth, 768) for part in done]).astype(F32)
    d_down = jnp.stack([jnp.swapaxes(part[3].reshape(depth, 768), 0, 1) for part in done]).astype(F32)
    return (
        output, hidden_grad, memory_grad, *parted(d_in), d_out, d_up, d_down,
        head_grad, ffn_grad, stats[:, 4:6], stats[:, 0:2], stats[:, 2:4],
    )


def solution(mesh):
    rows = P(("fsdp", "ctx", "tp"), None)
    inner = P(None, "fsdp", "tp")
    outer = P(None, "tp", "fsdp")
    weights = (inner, inner, inner, outer, inner, outer)
    biases = (P(None, None, "tp"), P(None, "tp"), P(), P(), P())
    return jax.shard_map(
        shards,
        mesh=mesh,
        in_specs=(rows, rows, P("fsdp", "ctx", None), P("fsdp", None), P()) + weights + biases,
        out_specs=(rows, rows, P()) + weights + biases,
        check_vma=False,
    )
```

```python
import functools

import jax
import jax.numpy as jnp
from jax import lax
from jax.experimental import pallas as pl
from jax.experimental.pallas import tpu as pltpu
from jax.sharding import PartitionSpec as P

EPSILON = 1e-05
MASKED = -1000000000.0
MESH = pl.DeviceIdType.MESH
F32 = jnp.float32
BF16 = jnp.bfloat16
ORDER = ((0, 1), (1, 0), (2, 2), (3, 3))


def mm(left, right):
    return jnp.dot(left, right, preferred_element_type=F32)


def mm_nt(left, right):
    return lax.dot_general(left, right, (((1,), (1,)), ((), ())), preferred_element_type=F32)


def mm_tn(left, right):
    return lax.dot_general(left, right, (((0,), (0,)), ((), ())), preferred_element_type=F32)


def rcopy(src, dst, send_sem, recv_sem, device):
    return pltpu.make_async_remote_copy(
        src_ref=src,
        dst_ref=dst,
        send_sem=send_sem,
        recv_sem=recv_sem,
        device_id=device,
        device_id_type=MESH,
    )


def mate_of(c):
    return c + 1 - 2 * (c % 2)


def across_of(c):
    return (c + 2) % 4


def signal(sem, device):
    pl.semaphore_signal(sem, inc=1, device_id=device, device_id_type=MESH)


def ordered(place, step):
    half = place // 2
    inner = place + half * (3 - 2 * place)
    first, second = ORDER[step]
    chunk = first + inner * (second - first)
    return chunk + half * (3 - 2 * chunk)


def ordered_by(place, step):
    half = place // 2
    inner = place + half * (3 - 2 * place)
    chunk = step + inner * (1 - 2 * step) * ((3 - step) // 2)
    return chunk + half * (3 - 2 * chunk)


def dma(*shape):
    return pltpu.SemaphoreType.DMA(shape)


class Rider:
    def __init__(self, array, out, make, scratch, chunks=0, summed=None):
        self.array, self.out, self.make, self.scratch, self.chunks = array, out, make, scratch, chunks
        self.summed = summed
        self.late = self.hopped = False

    def later(self, hopped=False):
        self.late, self.hopped = True, hopped
        return self


class Copies:
    def __init__(self, steps, here, scratch):
        self.steps, self.here = steps, here
        self.send, self.recv, self.leg, self.stage = scratch
        self.came = False

    def greetings(self):
        return [(origin, when, weight) for _, origin, _, _, when, weight in self.steps]

    def copies(self):
        for number, (to, _, source, target, when, _) in enumerate(self.steps):
            yield rcopy(source, target, self.send.at[number], self.recv.at[number], to), when

    def inward(self):
        return pltpu.make_async_copy(self.here[0], self.stage, self.leg.at[0])

    def outward(self):
        return pltpu.make_async_copy(self.stage, self.here[1], self.leg.at[1])

    def start(self):
        for copy, when in self.copies():
            guarded(when, copy.start)
        guarded(self.here[2], self.inward().start)

    def turn(self):
        guarded(self.here[2], self.inward().wait)
        guarded(self.here[2], self.outward().start)

    def arrive(self):
        self.came = True
        for copy, when in self.copies():
            guarded(when, copy.wait_recv)
        guarded(self.here[2], self.outward().wait)

    def finish(self):
        if not self.came:
            self.arrive()
        for copy, when in self.copies():
            guarded(when, copy.wait_send)


class FlipGather:
    def __init__(self, source, target, place, scratch):
        self.source, self.target = source, target
        self.f, self.c, self.t = place
        self.size = target.shape[0]
        self.send, self.recv, self.on_send, self.on_recv, self.leg, self.stage = scratch
        self.moves = self.c > 0

    def greetings(self):
        there = {"tp": flipped_place(self.c, self.t)}
        ring = [({"fsdp": (self.f + self.size - k) % self.size}, None, 1) for k in range(1, self.size)]
        return [(there, self.moves, (self.c + 3) // 4)] + ring

    def first(self, chunk):
        there = {"tp": flipped_place(self.c, self.t)}
        return rcopy(
            self.source.at[chunk], self.target.at[self.f, chunk], self.send.at[chunk], self.recv.at[chunk], there
        )

    def second(self, chunk, k, moved):
        source = self.target.at[self.f, chunk] if moved else self.source.at[chunk]
        device = {"fsdp": (self.f + k) % self.size}
        return rcopy(
            source, self.target.at[self.f, chunk], self.on_send.at[k - 1, chunk], self.on_recv.at[k - 1, chunk], device
        )

    def inward(self):
        return pltpu.make_async_copy(self.source, self.stage, self.leg.at[0])

    def outward(self):
        return pltpu.make_async_copy(self.stage, self.target.at[self.f], self.leg.at[1])

    def start(self):
        @pl.when(self.moves)
        def _():
            for chunk in range(self.source.shape[0]):
                self.first(chunk).start()

        @pl.when(self.c == 0)
        def _():
            self.inward().start()

    def hop(self, chunk):
        @pl.when(self.moves)
        def _():
            self.first(chunk).wait_recv()
            for k in range(1, self.size):
                self.second(chunk, k, True).start()

        @pl.when(self.c == 0)
        def _():
            for k in range(1, self.size):
                self.second(chunk, k, False).start()

    def turn(self):
        @pl.when(self.c == 0)
        def _():
            self.inward().wait()
            self.outward().start()

    def finish(self):
        @pl.when(self.moves)
        def _():
            for chunk in range(self.source.shape[0]):
                self.first(chunk).wait_send()

        for chunk in range(self.source.shape[0]):
            for k in range(1, self.size):
                self.second(chunk, k, False).wait()

        @pl.when(self.c == 0)
        def _():
            self.outward().wait()


class ScatterFlip:
    def __init__(self, source, target, place, scratch):
        self.source, self.target = source, target
        self.f, self.c, self.t = place
        self.size = source.shape[0]
        self.here = False
        self.send, self.recv, self.on_send, self.on_recv, self.leg, self.got, self.out = scratch
        self.moves = self.c > 0

    def greetings(self):
        there = {"tp": flipped_place(self.c, self.t)}
        ring = [({"fsdp": (self.f + self.size - k) % self.size}, None, 1) for k in range(1, self.size)]
        return [(there, self.moves, (self.c + 3) // 4)] + ring

    def first(self, chunk, k):
        to = (self.f + k) % self.size
        return rcopy(
            self.source.at[to, chunk], self.got.at[k, chunk],
            self.send.at[k - 1, chunk], self.recv.at[k - 1, chunk], {"fsdp": to},
        )

    def own(self, chunk):
        return pltpu.make_async_copy(
            self.source.at[self.f, chunk], self.got.at[0, chunk], self.leg.at[chunk]
        )

    def second(self, chunk):
        there = {"tp": flipped_place(self.c, self.t)}
        return rcopy(self.out.at[chunk], self.target.at[chunk], self.on_send.at[chunk], self.on_recv.at[chunk], there)

    def stays(self, chunk):
        return pltpu.make_async_copy(self.out.at[chunk], self.target.at[chunk], self.on_send.at[chunk])

    def start(self):
        for chunk in range(self.target.shape[0]):
            for k in range(1, self.size):
                self.first(chunk, k).start()
            self.own(chunk).start()

    def hop(self, chunk):
        self.own(chunk).wait()
        total = self.got[0, chunk].astype(F32)
        for k in range(1, self.size):
            self.first(chunk, k).wait_recv()
            total += self.got[k, chunk].astype(F32)
        self.out[chunk] = total.astype(BF16)

        @pl.when(self.moves)
        def _():
            self.second(chunk).start()

        @pl.when(self.c == 0)
        def _():
            self.stays(chunk).start()

    def turn(self):
        pass

    def arrive(self):
        self.here = True
        for chunk in range(self.target.shape[0]):
            guarded(self.moves, self.second(chunk).wait_recv)
            guarded(self.c == 0, self.stays(chunk).wait)

    def finish(self):
        if not self.here:
            self.arrive()
        for chunk in range(self.target.shape[0]):
            for k in range(1, self.size):
                self.first(chunk, k).wait_send()
            guarded(self.moves, self.second(chunk).wait_send)


class CtxGather:
    def __init__(self, pick, source, target, place, scratch):
        self.source, self.target, self.pick = source, target, pick
        self.c = place[1]
        self.send, self.recv, self.leg, self.stage = scratch

    def greetings(self):
        return [({"ctx": mate_of(self.c)}, None, 1), ({"ctx": across_of(self.c)}, None, 1)]

    def copy(self, number):
        c = self.c
        device = across_of(c) if number == 0 else mate_of(c)
        source = self.pick(self.target, across_of(c)) if number == 2 else self.source
        slot = across_of(c) if number == 2 else c
        return rcopy(source, self.pick(self.target, slot), self.send.at[number], self.recv.at[number], {"ctx": device})

    def inward(self):
        return pltpu.make_async_copy(self.source, self.stage, self.leg.at[0])

    def outward(self):
        return pltpu.make_async_copy(self.stage, self.pick(self.target, self.c), self.leg.at[1])

    def start(self):
        self.copy(0).start()
        self.copy(1).start()
        self.inward().start()

    def turn(self):
        self.inward().wait()
        self.outward().start()
        self.copy(0).wait_recv()
        self.copy(2).start()

    def finish(self):
        self.copy(0).wait_send()
        self.copy(1).wait()
        self.copy(2).wait()
        self.outward().wait()


class CtxScatter:
    def __init__(self, pick, source, target, place, scratch):
        self.source, self.target, self.pick = source, target, pick
        self.c, self.came = place[1], False
        self.send, self.recv, self.leg, self.stage, self.cross, self.far, self.total = scratch

    def greetings(self):
        return [({"ctx": mate_of(self.c)}, None, 1), ({"ctx": across_of(self.c)}, None, 1)]

    def copy(self, number):
        c = self.c
        device = across_of(c) if number == 2 else mate_of(c)
        source = (self.pick(self.source, 3 - c), self.pick(self.source, mate_of(c)), self.total)[number]
        target = (self.far, self.target.at[1], self.target.at[2])[number]
        return rcopy(source, target, self.send.at[number], self.recv.at[number], {"ctx": device})

    def inward(self):
        return pltpu.make_async_copy(self.pick(self.source, self.c), self.stage, self.leg.at[0])

    def outward(self):
        return pltpu.make_async_copy(self.stage, self.target.at[0], self.leg.at[1])

    def beside(self):
        return pltpu.make_async_copy(self.pick(self.source, across_of(self.c)), self.cross, self.leg.at[2])

    def start(self):
        self.copy(0).start()
        self.beside().start()
        self.copy(1).start()
        self.inward().start()

    def turn(self):
        self.copy(0).wait_recv()
        self.beside().wait()
        self.total[...] = (self.cross[...].astype(F32) + self.far[...].astype(F32)).astype(self.total.dtype)
        self.copy(2).start()
        self.inward().wait()
        self.outward().start()

    def arrive(self):
        self.came = True
        self.copy(1).wait_recv()
        self.copy(2).wait_recv()
        self.outward().wait()

    def finish(self):
        if not self.came:
            self.arrive()
        for number in range(3):
            self.copy(number).wait_send()


class Riding:
    def __init__(self, riders, sources, targets, scratch, fetches, results, puts):
        self.fetches, self.results, self.puts = fetches, results, puts
        self.gone = [False] * len(puts)
        place = tuple(lax.axis_index(axis) for axis in ("fsdp", "ctx", "tp"))
        scratch = list(scratch)
        self.rides, self.hops, self.late, self.hopped = [], [], [], []
        self.firsts, self.seconds, self.begun, self.turned, self.sums = [], [], [], [], {}
        for rider, target in zip(riders, targets):
            own = [scratch.pop(0) for _ in rider.scratch]
            chained = isinstance(rider.array, int)
            source = targets[rider.array] if chained else sources.pop(0)
            if rider.summed is not None:
                terms, total, sem = (scratch.pop(0) for _ in range(3))
                self.sums[len(self.seconds)] = (pltpu.make_async_copy(source, terms, sem.at[0]), terms, total)
                source = total
            ride = rider.make(source, target, place, own)
            self.rides.append(ride)
            if chained:
                self.firsts.append(self.rides[rider.array])
                self.seconds.append(ride)
                self.late.append(ride)
            if rider.late:
                self.late.append(ride)
            if rider.hopped:
                self.hopped.append(ride)
            self.hops += [(ride, chunk) for chunk in range(rider.chunks)]

    def ready(self):
        for fetch in self.fetches:
            fetch.wait()

    def put(self, *refs):
        for ref in refs:
            slot = [ref is result for result in self.results].index(True)
            self.gone[slot] = True
            self.puts[slot].start()

    def close(self):
        for slot, put in enumerate(self.puts):
            if not self.gone[slot]:
                put.start()
        for put in self.puts:
            put.wait()

    def greet(self, barrier):
        count = 0
        for ride in self.rides:
            for origin, when, weight in ride.greetings():
                guarded(when, functools.partial(signal, barrier, origin))
                count = count + weight
        return count

    def begin(self, ride):
        self.begun.append(ride)
        ride.start()

    def start(self):
        for ride in self.rides:
            if ride not in self.late:
                self.begin(ride)

    def start_late(self):
        for ride in self.late:
            if ride not in self.hopped + self.seconds:
                self.begin(ride)

    def one_hop(self, at):
        ride, chunk = self.hops[at]
        ride.hop(chunk)
        if at == len(self.hops) - 1:
            for ride in self.hopped:
                self.begin(ride)

    def turn(self):
        for ride in self.begun:
            if ride not in self.turned + self.seconds:
                self.turned.append(ride)
                ride.turn()

    def turn_when(self, when):
        if self.rides:
            pl.when(when)(self.turn)

    def chain(self):
        for number, (first, second) in enumerate(zip(self.firsts, self.seconds)):
            first.arrive()
            if number in self.sums:
                fetch, terms, total = self.sums[number]
                fetch.start()
                fetch.wait()
                axes = tuple(range(len(terms.shape) - len(total.shape)))
                total[...] = jnp.sum(terms[...].astype(F32), axis=axes).astype(total.dtype)
            self.begin(second)

    def chain_turn(self):
        for second in self.seconds:
            self.turned.append(second)
            second.turn()

    def finish(self):
        for ride in self.rides:
            if ride not in self.turned:
                ride.turn()
        for ride in self.rides:
            ride.finish()


def guarded(when, action):
    if when is None:
        action()
    else:
        pl.when(when)(action)


def call(kernel, operands, out_shapes, scratch, collective_id, name, cost, riders=(), smem=()):
    n_in, n_out, n_scratch, n_ride = len(operands), len(out_shapes), len(scratch), len(riders)
    large = [i for i in range(n_in) if i not in smem]
    carried = [rider.array for rider in riders if not isinstance(rider.array, int)]

    def body(*refs):
        refs = list(refs)
        take = lambda n: [refs.pop(0) for _ in range(n)]
        ins, sources, outs, targets = take(n_in), take(len(carried)), take(n_out), take(n_ride)
        near_ins, near_outs, (in_sem, out_sem), own = take(len(large)), take(n_out), take(2), take(n_scratch)
        fetches = [
            pltpu.make_async_copy(ins[i], near, in_sem.at[slot]) for slot, (i, near) in enumerate(zip(large, near_ins))
        ]
        for fetch in fetches:
            fetch.start()
        for i, near in zip(large, near_ins):
            ins[i] = near
        puts = [pltpu.make_async_copy(near, far, out_sem.at[i]) for i, (near, far) in enumerate(zip(near_outs, outs))]
        ride = Riding(riders, sources, targets, refs, fetches, near_outs, puts)
        kernel(ride, *ins, *near_outs, *own)
        ride.close()

    params = dict(vmem_limit_bytes=60 * 1024 * 1024)
    if collective_id is not None:
        params.update(collective_id=collective_id, has_side_effects=True)
    extra = []
    for rider in riders:
        extra += rider.scratch
        if rider.summed is not None:
            terms, total = riders[rider.array].out, rider.summed
            extra += [pltpu.VMEM(terms.shape, terms.dtype), pltpu.VMEM(total.shape, total.dtype), dma(1)]
    anywhere = pl.BlockSpec(memory_space=pl.ANY)
    near = [pltpu.VMEM(operands[i].shape, operands[i].dtype) for i in large]
    near += [pltpu.VMEM(out.shape, out.dtype) for out in out_shapes]
    results = pl.pallas_call(
        body,
        out_shape=list(out_shapes) + [rider.out for rider in riders],
        in_specs=[pl.BlockSpec(memory_space=pltpu.SMEM) if i in smem else anywhere for i in range(n_in)]
        + [anywhere] * len(carried),
        out_specs=[anywhere] * (n_out + n_ride),
        scratch_shapes=near + [dma(max(len(large), 1)), dma(max(n_out, 1))] + list(scratch) + extra,
        compiler_params=pltpu.CompilerParams(**params),
        cost_estimate=pl.CostEstimate(flops=cost[0], bytes_accessed=cost[1], transcendentals=cost[2]),
        name=name,
    )(*operands, *carried)
    return results[:n_out], results[n_out:]


def copies_rider(array, out, steps, stage, plan):
    def make(source, target, place, scratch):
        return Copies(*plan(source, target, *place), scratch)

    scratch = [dma(steps), dma(steps), dma(2), pltpu.VMEM(stage, array.dtype)]
    return Rider(array, out, make, scratch)


def flip_gather(own, size):
    own = own.reshape(2, own.shape[0] // 2, own.shape[1])
    scratch = [dma(2), dma(2), dma(size - 1, 2), dma(size - 1, 2), dma(2), pltpu.VMEM(own.shape, own.dtype)]
    return Rider(own, sds(size, *own.shape), FlipGather, scratch, chunks=2)


def scatter_flip(parts):
    size, n = parts.shape[0], parts.shape[1]
    shape = parts.shape[1:]
    scratch = [
        dma(size - 1, n), dma(size - 1, n), dma(n), dma(n), dma(n),
        pltpu.VMEM((size, *shape), BF16), pltpu.VMEM(shape, BF16),
    ]
    return Rider(parts, sds(*shape), ScatterFlip, scratch, chunks=n)


def fsdp_gather(own, size):
    def make(source, target, f, c, t):
        steps = [
            ({"fsdp": (f + k) % size}, {"fsdp": (f + size - k) % size}, source, target.at[f], None, 1)
            for k in range(1, size)
        ]
        return steps, (source, target.at[f], None)

    return copies_rider(own, sds(size, *own.shape, dtype=own.dtype), size - 1, own.shape, make)


def fsdp_scatter(parts, size):
    out = sds(size, parts.shape[0], *parts.shape[2:], dtype=parts.dtype)

    def make(source, target, f, c, t):
        steps = [
            (
                {"fsdp": (f + k) % size}, {"fsdp": (f + size - k) % size},
                source.at[:, (f + k) % size], target.at[k], None, 1,
            )
            for k in range(1, size)
        ]
        return steps, (source.at[:, f], target.at[0], None)

    return copies_rider(parts, out, size - 1, out.shape[1:], make)


def slot_of(axis):
    def pick(ref, slot):
        return ref.at[slot] if axis == 0 else ref.at[:, :, slot]

    return pick


def ctx_gather(own, axis=0, first=None, summed=False):
    scratch = [dma(3), dma(3), dma(2), pltpu.VMEM(own.shape, own.dtype)]
    out = sds(*own.shape[:axis], 4, *own.shape[axis:], dtype=own.dtype)
    make = functools.partial(CtxGather, slot_of(axis))
    return Rider(own if first is None else first, out, make, scratch, summed=own if summed else None)


def ctx_scatter(parts, axis=0, first=None):
    shape = parts.shape[:axis] + parts.shape[axis + 1 :]

    buffer = pltpu.VMEM(shape, parts.dtype)
    scratch = [dma(3), dma(3), dma(3), buffer, buffer, buffer, buffer]
    array = parts if first is None else first
    return Rider(array, sds(3, *shape, dtype=parts.dtype), functools.partial(CtxScatter, slot_of(axis)), scratch)


def flipped_place(c, t):
    return 2 * ((t // 2 + c % 2) % 2) + (t % 2 + c // 2) % 2


def tp_flip(own):
    def make(source, target, f, c, t):
        other = {"tp": flipped_place(c, t)}
        return [(other, other, source, target, c > 0, (c + 3) // 4)], (source, target, c == 0)

    return copies_rider(own, sds(*own.shape, dtype=own.dtype), 1, own.shape, make)


def plane(size):
    return [(kt, kf) for kt in (2, 3, 1, 0) for kf in range(size) if kt + kf > 0]


def plane_gather(own, size):
    def make(source, target, f, c, t):
        steps = [
            (
                {"fsdp": (f + kf) % size, "tp": (t + kt) % 4},
                {"fsdp": (f + size - kf) % size, "tp": (t + 4 - kt) % 4},
                source, target.at[t, f], None, 1,
            )
            for kt, kf in plane(size)
        ]
        return steps, (source, target.at[t, f], None)

    return copies_rider(own, sds(4, size, *own.shape, dtype=own.dtype), 4 * size - 1, own.shape, make)


def plane_scatter(parts, size):
    def make(source, target, f, c, t):
        steps = [
            (
                {"fsdp": (f + kf) % size, "tp": (t + kt) % 4},
                {"fsdp": (f + size - kf) % size, "tp": (t + 4 - kt) % 4},
                source.at[(t + kt) % 4, (f + kf) % size], target.at[kt, kf], None, 1,
            )
            for kt, kf in plane(size)
        ]
        return steps, (source.at[t, f], target.at[0, 0], None)

    return copies_rider(parts, sds(*parts.shape, dtype=parts.dtype), 4 * size - 1, parts.shape[2:], make)


class SmallSum:
    def __init__(self, source, target, place, scratch):
        self.source, self.target = source, target
        self.f, self.c, self.t = place
        self.size = target.shape[1]
        self.send, self.recv, self.on_send, self.on_recv, self.leg, self.terms, self.total = scratch

    def greetings(self):
        around = [({"ctx": (self.c + 4 - k) % 4}, None, 1) for k in (1, 2, 3)]
        return around + [
            ({"fsdp": (self.f + self.size - kf) % self.size, "tp": (self.t + 4 - kt) % 4}, None, 1)
            for kt, kf in plane(self.size)
        ]

    def first(self, k):
        device = {"ctx": (self.c + k) % 4}
        return rcopy(self.source, self.terms.at[self.c], self.send.at[k - 1], self.recv.at[k - 1], device)

    def own(self):
        return pltpu.make_async_copy(self.source, self.terms.at[self.c], self.leg.at[0])

    def second(self, number):
        kt, kf = plane(self.size)[number]
        device = {"fsdp": (self.f + kf) % self.size, "tp": (self.t + kt) % 4}
        target = self.target.at[self.t, self.f]
        return rcopy(self.total, target, self.on_send.at[number], self.on_recv.at[number], device)

    def stays(self):
        return pltpu.make_async_copy(self.total, self.target.at[self.t, self.f], self.leg.at[1])

    def start(self):
        for k in (2, 3, 1):
            self.first(k).start()
        self.own().start()

    def turn(self):
        self.own().wait()
        for k in (1, 2, 3):
            self.first(k).wait_recv()
        self.total[...] = self.terms[0] + self.terms[1] + self.terms[2] + self.terms[3]
        for number in range(4 * self.size - 1):
            self.second(number).start()
        self.stays().start()

    def finish(self):
        for k in (1, 2, 3):
            self.first(k).wait_send()
        for number in range(4 * self.size - 1):
            self.second(number).wait()
        self.stays().wait()


def small_sum(own, size, first=None):
    many = 4 * size - 1
    scratch = [
        dma(3), dma(3), dma(many), dma(many), dma(2),
        pltpu.VMEM((4, *own.shape), own.dtype), pltpu.VMEM(own.shape, own.dtype),
    ]
    out = sds(4, size, *own.shape, dtype=own.dtype)
    return Rider(own if first is None else first, out, SmallSum, scratch, summed=None if first is None else own)


def carry_kernel(ride):
    barrier = pltpu.get_barrier_semaphore()
    pl.semaphore_wait(barrier, ride.greet(barrier))
    ride.start()
    ride.turn()
    ride.start_late()
    ride.chain()
    ride.turn()
    ride.chain_turn()
    ride.finish()


def carry(riders, cid):
    return call(carry_kernel, (), (), (), cid, "carry", (1 << 20, 1 << 20, 0), riders)[1]


def sds(*shape, dtype=BF16):
    return jax.ShapeDtypeStruct(shape, dtype)


FAR = 1e30


def inner_kernel(
    fetch, ride, flag_ref, x_ref, w_ref, b_ref, xg_ref, qw_ref, kv_ref, o_ref, lse_ref, *rest
):
    if fetch:
        full_ref, w_send, w_recv, *rest = rest
    (
        qbuf, qm_ref, m_ref, acc_ref, vt_ref, x_recv, x_right, x_left,
        k1_send, k1_recv, k2_send, k2_recv, kf_send, kf_recv, q_send, q_recv,
    ) = rest
    c = lax.axis_index("ctx")
    t = lax.axis_index("tp")
    f, size = lax.axis_index("fsdp"), lax.axis_size("fsdp")
    barrier = pltpu.get_barrier_semaphore()
    for device in (mate_of(c), across_of(c), 3 - c):
        signal(barrier, {"ctx": device})

    @pl.when(t > 0)
    def _():
        signal(barrier, {"tp": t - 1})

    @pl.when(t < 3)
    def _():
        signal(barrier, {"tp": t + 1})

    if fetch:
        for k in range(1, size):
            signal(barrier, {"fsdp": (f + size - k) % size})
    ends = (t // 3) + (3 - t) // 3
    count = 5 - ends + ride.greet(barrier) + (size - 1 if fetch else 0)
    m_ref[...] = jnp.full_like(m_ref, MASKED)
    acc_ref[...] = jnp.zeros_like(acc_ref)
    vt_ref[:, :, :, 64:80] = jnp.ones((4, 4, 3, 16, 256), BF16)
    ride.ready()
    pl.semaphore_wait(barrier, count)

    def right(src, chunk, step):
        return rcopy(src, xg_ref.at[chunk], x_right.at[step], x_recv.at[chunk], {"tp": t + 1})

    def left(src, chunk, step):
        return rcopy(src, xg_ref.at[chunk], x_left.at[step], x_recv.at[chunk], {"tp": t - 1})

    def arrived(chunk):
        rcopy(xg_ref.at[chunk], xg_ref.at[chunk], x_right.at[0], x_recv.at[chunk], {"tp": t}).wait_recv()

    @pl.when(t < 3)
    def _():
        right(x_ref, t, 0).start()

    @pl.when(t > 0)
    def _():
        left(x_ref, t, 0).start()

    def weight(k):
        device = {"fsdp": (f + k) % size}
        return rcopy(w_ref, full_ref.at[f], w_send.at[k - 1], w_recv.at[k - 1], device)

    if fetch:
        for k in range(1, size):
            weight(k).start()
        full_ref[f] = w_ref[...]
    xg_ref[t] = x_ref[...]
    ride.start()
    if fetch:
        for k in range(1, size):
            weight(k).wait_recv()

    def mate(chunk):
        part = kv_ref.at[c, chunk]
        return rcopy(part, part, k1_send.at[chunk], k1_recv.at[chunk], {"ctx": mate_of(c)})

    def across(chunk):
        part = kv_ref.at[c, chunk]
        return rcopy(part, part, k2_send.at[chunk], k2_recv.at[chunk], {"ctx": across_of(c)})

    def onward(chunk):
        part = kv_ref.at[across_of(c), chunk]
        return rcopy(part, part, kf_send.at[chunk], kf_recv.at[chunk], {"ctx": mate_of(c)})

    def partner(slot):
        return rcopy(qbuf.at[slot], qw_ref.at[2 * slot + 1], q_send.at[slot], q_recv.at[slot], {"ctx": 3 - c})

    def project(step):
        chunk = ordered(t, step)
        w = full_ref[...].reshape(768, 640) if fetch else w_ref[...]
        made = mm(xg_ref[chunk], w) + b_ref[...]
        kv_ref[c, chunk] = made[:, 256:].astype(BF16)
        across(chunk).start()
        mate(chunk).start()
        query = (made[:, :256] * 0.125).astype(BF16)

        @pl.when(chunk % 2 == 0)
        def _():
            qw_ref[chunk] = query

        @pl.when(chunk % 2 == 1)
        def _():
            qbuf[chunk // 2] = query
            partner(chunk // 2).start()

    low = lax.broadcasted_iota(jnp.int32, (256, 128), 1) < 64

    def complete(step):
        chunk = ordered(t, step)
        across(chunk).wait_recv()
        onward(chunk).start()
        mate(chunk).wait_recv()

        @pl.when(chunk % 2 == 1)
        def _():
            partner(chunk // 2).wait_recv()

        pair = qw_ref[chunk, :, 0:128]
        none = jnp.zeros_like(pair)
        qm_ref[0, chunk] = jnp.where(low, pair, none)
        qm_ref[1, chunk] = jnp.where(low, none, pair)
        qm_ref[2, chunk] = qw_ref[chunk, :, 128:256]
        onward(chunk).wait_recv()
        for segment in range(4):
            pair = jnp.transpose(kv_ref[segment, chunk, :, 256:384], (1, 0))
            mixed = jnp.transpose(kv_ref[segment, chunk, :, 128:256], (1, 0))
            for head, rows in enumerate((pair[0:64], pair[64:128], mixed[0:64])):
                vt_ref[segment, chunk, head, 0:64] = rows

    def items(step):
        @pl.loop(step * step, (step + 1) * (step + 1))
        def _(item):
            number = item - step * step
            second = number // (step + 1)
            query_at = ordered_by(t, step + second * (number - 2 * step - 1))
            key_at = ordered_by(t, number + second * (step - number))
            half = query_at % 2

            def visit(segments):
                seen = [flag_ref[half, segment] > 0 for segment in segments]
                far = [jnp.where(one, 0.0, FAR) for one in seen]
                scores, most, made = [], [], []
                for head in range(3):
                    query, at = qm_ref[head, query_at], 128 * (head // 2)
                    rows = [mm_nt(kv_ref[segment, key_at, :, at : at + 128], query) for segment in segments]
                    new = m_ref[query_at, head : head + 1]
                    for one, row in zip(seen, rows):
                        new = jnp.maximum(new, jnp.where(one, jnp.max(row, axis=0, keepdims=True), MASKED))
                    scores.append(rows)
                    most.append(new)
                for head in range(3):
                    total = acc_ref[query_at, head] * jnp.exp(m_ref[query_at, head : head + 1] - most[head])
                    for segment, row, off in zip(segments, scores[head], far):
                        probs = jnp.exp(row - (most[head] + off)).astype(BF16)
                        total += mm(vt_ref[segment, key_at, head], probs)
                    made.append(total)
                for head in range(3):
                    m_ref[query_at, head : head + 1] = most[head]
                    acc_ref[query_at, head] = made[head]

            length = c + 1 + half * (3 - 2 * c)

            @pl.loop(0, length // 2)
            def _(two):
                visit((2 * two, 2 * two + 1))

            @pl.when(length % 2 == 1)
            def _():
                visit((length - 1,))

            if step == 3:
                for n in range(1, len(ride.hops)):
                    pl.when(item == 9 + 2 * n)(functools.partial(ride.one_hop, n))

    project(0)
    for step in range(1, 4):

        @pl.when(t - step >= 0)
        def _():
            arrived(t - step)

            @pl.when(t < 3)
            def _():
                right(xg_ref.at[t - step], t - step, step).start()

        @pl.when(t + step <= 3)
        def _():
            arrived(t + step)

            @pl.when(t > 0)
            def _():
                left(xg_ref.at[t + step], t + step, step).start()

        project(step)
        if step == 2:
            ride.turn()
        if step == 3:
            ride.start_late()
            ride.chain()
            ride.put(xg_ref)
        complete(step - 1)
        items(step - 1)
    complete(3)
    if ride.hops:
        ride.one_hop(0)
    ride.turn()
    ride.chain_turn()
    ride.put(qw_ref, kv_ref)
    items(3)
    for quarter in range(4):
        whole = [acc_ref[quarter, head, 64:65] for head in range(3)]
        parts = [acc_ref[quarter, head, 0:64] / whole[head] for head in range(3)]
        for at, pair in ((0, parts[0:2]), (128, [parts[2], jnp.zeros_like(parts[2])])):
            turned = jnp.transpose(jnp.concatenate(pair, axis=0), (1, 0)).astype(BF16)
            o_ref[quarter, :, at : min(at + 128, 192)] = turned[:, : min(128, 192 - at)]
        for head in range(3):
            lse_ref[quarter, head : head + 1] = m_ref[quarter, head : head + 1] + jnp.log(whole[head])
        lse_ref[quarter, 3:8] = jnp.zeros((5, 256), F32)
    ride.put(o_ref, lse_ref)
    for chunk in range(4):
        mate(chunk).wait_send()
        across(chunk).wait_send()
        onward(chunk).wait_send()
    for slot in range(2):
        partner(slot).wait_send()

    @pl.when(t < 3)
    def _():
        right(x_ref, t, 0).wait_send()

    @pl.when(t > 0)
    def _():
        left(x_ref, t, 0).wait_send()

    for step in (1, 2):

        @pl.when((t - step >= 0) & (t < 3))
        def _():
            right(xg_ref.at[t - step], t - step, step).wait_send()

        @pl.when((t + step <= 3) & (t > 0))
        def _():
            left(xg_ref.at[t + step], t + step, step).wait_send()

    if fetch:
        for k in range(1, size):
            weight(k).wait_send()
    ride.finish()


def inner(x, w, b, flags, cid, riders=(), fetch=False):
    outs = [
        sds(4, 256, 768), sds(4, 256, 256), sds(4, 4, 256, 384), sds(4, 256, 192), sds(4, 8, 256, dtype=F32),
    ]
    scratch = [
        pltpu.VMEM((2, 256, 256), BF16),
        pltpu.VMEM((3, 4, 256, 128), BF16), pltpu.VMEM((4, 8, 256), F32), pltpu.VMEM((4, 3, 80, 256), F32),
        pltpu.VMEM((4, 4, 3, 80, 256), BF16),
        dma(4), dma(3), dma(3),
        dma(4), dma(4), dma(4), dma(4), dma(4), dma(4), dma(2), dma(2),
    ]
    if fetch:
        size = lax.axis_size("fsdp")
        outs.append(sds(size, *w.shape))
        scratch = [dma(size - 1), dma(size - 1)] + scratch
    cost = (2 * 1024 * 768 * 640 + 5 * 512 * 1024 * 64 * 12, 14 << 20, 5 * 512 * 1024 * 3)
    kernel = functools.partial(inner_kernel, fetch)
    res, ridden = call(kernel, (flags, x, w, b), outs, scratch, cid, "inner", cost, riders, smem=(0,))
    full = res[5].reshape(768, 640) if fetch else w
    xg, qw, kv, o, lse = res[:5]
    return (
        xg.reshape(1024, 768), qw.reshape(1024, 256), kv.reshape(4, 1024, 384),
        o.reshape(1024, 192), lse, full, ridden,
    )


def norm_stats(summed):
    row_mean = jnp.mean(summed, axis=-1, keepdims=True)
    centered = summed - row_mean
    variance = jnp.mean(centered * centered, axis=-1, keepdims=True)
    scale = lax.rsqrt(variance + EPSILON)
    return centered * scale, scale


def norm_back(grad, xhat, scale, gain):
    scaled = grad * gain
    first = jnp.mean(scaled, axis=-1, keepdims=True)
    second = jnp.mean(scaled * xhat, axis=-1, keepdims=True)
    return scale * (scaled - first - xhat * second)


def gelu_both(up):
    phi = 0.5 * (1.0 + lax.erf(up * 0.7071067811865476))
    slope = phi + up * jnp.exp(-0.5 * up * up) * 0.3989422804014327
    return (up * phi).astype(BF16), slope.astype(BF16)


PIECE = 128


def exchange(c, ref, feed, mine_ref, part_ref, send_ref, got_ref, a_send, a_recv, s_send, s_recv, meanwhile):
    mate, across, far = mate_of(c), across_of(c), 3 - c
    pieces = (pl.ds(0, PIECE), pl.ds(PIECE, PIECE))

    def gather(slot, index, p, device):
        part = ref.at[slot, pieces[p]]
        return rcopy(part, part, a_send.at[index, p], a_recv.at[index, p], {"ctx": device})

    def scatter(index, p, device):
        source, target = send_ref.at[index, pieces[p]], got_ref.at[index, pieces[p]]
        return rcopy(source, target, s_send.at[index, p], s_recv.at[index, p], {"ctx": device})

    for p in range(2):
        gather(c, 1, p, across).start()
    for p in range(2):
        gather(c, 0, p, mate).start()
    mine_ref[...] += feed(c, pl.ds(0, 2 * PIECE))
    for p in range(2):
        gather(mate, 0, p, mate).wait_recv()
    send_ref[0] = feed(mate, pl.ds(0, 2 * PIECE)).astype(BF16)
    for p in range(2):
        scatter(0, p, mate).start()

    def take_across(p):
        gather(across, 1, p, across).wait_recv()
        gather(across, 2, p, mate).start()
        part_ref[pieces[p]] = feed(across, pieces[p])

    def take_far(p):
        gather(far, 2, p, mate).wait_recv()
        send_ref[1, pieces[p]] = feed(far, pieces[p]).astype(BF16)
        scatter(1, p, mate).start()

    def join(p):
        scatter(1, p, mate).wait_recv()
        send_ref[2, pieces[p]] = (part_ref[pieces[p]] + got_ref[1, pieces[p]].astype(F32)).astype(BF16)
        scatter(2, p, across).start()

    take_across(0)
    take_far(0)
    take_across(1)
    join(0)
    take_far(1)
    join(1)
    meanwhile()
    for p in range(2):
        scatter(0, p, mate).wait_recv()
        scatter(2, p, across).wait_recv()

    def settle():
        for p in range(2):
            for index in range(3):
                gather(c, index, p, mate).wait_send()
                scatter(index, p, mate).wait_send()

    return mine_ref[...] + got_ref[0].astype(F32) + got_ref[2].astype(F32), settle


def block_kernel(
    ride, o_ref, wo_ref, w1_ref, w2_ref, b1_ref, vec_ref, stream_ref,
    out_ref, low_ref, xhat1_ref, r1_ref, xhat2_ref, r2_ref, xg_ref, act_ref, slope_ref, rows_ref, down_ref,
    w_send, w_recv, mine_ref, part_ref, send_ref, got_ref, o_send, o_recv, a_send, a_recv, s_send, s_recv,
):
    c = lax.axis_index("ctx")
    t = lax.axis_index("tp")
    barrier = pltpu.get_barrier_semaphore()
    for place in range(4):

        @pl.when((t % 2 == 0) & (t != place))
        def _():
            signal(barrier, {"tp": place})

        @pl.when(t % 2 == 1)
        def _():
            signal(barrier, {"ctx": 3 - c, "tp": place})

    signal(barrier, {"ctx": mate_of(c)})
    signal(barrier, {"ctx": across_of(c)})
    f, size = lax.axis_index("fsdp"), lax.axis_size("fsdp")
    for k in range(1, size):
        signal(barrier, {"fsdp": (f + size - k) % size})
    count = 5 + t % 2 + size - 1 + ride.greet(barrier)
    ride.ready()
    pl.semaphore_wait(barrier, count)

    def weight(k):
        device = {"fsdp": (f + k) % size}
        return rcopy(w2_ref, down_ref.at[f], w_send.at[k - 1], w_recv.at[k - 1], device)

    def give(quarter):
        device = {"tp": quarter} if quarter % 2 == 0 else {"ctx": 3 - c, "tp": quarter}
        return rcopy(o_ref.at[quarter], rows_ref.at[t], o_send.at[quarter], o_recv.at[t], device)

    def given(group):
        rcopy(rows_ref.at[group], rows_ref.at[group], o_send.at[0], o_recv.at[group], {"tp": t}).wait_recv()

    for quarter in (3, 2, 1, 0):
        if quarter % 2 == 0:

            @pl.when(t != quarter)
            def _():
                give(quarter).start()

            @pl.when(t == quarter)
            def _():
                rows_ref[quarter] = o_ref[quarter]

        else:
            give(quarter).start()
    for k in range(1, size):
        weight(k).start()
    down_ref[f] = w2_ref[...]
    branch = stream_ref[...] + vec_ref[0:1]
    for group in range(4):

        @pl.when((t % 2 == 1) | (t != group))
        def _():
            given(group)

        branch += mm_nt(rows_ref[group], wo_ref[group])
    ride.start()
    xhat, scale = norm_stats(branch)
    xhat1_ref[...] = xhat
    r1_ref[...] = jnp.broadcast_to(scale, r1_ref.shape)
    normed = xhat * vec_ref[2:3] + vec_ref[3:4]
    xg_ref[c] = normed.astype(BF16)
    mine_ref[...] = normed + vec_ref[1:2]
    for k in range(1, size):
        weight(k).wait_recv()

    def feed(segment, rows):
        up = mm(xg_ref[segment, rows], w1_ref[...]) + b1_ref[...]
        act, slope = gelu_both(up)
        act_ref[segment, rows] = act
        slope_ref[segment, rows] = slope
        return mm_nt(act, down_ref[...].reshape(768, 768))

    def meanwhile():
        ride.turn()
        ride.put(xhat1_ref, r1_ref, xg_ref, act_ref, slope_ref, rows_ref, down_ref)

    summed, settle = exchange(
        c, xg_ref, feed, mine_ref, part_ref, send_ref, got_ref, a_send, a_recv, s_send, s_recv, meanwhile
    )
    xhat, scale = norm_stats(summed)
    xhat2_ref[...] = xhat
    r2_ref[...] = jnp.broadcast_to(scale, r2_ref.shape)
    out = xhat * vec_ref[4:5] + vec_ref[5:6]
    out_ref[...] = out
    low_ref[...] = out.astype(BF16)
    ride.put(out_ref, low_ref, xhat2_ref, r2_ref)
    for quarter in range(4):
        if quarter % 2 == 0:

            @pl.when(t != quarter)
            def _():
                give(quarter).wait_send()

        else:
            give(quarter).wait_send()
    for k in range(1, size):
        weight(k).wait_send()
    settle()
    ride.finish()


def block(o, wo, w1, w2, b1, vecs, stream, cid, riders=()):
    size = lax.axis_size("fsdp")
    f = functools.partial(sds, dtype=F32)
    outs = [
        f(256, 768), sds(256, 768), f(256, 768), f(256, 128), f(256, 768), f(256, 128),
        sds(4, 256, 768), sds(4, 256, 768), sds(4, 256, 768), sds(4, 256, 192), sds(size, *w2.shape),
    ]
    scratch = [
        dma(size - 1), dma(size - 1),
        pltpu.VMEM((256, 768), F32),
        pltpu.VMEM((256, 768), F32),
        pltpu.VMEM((3, 256, 768), BF16),
        pltpu.VMEM((3, 256, 768), BF16),
        dma(4), dma(4), dma(3, 2), dma(3, 2), dma(3, 2), dma(3, 2),
    ]
    cost = (2 * 256 * 768 * 768 + 4 * 1024 * 768 * 768, 16 << 20, 1 << 20)
    operands = (o.reshape(4, 256, 192), wo, w1, w2, b1, vecs, stream)
    res, ridden = call(block_kernel, operands, outs, scratch, cid, "block", cost, riders)
    flat = lambda a: a.reshape(1024, 768)
    return tuple(res[:6]) + (flat(res[6]), flat(res[7]), flat(res[8]), res[9], res[10].reshape(768, 768), ridden)


def block_back_kernel(
    ride, grad_ref, xhat2_ref, r2_ref, xhat1_ref, r1_ref, vec_ref, slope_ref, w1_ref, w2_ref, wo_ref,
    xg_ref, act_ref, rows_ref, back_ref, do_ref, stat_ref, dup_ref, ddown_ref, dout_ref,
    w_send, w_recv, term_ref, all_up_ref, gg_ref, gu_ref, mine_ref, part_ref, send_ref, got_ref, dsend_ref, d_send, d_recv, a_send, a_recv, s_send, s_recv,
):
    c = lax.axis_index("ctx")
    t = lax.axis_index("tp")
    barrier = pltpu.get_barrier_semaphore()
    for place in range(4):
        if place % 2 == 0:

            @pl.when(t != place)
            def _():
                signal(barrier, {"tp": place})

        else:
            signal(barrier, {"ctx": 3 - c, "tp": place})
    signal(barrier, {"ctx": mate_of(c)})
    signal(barrier, {"ctx": across_of(c)})
    f, size = lax.axis_index("fsdp"), lax.axis_size("fsdp")
    depth = dup_ref.shape[0]
    for k in range(1, size):
        signal(barrier, {"fsdp": (f + size - k) % size})
    count = 5 + t % 2 + size - 1 + ride.greet(barrier)
    ride.ready()
    pl.semaphore_wait(barrier, count)

    def row(values):
        return jnp.sum(values, axis=0, keepdims=True)

    grad = grad_ref[...]
    back_two = norm_back(grad, xhat2_ref[...], r2_ref[:, 0:1], vec_ref[4:5])
    g2 = back_two.astype(BF16)
    gg_ref[c] = g2
    mine_ref[...] = back_two
    ride.start()
    stat_ref[1:2] = row(grad * xhat2_ref[...])
    stat_ref[3:4] = row(grad)
    stat_ref[5:6] = row(g2.astype(F32))
    stat_ref[6:8] = jnp.zeros((2, 768), F32)

    def feed(segment, rows):
        gu = (mm(gg_ref[segment, rows], w2_ref[...]) * slope_ref[segment, rows].astype(F32)).astype(BF16)
        gu_ref[segment, rows] = gu
        stat_ref[6:7] += row(gu.astype(F32))
        return mm_nt(gu, w1_ref[...])

    tall = lambda ref: ref[...].reshape(1024, 768)

    def slice_of(place):
        return pl.ds(pl.multiple_of(place * depth, depth), depth)

    def term(k):
        to = (f + k) % size
        return rcopy(
            all_up_ref.at[slice_of(to)], term_ref.at[k - 1], w_send.at[k - 1], w_recv.at[k - 1], {"fsdp": to}
        )

    def meanwhile():
        @pl.loop(0, 3)
        def _(tile):
            cols = pl.ds(pl.multiple_of(tile * 256, 256), 256)
            all_up_ref[cols] = mm_tn(xg_ref[:, cols], tall(gu_ref)).astype(BF16)

        for k in range(1, size):
            term(k).start()

        @pl.loop(0, 3)
        def _(tile):
            cols = pl.ds(pl.multiple_of(tile * 256, 256), 256)
            ddown_ref[cols] = mm_tn(gg_ref[:, :, cols].reshape(1024, 256), act_ref[...]).astype(BF16)

        ride.put(ddown_ref)
        ride.turn()

    grad_normed, settle = exchange(
        c, gg_ref, feed, mine_ref, part_ref, send_ref, got_ref, a_send, a_recv, s_send, s_recv, meanwhile
    )
    back_one = norm_back(grad_normed, xhat1_ref[...], r1_ref[:, 0:1], vec_ref[2:3])
    back_ref[...] = back_one
    g1 = back_one.astype(BF16)

    def give_near(group):
        return rcopy(dsend_ref.at[group], do_ref.at[t], d_send.at[group], d_recv.at[t], {"tp": group})

    def give_far(group):
        return rcopy(dsend_ref.at[group], do_ref.at[t], d_send.at[group], d_recv.at[t], {"ctx": 3 - c, "tp": group})

    for group in range(4):
        dsend_ref[group] = mm(g1, wo_ref[group]).astype(BF16)

        @pl.when((t % 2 == 0) & (t == group))
        def _():
            do_ref[t] = dsend_ref[group]

        @pl.when((t % 2 == 0) & (t != group))
        def _():
            give_near(group).start()

        @pl.when(t % 2 == 1)
        def _():
            give_far(group).start()

    stat_ref[0:1] = row(grad_normed * xhat1_ref[...])
    stat_ref[2:3] = row(grad_normed)
    stat_ref[4:5] = row(g1.astype(F32))
    for group in range(4):
        dout_ref[group] = mm_tn(g1, rows_ref[group]).astype(BF16)
    ride.put(back_ref, stat_ref, dout_ref)
    ride.chain()
    total = all_up_ref[slice_of(f)].astype(F32)
    for k in range(1, size):
        term(k).wait_recv()
        total += term_ref[k - 1].astype(F32)
    dup_ref[...] = total.astype(BF16)
    ride.put(dup_ref)
    for quarter in range(4):

        def taken():
            rcopy(do_ref.at[quarter], do_ref.at[quarter], d_send.at[0], d_recv.at[quarter], {"tp": t}).wait_recv()

        if quarter % 2 == 0:
            pl.when(t != quarter)(taken)
        else:
            taken()
    for group in range(4):

        @pl.when((t % 2 == 1) | (t != group))
        def _():
            give_near(group).wait_send()

    ride.chain_turn()
    for k in range(1, size):
        term(k).wait_send()
    settle()
    ride.finish()


def block_back(grad, xhat2, r2, xhat1, r1, vecs, slope, w1, w2, wo, xg, act, rows, cid, riders=()):
    f = functools.partial(sds, dtype=F32)
    size = lax.axis_size("fsdp")
    depth = 768 // size
    outs = [
        f(256, 768), sds(4, 256, 192), f(8, 768), sds(depth, 768), sds(768, 768), sds(4, 768, 192),
    ]
    scratch = [
        dma(size - 1), dma(size - 1), pltpu.VMEM((size - 1, depth, 768), BF16), pltpu.VMEM((768, 768), BF16),
        pltpu.VMEM((4, 256, 768), BF16),
        pltpu.VMEM((4, 256, 768), BF16),
        pltpu.VMEM((256, 768), F32),
        pltpu.VMEM((256, 768), F32),
        pltpu.VMEM((3, 256, 768), BF16),
        pltpu.VMEM((3, 256, 768), BF16),
        pltpu.VMEM((4, 256, 192), BF16),
        dma(4), dma(4), dma(3, 2), dma(3, 2), dma(3, 2), dma(3, 2),
    ]
    cost = (4 * 256 * 768 * 768 + 8 * 1024 * 768 * 768, 20 << 20, 1 << 10)
    operands = (grad, xhat2, r2, xhat1, r1, vecs, slope.reshape(4, 256, 768), w1, w2, wo, xg, act, rows)
    res, ridden = call(block_back_kernel, operands, outs, scratch, cid, "block_back", cost, riders)
    back, do, stats, d_up, d_down, d_out = res
    return back, do.reshape(1024, 192), stats, d_up, d_down, d_out, ridden


def inner_back_kernel(
    ride, flag_ref, qw_ref, kv_ref, do_ref, o_ref, lse_ref, w_ref, back_ref, xg_ref, mark_ref,
    grad_ref, low_ref, din_ref, sum_out_ref, mem_ref,
    qm_ref, dm_ref, row_ref, acc_ref, wide_ref, dkv_ref, dqs_ref,
    w_send, w_recv, term_ref, all_in_ref, dq_ref, own_ref, part_ref,
    near_ref, join_ref, sum_ref, far_ref, pass_ref, take_ref,
    q_send, q_recv, n_send, n_recv, j_send, j_recv, f_send, f_recv, p_send, p_recv,
):
    c = lax.axis_index("ctx")
    t = lax.axis_index("tp")
    f, size = lax.axis_index("fsdp"), lax.axis_size("fsdp")
    depth = din_ref.shape[0]
    mate, across, far = mate_of(c), across_of(c), 3 - c
    barrier = pltpu.get_barrier_semaphore()
    for device in (mate, across, far):
        signal(barrier, {"ctx": device})

    @pl.when(t > 0)
    def _():
        signal(barrier, {"tp": t - 1})

    @pl.when(t < 3)
    def _():
        signal(barrier, {"tp": t + 1})

    for k in range(1, size):
        signal(barrier, {"fsdp": (f + size - k) % size})
    ends = (t // 3) + (3 - t) // 3
    count = 5 - ends + size - 1 + ride.greet(barrier)
    ride.ready()

    low = lax.broadcasted_iota(jnp.int32, (1024, 128), 1) < 64
    pair = qw_ref[:, 0:128]
    none = jnp.zeros_like(pair)
    qm_ref[0] = jnp.where(low, pair, none)
    qm_ref[1] = jnp.where(low, none, pair)
    qm_ref[2] = qw_ref[:, 128:256]
    pair = do_ref[:, 0:128]
    dm_ref[0] = jnp.where(low, pair, none)
    dm_ref[1] = jnp.where(low, none, pair)
    dm_ref[2] = jnp.concatenate([do_ref[:, 128:192], none[:, :64]], axis=1)
    product = do_ref[...].astype(F32) * o_ref[...].astype(F32)
    head_row = lax.broadcasted_iota(jnp.int32, (8, 192), 0)
    head_of = lax.broadcasted_iota(jnp.int32, (8, 192), 1) // 64
    delta = lax.dot_general(
        (head_row == head_of).astype(F32), product, (((1,), (1,)), ((), ())),
        precision=lax.Precision.HIGHEST, preferred_element_type=F32,
    )
    for quarter in range(4):
        row_ref[quarter, 0:8] = lse_ref[quarter]
        row_ref[quarter, 8:16] = delta[:, quarter * 256 : (quarter + 1) * 256]
    acc_ref[...] = jnp.zeros_like(acc_ref)
    wide_ref[...] = jnp.zeros_like(wide_ref)
    pl.semaphore_wait(barrier, count)
    ride.start()

    def partner(slot):
        return rcopy(dqs_ref.at[slot], dq_ref.at[2 * slot + 1], q_send.at[slot], q_recv.at[slot], {"ctx": far})

    def near(chunk):
        return rcopy(dkv_ref.at[mate, chunk], near_ref.at[chunk], n_send.at[chunk], n_recv.at[chunk], {"ctx": mate})

    def join(chunk):
        return rcopy(dkv_ref.at[far, chunk], join_ref.at[chunk], j_send.at[chunk], j_recv.at[chunk], {"ctx": mate})

    def cross(chunk):
        return rcopy(sum_ref.at[chunk], far_ref.at[chunk], f_send.at[chunk], f_recv.at[chunk], {"ctx": across})

    pieces = (pl.ds(0, PIECE), pl.ds(PIECE, PIECE))

    def onward(side, chunk, p):
        return rcopy(
            pass_ref.at[chunk, pieces[p]], take_ref.at[side, chunk, pieces[p]],
            p_send.at[chunk, p], p_recv.at[side, chunk, p], {"tp": t - 1 + 2 * side},
        )

    def passed(side, chunk, p):
        part = take_ref.at[side, chunk, pieces[p]]
        rcopy(part, part, p_send.at[0, p], p_recv.at[side, chunk, p], {"tp": t}).wait_recv()

    chunks = [ordered(t, 3 - k) for k in range(4)]
    at_end = (t == 0) | (t == 3)

    def leave(k):
        chunk = chunks[k]
        dkv_ref[:, chunk] = wide_ref[:, chunk].astype(BF16)
        join(chunk).start()
        near(chunk).start()
        query = (acc_ref[chunk].astype(BF16).astype(F32) * 0.125).astype(BF16)

        @pl.when(chunk % 2 == 0)
        def _():
            dq_ref[chunk] = query

        @pl.when(chunk % 2 == 1)
        def _():
            dqs_ref[chunk // 2] = query
            partner(chunk // 2).start()

    def go_across(k):
        chunk = chunks[k]
        join(chunk).wait_recv()
        sum_ref[chunk] = (dkv_ref[across, chunk].astype(F32) + join_ref[chunk].astype(F32)).astype(BF16)
        cross(chunk).start()

    def gather_up(k):
        chunk = chunks[k]
        if k < 3:

            @pl.when(chunk % 2 == 1)
            def _():
                partner(chunk // 2).wait_recv()

        near(chunk).wait_recv()
        cross(chunk).wait_recv()
        own = (
            dkv_ref[c, chunk].astype(F32) + near_ref[chunk].astype(F32) + far_ref[chunk].astype(F32)
        ).astype(BF16)
        own_ref[chunk] = own
        part_ref[chunk] = mm_nt(dq_ref[chunk], w_ref[:, 0:256]) + mm_nt(own, w_ref[:, 256:640])

    def relay(k):
        chunk = chunks[k]

        def move(side, first):
            for p in range(2):

                @pl.when(jnp.logical_not(first))
                def _():
                    passed(side, chunk, p)
                    total = part_ref[chunk, pieces[p]] + take_ref[side, chunk, pieces[p]].astype(F32)
                    pass_ref[chunk, pieces[p]] = total.astype(BF16)

                @pl.when(first)
                def _():
                    pass_ref[chunk, pieces[p]] = part_ref[chunk, pieces[p]].astype(BF16)

                onward(side, chunk, p).start()

        @pl.when(chunk < t)
        def _():
            move(0, t == 3)

        @pl.when(chunk > t)
        def _():
            move(1, t == 0)

    def relay_ends(k):
        pl.when(at_end)(functools.partial(relay, k))

    def relay_inner(k):
        pl.when(jnp.logical_not(at_end))(functools.partial(relay, k))

    low_keys = lax.broadcasted_iota(jnp.int32, (256, 128), 1) < 64

    def one_item(item, done):
        phase = (item + 9) // 16 + (item + 4) // 16 + (item + 1) // 16
        number = item - phase * (8 - phase)
        second = number // (4 - phase)
        query_at = ordered_by(t, 3 - (phase + second * (number - 3 + phase)))
        key_at = ordered_by(t, 3 - (phase + (1 - second) * number))
        half = query_at % 2
        rows = pl.ds(pl.multiple_of(query_at * 256, 256), 256)

        def visit(segments):
            queries = [qm_ref[head, rows] for head in range(3)]
            grads = [dm_ref[head, rows] for head in range(3)]
            made = []
            for segment in segments:
                penalty = jnp.where(flag_ref[half, segment] > 0, 0.0, FAR)
                key_pair = kv_ref[segment, key_at, :, 0:128]
                mixed = kv_ref[segment, key_at, :, 128:256]
                value_pair = kv_ref[segment, key_at, :, 256:384]
                for head in range(3):
                    shift = row_ref[query_at, head : head + 1] + penalty
                    prob = jnp.exp(mm_nt(key_pair if head < 2 else mixed, queries[head]) - shift)
                    grad_prob = mm_nt(value_pair if head < 2 else mixed, grads[head])
                    grad_score = (prob * (grad_prob - row_ref[query_at, 8 + head : 9 + head])).astype(BF16)
                    made.append((prob.astype(BF16), grad_score))
            pair_sum, mixed_sum = 0.0, 0.0
            for number, segment in enumerate(segments):
                (p0, g0), (p1, g1), (p2, g2) = made[3 * number : 3 * number + 3]
                for_keys = mm(g0, queries[0]) + mm(g1, queries[1])
                for_mixed = mm(g2, queries[2]) + mm(p2, grads[2])
                for_values = mm(p0, grads[0]) + mm(p1, grads[1])
                wide_ref[segment, key_at] += jnp.concatenate([for_keys, for_mixed, for_values], axis=1)
                key_pair = kv_ref[segment, key_at, :, 0:128]
                nothing = jnp.zeros_like(key_pair)
                pair_sum += mm_tn(g0, jnp.where(low_keys, key_pair, nothing))
                pair_sum += mm_tn(g1, jnp.where(low_keys, nothing, key_pair))
                mixed_sum += mm_tn(g2, jnp.where(low_keys, nothing, kv_ref[segment, key_at, :, 128:256]))
            acc_ref[query_at] += jnp.concatenate([pair_sum, mixed_sum], axis=1)

        length = c + 1 + half * (3 - 2 * c)

        @pl.loop(0, length // 2)
        def _(two):
            visit((2 * two, 2 * two + 1))

        @pl.when(length % 2 == 1)
        def _():
            visit((length - 1,))

        now = done + length

        def at(place, action, k):
            pl.when(item == place)(functools.partial(action, k))

        def once(amount, action, k):
            pl.when((done < amount) & (now >= amount))(functools.partial(action, k))

        for n in range(len(ride.hops)):
            once(RIDE_HOPS[n], ride.one_hop, n)
        ride.turn_when((done < 14) & (now >= 14))
        for k, place in enumerate((6, 11, 14)):
            at(place, leave, k)
        once(24, go_across, 0)
        once(31, gather_up, 0)
        once(31, relay_ends, 0)
        once(32, go_across, 1)
        once(38, gather_up, 1)
        once(38, relay_ends, 1)
        return now

    lax.fori_loop(0, 16, one_item, 0)
    leave(3)
    go_across(2)
    relay_inner(0)
    go_across(3)
    gather_up(2)
    relay_ends(2)
    relay_inner(1)

    def slice_of(place):
        return pl.ds(pl.multiple_of(place * depth, depth), depth)

    spans = (pl.ds(0, 256), pl.ds(256, 256), pl.ds(512, 128))

    def term(k, span):
        to, cols = (f + k) % size, spans[span]
        return rcopy(
            all_in_ref.at[slice_of(to), cols], term_ref.at[k - 1, :, cols],
            w_send.at[k - 1, span], w_recv.at[k - 1, span], {"fsdp": to},
        )


    @pl.when(t % 2 == 1)
    def _():
        partner(t // 2).wait_recv()

    query = dq_ref[...].reshape(1024, 256)
    for span in range(3):
        if span == 0:
            ride.chain()
        if span == 1:
            relay_inner(2)
            gather_up(3)
            ride.chain_turn()
        own = own_ref[...].reshape(1024, 384)
        made = (query, own[:, 0:256], own[:, 256:384])[span]
        all_in_ref[:, spans[span]] = mm_tn(xg_ref[...], made).astype(BF16)
        for k in range(1, size):
            term(k, span).start()

    sum_out_ref[0:1, 0:256] = jnp.sum(query.astype(F32), axis=0, keepdims=True)
    sum_out_ref[0:1, 256:640] = jnp.sum(own.astype(F32), axis=0, keepdims=True)
    ride.put(sum_out_ref)
    grad_ref[...] = part_ref[t] + back_ref[...]

    for side, there in ((0, t < 3), (1, t > 0)):

        @pl.when(there)
        def _():
            for p in range(2):
                passed(side, t, p)
                grad_ref[pieces[p]] += take_ref[side, t, pieces[p]].astype(F32)

    low_ref[...] = grad_ref[...].astype(BF16)
    ride.put(grad_ref, low_ref)
    mem_ref[...] = lax.dot_general(
        mark_ref[...], grad_ref[...], (((0,), (0,)), ((), ())),
        precision=lax.Precision.HIGHEST, preferred_element_type=F32,
    )
    ride.put(mem_ref)
    total = all_in_ref[slice_of(f)].astype(F32)
    for k in range(1, size):
        for span in range(3):
            term(k, span).wait_recv()
        total += term_ref[k - 1].astype(F32)
    din_ref[...] = total.astype(BF16)
    ride.put(din_ref)
    for k in range(1, size):
        for span in range(3):
            term(k, span).wait_send()
    for chunk in range(4):
        join(chunk).wait_send()
        near(chunk).wait_send()
        cross(chunk).wait_send()

        @pl.when(t != chunk)
        def _():
            for p in range(2):
                onward(1, chunk, p).wait_send()

    for slot in range(2):
        partner(slot).wait_send()
    ride.finish()


RIDE_HOPS = (8, 11, 14, 17)


def inner_back(qw, kv, do, o, lse, flags, w, back_one, xg, marks, cid, riders=()):
    size = lax.axis_size("fsdp")
    depth = 768 // size
    f = functools.partial(sds, dtype=F32)
    outs = [f(256, 768), sds(256, 768), sds(depth, 640), f(8, 640), f(marks.shape[1], 768)]
    scratch = [
        pltpu.VMEM((3, 1024, 128), BF16), pltpu.VMEM((3, 1024, 128), BF16), pltpu.VMEM((4, 16, 256), F32),
        pltpu.VMEM((4, 256, 256), F32), pltpu.VMEM((4, 4, 256, 384), F32), pltpu.VMEM((4, 4, 256, 384), BF16),
        pltpu.VMEM((2, 256, 256), BF16),
        dma(size - 1, 3), dma(size - 1, 3), pltpu.VMEM((size - 1, depth, 640), BF16), pltpu.VMEM((768, 640), BF16),
        pltpu.VMEM((4, 256, 256), BF16), pltpu.VMEM((4, 256, 384), BF16),
        pltpu.VMEM((4, 256, 768), F32),
        pltpu.VMEM((4, 256, 384), BF16), pltpu.VMEM((4, 256, 384), BF16),
        pltpu.VMEM((4, 256, 384), BF16), pltpu.VMEM((4, 256, 384), BF16),
        pltpu.VMEM((4, 256, 768), BF16), pltpu.VMEM((2, 4, 256, 768), BF16),
        dma(2), dma(2), dma(4), dma(4), dma(4), dma(4), dma(4), dma(4), dma(4, 2), dma(2, 4, 2),
    ]
    cost = (5 * 512 * 1024 * 64 * 30 + 4 * 1024 * 768 * 640, 16 << 20, 5 * 512 * 1024 * 3)
    operands = (flags, qw, kv.reshape(4, 4, 256, 384), do, o, lse, w, back_one, xg, marks)
    res, ridden = call(inner_back_kernel, operands, outs, scratch, cid, "inner_back", cost, riders, smem=(0,))
    return (*res[:3], res[3][0], res[4], ridden)


def ancestry(parent_row):
    seg_count = parent_row.shape[0]
    segment_ids = jnp.arange(seg_count, dtype=jnp.int32)
    parent_hop = (parent_row[:, None] == segment_ids[None, :]).astype(jnp.int32)
    reached = (segment_ids[:, None] == segment_ids[None, :]).astype(jnp.int32)
    on_path = reached
    for hop_number in range(seg_count - 1):
        reached = jnp.dot(reached, parent_hop)
        on_path = jnp.maximum(on_path, reached)
    return on_path


def joined(query, key, value, gap):
    return jnp.concatenate(
        [
            query[..., :128], gap, query[..., 128:],
            key[..., :128], value[..., 128:], key[..., 128:], value[..., :128],
        ],
        axis=-1,
    )


def parted(grads):
    query = jnp.concatenate([grads[..., :128], grads[..., 192:256]], axis=-1)
    key = jnp.concatenate([grads[..., 256:384], grads[..., 448:512]], axis=-1)
    value = jnp.concatenate([grads[..., 512:640], grads[..., 384:448]], axis=-1)
    return query, key, value


def added(terms, axes=(0,)):
    return jnp.sum(terms.astype(F32), axis=axes)


def low(values):
    return values.astype(BF16)


def shards(
    hidden, cotangent, mem_pos, parents, memory, wq, wk, wv, wo, w1, w2,
    head_bias, ffn_bias, out_bias, norm_gains, norm_shifts,
):
    c = lax.axis_index("ctx")
    t = lax.axis_index("tp")
    size = lax.axis_size("fsdp")
    layers = wq.shape[0]
    share = hidden.shape[0]
    depth = wq.shape[1]
    piece = depth // 4
    positions = t * share + jnp.arange(share, dtype=jnp.int32)
    marks = (mem_pos[0, 0][None, :] == positions[:, None]).astype(F32)
    stream = hidden.astype(F32) + jnp.dot(
        marks, memory, precision=lax.Precision.HIGHEST, preferred_element_type=F32
    )
    on_path = ancestry(parents[0])
    ids = jnp.arange(4, dtype=jnp.int32)
    pick = lambda seg: jnp.sum(on_path * (ids == seg).astype(jnp.int32)[:, None], axis=0)
    flags = jnp.stack([pick(c), pick(3 - c)])

    gap = jnp.zeros(wq.shape[:2] + (64,), BF16)
    own_in = joined(wq, wk, wv, gap)
    none = jnp.zeros((layers, 192), F32)
    in_bias = joined(head_bias[:, 0], none, head_bias[:, 1], jnp.zeros((layers, 64), F32))
    down_turned = jnp.swapaxes(w2, 1, 2)
    out_turned = jnp.swapaxes(wo, 1, 2).reshape(layers, 4, piece, 192)
    out_piece = lax.dynamic_index_in_dim(out_turned, c, axis=1, keepdims=False)

    def vectors(n):
        norms = [norm_gains[n, 0], norm_shifts[n, 0], norm_gains[n, 1], norm_shifts[n, 1]]
        return jnp.concatenate([out_bias[n], jnp.stack(norms), jnp.zeros((2, 768), F32)])

    saved, weights = [], []
    rounded = low(stream)
    riders = [plane_gather(out_piece[0], size), ctx_gather(sds(4, size, piece, 192), axis=2, first=0)]
    riders += [flip_gather(w1[0], size).later(), tp_flip(down_turned[0]).later(hopped=True), tp_flip(ffn_bias)]
    xg, qw, kv, o, lse, w_in, got = inner(rounded, own_in[0], in_bias[0][None], flags, 0, riders, fetch=True)
    _, out, w_up, down, units = got
    for n in range(layers):
        last = n == layers - 1
        w_out = out.reshape(4, 768, 192)
        w_up = w_up.reshape(768, 768)
        vecs = vectors(n)
        riders = []
        if not last:
            riders = [
                tp_flip(w1[n + 1]),
                plane_gather(out_piece[n + 1], size), fsdp_gather(own_in[n + 1], size),
            ]
        stream, rounded, xhat1, r1, xhat2, r2, xg2, act, slope, rows, w_down, got = block(
            o, w_out, w_up, down, units[n][None], vecs, stream, 16 * n + 2, riders
        )
        weights.append((w_in, w_up, w_down, w_out, vecs))
        saved.append((xg, qw, kv, o, lse, xhat1, r1, xhat2, r2, xg2, act, slope, rows))
        if not last:
            up, out, w_in = got
            riders = [ctx_gather(out, axis=2), tp_flip(down_turned[n + 1]).later(), fsdp_gather(up, size)]
            xg, qw, kv, o, lse, w_in, (out, down, w_up) = inner(
                rounded, w_in.reshape(768, 640), in_bias[n + 1][None], flags, 16 * n + 16, riders
            )
    output = rounded

    grad = cotangent.astype(F32)
    small, heads = [None] * layers, [None] * layers
    done = [None] * layers
    above = None
    for n in reversed(range(layers)):
        w_in, w_up, w_down, w_out, vecs = weights[n]
        xg, qw, kv, o, lse, xhat1, r1, xhat2, r2, xg2, act, slope, rows = saved[n]
        riders = []
        if above is not None:
            riders = [plane_scatter(above["out"], size), ctx_scatter(above["in"])]
            riders += [ctx_gather(sds(piece, 192), first=0, summed=True)]
            riders += [ctx_gather(sds(piece, 640), first=1, summed=True)]
        back_one, do, small[n], d_up, d_down, d_out, got = block_back(
            grad, xhat2, r2, xhat1, r1, vecs, slope, w_up, w_down, w_out, xg2, act, rows, 16 * n + 3, riders
        )
        quarters = sds(4, depth // 4, 768)
        riders = [
            tp_flip(d_up.reshape(quarters.shape)), scatter_flip(d_down.reshape(size, *quarters.shape)),
            ctx_scatter(d_out.reshape(4, size, 4, piece, 192), axis=2),
            ctx_scatter(quarters, first=0), ctx_scatter(quarters, first=1),
        ]
        if above is not None:
            done[n + 1] = tuple(got[2:4])
            riders += [ctx_gather(above["up"]), ctx_gather(above["down"])]
        grad, low_grad, d_in, sums, memory_part, got = inner_back(
            qw, kv, do, o, lse, flags, w_in, back_one, xg, marks, 16 * n + 4, riders
        )
        if above is not None:
            done[n + 1] = (done[n + 1][1], done[n + 1][0], got[5], got[6])
        d_query_bias, _, d_value_bias = parted(sums)
        heads[n] = jnp.stack([d_query_bias, d_value_bias])
        above = {
            "up": low(added(got[3])),
            "down": low(added(got[4])),
            "in": d_in.reshape(4, depth // 4, 640),
            "out": low(added(got[2])),
        }
    hidden_grad = low_grad
    small = jnp.stack(small)
    place = (ids == t).astype(F32)
    unit = (ids == flipped_place(c, t)).astype(F32)
    head_rows = (jnp.stack(heads)[:, :, None, :] * place[None, None, :, None]).reshape(2 * layers, 768)
    unit_rows = (small[:, 6][:, None, :] * unit[None, :, None]).reshape(4 * layers, 768)
    stat_rows = small[:, :6].reshape(6 * layers, 768)
    filled = 12 * layers + memory_part.shape[0]
    slices = 4 * size
    width = -(-filled // slices)
    rest = jnp.zeros((width * slices - filled, 768), F32)
    sums = jnp.concatenate([stat_rows, unit_rows, head_rows, memory_part, rest])
    sums = sums.reshape(4, size, width, 768)
    riders = [ctx_scatter(above["in"]), plane_scatter(above["out"], size), plane_scatter(sums, size)]
    riders += [ctx_gather(above["up"]).later(), ctx_gather(above["down"]).later()]
    riders += [ctx_gather(sds(piece, 640), first=0, summed=True), ctx_gather(sds(piece, 192), first=1, summed=True)]
    got = carry(riders + [small_sum(sds(width, 768, dtype=F32), size, first=2)], 6)[3:]
    done[0] = (got[2], got[3], got[0], got[1])
    totals = got[4].reshape(width * slices, 768)
    stats = totals[: 6 * layers].reshape(layers, 6, 768)
    at = 6 * layers
    ffn_rows = totals[at : at + 4 * layers].reshape(layers, 4, 768)
    ffn_grad = jnp.sum(ffn_rows * place[None, :, None], axis=1)
    at += 4 * layers
    head_sums = totals[at : at + 2 * layers].reshape(layers, 2, 4, 192)
    head_grad = jnp.sum(head_sums * place[None, None, :, None], axis=2)
    at += 2 * layers
    memory_grad = totals[at : at + memory_part.shape[0]]
    d_in = jnp.stack([part[0].reshape(depth, 640) for part in done]).astype(F32)
    d_out = jnp.stack([jnp.swapaxes(part[1].reshape(depth, 192), 0, 1) for part in done]).astype(F32)
    d_up = jnp.stack([part[2].reshape(depth, 768) for part in done]).astype(F32)
    d_down = jnp.stack([jnp.swapaxes(part[3].reshape(depth, 768), 0, 1) for part in done]).astype(F32)
    return (
        output, hidden_grad, memory_grad, *parted(d_in), d_out, d_up, d_down,
        head_grad, ffn_grad, stats[:, 4:6], stats[:, 0:2], stats[:, 2:4],
    )


def solution(mesh):
    rows = P(("fsdp", "ctx", "tp"), None)
    inner = P(None, "fsdp", "tp")
    outer = P(None, "tp", "fsdp")
    weights = (inner, inner, inner, outer, inner, outer)
    biases = (P(None, None, "tp"), P(None, "tp"), P(), P(), P())
    return jax.shard_map(
        shards,
        mesh=mesh,
        in_specs=(rows, rows, P("fsdp", "ctx", None), P("fsdp", None), P()) + weights + biases,
        out_specs=(rows, rows, P()) + weights + biases,
        check_vma=False,
    )
```

```python
import functools

import jax
import jax.numpy as jnp
from jax import lax
from jax.experimental import pallas as pl
from jax.experimental.pallas import tpu as pltpu
from jax.sharding import PartitionSpec as P

EPSILON = 1e-05
MASKED = -1000000000.0
MESH = pl.DeviceIdType.MESH
F32 = jnp.float32
BF16 = jnp.bfloat16
ORDER = ((0, 1), (1, 0), (2, 2), (3, 3))


def mm(left, right):
    return jnp.dot(left, right, preferred_element_type=F32)


def mm_nt(left, right):
    return lax.dot_general(left, right, (((1,), (1,)), ((), ())), preferred_element_type=F32)


def mm_tn(left, right):
    return lax.dot_general(left, right, (((0,), (0,)), ((), ())), preferred_element_type=F32)


def rcopy(src, dst, send_sem, recv_sem, device):
    return pltpu.make_async_remote_copy(
        src_ref=src,
        dst_ref=dst,
        send_sem=send_sem,
        recv_sem=recv_sem,
        device_id=device,
        device_id_type=MESH,
    )


def mate_of(c):
    return c + 1 - 2 * (c % 2)


def across_of(c):
    return (c + 2) % 4


def signal(sem, device):
    pl.semaphore_signal(sem, inc=1, device_id=device, device_id_type=MESH)


def ordered(place, step):
    half = place // 2
    inner = place + half * (3 - 2 * place)
    first, second = ORDER[step]
    chunk = first + inner * (second - first)
    return chunk + half * (3 - 2 * chunk)


def ordered_by(place, step):
    half = place // 2
    inner = place + half * (3 - 2 * place)
    chunk = step + inner * (1 - 2 * step) * ((3 - step) // 2)
    return chunk + half * (3 - 2 * chunk)


def mark_path(parent_ref, flag_ref, c):
    for half, first in enumerate((c, 3 - c)):
        path = [first]
        for _ in range(3):
            path.append(parent_ref[0, path[-1]])
        for other in range(4):
            found = path[0] == other
            for segment in path[1:]:
                found = found | (segment == other)
            flag_ref[half, other] = found.astype(jnp.int32)


def dma(*shape):
    return pltpu.SemaphoreType.DMA(shape)


class Rider:
    def __init__(self, array, out, make, scratch, chunks=0, summed=None):
        self.array, self.out, self.make, self.scratch, self.chunks = array, out, make, scratch, chunks
        self.summed = summed
        self.late = self.hopped = False

    def later(self, hopped=False):
        self.late, self.hopped = True, hopped
        return self


class Copies:
    def __init__(self, steps, here, scratch):
        self.steps, self.here = steps, here
        self.send, self.recv, self.leg, self.stage = scratch
        self.came = False

    def greetings(self):
        return [(origin, when, weight) for _, origin, _, _, when, weight in self.steps]

    def copies(self):
        for number, (to, _, source, target, when, _) in enumerate(self.steps):
            yield rcopy(source, target, self.send.at[number], self.recv.at[number], to), when

    def inward(self):
        return pltpu.make_async_copy(self.here[0], self.stage, self.leg.at[0])

    def outward(self):
        return pltpu.make_async_copy(self.stage, self.here[1], self.leg.at[1])

    def start(self):
        for copy, when in self.copies():
            guarded(when, copy.start)
        guarded(self.here[2], self.inward().start)

    def turn(self):
        guarded(self.here[2], self.inward().wait)
        guarded(self.here[2], self.outward().start)

    def arrive(self):
        self.came = True
        for copy, when in self.copies():
            guarded(when, copy.wait_recv)
        guarded(self.here[2], self.outward().wait)

    def finish(self):
        if not self.came:
            self.arrive()
        for copy, when in self.copies():
            guarded(when, copy.wait_send)


class FlipGather:
    def __init__(self, source, target, place, scratch):
        self.source, self.target = source, target
        self.f, self.c, self.t = place
        self.size = target.shape[0]
        self.send, self.recv, self.on_send, self.on_recv, self.leg, self.stage = scratch
        self.moves = self.c > 0

    def greetings(self):
        there = {"tp": flipped_place(self.c, self.t)}
        ring = [({"fsdp": (self.f + self.size - k) % self.size}, None, 1) for k in range(1, self.size)]
        return [(there, self.moves, (self.c + 3) // 4)] + ring

    def first(self, chunk):
        there = {"tp": flipped_place(self.c, self.t)}
        return rcopy(
            self.source.at[chunk], self.target.at[self.f, chunk], self.send.at[chunk], self.recv.at[chunk], there
        )

    def second(self, chunk, k, moved):
        source = self.target.at[self.f, chunk] if moved else self.source.at[chunk]
        device = {"fsdp": (self.f + k) % self.size}
        return rcopy(
            source, self.target.at[self.f, chunk], self.on_send.at[k - 1, chunk], self.on_recv.at[k - 1, chunk], device
        )

    def inward(self):
        return pltpu.make_async_copy(self.source, self.stage, self.leg.at[0])

    def outward(self):
        return pltpu.make_async_copy(self.stage, self.target.at[self.f], self.leg.at[1])

    def start(self):
        @pl.when(self.moves)
        def _():
            for chunk in range(self.source.shape[0]):
                self.first(chunk).start()

        @pl.when(self.c == 0)
        def _():
            self.inward().start()

    def hop(self, chunk):
        @pl.when(self.moves)
        def _():
            self.first(chunk).wait_recv()
            for k in range(1, self.size):
                self.second(chunk, k, True).start()

        @pl.when(self.c == 0)
        def _():
            for k in range(1, self.size):
                self.second(chunk, k, False).start()

    def turn(self):
        @pl.when(self.c == 0)
        def _():
            self.inward().wait()
            self.outward().start()

    def finish(self):
        @pl.when(self.moves)
        def _():
            for chunk in range(self.source.shape[0]):
                self.first(chunk).wait_send()

        for chunk in range(self.source.shape[0]):
            for k in range(1, self.size):
                self.second(chunk, k, False).wait()

        @pl.when(self.c == 0)
        def _():
            self.outward().wait()


class ScatterFlip:
    def __init__(self, source, target, place, scratch):
        self.source, self.target = source, target
        self.f, self.c, self.t = place
        self.size = source.shape[0]
        self.here = False
        self.send, self.recv, self.on_send, self.on_recv, self.leg, self.got, self.out = scratch
        self.moves = self.c > 0

    def greetings(self):
        there = {"tp": flipped_place(self.c, self.t)}
        ring = [({"fsdp": (self.f + self.size - k) % self.size}, None, 1) for k in range(1, self.size)]
        return [(there, self.moves, (self.c + 3) // 4)] + ring

    def first(self, chunk, k):
        to = (self.f + k) % self.size
        return rcopy(
            self.source.at[to, chunk], self.got.at[k, chunk],
            self.send.at[k - 1, chunk], self.recv.at[k - 1, chunk], {"fsdp": to},
        )

    def own(self, chunk):
        return pltpu.make_async_copy(
            self.source.at[self.f, chunk], self.got.at[0, chunk], self.leg.at[chunk]
        )

    def second(self, chunk):
        there = {"tp": flipped_place(self.c, self.t)}
        return rcopy(self.out.at[chunk], self.target.at[chunk], self.on_send.at[chunk], self.on_recv.at[chunk], there)

    def stays(self, chunk):
        return pltpu.make_async_copy(self.out.at[chunk], self.target.at[chunk], self.on_send.at[chunk])

    def start(self):
        for chunk in range(self.target.shape[0]):
            for k in range(1, self.size):
                self.first(chunk, k).start()
            self.own(chunk).start()

    def hop(self, chunk):
        self.own(chunk).wait()
        total = self.got[0, chunk].astype(F32)
        for k in range(1, self.size):
            self.first(chunk, k).wait_recv()
            total += self.got[k, chunk].astype(F32)
        self.out[chunk] = total.astype(BF16)

        @pl.when(self.moves)
        def _():
            self.second(chunk).start()

        @pl.when(self.c == 0)
        def _():
            self.stays(chunk).start()

    def turn(self):
        pass

    def arrive(self):
        self.here = True
        for chunk in range(self.target.shape[0]):
            guarded(self.moves, self.second(chunk).wait_recv)
            guarded(self.c == 0, self.stays(chunk).wait)

    def finish(self):
        if not self.here:
            self.arrive()
        for chunk in range(self.target.shape[0]):
            for k in range(1, self.size):
                self.first(chunk, k).wait_send()
            guarded(self.moves, self.second(chunk).wait_send)


class CtxGather:
    def __init__(self, pick, source, target, place, scratch):
        self.source, self.target, self.pick = source, target, pick
        self.c = place[1]
        self.send, self.recv, self.leg, self.stage = scratch

    def greetings(self):
        return [({"ctx": mate_of(self.c)}, None, 1), ({"ctx": across_of(self.c)}, None, 1)]

    def copy(self, number):
        c = self.c
        device = across_of(c) if number == 0 else mate_of(c)
        source = self.pick(self.target, across_of(c)) if number == 2 else self.source
        slot = across_of(c) if number == 2 else c
        return rcopy(source, self.pick(self.target, slot), self.send.at[number], self.recv.at[number], {"ctx": device})

    def inward(self):
        return pltpu.make_async_copy(self.source, self.stage, self.leg.at[0])

    def outward(self):
        return pltpu.make_async_copy(self.stage, self.pick(self.target, self.c), self.leg.at[1])

    def start(self):
        self.copy(0).start()
        self.copy(1).start()
        self.inward().start()

    def turn(self):
        self.inward().wait()
        self.outward().start()
        self.copy(0).wait_recv()
        self.copy(2).start()

    def finish(self):
        self.copy(0).wait_send()
        self.copy(1).wait()
        self.copy(2).wait()
        self.outward().wait()


class CtxScatter:
    def __init__(self, pick, source, target, place, scratch):
        self.source, self.target, self.pick = source, target, pick
        self.c, self.came = place[1], False
        self.send, self.recv, self.leg, self.stage, self.cross, self.far, self.total = scratch

    def greetings(self):
        return [({"ctx": mate_of(self.c)}, None, 1), ({"ctx": across_of(self.c)}, None, 1)]

    def copy(self, number):
        c = self.c
        device = across_of(c) if number == 2 else mate_of(c)
        source = (self.pick(self.source, 3 - c), self.pick(self.source, mate_of(c)), self.total)[number]
        target = (self.far, self.target.at[1], self.target.at[2])[number]
        return rcopy(source, target, self.send.at[number], self.recv.at[number], {"ctx": device})

    def inward(self):
        return pltpu.make_async_copy(self.pick(self.source, self.c), self.stage, self.leg.at[0])

    def outward(self):
        return pltpu.make_async_copy(self.stage, self.target.at[0], self.leg.at[1])

    def beside(self):
        return pltpu.make_async_copy(self.pick(self.source, across_of(self.c)), self.cross, self.leg.at[2])

    def start(self):
        self.copy(0).start()
        self.beside().start()
        self.copy(1).start()
        self.inward().start()

    def turn(self):
        self.copy(0).wait_recv()
        self.beside().wait()
        self.total[...] = (self.cross[...].astype(F32) + self.far[...].astype(F32)).astype(self.total.dtype)
        self.copy(2).start()
        self.inward().wait()
        self.outward().start()

    def arrive(self):
        self.came = True
        self.copy(1).wait_recv()
        self.copy(2).wait_recv()
        self.outward().wait()

    def finish(self):
        if not self.came:
            self.arrive()
        for number in range(3):
            self.copy(number).wait_send()


class Riding:
    def __init__(self, riders, sources, targets, scratch, fetches, results, puts):
        self.fetches, self.results, self.puts = fetches, results, puts
        self.gone = [False] * len(puts)
        place = tuple(lax.axis_index(axis) for axis in ("fsdp", "ctx", "tp"))
        scratch = list(scratch)
        self.rides, self.hops, self.late, self.hopped = [], [], [], []
        self.firsts, self.seconds, self.begun, self.turned, self.sums = [], [], [], [], {}
        self.stores, self.stored = [], 0
        for rider, target in zip(riders, targets):
            own = [scratch.pop(0) for _ in rider.scratch]
            chained = isinstance(rider.array, int)
            source = targets[rider.array] if chained else sources.pop(0)
            if rider.make is None:
                terms, total, sem = own
                fetch = pltpu.make_async_copy(source, terms, sem.at[0])
                self.stores.append((self.rides[rider.array], fetch, terms, total, total_copy(total, target, sem)))
                continue
            if rider.summed is not None:
                terms, total, sem = (scratch.pop(0) for _ in range(3))
                self.sums[len(self.seconds)] = (pltpu.make_async_copy(source, terms, sem.at[0]), terms, total)
                source = total
            ride = rider.make(source, target, place, own)
            self.rides.append(ride)
            if chained:
                self.firsts.append(self.rides[rider.array])
                self.seconds.append(ride)
                self.late.append(ride)
            if rider.late:
                self.late.append(ride)
            if rider.hopped:
                self.hopped.append(ride)
            self.hops += [(ride, chunk) for chunk in range(rider.chunks)]

    def ready(self):
        for fetch in self.fetches:
            fetch.wait()

    def put(self, *refs):
        for ref in refs:
            slot = [ref is result for result in self.results].index(True)
            self.gone[slot] = True
            self.puts[slot].start()

    def close(self):
        for slot, put in enumerate(self.puts):
            if not self.gone[slot]:
                put.start()
        for put in self.puts:
            put.wait()

    def greet(self, barrier):
        count = 0
        for ride in self.rides:
            for origin, when, weight in ride.greetings():
                guarded(when, functools.partial(signal, barrier, origin))
                count = count + weight
        return count

    def begin(self, ride):
        self.begun.append(ride)
        ride.start()

    def start(self):
        for ride in self.rides:
            if ride not in self.late:
                self.begin(ride)

    def start_late(self):
        for ride in self.late:
            if ride not in self.hopped + self.seconds:
                self.begin(ride)

    def one_hop(self, at):
        ride, chunk = self.hops[at]
        ride.hop(chunk)
        if at == len(self.hops) - 1:
            for ride in self.hopped:
                self.begin(ride)

    def turn(self):
        for ride in self.begun:
            if ride not in self.turned + self.seconds:
                self.turned.append(ride)
                ride.turn()

    def turn_when(self, when):
        if self.rides:
            pl.when(when)(self.turn)

    def chain(self):
        for number, (first, second) in enumerate(zip(self.firsts, self.seconds)):
            first.arrive()
            if number in self.sums:
                fetch, terms, total = self.sums[number]
                fetch.start()
                fetch.wait()
                axes = tuple(range(len(terms.shape) - len(total.shape)))
                total[...] = jnp.sum(terms[...].astype(F32), axis=axes).astype(total.dtype)
            self.begin(second)

    def chain_turn(self):
        for second in self.seconds:
            self.turned.append(second)
            second.turn()

    def store(self, count):
        batch = self.stores[self.stored : self.stored + count]
        for first, fetch, *_ in batch:
            first.arrive()
            fetch.start()
        for _, fetch, terms, total, put in batch:
            fetch.wait()
            total[...] = jnp.sum(terms[...].astype(F32), axis=0).astype(total.dtype)
            put.start()
        self.stored += count

    def finish(self):
        for ride in self.rides:
            if ride not in self.turned:
                ride.turn()
        self.store(len(self.stores))
        for ride in self.rides:
            ride.finish()
        for store in self.stores:
            store[4].wait()


def total_copy(total, target, sem):
    return pltpu.make_async_copy(total, target, sem.at[1])


def guarded(when, action):
    if when is None:
        action()
    else:
        pl.when(when)(action)


def call(kernel, operands, out_shapes, scratch, collective_id, name, cost, riders=(), smem=()):
    n_in, n_out, n_scratch, n_ride = len(operands), len(out_shapes), len(scratch), len(riders)
    large = [i for i in range(n_in) if i not in smem]
    carried = [rider.array for rider in riders if not isinstance(rider.array, int)]

    def body(*refs):
        refs = list(refs)
        take = lambda n: [refs.pop(0) for _ in range(n)]
        ins, sources, outs, targets = take(n_in), take(len(carried)), take(n_out), take(n_ride)
        near_ins, near_outs, (in_sem, out_sem), own = take(len(large)), take(n_out), take(2), take(n_scratch)
        fetches = [
            pltpu.make_async_copy(ins[i], near, in_sem.at[slot]) for slot, (i, near) in enumerate(zip(large, near_ins))
        ]
        for fetch in fetches:
            fetch.start()
        for i, near in zip(large, near_ins):
            ins[i] = near
        puts = [pltpu.make_async_copy(near, far, out_sem.at[i]) for i, (near, far) in enumerate(zip(near_outs, outs))]
        ride = Riding(riders, sources, targets, refs, fetches, near_outs, puts)
        kernel(ride, *ins, *near_outs, *own)
        ride.close()

    params = dict(vmem_limit_bytes=60 * 1024 * 1024)
    if collective_id is not None:
        params.update(collective_id=collective_id, has_side_effects=True)
    extra = []
    for rider in riders:
        extra += rider.scratch
        if rider.summed is not None:
            terms, total = riders[rider.array].out, rider.summed
            extra += [pltpu.VMEM(terms.shape, terms.dtype), pltpu.VMEM(total.shape, total.dtype), dma(1)]
    anywhere = pl.BlockSpec(memory_space=pl.ANY)
    near = [pltpu.VMEM(operands[i].shape, operands[i].dtype) for i in large]
    near += [pltpu.VMEM(out.shape, out.dtype) for out in out_shapes]
    results = pl.pallas_call(
        body,
        out_shape=list(out_shapes) + [rider.out for rider in riders],
        in_specs=[pl.BlockSpec(memory_space=pltpu.SMEM) if i in smem else anywhere for i in range(n_in)]
        + [anywhere] * len(carried),
        out_specs=[anywhere] * (n_out + n_ride),
        scratch_shapes=near + [dma(max(len(large), 1)), dma(max(n_out, 1))] + list(scratch) + extra,
        compiler_params=pltpu.CompilerParams(**params),
        cost_estimate=pl.CostEstimate(flops=cost[0], bytes_accessed=cost[1], transcendentals=cost[2]),
        name=name,
    )(*operands, *carried)
    return results[:n_out], results[n_out:]


def copies_rider(array, out, steps, stage, plan):
    def make(source, target, place, scratch):
        return Copies(*plan(source, target, *place), scratch)

    scratch = [dma(steps), dma(steps), dma(2), pltpu.VMEM(stage, array.dtype)]
    return Rider(array, out, make, scratch)


def flip_gather(own, size):
    own = own.reshape(2, own.shape[0] // 2, own.shape[1])
    scratch = [dma(2), dma(2), dma(size - 1, 2), dma(size - 1, 2), dma(2), pltpu.VMEM(own.shape, own.dtype)]
    return Rider(own, sds(size, *own.shape), FlipGather, scratch, chunks=2)


def scatter_flip(parts):
    size, n = parts.shape[0], parts.shape[1]
    shape = parts.shape[1:]
    scratch = [
        dma(size - 1, n), dma(size - 1, n), dma(n), dma(n), dma(n),
        pltpu.VMEM((size, *shape), BF16), pltpu.VMEM(shape, BF16),
    ]
    return Rider(parts, sds(*shape), ScatterFlip, scratch, chunks=n)


def fsdp_gather(own, size):
    def make(source, target, f, c, t):
        steps = [
            ({"fsdp": (f + k) % size}, {"fsdp": (f + size - k) % size}, source, target.at[f], None, 1)
            for k in range(1, size)
        ]
        return steps, (source, target.at[f], None)

    return copies_rider(own, sds(size, *own.shape, dtype=own.dtype), size - 1, own.shape, make)


def fsdp_scatter(parts, size):
    out = sds(size, parts.shape[0], *parts.shape[2:], dtype=parts.dtype)

    def make(source, target, f, c, t):
        steps = [
            (
                {"fsdp": (f + k) % size}, {"fsdp": (f + size - k) % size},
                source.at[:, (f + k) % size], target.at[k], None, 1,
            )
            for k in range(1, size)
        ]
        return steps, (source.at[:, f], target.at[0], None)

    return copies_rider(parts, out, size - 1, out.shape[1:], make)


def slot_of(axis):
    def pick(ref, slot):
        return ref.at[slot] if axis == 0 else ref.at[:, :, slot]

    return pick


def ctx_gather(own, axis=0, first=None, summed=False):
    scratch = [dma(3), dma(3), dma(2), pltpu.VMEM(own.shape, own.dtype)]
    out = sds(*own.shape[:axis], 4, *own.shape[axis:], dtype=own.dtype)
    make = functools.partial(CtxGather, slot_of(axis))
    return Rider(own if first is None else first, out, make, scratch, summed=own if summed else None)


def ctx_scatter(parts, axis=0, first=None):
    shape = parts.shape[:axis] + parts.shape[axis + 1 :]

    buffer = pltpu.VMEM(shape, parts.dtype)
    scratch = [dma(3), dma(3), dma(3), buffer, buffer, buffer, buffer]
    array = parts if first is None else first
    return Rider(array, sds(3, *shape, dtype=parts.dtype), functools.partial(CtxScatter, slot_of(axis)), scratch)


def flipped_place(c, t):
    return 2 * ((t // 2 + c % 2) % 2) + (t % 2 + c // 2) % 2


def tp_flip(own):
    def make(source, target, f, c, t):
        other = {"tp": flipped_place(c, t)}
        return [(other, other, source, target, c > 0, (c + 3) // 4)], (source, target, c == 0)

    return copies_rider(own, sds(*own.shape, dtype=own.dtype), 1, own.shape, make)


def plane(size):
    return [(kt, kf) for kt in (2, 3, 1, 0) for kf in range(size) if kt + kf > 0]


def plane_gather(own, size):
    def make(source, target, f, c, t):
        steps = [
            (
                {"fsdp": (f + kf) % size, "tp": (t + kt) % 4},
                {"fsdp": (f + size - kf) % size, "tp": (t + 4 - kt) % 4},
                source, target.at[t, f], None, 1,
            )
            for kt, kf in plane(size)
        ]
        return steps, (source, target.at[t, f], None)

    return copies_rider(own, sds(4, size, *own.shape, dtype=own.dtype), 4 * size - 1, own.shape, make)


def plane_scatter(parts, size):
    def make(source, target, f, c, t):
        steps = [
            (
                {"fsdp": (f + kf) % size, "tp": (t + kt) % 4},
                {"fsdp": (f + size - kf) % size, "tp": (t + 4 - kt) % 4},
                source.at[(t + kt) % 4, (f + kf) % size], target.at[kt, kf], None, 1,
            )
            for kt, kf in plane(size)
        ]
        return steps, (source.at[t, f], target.at[0, 0], None)

    return copies_rider(parts, sds(*parts.shape, dtype=parts.dtype), 4 * size - 1, parts.shape[2:], make)


class SmallSum:
    def __init__(self, source, target, place, scratch):
        self.source, self.target = source, target
        self.f, self.c, self.t = place
        self.size = target.shape[1]
        self.send, self.recv, self.on_send, self.on_recv, self.leg, self.terms, self.total = scratch

    def greetings(self):
        around = [({"ctx": (self.c + 4 - k) % 4}, None, 1) for k in (1, 2, 3)]
        return around + [
            ({"fsdp": (self.f + self.size - kf) % self.size, "tp": (self.t + 4 - kt) % 4}, None, 1)
            for kt, kf in plane(self.size)
        ]

    def first(self, k):
        device = {"ctx": (self.c + k) % 4}
        return rcopy(self.source, self.terms.at[self.c], self.send.at[k - 1], self.recv.at[k - 1], device)

    def own(self):
        return pltpu.make_async_copy(self.source, self.terms.at[self.c], self.leg.at[0])

    def second(self, number):
        kt, kf = plane(self.size)[number]
        device = {"fsdp": (self.f + kf) % self.size, "tp": (self.t + kt) % 4}
        target = self.target.at[self.t, self.f]
        return rcopy(self.total, target, self.on_send.at[number], self.on_recv.at[number], device)

    def stays(self):
        return pltpu.make_async_copy(self.total, self.target.at[self.t, self.f], self.leg.at[1])

    def start(self):
        for k in (2, 3, 1):
            self.first(k).start()
        self.own().start()

    def turn(self):
        self.own().wait()
        for k in (1, 2, 3):
            self.first(k).wait_recv()
        self.total[...] = self.terms[0] + self.terms[1] + self.terms[2] + self.terms[3]
        for number in range(4 * self.size - 1):
            self.second(number).start()
        self.stays().start()

    def finish(self):
        for k in (1, 2, 3):
            self.first(k).wait_send()
        for number in range(4 * self.size - 1):
            self.second(number).wait()
        self.stays().wait()


def stored_sum(first, terms):
    total = sds(*terms.shape[1:], dtype=terms.dtype)
    scratch = [pltpu.VMEM(terms.shape, terms.dtype), pltpu.VMEM(total.shape, total.dtype), dma(2)]
    return Rider(first, total, None, scratch)


def small_sum(own, size, first=None):
    many = 4 * size - 1
    scratch = [
        dma(3), dma(3), dma(many), dma(many), dma(2),
        pltpu.VMEM((4, *own.shape), own.dtype), pltpu.VMEM(own.shape, own.dtype),
    ]
    out = sds(4, size, *own.shape, dtype=own.dtype)
    return Rider(own if first is None else first, out, SmallSum, scratch, summed=None if first is None else own)


def carry_kernel(ride):
    barrier = pltpu.get_barrier_semaphore()
    pl.semaphore_wait(barrier, ride.greet(barrier))
    ride.start()
    ride.turn()
    ride.start_late()
    ride.chain()
    ride.turn()
    ride.chain_turn()
    ride.finish()


def carry(riders, cid):
    return call(carry_kernel, (), (), (), cid, "carry", (1 << 20, 1 << 20, 0), riders)[1]


def sds(*shape, dtype=BF16):
    return jax.ShapeDtypeStruct(shape, dtype)


FAR = 1e30


def inner_kernel(
    fetch, ride, parent_ref, x_ref, w_ref, b_ref, xg_ref, qw_ref, kv_ref, o_ref, lse_ref, *rest
):
    if fetch:
        full_ref, w_send, w_recv, *rest = rest
    (
        qbuf, qm_ref, m_ref, acc_ref, vt_ref, x_recv, x_right, x_left,
        k1_send, k1_recv, k2_send, k2_recv, kf_send, kf_recv, q_send, q_recv, flag_ref,
    ) = rest
    c = lax.axis_index("ctx")
    mark_path(parent_ref, flag_ref, c)
    t = lax.axis_index("tp")
    f, size = lax.axis_index("fsdp"), lax.axis_size("fsdp")
    barrier = pltpu.get_barrier_semaphore()
    for device in (mate_of(c), across_of(c), 3 - c):
        signal(barrier, {"ctx": device})

    @pl.when(t > 0)
    def _():
        signal(barrier, {"tp": t - 1})

    @pl.when(t < 3)
    def _():
        signal(barrier, {"tp": t + 1})

    if fetch:
        for k in range(1, size):
            signal(barrier, {"fsdp": (f + size - k) % size})
    ends = (t // 3) + (3 - t) // 3
    count = 5 - ends + ride.greet(barrier) + (size - 1 if fetch else 0)
    m_ref[...] = jnp.full_like(m_ref, MASKED)
    acc_ref[...] = jnp.zeros_like(acc_ref)
    vt_ref[:, :, :, 64:80] = jnp.ones((4, 4, 3, 16, 256), BF16)
    ride.ready()
    pl.semaphore_wait(barrier, count)

    def right(src, chunk, step):
        return rcopy(src, xg_ref.at[chunk], x_right.at[step], x_recv.at[chunk], {"tp": t + 1})

    def left(src, chunk, step):
        return rcopy(src, xg_ref.at[chunk], x_left.at[step], x_recv.at[chunk], {"tp": t - 1})

    def arrived(chunk):
        rcopy(xg_ref.at[chunk], xg_ref.at[chunk], x_right.at[0], x_recv.at[chunk], {"tp": t}).wait_recv()

    @pl.when(t < 3)
    def _():
        right(x_ref, t, 0).start()

    @pl.when(t > 0)
    def _():
        left(x_ref, t, 0).start()

    def weight(k):
        device = {"fsdp": (f + k) % size}
        return rcopy(w_ref, full_ref.at[f], w_send.at[k - 1], w_recv.at[k - 1], device)

    if fetch:
        for k in range(1, size):
            weight(k).start()
        full_ref[f] = w_ref[...]
    xg_ref[t] = x_ref[...]
    ride.start()
    if fetch:
        for k in range(1, size):
            weight(k).wait_recv()

    def mate(chunk):
        part = kv_ref.at[c, chunk]
        return rcopy(part, part, k1_send.at[chunk], k1_recv.at[chunk], {"ctx": mate_of(c)})

    def across(chunk):
        part = kv_ref.at[c, chunk]
        return rcopy(part, part, k2_send.at[chunk], k2_recv.at[chunk], {"ctx": across_of(c)})

    def onward(chunk):
        part = kv_ref.at[across_of(c), chunk]
        return rcopy(part, part, kf_send.at[chunk], kf_recv.at[chunk], {"ctx": mate_of(c)})

    def partner(slot):
        return rcopy(qbuf.at[slot], qw_ref.at[2 * slot + 1], q_send.at[slot], q_recv.at[slot], {"ctx": 3 - c})

    def project(step):
        chunk = ordered(t, step)
        w = full_ref[...].reshape(768, 640) if fetch else w_ref[...]
        made = mm(xg_ref[chunk], w) + b_ref[...]
        kv_ref[c, chunk] = made[:, 256:].astype(BF16)
        across(chunk).start()
        mate(chunk).start()
        query = (made[:, :256] * 0.125).astype(BF16)

        @pl.when(chunk % 2 == 0)
        def _():
            qw_ref[chunk] = query

        @pl.when(chunk % 2 == 1)
        def _():
            qbuf[chunk // 2] = query
            partner(chunk // 2).start()

    low = lax.broadcasted_iota(jnp.int32, (256, 128), 1) < 64

    def complete(step):
        chunk = ordered(t, step)
        across(chunk).wait_recv()
        onward(chunk).start()
        mate(chunk).wait_recv()

        @pl.when(chunk % 2 == 1)
        def _():
            partner(chunk // 2).wait_recv()

        pair = qw_ref[chunk, :, 0:128]
        none = jnp.zeros_like(pair)
        qm_ref[0, chunk] = jnp.where(low, pair, none)
        qm_ref[1, chunk] = jnp.where(low, none, pair)
        qm_ref[2, chunk] = qw_ref[chunk, :, 128:256]
        onward(chunk).wait_recv()
        for segment in range(4):
            pair = jnp.transpose(kv_ref[segment, chunk, :, 256:384], (1, 0))
            mixed = jnp.transpose(kv_ref[segment, chunk, :, 128:256], (1, 0))
            for head, rows in enumerate((pair[0:64], pair[64:128], mixed[0:64])):
                vt_ref[segment, chunk, head, 0:64] = rows

    def items(step):
        @pl.loop(step * step, (step + 1) * (step + 1))
        def _(item):
            number = item - step * step
            second = number // (step + 1)
            query_at = ordered_by(t, step + second * (number - 2 * step - 1))
            key_at = ordered_by(t, number + second * (step - number))
            half = query_at % 2

            def visit(segments):
                seen = [flag_ref[half, segment] > 0 for segment in segments]
                far = [jnp.where(one, 0.0, FAR) for one in seen]
                scores, most, made = [], [], []
                for head in range(3):
                    query, at = qm_ref[head, query_at], 128 * (head // 2)
                    rows = [mm_nt(kv_ref[segment, key_at, :, at : at + 128], query) for segment in segments]
                    new = m_ref[query_at, head : head + 1]
                    for one, row in zip(seen, rows):
                        new = jnp.maximum(new, jnp.where(one, jnp.max(row, axis=0, keepdims=True), MASKED))
                    scores.append(rows)
                    most.append(new)
                for head in range(3):
                    total = acc_ref[query_at, head] * jnp.exp(m_ref[query_at, head : head + 1] - most[head])
                    for segment, row, off in zip(segments, scores[head], far):
                        probs = jnp.exp(row - (most[head] + off)).astype(BF16)
                        total += mm(vt_ref[segment, key_at, head], probs)
                    made.append(total)
                for head in range(3):
                    m_ref[query_at, head : head + 1] = most[head]
                    acc_ref[query_at, head] = made[head]

            length = c + 1 + half * (3 - 2 * c)

            @pl.loop(0, length // 2)
            def _(two):
                visit((2 * two, 2 * two + 1))

            @pl.when(length % 2 == 1)
            def _():
                visit((length - 1,))

            if step == 3:
                for n in range(1, len(ride.hops)):
                    pl.when(item == 9 + 2 * n)(functools.partial(ride.one_hop, n))

    project(0)
    for step in range(1, 4):

        @pl.when(t - step >= 0)
        def _():
            arrived(t - step)

            @pl.when(t < 3)
            def _():
                right(xg_ref.at[t - step], t - step, step).start()

        @pl.when(t + step <= 3)
        def _():
            arrived(t + step)

            @pl.when(t > 0)
            def _():
                left(xg_ref.at[t + step], t + step, step).start()

        project(step)
        if step == 2:
            ride.turn()
        if step == 3:
            ride.start_late()
            ride.chain()
            ride.put(xg_ref)
        complete(step - 1)
        items(step - 1)
    complete(3)
    if ride.hops:
        ride.one_hop(0)
    ride.turn()
    ride.chain_turn()
    ride.put(qw_ref, kv_ref)
    items(3)
    for quarter in range(4):
        whole = [acc_ref[quarter, head, 64:65] for head in range(3)]
        parts = [acc_ref[quarter, head, 0:64] / whole[head] for head in range(3)]
        for at, pair in ((0, parts[0:2]), (128, [parts[2], jnp.zeros_like(parts[2])])):
            turned = jnp.transpose(jnp.concatenate(pair, axis=0), (1, 0)).astype(BF16)
            o_ref[quarter, :, at : min(at + 128, 192)] = turned[:, : min(128, 192 - at)]
        for head in range(3):
            lse_ref[quarter, head : head + 1] = m_ref[quarter, head : head + 1] + jnp.log(whole[head])
        lse_ref[quarter, 3:8] = jnp.zeros((5, 256), F32)
    ride.put(o_ref, lse_ref)
    for chunk in range(4):
        mate(chunk).wait_send()
        across(chunk).wait_send()
        onward(chunk).wait_send()
    for slot in range(2):
        partner(slot).wait_send()

    @pl.when(t < 3)
    def _():
        right(x_ref, t, 0).wait_send()

    @pl.when(t > 0)
    def _():
        left(x_ref, t, 0).wait_send()

    for step in (1, 2):

        @pl.when((t - step >= 0) & (t < 3))
        def _():
            right(xg_ref.at[t - step], t - step, step).wait_send()

        @pl.when((t + step <= 3) & (t > 0))
        def _():
            left(xg_ref.at[t + step], t + step, step).wait_send()

    if fetch:
        for k in range(1, size):
            weight(k).wait_send()
    ride.finish()


def inner(x, w, b, parents, cid, riders=(), fetch=False):
    outs = [
        sds(4, 256, 768), sds(4, 256, 256), sds(4, 4, 256, 384), sds(4, 256, 192), sds(4, 8, 256, dtype=F32),
    ]
    scratch = [
        pltpu.VMEM((2, 256, 256), BF16),
        pltpu.VMEM((3, 4, 256, 128), BF16), pltpu.VMEM((4, 8, 256), F32), pltpu.VMEM((4, 3, 80, 256), F32),
        pltpu.VMEM((4, 4, 3, 80, 256), BF16),
        dma(4), dma(3), dma(3),
        dma(4), dma(4), dma(4), dma(4), dma(4), dma(4), dma(2), dma(2), pltpu.SMEM((2, 4), jnp.int32),
    ]
    if fetch:
        size = lax.axis_size("fsdp")
        outs.append(sds(size, *w.shape))
        scratch = [dma(size - 1), dma(size - 1)] + scratch
    cost = (2 * 1024 * 768 * 640 + 5 * 512 * 1024 * 64 * 12, 14 << 20, 5 * 512 * 1024 * 3)
    kernel = functools.partial(inner_kernel, fetch)
    res, ridden = call(kernel, (parents, x, w, b), outs, scratch, cid, "inner", cost, riders, smem=(0,))
    full = res[5].reshape(768, 640) if fetch else w
    xg, qw, kv, o, lse = res[:5]
    return (
        xg.reshape(1024, 768), qw.reshape(1024, 256), kv.reshape(4, 1024, 384),
        o.reshape(1024, 192), lse, full, ridden,
    )


def norm_stats(summed):
    row_mean = jnp.mean(summed, axis=-1, keepdims=True)
    centered = summed - row_mean
    variance = jnp.mean(centered * centered, axis=-1, keepdims=True)
    scale = lax.rsqrt(variance + EPSILON)
    return centered * scale, scale


def norm_back(grad, xhat, scale, gain):
    scaled = grad * gain
    first = jnp.mean(scaled, axis=-1, keepdims=True)
    second = jnp.mean(scaled * xhat, axis=-1, keepdims=True)
    return scale * (scaled - first - xhat * second)


def gelu_both(up):
    phi = 0.5 * (1.0 + lax.erf(up * 0.7071067811865476))
    slope = phi + up * jnp.exp(-0.5 * up * up) * 0.3989422804014327
    return (up * phi).astype(BF16), slope.astype(BF16)


PIECE = 128


def exchange(c, ref, feed, mine_ref, part_ref, send_ref, got_ref, a_send, a_recv, s_send, s_recv, meanwhile):
    mate, across, far = mate_of(c), across_of(c), 3 - c
    pieces = (pl.ds(0, PIECE), pl.ds(PIECE, PIECE))

    def gather(slot, index, p, device):
        part = ref.at[slot, pieces[p]]
        return rcopy(part, part, a_send.at[index, p], a_recv.at[index, p], {"ctx": device})

    def scatter(index, p, device):
        source, target = send_ref.at[index, pieces[p]], got_ref.at[index, pieces[p]]
        return rcopy(source, target, s_send.at[index, p], s_recv.at[index, p], {"ctx": device})

    for p in range(2):
        gather(c, 1, p, across).start()
    for p in range(2):
        gather(c, 0, p, mate).start()
    mine_ref[...] += feed(c, pl.ds(0, 2 * PIECE))
    for p in range(2):
        gather(mate, 0, p, mate).wait_recv()
    send_ref[0] = feed(mate, pl.ds(0, 2 * PIECE)).astype(BF16)
    for p in range(2):
        scatter(0, p, mate).start()

    def take_across(p):
        gather(across, 1, p, across).wait_recv()
        gather(across, 2, p, mate).start()
        part_ref[pieces[p]] = feed(across, pieces[p])

    def take_far(p):
        gather(far, 2, p, mate).wait_recv()
        send_ref[1, pieces[p]] = feed(far, pieces[p]).astype(BF16)
        scatter(1, p, mate).start()

    def join(p):
        scatter(1, p, mate).wait_recv()
        send_ref[2, pieces[p]] = (part_ref[pieces[p]] + got_ref[1, pieces[p]].astype(F32)).astype(BF16)
        scatter(2, p, across).start()

    take_across(0)
    take_far(0)
    take_across(1)
    join(0)
    take_far(1)
    join(1)
    meanwhile()
    for p in range(2):
        scatter(0, p, mate).wait_recv()
        scatter(2, p, across).wait_recv()

    def settle():
        for p in range(2):
            for index in range(3):
                gather(c, index, p, mate).wait_send()
                scatter(index, p, mate).wait_send()

    return mine_ref[...] + got_ref[0].astype(F32) + got_ref[2].astype(F32), settle


def block_kernel(
    ride, o_ref, wo_ref, w1_ref, w2_ref, b1_ref, vec_ref, stream_ref,
    out_ref, low_ref, xhat1_ref, r1_ref, xhat2_ref, r2_ref, xg_ref, act_ref, slope_ref, rows_ref, down_ref,
    w_send, w_recv, mine_ref, part_ref, send_ref, got_ref, o_send, o_recv, a_send, a_recv, s_send, s_recv,
):
    c = lax.axis_index("ctx")
    t = lax.axis_index("tp")
    barrier = pltpu.get_barrier_semaphore()
    for place in range(4):

        @pl.when((t % 2 == 0) & (t != place))
        def _():
            signal(barrier, {"tp": place})

        @pl.when(t % 2 == 1)
        def _():
            signal(barrier, {"ctx": 3 - c, "tp": place})

    signal(barrier, {"ctx": mate_of(c)})
    signal(barrier, {"ctx": across_of(c)})
    f, size = lax.axis_index("fsdp"), lax.axis_size("fsdp")
    for k in range(1, size):
        signal(barrier, {"fsdp": (f + size - k) % size})
    count = 5 + t % 2 + size - 1 + ride.greet(barrier)
    ride.ready()
    pl.semaphore_wait(barrier, count)

    def weight(k):
        device = {"fsdp": (f + k) % size}
        return rcopy(w2_ref, down_ref.at[f], w_send.at[k - 1], w_recv.at[k - 1], device)

    def give(quarter):
        device = {"tp": quarter} if quarter % 2 == 0 else {"ctx": 3 - c, "tp": quarter}
        return rcopy(o_ref.at[quarter], rows_ref.at[t], o_send.at[quarter], o_recv.at[t], device)

    def given(group):
        rcopy(rows_ref.at[group], rows_ref.at[group], o_send.at[0], o_recv.at[group], {"tp": t}).wait_recv()

    for quarter in (3, 2, 1, 0):
        if quarter % 2 == 0:

            @pl.when(t != quarter)
            def _():
                give(quarter).start()

            @pl.when(t == quarter)
            def _():
                rows_ref[quarter] = o_ref[quarter]

        else:
            give(quarter).start()
    for k in range(1, size):
        weight(k).start()
    down_ref[f] = w2_ref[...]
    branch = stream_ref[...] + vec_ref[0:1]
    for group in range(4):

        @pl.when((t % 2 == 1) | (t != group))
        def _():
            given(group)

        branch += mm_nt(rows_ref[group], wo_ref[group])
    ride.start()
    xhat, scale = norm_stats(branch)
    xhat1_ref[...] = xhat
    r1_ref[...] = jnp.broadcast_to(scale, r1_ref.shape)
    normed = xhat * vec_ref[2:3] + vec_ref[3:4]
    xg_ref[c] = normed.astype(BF16)
    mine_ref[...] = normed + vec_ref[1:2]
    for k in range(1, size):
        weight(k).wait_recv()

    def feed(segment, rows):
        up = mm(xg_ref[segment, rows], w1_ref[...]) + b1_ref[...]
        act, slope = gelu_both(up)
        act_ref[segment, rows] = act
        slope_ref[segment, rows] = slope
        return mm_nt(act, down_ref[...].reshape(768, 768))

    def meanwhile():
        ride.turn()
        ride.put(xhat1_ref, r1_ref, xg_ref, act_ref, slope_ref, rows_ref, down_ref)

    summed, settle = exchange(
        c, xg_ref, feed, mine_ref, part_ref, send_ref, got_ref, a_send, a_recv, s_send, s_recv, meanwhile
    )
    xhat, scale = norm_stats(summed)
    xhat2_ref[...] = xhat
    r2_ref[...] = jnp.broadcast_to(scale, r2_ref.shape)
    out = xhat * vec_ref[4:5] + vec_ref[5:6]
    out_ref[...] = out
    low_ref[...] = out.astype(BF16)
    ride.put(out_ref, low_ref, xhat2_ref, r2_ref)
    for quarter in range(4):
        if quarter % 2 == 0:

            @pl.when(t != quarter)
            def _():
                give(quarter).wait_send()

        else:
            give(quarter).wait_send()
    for k in range(1, size):
        weight(k).wait_send()
    settle()
    ride.finish()


def block(o, wo, w1, w2, b1, vecs, stream, cid, riders=()):
    size = lax.axis_size("fsdp")
    f = functools.partial(sds, dtype=F32)
    outs = [
        f(256, 768), sds(256, 768), f(256, 768), f(256, 128), f(256, 768), f(256, 128),
        sds(4, 256, 768), sds(4, 256, 768), sds(4, 256, 768), sds(4, 256, 192), sds(size, *w2.shape),
    ]
    scratch = [
        dma(size - 1), dma(size - 1),
        pltpu.VMEM((256, 768), F32),
        pltpu.VMEM((256, 768), F32),
        pltpu.VMEM((3, 256, 768), BF16),
        pltpu.VMEM((3, 256, 768), BF16),
        dma(4), dma(4), dma(3, 2), dma(3, 2), dma(3, 2), dma(3, 2),
    ]
    cost = (2 * 256 * 768 * 768 + 4 * 1024 * 768 * 768, 16 << 20, 1 << 20)
    operands = (o.reshape(4, 256, 192), wo, w1, w2, b1, vecs, stream)
    res, ridden = call(block_kernel, operands, outs, scratch, cid, "block", cost, riders)
    flat = lambda a: a.reshape(1024, 768)
    return tuple(res[:6]) + (flat(res[6]), flat(res[7]), flat(res[8]), res[9], res[10].reshape(768, 768), ridden)


def block_back_kernel(
    ride, grad_ref, xhat2_ref, r2_ref, xhat1_ref, r1_ref, vec_ref, slope_ref, w1_ref, w2_ref, wo_ref,
    xg_ref, act_ref, rows_ref, back_ref, do_ref, stat_ref, dup_ref, ddown_ref, dout_ref,
    w_send, w_recv, term_ref, all_up_ref, gg_ref, gu_ref, mine_ref, part_ref, send_ref, got_ref, dsend_ref, d_send, d_recv, a_send, a_recv, s_send, s_recv,
):
    c = lax.axis_index("ctx")
    t = lax.axis_index("tp")
    barrier = pltpu.get_barrier_semaphore()
    for place in range(4):
        if place % 2 == 0:

            @pl.when(t != place)
            def _():
                signal(barrier, {"tp": place})

        else:
            signal(barrier, {"ctx": 3 - c, "tp": place})
    signal(barrier, {"ctx": mate_of(c)})
    signal(barrier, {"ctx": across_of(c)})
    f, size = lax.axis_index("fsdp"), lax.axis_size("fsdp")
    depth = dup_ref.shape[0]
    for k in range(1, size):
        signal(barrier, {"fsdp": (f + size - k) % size})
    count = 5 + t % 2 + size - 1 + ride.greet(barrier)
    ride.ready()
    pl.semaphore_wait(barrier, count)

    def row(values):
        return jnp.sum(values, axis=0, keepdims=True)

    grad = grad_ref[...]
    back_two = norm_back(grad, xhat2_ref[...], r2_ref[:, 0:1], vec_ref[4:5])
    g2 = back_two.astype(BF16)
    gg_ref[c] = g2
    mine_ref[...] = back_two
    ride.start()
    stat_ref[1:2] = row(grad * xhat2_ref[...])
    stat_ref[3:4] = row(grad)
    stat_ref[5:6] = row(g2.astype(F32))
    stat_ref[6:8] = jnp.zeros((2, 768), F32)

    def feed(segment, rows):
        gu = (mm(gg_ref[segment, rows], w2_ref[...]) * slope_ref[segment, rows].astype(F32)).astype(BF16)
        gu_ref[segment, rows] = gu
        stat_ref[6:7] += row(gu.astype(F32))
        return mm_nt(gu, w1_ref[...])

    tall = lambda ref: ref[...].reshape(1024, 768)

    def slice_of(place):
        return pl.ds(pl.multiple_of(place * depth, depth), depth)

    def term(k):
        to = (f + k) % size
        return rcopy(
            all_up_ref.at[slice_of(to)], term_ref.at[k - 1], w_send.at[k - 1], w_recv.at[k - 1], {"fsdp": to}
        )

    def meanwhile():
        @pl.loop(0, 3)
        def _(tile):
            cols = pl.ds(pl.multiple_of(tile * 256, 256), 256)
            all_up_ref[cols] = mm_tn(xg_ref[:, cols], tall(gu_ref)).astype(BF16)

        for k in range(1, size):
            term(k).start()

        @pl.loop(0, 3)
        def _(tile):
            cols = pl.ds(pl.multiple_of(tile * 256, 256), 256)
            ddown_ref[cols] = mm_tn(gg_ref[:, :, cols].reshape(1024, 256), act_ref[...]).astype(BF16)

        ride.put(ddown_ref)
        ride.turn()

    grad_normed, settle = exchange(
        c, gg_ref, feed, mine_ref, part_ref, send_ref, got_ref, a_send, a_recv, s_send, s_recv, meanwhile
    )
    back_one = norm_back(grad_normed, xhat1_ref[...], r1_ref[:, 0:1], vec_ref[2:3])
    back_ref[...] = back_one
    g1 = back_one.astype(BF16)

    def give_near(group):
        return rcopy(dsend_ref.at[group], do_ref.at[t], d_send.at[group], d_recv.at[t], {"tp": group})

    def give_far(group):
        return rcopy(dsend_ref.at[group], do_ref.at[t], d_send.at[group], d_recv.at[t], {"ctx": 3 - c, "tp": group})

    for group in range(4):
        dsend_ref[group] = mm(g1, wo_ref[group]).astype(BF16)

        @pl.when((t % 2 == 0) & (t == group))
        def _():
            do_ref[t] = dsend_ref[group]

        @pl.when((t % 2 == 0) & (t != group))
        def _():
            give_near(group).start()

        @pl.when(t % 2 == 1)
        def _():
            give_far(group).start()

    stat_ref[0:1] = row(grad_normed * xhat1_ref[...])
    stat_ref[2:3] = row(grad_normed)
    stat_ref[4:5] = row(g1.astype(F32))
    for group in range(4):
        dout_ref[group] = mm_tn(g1, rows_ref[group]).astype(BF16)
    ride.put(back_ref, stat_ref, dout_ref)
    ride.chain()
    total = all_up_ref[slice_of(f)].astype(F32)
    for k in range(1, size):
        term(k).wait_recv()
        total += term_ref[k - 1].astype(F32)
    dup_ref[...] = total.astype(BF16)
    ride.put(dup_ref)
    for quarter in range(4):

        def taken():
            rcopy(do_ref.at[quarter], do_ref.at[quarter], d_send.at[0], d_recv.at[quarter], {"tp": t}).wait_recv()

        if quarter % 2 == 0:
            pl.when(t != quarter)(taken)
        else:
            taken()
    for group in range(4):

        @pl.when((t % 2 == 1) | (t != group))
        def _():
            give_near(group).wait_send()

    ride.chain_turn()
    for k in range(1, size):
        term(k).wait_send()
    settle()
    ride.finish()


def block_back(grad, xhat2, r2, xhat1, r1, vecs, slope, w1, w2, wo, xg, act, rows, cid, riders=()):
    f = functools.partial(sds, dtype=F32)
    size = lax.axis_size("fsdp")
    depth = 768 // size
    outs = [
        f(256, 768), sds(4, 256, 192), f(8, 768), sds(depth, 768), sds(768, 768), sds(4, 768, 192),
    ]
    scratch = [
        dma(size - 1), dma(size - 1), pltpu.VMEM((size - 1, depth, 768), BF16), pltpu.VMEM((768, 768), BF16),
        pltpu.VMEM((4, 256, 768), BF16),
        pltpu.VMEM((4, 256, 768), BF16),
        pltpu.VMEM((256, 768), F32),
        pltpu.VMEM((256, 768), F32),
        pltpu.VMEM((3, 256, 768), BF16),
        pltpu.VMEM((3, 256, 768), BF16),
        pltpu.VMEM((4, 256, 192), BF16),
        dma(4), dma(4), dma(3, 2), dma(3, 2), dma(3, 2), dma(3, 2),
    ]
    cost = (4 * 256 * 768 * 768 + 8 * 1024 * 768 * 768, 20 << 20, 1 << 10)
    operands = (grad, xhat2, r2, xhat1, r1, vecs, slope.reshape(4, 256, 768), w1, w2, wo, xg, act, rows)
    res, ridden = call(block_back_kernel, operands, outs, scratch, cid, "block_back", cost, riders)
    back, do, stats, d_up, d_down, d_out = res
    return back, do.reshape(1024, 192), stats, d_up, d_down, d_out, ridden


def inner_back_kernel(
    ride, parent_ref, qw_ref, kv_ref, do_ref, o_ref, lse_ref, w_ref, back_ref, xg_ref, mark_ref,
    grad_ref, low_ref, din_ref, sum_out_ref, mem_ref,
    qm_ref, dm_ref, row_ref, acc_ref, wide_ref, dkv_ref, dqs_ref,
    w_send, w_recv, term_ref, all_in_ref, dq_ref, own_ref, part_ref,
    near_ref, join_ref, sum_ref, far_ref, pass_ref, take_ref,
    q_send, q_recv, n_send, n_recv, j_send, j_recv, f_send, f_recv, p_send, p_recv, flag_ref,
):
    c = lax.axis_index("ctx")
    mark_path(parent_ref, flag_ref, c)
    t = lax.axis_index("tp")
    f, size = lax.axis_index("fsdp"), lax.axis_size("fsdp")
    depth = din_ref.shape[0]
    mate, across, far = mate_of(c), across_of(c), 3 - c
    barrier = pltpu.get_barrier_semaphore()
    for device in (mate, across, far):
        signal(barrier, {"ctx": device})

    @pl.when(t > 0)
    def _():
        signal(barrier, {"tp": t - 1})

    @pl.when(t < 3)
    def _():
        signal(barrier, {"tp": t + 1})

    for k in range(1, size):
        signal(barrier, {"fsdp": (f + size - k) % size})
    ends = (t // 3) + (3 - t) // 3
    count = 5 - ends + size - 1 + ride.greet(barrier)
    ride.ready()

    low = lax.broadcasted_iota(jnp.int32, (1024, 128), 1) < 64
    pair = qw_ref[:, 0:128]
    none = jnp.zeros_like(pair)
    qm_ref[0] = jnp.where(low, pair, none)
    qm_ref[1] = jnp.where(low, none, pair)
    qm_ref[2] = qw_ref[:, 128:256]
    pair = do_ref[:, 0:128]
    dm_ref[0] = jnp.where(low, pair, none)
    dm_ref[1] = jnp.where(low, none, pair)
    dm_ref[2] = jnp.concatenate([do_ref[:, 128:192], none[:, :64]], axis=1)
    product = do_ref[...].astype(F32) * o_ref[...].astype(F32)
    head_row = lax.broadcasted_iota(jnp.int32, (8, 192), 0)
    head_of = lax.broadcasted_iota(jnp.int32, (8, 192), 1) // 64
    delta = lax.dot_general(
        (head_row == head_of).astype(F32), product, (((1,), (1,)), ((), ())),
        precision=lax.Precision.HIGHEST, preferred_element_type=F32,
    )
    for quarter in range(4):
        row_ref[quarter, 0:8] = lse_ref[quarter]
        row_ref[quarter, 8:16] = delta[:, quarter * 256 : (quarter + 1) * 256]
    acc_ref[...] = jnp.zeros_like(acc_ref)
    wide_ref[...] = jnp.zeros_like(wide_ref)
    pl.semaphore_wait(barrier, count)
    ride.start()

    def partner(slot):
        return rcopy(dqs_ref.at[slot], dq_ref.at[2 * slot + 1], q_send.at[slot], q_recv.at[slot], {"ctx": far})

    def near(chunk):
        return rcopy(dkv_ref.at[mate, chunk], near_ref.at[chunk], n_send.at[chunk], n_recv.at[chunk], {"ctx": mate})

    def join(chunk):
        return rcopy(dkv_ref.at[far, chunk], join_ref.at[chunk], j_send.at[chunk], j_recv.at[chunk], {"ctx": mate})

    def cross(chunk):
        return rcopy(sum_ref.at[chunk], far_ref.at[chunk], f_send.at[chunk], f_recv.at[chunk], {"ctx": across})

    pieces = (pl.ds(0, PIECE), pl.ds(PIECE, PIECE))

    def onward(side, chunk, p):
        return rcopy(
            pass_ref.at[chunk, pieces[p]], take_ref.at[side, chunk, pieces[p]],
            p_send.at[chunk, p], p_recv.at[side, chunk, p], {"tp": t - 1 + 2 * side},
        )

    def passed(side, chunk, p):
        part = take_ref.at[side, chunk, pieces[p]]
        rcopy(part, part, p_send.at[0, p], p_recv.at[side, chunk, p], {"tp": t}).wait_recv()

    chunks = [ordered(t, 3 - k) for k in range(4)]
    at_end = (t == 0) | (t == 3)

    def leave(k):
        chunk = chunks[k]
        dkv_ref[:, chunk] = wide_ref[:, chunk].astype(BF16)
        join(chunk).start()
        near(chunk).start()
        query = (acc_ref[chunk].astype(BF16).astype(F32) * 0.125).astype(BF16)

        @pl.when(chunk % 2 == 0)
        def _():
            dq_ref[chunk] = query

        @pl.when(chunk % 2 == 1)
        def _():
            dqs_ref[chunk // 2] = query
            partner(chunk // 2).start()

    def go_across(k):
        chunk = chunks[k]
        join(chunk).wait_recv()
        sum_ref[chunk] = (dkv_ref[across, chunk].astype(F32) + join_ref[chunk].astype(F32)).astype(BF16)
        cross(chunk).start()

    def gather_up(k):
        chunk = chunks[k]
        if k < 3:

            @pl.when(chunk % 2 == 1)
            def _():
                partner(chunk // 2).wait_recv()

        near(chunk).wait_recv()
        cross(chunk).wait_recv()
        own = (
            dkv_ref[c, chunk].astype(F32) + near_ref[chunk].astype(F32) + far_ref[chunk].astype(F32)
        ).astype(BF16)
        own_ref[chunk] = own
        part_ref[chunk] = mm_nt(dq_ref[chunk], w_ref[:, 0:256]) + mm_nt(own, w_ref[:, 256:640])

    def relay(k):
        chunk = chunks[k]

        def move(side, first):
            for p in range(2):

                @pl.when(jnp.logical_not(first))
                def _():
                    passed(side, chunk, p)
                    total = part_ref[chunk, pieces[p]] + take_ref[side, chunk, pieces[p]].astype(F32)
                    pass_ref[chunk, pieces[p]] = total.astype(BF16)

                @pl.when(first)
                def _():
                    pass_ref[chunk, pieces[p]] = part_ref[chunk, pieces[p]].astype(BF16)

                onward(side, chunk, p).start()

        @pl.when(chunk < t)
        def _():
            move(0, t == 3)

        @pl.when(chunk > t)
        def _():
            move(1, t == 0)

    def relay_ends(k):
        pl.when(at_end)(functools.partial(relay, k))

    def relay_inner(k):
        pl.when(jnp.logical_not(at_end))(functools.partial(relay, k))

    low_keys = lax.broadcasted_iota(jnp.int32, (256, 128), 1) < 64

    def one_item(item, done):
        phase = (item + 9) // 16 + (item + 4) // 16 + (item + 1) // 16
        number = item - phase * (8 - phase)
        second = number // (4 - phase)
        query_at = ordered_by(t, 3 - (phase + second * (number - 3 + phase)))
        key_at = ordered_by(t, 3 - (phase + (1 - second) * number))
        half = query_at % 2
        rows = pl.ds(pl.multiple_of(query_at * 256, 256), 256)

        def visit(segments):
            queries = [qm_ref[head, rows] for head in range(3)]
            grads = [dm_ref[head, rows] for head in range(3)]
            made = []
            for segment in segments:
                penalty = jnp.where(flag_ref[half, segment] > 0, 0.0, FAR)
                key_pair = kv_ref[segment, key_at, :, 0:128]
                mixed = kv_ref[segment, key_at, :, 128:256]
                value_pair = kv_ref[segment, key_at, :, 256:384]
                for head in range(3):
                    shift = row_ref[query_at, head : head + 1] + penalty
                    prob = jnp.exp(mm_nt(key_pair if head < 2 else mixed, queries[head]) - shift)
                    grad_prob = mm_nt(value_pair if head < 2 else mixed, grads[head])
                    grad_score = (prob * (grad_prob - row_ref[query_at, 8 + head : 9 + head])).astype(BF16)
                    made.append((prob.astype(BF16), grad_score))
            pair_sum, mixed_sum = 0.0, 0.0
            for number, segment in enumerate(segments):
                (p0, g0), (p1, g1), (p2, g2) = made[3 * number : 3 * number + 3]
                for_keys = mm(g0, queries[0]) + mm(g1, queries[1])
                for_mixed = mm(g2, queries[2]) + mm(p2, grads[2])
                for_values = mm(p0, grads[0]) + mm(p1, grads[1])
                wide_ref[segment, key_at] += jnp.concatenate([for_keys, for_mixed, for_values], axis=1)
                key_pair = kv_ref[segment, key_at, :, 0:128]
                nothing = jnp.zeros_like(key_pair)
                pair_sum += mm_tn(g0, jnp.where(low_keys, key_pair, nothing))
                pair_sum += mm_tn(g1, jnp.where(low_keys, nothing, key_pair))
                mixed_sum += mm_tn(g2, jnp.where(low_keys, nothing, kv_ref[segment, key_at, :, 128:256]))
            acc_ref[query_at] += jnp.concatenate([pair_sum, mixed_sum], axis=1)

        length = c + 1 + half * (3 - 2 * c)

        @pl.loop(0, length // 2)
        def _(two):
            visit((2 * two, 2 * two + 1))

        @pl.when(length % 2 == 1)
        def _():
            visit((length - 1,))

        now = done + length

        def at(place, action, k):
            pl.when(item == place)(functools.partial(action, k))

        def once(amount, action, k):
            pl.when((done < amount) & (now >= amount))(functools.partial(action, k))

        for n in range(len(ride.hops)):
            once(RIDE_HOPS[n], ride.one_hop, n)
        ride.turn_when((done < 14) & (now >= 14))
        for k, place in enumerate((6, 11, 14)):
            at(place, leave, k)
        once(24, go_across, 0)
        once(31, gather_up, 0)
        once(31, relay_ends, 0)
        once(32, go_across, 1)
        once(38, gather_up, 1)
        once(38, relay_ends, 1)
        return now

    lax.fori_loop(0, 16, one_item, 0)
    leave(3)
    go_across(2)
    relay_inner(0)
    go_across(3)
    gather_up(2)
    relay_ends(2)
    relay_inner(1)

    def slice_of(place):
        return pl.ds(pl.multiple_of(place * depth, depth), depth)

    spans = (pl.ds(0, 256), pl.ds(256, 256), pl.ds(512, 128))

    def term(k, span):
        to, cols = (f + k) % size, spans[span]
        return rcopy(
            all_in_ref.at[slice_of(to), cols], term_ref.at[k - 1, :, cols],
            w_send.at[k - 1, span], w_recv.at[k - 1, span], {"fsdp": to},
        )


    @pl.when(t % 2 == 1)
    def _():
        partner(t // 2).wait_recv()

    query = dq_ref[...].reshape(1024, 256)
    for span in range(3):
        if span == 0:
            ride.chain()
        if span == 1:
            relay_inner(2)
            gather_up(3)
            ride.chain_turn()
        own = own_ref[...].reshape(1024, 384)
        made = (query, own[:, 0:256], own[:, 256:384])[span]
        all_in_ref[:, spans[span]] = mm_tn(xg_ref[...], made).astype(BF16)
        for k in range(1, size):
            term(k, span).start()

    sum_out_ref[0:1, 0:256] = jnp.sum(query.astype(F32), axis=0, keepdims=True)
    sum_out_ref[0:1, 256:640] = jnp.sum(own.astype(F32), axis=0, keepdims=True)
    ride.put(sum_out_ref)
    ride.store(1)
    grad_ref[...] = part_ref[t] + back_ref[...]

    for side, there in ((0, t < 3), (1, t > 0)):

        @pl.when(there)
        def _():
            for p in range(2):
                passed(side, t, p)
                grad_ref[pieces[p]] += take_ref[side, t, pieces[p]].astype(F32)

    low_ref[...] = grad_ref[...].astype(BF16)
    ride.put(grad_ref, low_ref)
    mem_ref[...] = lax.dot_general(
        mark_ref[...], grad_ref[...], (((0,), (0,)), ((), ())),
        precision=lax.Precision.HIGHEST, preferred_element_type=F32,
    )
    ride.put(mem_ref)
    total = all_in_ref[slice_of(f)].astype(F32)
    for k in range(1, size):
        for span in range(3):
            term(k, span).wait_recv()
        total += term_ref[k - 1].astype(F32)
    din_ref[...] = total.astype(BF16)
    ride.put(din_ref)
    for k in range(1, size):
        for span in range(3):
            term(k, span).wait_send()
    for chunk in range(4):
        join(chunk).wait_send()
        near(chunk).wait_send()
        cross(chunk).wait_send()

        @pl.when(t != chunk)
        def _():
            for p in range(2):
                onward(1, chunk, p).wait_send()

    for slot in range(2):
        partner(slot).wait_send()
    ride.finish()


RIDE_HOPS = (8, 11, 14, 17)


def inner_back(qw, kv, do, o, lse, parents, w, back_one, xg, marks, cid, riders=()):
    size = lax.axis_size("fsdp")
    depth = 768 // size
    f = functools.partial(sds, dtype=F32)
    outs = [f(256, 768), sds(256, 768), sds(depth, 640), f(8, 640), f(marks.shape[1], 768)]
    scratch = [
        pltpu.VMEM((3, 1024, 128), BF16), pltpu.VMEM((3, 1024, 128), BF16), pltpu.VMEM((4, 16, 256), F32),
        pltpu.VMEM((4, 256, 256), F32), pltpu.VMEM((4, 4, 256, 384), F32), pltpu.VMEM((4, 4, 256, 384), BF16),
        pltpu.VMEM((2, 256, 256), BF16),
        dma(size - 1, 3), dma(size - 1, 3), pltpu.VMEM((size - 1, depth, 640), BF16), pltpu.VMEM((768, 640), BF16),
        pltpu.VMEM((4, 256, 256), BF16), pltpu.VMEM((4, 256, 384), BF16),
        pltpu.VMEM((4, 256, 768), F32),
        pltpu.VMEM((4, 256, 384), BF16), pltpu.VMEM((4, 256, 384), BF16),
        pltpu.VMEM((4, 256, 384), BF16), pltpu.VMEM((4, 256, 384), BF16),
        pltpu.VMEM((4, 256, 768), BF16), pltpu.VMEM((2, 4, 256, 768), BF16),
        dma(2), dma(2), dma(4), dma(4), dma(4), dma(4), dma(4), dma(4), dma(4, 2), dma(2, 4, 2),
        pltpu.SMEM((2, 4), jnp.int32),
    ]
    cost = (5 * 512 * 1024 * 64 * 30 + 4 * 1024 * 768 * 640, 16 << 20, 5 * 512 * 1024 * 3)
    operands = (parents, qw, kv.reshape(4, 4, 256, 384), do, o, lse, w, back_one, xg, marks)
    res, ridden = call(inner_back_kernel, operands, outs, scratch, cid, "inner_back", cost, riders, smem=(0,))
    return (*res[:3], res[3][0], res[4], ridden)


def joined(query, key, value, gap):
    return jnp.concatenate(
        [
            query[..., :128], gap, query[..., 128:],
            key[..., :128], value[..., 128:], key[..., 128:], value[..., :128],
        ],
        axis=-1,
    )


def parted(grads):
    query = jnp.concatenate([grads[..., :128], grads[..., 192:256]], axis=-1)
    key = jnp.concatenate([grads[..., 256:384], grads[..., 448:512]], axis=-1)
    value = jnp.concatenate([grads[..., 512:640], grads[..., 384:448]], axis=-1)
    return query, key, value


def added(terms, axes=(0,)):
    return jnp.sum(terms.astype(F32), axis=axes)


def low(values):
    return values.astype(BF16)


def shards(
    hidden, cotangent, mem_pos, parents, memory, wq, wk, wv, wo, w1, w2,
    head_bias, ffn_bias, out_bias, norm_gains, norm_shifts,
):
    c = lax.axis_index("ctx")
    t = lax.axis_index("tp")
    size = lax.axis_size("fsdp")
    layers = wq.shape[0]
    share = hidden.shape[0]
    depth = wq.shape[1]
    piece = depth // 4
    positions = t * share + jnp.arange(share, dtype=jnp.int32)
    marks = (mem_pos[0, 0][None, :] == positions[:, None]).astype(F32)
    stream = hidden.astype(F32) + jnp.dot(
        marks, memory, precision=lax.Precision.HIGHEST, preferred_element_type=F32
    )
    ids = jnp.arange(4, dtype=jnp.int32)

    gap = jnp.zeros(wq.shape[:2] + (64,), BF16)
    own_in = joined(wq, wk, wv, gap)
    none = jnp.zeros((layers, 192), F32)
    in_bias = joined(head_bias[:, 0], none, head_bias[:, 1], jnp.zeros((layers, 64), F32))
    down_turned = jnp.swapaxes(w2, 1, 2)
    out_turned = jnp.swapaxes(wo, 1, 2).reshape(layers, 4, piece, 192)
    out_piece = lax.dynamic_index_in_dim(out_turned, c, axis=1, keepdims=False)

    def vectors(n):
        norms = [norm_gains[n, 0], norm_shifts[n, 0], norm_gains[n, 1], norm_shifts[n, 1]]
        return jnp.concatenate([out_bias[n], jnp.stack(norms), jnp.zeros((2, 768), F32)])

    saved, weights = [], []
    rounded = low(stream)
    riders = [plane_gather(out_piece[0], size), ctx_gather(sds(4, size, piece, 192), axis=2, first=0)]
    riders += [flip_gather(w1[0], size).later(), tp_flip(down_turned[0]).later(hopped=True), tp_flip(ffn_bias)]
    xg, qw, kv, o, lse, w_in, got = inner(rounded, own_in[0], in_bias[0][None], parents, 0, riders, fetch=True)
    _, out, w_up, down, units = got
    for n in range(layers):
        last = n == layers - 1
        w_out = out.reshape(4, 768, 192)
        w_up = w_up.reshape(768, 768)
        vecs = vectors(n)
        riders = []
        if not last:
            riders = [
                tp_flip(w1[n + 1]),
                plane_gather(out_piece[n + 1], size), fsdp_gather(own_in[n + 1], size),
            ]
        stream, rounded, xhat1, r1, xhat2, r2, xg2, act, slope, rows, w_down, got = block(
            o, w_out, w_up, down, units[n][None], vecs, stream, 16 * n + 2, riders
        )
        weights.append((w_in, w_up, w_down, w_out, vecs))
        saved.append((xg, qw, kv, o, lse, xhat1, r1, xhat2, r2, xg2, act, slope, rows))
        if not last:
            up, out, w_in = got
            riders = [ctx_gather(out, axis=2), tp_flip(down_turned[n + 1]).later(), fsdp_gather(up, size)]
            xg, qw, kv, o, lse, w_in, (out, down, w_up) = inner(
                rounded, w_in.reshape(768, 640), in_bias[n + 1][None], parents, 16 * n + 16, riders
            )
    output = rounded

    grad = cotangent.astype(F32)
    small, heads = [None] * layers, [None] * layers
    done = [None] * layers
    above = None
    for n in reversed(range(layers)):
        w_in, w_up, w_down, w_out, vecs = weights[n]
        xg, qw, kv, o, lse, xhat1, r1, xhat2, r2, xg2, act, slope, rows = saved[n]
        riders = []
        if above is not None:
            riders = [plane_scatter(above["out"], size), ctx_scatter(above["in"])]
            riders += [ctx_gather(sds(piece, 192), first=0, summed=True)]
            riders += [ctx_gather(sds(piece, 640), first=1, summed=True)]
        back_one, do, small[n], d_up, d_down, d_out, got = block_back(
            grad, xhat2, r2, xhat1, r1, vecs, slope, w_up, w_down, w_out, xg2, act, rows, 16 * n + 3, riders
        )
        quarters = sds(4, depth // 4, 768)
        riders = [
            tp_flip(d_up.reshape(quarters.shape)), scatter_flip(d_down.reshape(size, *quarters.shape)),
            ctx_scatter(d_out.reshape(4, size, 4, piece, 192), axis=2),
            ctx_scatter(quarters, first=0), ctx_scatter(quarters, first=1),
        ]
        riders += [stored_sum(at, riders[at].out) for at in (2, 3, 4)]
        if above is not None:
            done[n + 1] = tuple(got[2:4])
            riders += [ctx_gather(above["up"]), ctx_gather(above["down"])]
        grad, low_grad, d_in, sums, memory_part, got = inner_back(
            qw, kv, do, o, lse, parents, w_in, back_one, xg, marks, 16 * n + 4, riders
        )
        if above is not None:
            done[n + 1] = (done[n + 1][1], done[n + 1][0], got[8], got[9])
        d_query_bias, _, d_value_bias = parted(sums)
        heads[n] = jnp.stack([d_query_bias, d_value_bias])
        above = {
            "up": got[6],
            "down": got[7],
            "in": d_in.reshape(4, depth // 4, 640),
            "out": got[5],
        }
    hidden_grad = low_grad
    small = jnp.stack(small)
    place = (ids == t).astype(F32)
    unit = (ids == flipped_place(c, t)).astype(F32)
    head_rows = (jnp.stack(heads)[:, :, None, :] * place[None, None, :, None]).reshape(2 * layers, 768)
    unit_rows = (small[:, 6][:, None, :] * unit[None, :, None]).reshape(4 * layers, 768)
    stat_rows = small[:, :6].reshape(6 * layers, 768)
    filled = 12 * layers + memory_part.shape[0]
    slices = 4 * size
    width = -(-filled // slices)
    rest = jnp.zeros((width * slices - filled, 768), F32)
    sums = jnp.concatenate([stat_rows, unit_rows, head_rows, memory_part, rest])
    sums = sums.reshape(4, size, width, 768)
    riders = [ctx_scatter(above["in"]), plane_scatter(above["out"], size), plane_scatter(sums, size)]
    riders += [ctx_gather(above["up"]).later(), ctx_gather(above["down"]).later()]
    riders += [ctx_gather(sds(piece, 640), first=0, summed=True), ctx_gather(sds(piece, 192), first=1, summed=True)]
    got = carry(riders + [small_sum(sds(width, 768, dtype=F32), size, first=2)], 6)[3:]
    done[0] = (got[2], got[3], got[0], got[1])
    totals = got[4].reshape(width * slices, 768)
    stats = totals[: 6 * layers].reshape(layers, 6, 768)
    at = 6 * layers
    ffn_rows = totals[at : at + 4 * layers].reshape(layers, 4, 768)
    ffn_grad = jnp.sum(ffn_rows * place[None, :, None], axis=1)
    at += 4 * layers
    head_sums = totals[at : at + 2 * layers].reshape(layers, 2, 4, 192)
    head_grad = jnp.sum(head_sums * place[None, None, :, None], axis=2)
    at += 2 * layers
    memory_grad = totals[at : at + memory_part.shape[0]]
    d_in = jnp.stack([part[0].reshape(depth, 640) for part in done]).astype(F32)
    d_out = jnp.stack([jnp.swapaxes(part[1].reshape(depth, 192), 0, 1) for part in done]).astype(F32)
    d_up = jnp.stack([part[2].reshape(depth, 768) for part in done]).astype(F32)
    d_down = jnp.stack([jnp.swapaxes(part[3].reshape(depth, 768), 0, 1) for part in done]).astype(F32)
    return (
        output, hidden_grad, memory_grad, *parted(d_in), d_out, d_up, d_down,
        head_grad, ffn_grad, stats[:, 4:6], stats[:, 0:2], stats[:, 2:4],
    )


def solution(mesh):
    rows = P(("fsdp", "ctx", "tp"), None)
    inner = P(None, "fsdp", "tp")
    outer = P(None, "tp", "fsdp")
    weights = (inner, inner, inner, outer, inner, outer)
    biases = (P(None, None, "tp"), P(None, "tp"), P(), P(), P())
    return jax.shard_map(
        shards,
        mesh=mesh,
        in_specs=(rows, rows, P("fsdp", "ctx", None), P("fsdp", None), P()) + weights + biases,
        out_specs=(rows, rows, P()) + weights + biases,
        check_vma=False,
    )
```

```python
import functools

import jax
import jax.numpy as jnp
from jax import lax
from jax.experimental import pallas as pl
from jax.experimental.pallas import tpu as pltpu
from jax.sharding import PartitionSpec as P

EPSILON = 1e-05
MASKED = -1000000000.0
MESH = pl.DeviceIdType.MESH
F32 = jnp.float32
BF16 = jnp.bfloat16
ORDER = ((0, 1), (1, 0), (2, 2), (3, 3))


def mm(left, right):
    return jnp.dot(left, right, preferred_element_type=F32)


def mm_nt(left, right):
    return lax.dot_general(left, right, (((1,), (1,)), ((), ())), preferred_element_type=F32)


def mm_tn(left, right):
    return lax.dot_general(left, right, (((0,), (0,)), ((), ())), preferred_element_type=F32)


def rcopy(src, dst, send_sem, recv_sem, device):
    return pltpu.make_async_remote_copy(
        src_ref=src,
        dst_ref=dst,
        send_sem=send_sem,
        recv_sem=recv_sem,
        device_id=device,
        device_id_type=MESH,
    )


def mate_of(c):
    return c + 1 - 2 * (c % 2)


def across_of(c):
    return (c + 2) % 4


def signal(sem, device):
    pl.semaphore_signal(sem, inc=1, device_id=device, device_id_type=MESH)


def ordered(place, step):
    half = place // 2
    inner = place + half * (3 - 2 * place)
    first, second = ORDER[step]
    chunk = first + inner * (second - first)
    return chunk + half * (3 - 2 * chunk)


def ordered_by(place, step):
    half = place // 2
    inner = place + half * (3 - 2 * place)
    chunk = step + inner * (1 - 2 * step) * ((3 - step) // 2)
    return chunk + half * (3 - 2 * chunk)


def mark_path(parent_ref, flag_ref, c):
    for half, first in enumerate((c, 3 - c)):
        path = [first]
        for _ in range(3):
            path.append(parent_ref[0, path[-1]])
        for other in range(4):
            found = path[0] == other
            for segment in path[1:]:
                found = found | (segment == other)
            flag_ref[half, other] = found.astype(jnp.int32)


def dma(*shape):
    return pltpu.SemaphoreType.DMA(shape)


class Rider:
    def __init__(self, array, out, make, scratch, chunks=0, summed=None):
        self.array, self.out, self.make, self.scratch, self.chunks = array, out, make, scratch, chunks
        self.summed = summed
        self.late = self.hopped = False

    def later(self, hopped=False):
        self.late, self.hopped = True, hopped
        return self


class Copies:
    def __init__(self, steps, here, scratch):
        self.steps, self.here = steps, here
        self.send, self.recv, self.leg, self.stage = scratch
        self.came = False

    def greetings(self):
        return [(origin, when, weight) for _, origin, _, _, when, weight in self.steps]

    def copies(self):
        for number, (to, _, source, target, when, _) in enumerate(self.steps):
            yield rcopy(source, target, self.send.at[number], self.recv.at[number], to), when

    def inward(self):
        return pltpu.make_async_copy(self.here[0], self.stage, self.leg.at[0])

    def outward(self):
        return pltpu.make_async_copy(self.stage, self.here[1], self.leg.at[1])

    def start(self):
        for copy, when in self.copies():
            guarded(when, copy.start)
        guarded(self.here[2], self.inward().start)

    def turn(self):
        guarded(self.here[2], self.inward().wait)
        guarded(self.here[2], self.outward().start)

    def arrive(self):
        self.came = True
        for copy, when in self.copies():
            guarded(when, copy.wait_recv)
        guarded(self.here[2], self.outward().wait)

    def finish(self):
        if not self.came:
            self.arrive()
        for copy, when in self.copies():
            guarded(when, copy.wait_send)


class FlipGather:
    def __init__(self, source, target, place, scratch):
        self.source, self.target = source, target
        self.f, self.c, self.t = place
        self.size = target.shape[0]
        self.send, self.recv, self.on_send, self.on_recv, self.leg, self.stage = scratch
        self.moves = self.c > 0

    def greetings(self):
        there = {"tp": flipped_place(self.c, self.t)}
        ring = [({"fsdp": (self.f + self.size - k) % self.size}, None, 1) for k in range(1, self.size)]
        return [(there, self.moves, (self.c + 3) // 4)] + ring

    def first(self, chunk):
        there = {"tp": flipped_place(self.c, self.t)}
        return rcopy(
            self.source.at[chunk], self.target.at[self.f, chunk], self.send.at[chunk], self.recv.at[chunk], there
        )

    def second(self, chunk, k, moved):
        source = self.target.at[self.f, chunk] if moved else self.source.at[chunk]
        device = {"fsdp": (self.f + k) % self.size}
        return rcopy(
            source, self.target.at[self.f, chunk], self.on_send.at[k - 1, chunk], self.on_recv.at[k - 1, chunk], device
        )

    def inward(self):
        return pltpu.make_async_copy(self.source, self.stage, self.leg.at[0])

    def outward(self):
        return pltpu.make_async_copy(self.stage, self.target.at[self.f], self.leg.at[1])

    def start(self):
        @pl.when(self.moves)
        def _():
            for chunk in range(self.source.shape[0]):
                self.first(chunk).start()

        @pl.when(self.c == 0)
        def _():
            self.inward().start()

    def hop(self, chunk):
        @pl.when(self.moves)
        def _():
            self.first(chunk).wait_recv()
            for k in range(1, self.size):
                self.second(chunk, k, True).start()

        @pl.when(self.c == 0)
        def _():
            for k in range(1, self.size):
                self.second(chunk, k, False).start()

    def turn(self):
        @pl.when(self.c == 0)
        def _():
            self.inward().wait()
            self.outward().start()

    def finish(self):
        @pl.when(self.moves)
        def _():
            for chunk in range(self.source.shape[0]):
                self.first(chunk).wait_send()

        for chunk in range(self.source.shape[0]):
            for k in range(1, self.size):
                self.second(chunk, k, False).wait()

        @pl.when(self.c == 0)
        def _():
            self.outward().wait()


class ScatterFlip:
    def __init__(self, source, target, place, scratch):
        self.source, self.target = source, target
        self.f, self.c, self.t = place
        self.size = source.shape[0]
        self.here = False
        self.send, self.recv, self.on_send, self.on_recv, self.leg, self.got, self.out = scratch
        self.moves = self.c > 0

    def greetings(self):
        there = {"tp": flipped_place(self.c, self.t)}
        ring = [({"fsdp": (self.f + self.size - k) % self.size}, None, 1) for k in range(1, self.size)]
        return [(there, self.moves, (self.c + 3) // 4)] + ring

    def first(self, chunk, k):
        to = (self.f + k) % self.size
        return rcopy(
            self.source.at[to, chunk], self.got.at[k, chunk],
            self.send.at[k - 1, chunk], self.recv.at[k - 1, chunk], {"fsdp": to},
        )

    def own(self, chunk):
        return pltpu.make_async_copy(
            self.source.at[self.f, chunk], self.got.at[0, chunk], self.leg.at[chunk]
        )

    def second(self, chunk):
        there = {"tp": flipped_place(self.c, self.t)}
        return rcopy(self.out.at[chunk], self.target.at[chunk], self.on_send.at[chunk], self.on_recv.at[chunk], there)

    def stays(self, chunk):
        return pltpu.make_async_copy(self.out.at[chunk], self.target.at[chunk], self.on_send.at[chunk])

    def start(self):
        for chunk in range(self.target.shape[0]):
            for k in range(1, self.size):
                self.first(chunk, k).start()
            self.own(chunk).start()

    def hop(self, chunk):
        self.own(chunk).wait()
        total = self.got[0, chunk].astype(F32)
        for k in range(1, self.size):
            self.first(chunk, k).wait_recv()
            total += self.got[k, chunk].astype(F32)
        self.out[chunk] = total.astype(BF16)

        @pl.when(self.moves)
        def _():
            self.second(chunk).start()

        @pl.when(self.c == 0)
        def _():
            self.stays(chunk).start()

    def turn(self):
        pass

    def arrive(self):
        self.here = True
        for chunk in range(self.target.shape[0]):
            guarded(self.moves, self.second(chunk).wait_recv)
            guarded(self.c == 0, self.stays(chunk).wait)

    def finish(self):
        if not self.here:
            self.arrive()
        for chunk in range(self.target.shape[0]):
            for k in range(1, self.size):
                self.first(chunk, k).wait_send()
            guarded(self.moves, self.second(chunk).wait_send)


class CtxGather:
    def __init__(self, pick, source, target, place, scratch):
        self.source, self.target, self.pick = source, target, pick
        self.c = place[1]
        self.send, self.recv, self.leg, self.stage = scratch

    def greetings(self):
        return [({"ctx": mate_of(self.c)}, None, 1), ({"ctx": across_of(self.c)}, None, 1)]

    def copy(self, number):
        c = self.c
        device = across_of(c) if number == 0 else mate_of(c)
        source = self.pick(self.target, across_of(c)) if number == 2 else self.source
        slot = across_of(c) if number == 2 else c
        return rcopy(source, self.pick(self.target, slot), self.send.at[number], self.recv.at[number], {"ctx": device})

    def inward(self):
        return pltpu.make_async_copy(self.source, self.stage, self.leg.at[0])

    def outward(self):
        return pltpu.make_async_copy(self.stage, self.pick(self.target, self.c), self.leg.at[1])

    def start(self):
        self.copy(0).start()
        self.copy(1).start()
        self.inward().start()

    def turn(self):
        self.inward().wait()
        self.outward().start()
        self.copy(0).wait_recv()
        self.copy(2).start()

    def finish(self):
        self.copy(0).wait_send()
        self.copy(1).wait()
        self.copy(2).wait()
        self.outward().wait()


class CtxScatter:
    def __init__(self, pick, source, target, place, scratch):
        self.source, self.target, self.pick = source, target, pick
        self.c, self.came = place[1], False
        self.send, self.recv, self.leg, self.stage, self.cross, self.far, self.total = scratch

    def greetings(self):
        return [({"ctx": mate_of(self.c)}, None, 1), ({"ctx": across_of(self.c)}, None, 1)]

    def copy(self, number):
        c = self.c
        device = across_of(c) if number == 2 else mate_of(c)
        source = (self.pick(self.source, 3 - c), self.pick(self.source, mate_of(c)), self.total)[number]
        target = (self.far, self.target.at[1], self.target.at[2])[number]
        return rcopy(source, target, self.send.at[number], self.recv.at[number], {"ctx": device})

    def inward(self):
        return pltpu.make_async_copy(self.pick(self.source, self.c), self.stage, self.leg.at[0])

    def outward(self):
        return pltpu.make_async_copy(self.stage, self.target.at[0], self.leg.at[1])

    def beside(self):
        return pltpu.make_async_copy(self.pick(self.source, across_of(self.c)), self.cross, self.leg.at[2])

    def start(self):
        self.copy(0).start()
        self.beside().start()
        self.copy(1).start()
        self.inward().start()

    def turn(self):
        self.copy(0).wait_recv()
        self.beside().wait()
        self.total[...] = (self.cross[...].astype(F32) + self.far[...].astype(F32)).astype(self.total.dtype)
        self.copy(2).start()
        self.inward().wait()
        self.outward().start()

    def arrive(self):
        self.came = True
        self.copy(1).wait_recv()
        self.copy(2).wait_recv()
        self.outward().wait()

    def finish(self):
        if not self.came:
            self.arrive()
        for number in range(3):
            self.copy(number).wait_send()


class Riding:
    def __init__(self, riders, sources, targets, scratch, fetches, results, puts):
        self.fetches, self.results, self.puts = fetches, results, puts
        self.gone = [False] * len(puts)
        place = tuple(lax.axis_index(axis) for axis in ("fsdp", "ctx", "tp"))
        scratch = list(scratch)
        self.rides, self.hops, self.late, self.hopped = [], [], [], []
        self.firsts, self.seconds, self.begun, self.turned, self.sums = [], [], [], [], {}
        self.stores, self.stored = [], 0
        for rider, target in zip(riders, targets):
            own = [scratch.pop(0) for _ in rider.scratch]
            chained = isinstance(rider.array, int)
            source = targets[rider.array] if chained else sources.pop(0)
            if rider.make is None:
                terms, total, sem = own
                fetch = pltpu.make_async_copy(source, terms, sem.at[0])
                self.stores.append((self.rides[rider.array], fetch, terms, total, total_copy(total, target, sem)))
                continue
            if rider.summed is not None:
                terms, total, sem = (scratch.pop(0) for _ in range(3))
                self.sums[len(self.seconds)] = (pltpu.make_async_copy(source, terms, sem.at[0]), terms, total)
                source = total
            ride = rider.make(source, target, place, own)
            self.rides.append(ride)
            if chained:
                self.firsts.append(self.rides[rider.array])
                self.seconds.append(ride)
                self.late.append(ride)
            if rider.late:
                self.late.append(ride)
            if rider.hopped:
                self.hopped.append(ride)
            self.hops += [(ride, chunk) for chunk in range(rider.chunks)]

    def ready(self):
        for fetch in self.fetches:
            fetch.wait()

    def put(self, *refs):
        for ref in refs:
            slot = [ref is result for result in self.results].index(True)
            self.gone[slot] = True
            self.puts[slot].start()

    def close(self):
        for slot, put in enumerate(self.puts):
            if not self.gone[slot]:
                put.start()
        for put in self.puts:
            put.wait()

    def greet(self, barrier):
        count = 0
        for ride in self.rides:
            for origin, when, weight in ride.greetings():
                guarded(when, functools.partial(signal, barrier, origin))
                count = count + weight
        return count

    def begin(self, ride):
        self.begun.append(ride)
        ride.start()

    def start(self):
        for ride in self.rides:
            if ride not in self.late:
                self.begin(ride)

    def start_late(self):
        for ride in self.late:
            if ride not in self.hopped + self.seconds:
                self.begin(ride)

    def one_hop(self, at):
        ride, chunk = self.hops[at]
        ride.hop(chunk)
        if at == len(self.hops) - 1:
            for ride in self.hopped:
                self.begin(ride)

    def turn(self):
        for ride in self.begun:
            if ride not in self.turned + self.seconds:
                self.turned.append(ride)
                ride.turn()

    def turn_when(self, when):
        if self.rides:
            pl.when(when)(self.turn)

    def chain(self):
        for number, (first, second) in enumerate(zip(self.firsts, self.seconds)):
            first.arrive()
            if number in self.sums:
                fetch, terms, total = self.sums[number]
                fetch.start()
                fetch.wait()
                axes = tuple(range(len(terms.shape) - len(total.shape)))
                total[...] = jnp.sum(terms[...].astype(F32), axis=axes).astype(total.dtype)
            self.begin(second)

    def chain_turn(self):
        for second in self.seconds:
            self.turned.append(second)
            second.turn()

    def store(self, count):
        batch = self.stores[self.stored : self.stored + count]
        for first, fetch, *_ in batch:
            first.arrive()
            fetch.start()
        for _, fetch, terms, total, put in batch:
            fetch.wait()
            total[...] = jnp.sum(terms[...].astype(F32), axis=0).astype(total.dtype)
            put.start()
        self.stored += count

    def finish(self):
        for ride in self.rides:
            if ride not in self.turned:
                ride.turn()
        self.store(len(self.stores))
        for ride in self.rides:
            ride.finish()
        for store in self.stores:
            store[4].wait()


def total_copy(total, target, sem):
    return pltpu.make_async_copy(total, target, sem.at[1])


def guarded(when, action):
    if when is None:
        action()
    else:
        pl.when(when)(action)


def call(kernel, operands, out_shapes, scratch, collective_id, name, cost, riders=(), smem=()):
    n_in, n_out, n_scratch, n_ride = len(operands), len(out_shapes), len(scratch), len(riders)
    large = [i for i in range(n_in) if i not in smem]
    carried = [rider.array for rider in riders if not isinstance(rider.array, int)]

    def body(*refs):
        refs = list(refs)
        take = lambda n: [refs.pop(0) for _ in range(n)]
        ins, sources, outs, targets = take(n_in), take(len(carried)), take(n_out), take(n_ride)
        near_ins, near_outs, (in_sem, out_sem), own = take(len(large)), take(n_out), take(2), take(n_scratch)
        fetches = [
            pltpu.make_async_copy(ins[i], near, in_sem.at[slot]) for slot, (i, near) in enumerate(zip(large, near_ins))
        ]
        for fetch in fetches:
            fetch.start()
        for i, near in zip(large, near_ins):
            ins[i] = near
        puts = [pltpu.make_async_copy(near, far, out_sem.at[i]) for i, (near, far) in enumerate(zip(near_outs, outs))]
        ride = Riding(riders, sources, targets, refs, fetches, near_outs, puts)
        kernel(ride, *ins, *near_outs, *own)
        ride.close()

    params = dict(vmem_limit_bytes=60 * 1024 * 1024)
    if collective_id is not None:
        params.update(collective_id=collective_id, has_side_effects=True)
    extra = []
    for rider in riders:
        extra += rider.scratch
        if rider.summed is not None:
            terms, total = riders[rider.array].out, rider.summed
            extra += [pltpu.VMEM(terms.shape, terms.dtype), pltpu.VMEM(total.shape, total.dtype), dma(1)]
    anywhere = pl.BlockSpec(memory_space=pl.ANY)
    near = [pltpu.VMEM(operands[i].shape, operands[i].dtype) for i in large]
    near += [pltpu.VMEM(out.shape, out.dtype) for out in out_shapes]
    results = pl.pallas_call(
        body,
        out_shape=list(out_shapes) + [rider.out for rider in riders],
        in_specs=[pl.BlockSpec(memory_space=pltpu.SMEM) if i in smem else anywhere for i in range(n_in)]
        + [anywhere] * len(carried),
        out_specs=[anywhere] * (n_out + n_ride),
        scratch_shapes=near + [dma(max(len(large), 1)), dma(max(n_out, 1))] + list(scratch) + extra,
        compiler_params=pltpu.CompilerParams(**params),
        cost_estimate=pl.CostEstimate(flops=cost[0], bytes_accessed=cost[1], transcendentals=cost[2]),
        name=name,
    )(*operands, *carried)
    return results[:n_out], results[n_out:]


def copies_rider(array, out, steps, stage, plan):
    def make(source, target, place, scratch):
        return Copies(*plan(source, target, *place), scratch)

    scratch = [dma(steps), dma(steps), dma(2), pltpu.VMEM(stage, array.dtype)]
    return Rider(array, out, make, scratch)


def flip_gather(own, size):
    own = own.reshape(2, own.shape[0] // 2, own.shape[1])
    scratch = [dma(2), dma(2), dma(size - 1, 2), dma(size - 1, 2), dma(2), pltpu.VMEM(own.shape, own.dtype)]
    return Rider(own, sds(size, *own.shape), FlipGather, scratch, chunks=2)


def scatter_flip(parts):
    size, n = parts.shape[0], parts.shape[1]
    shape = parts.shape[1:]
    scratch = [
        dma(size - 1, n), dma(size - 1, n), dma(n), dma(n), dma(n),
        pltpu.VMEM((size, *shape), BF16), pltpu.VMEM(shape, BF16),
    ]
    return Rider(parts, sds(*shape), ScatterFlip, scratch, chunks=n)


def fsdp_gather(own, size):
    def make(source, target, f, c, t):
        steps = [
            ({"fsdp": (f + k) % size}, {"fsdp": (f + size - k) % size}, source, target.at[f], None, 1)
            for k in range(1, size)
        ]
        return steps, (source, target.at[f], None)

    return copies_rider(own, sds(size, *own.shape, dtype=own.dtype), size - 1, own.shape, make)


def fsdp_scatter(parts, size):
    out = sds(size, parts.shape[0], *parts.shape[2:], dtype=parts.dtype)

    def make(source, target, f, c, t):
        steps = [
            (
                {"fsdp": (f + k) % size}, {"fsdp": (f + size - k) % size},
                source.at[:, (f + k) % size], target.at[k], None, 1,
            )
            for k in range(1, size)
        ]
        return steps, (source.at[:, f], target.at[0], None)

    return copies_rider(parts, out, size - 1, out.shape[1:], make)


def slot_of(axis):
    def pick(ref, slot):
        return ref.at[slot] if axis == 0 else ref.at[:, :, slot]

    return pick


def ctx_gather(own, axis=0, first=None, summed=False):
    scratch = [dma(3), dma(3), dma(2), pltpu.VMEM(own.shape, own.dtype)]
    out = sds(*own.shape[:axis], 4, *own.shape[axis:], dtype=own.dtype)
    make = functools.partial(CtxGather, slot_of(axis))
    return Rider(own if first is None else first, out, make, scratch, summed=own if summed else None)


def ctx_scatter(parts, axis=0, first=None):
    shape = parts.shape[:axis] + parts.shape[axis + 1 :]

    buffer = pltpu.VMEM(shape, parts.dtype)
    scratch = [dma(3), dma(3), dma(3), buffer, buffer, buffer, buffer]
    array = parts if first is None else first
    return Rider(array, sds(3, *shape, dtype=parts.dtype), functools.partial(CtxScatter, slot_of(axis)), scratch)


def flipped_place(c, t):
    return 2 * ((t // 2 + c % 2) % 2) + (t % 2 + c // 2) % 2


def tp_flip(own):
    def make(source, target, f, c, t):
        other = {"tp": flipped_place(c, t)}
        return [(other, other, source, target, c > 0, (c + 3) // 4)], (source, target, c == 0)

    return copies_rider(own, sds(*own.shape, dtype=own.dtype), 1, own.shape, make)


def plane(size):
    return [(kt, kf) for kt in (2, 3, 1, 0) for kf in range(size) if kt + kf > 0]


def plane_gather(own, size):
    def make(source, target, f, c, t):
        steps = [
            (
                {"fsdp": (f + kf) % size, "tp": (t + kt) % 4},
                {"fsdp": (f + size - kf) % size, "tp": (t + 4 - kt) % 4},
                source, target.at[t, f], None, 1,
            )
            for kt, kf in plane(size)
        ]
        return steps, (source, target.at[t, f], None)

    return copies_rider(own, sds(4, size, *own.shape, dtype=own.dtype), 4 * size - 1, own.shape, make)


def plane_scatter(parts, size):
    def make(source, target, f, c, t):
        steps = [
            (
                {"fsdp": (f + kf) % size, "tp": (t + kt) % 4},
                {"fsdp": (f + size - kf) % size, "tp": (t + 4 - kt) % 4},
                source.at[(t + kt) % 4, (f + kf) % size], target.at[kt, kf], None, 1,
            )
            for kt, kf in plane(size)
        ]
        return steps, (source.at[t, f], target.at[0, 0], None)

    return copies_rider(parts, sds(*parts.shape, dtype=parts.dtype), 4 * size - 1, parts.shape[2:], make)


class SmallSum:
    def __init__(self, source, target, place, scratch):
        self.source, self.target = source, target
        self.f, self.c, self.t = place
        self.size = target.shape[1]
        self.send, self.recv, self.on_send, self.on_recv, self.leg, self.terms, self.total = scratch

    def greetings(self):
        around = [({"ctx": (self.c + 4 - k) % 4}, None, 1) for k in (1, 2, 3)]
        return around + [
            ({"fsdp": (self.f + self.size - kf) % self.size, "tp": (self.t + 4 - kt) % 4}, None, 1)
            for kt, kf in plane(self.size)
        ]

    def first(self, k):
        device = {"ctx": (self.c + k) % 4}
        return rcopy(self.source, self.terms.at[self.c], self.send.at[k - 1], self.recv.at[k - 1], device)

    def own(self):
        return pltpu.make_async_copy(self.source, self.terms.at[self.c], self.leg.at[0])

    def second(self, number):
        kt, kf = plane(self.size)[number]
        device = {"fsdp": (self.f + kf) % self.size, "tp": (self.t + kt) % 4}
        target = self.target.at[self.t, self.f]
        return rcopy(self.total, target, self.on_send.at[number], self.on_recv.at[number], device)

    def stays(self):
        return pltpu.make_async_copy(self.total, self.target.at[self.t, self.f], self.leg.at[1])

    def start(self):
        for k in (2, 3, 1):
            self.first(k).start()
        self.own().start()

    def turn(self):
        self.own().wait()
        for k in (1, 2, 3):
            self.first(k).wait_recv()
        self.total[...] = self.terms[0] + self.terms[1] + self.terms[2] + self.terms[3]
        for number in range(4 * self.size - 1):
            self.second(number).start()
        self.stays().start()

    def finish(self):
        for k in (1, 2, 3):
            self.first(k).wait_send()
        for number in range(4 * self.size - 1):
            self.second(number).wait()
        self.stays().wait()


def stored_sum(first, terms):
    total = sds(*terms.shape[1:], dtype=terms.dtype)
    scratch = [pltpu.VMEM(terms.shape, terms.dtype), pltpu.VMEM(total.shape, total.dtype), dma(2)]
    return Rider(first, total, None, scratch)


def small_sum(own, size, first=None):
    many = 4 * size - 1
    scratch = [
        dma(3), dma(3), dma(many), dma(many), dma(2),
        pltpu.VMEM((4, *own.shape), own.dtype), pltpu.VMEM(own.shape, own.dtype),
    ]
    out = sds(4, size, *own.shape, dtype=own.dtype)
    return Rider(own if first is None else first, out, SmallSum, scratch, summed=None if first is None else own)


def carry_kernel(ride):
    barrier = pltpu.get_barrier_semaphore()
    pl.semaphore_wait(barrier, ride.greet(barrier))
    ride.start()
    ride.turn()
    ride.start_late()
    ride.chain()
    ride.turn()
    ride.chain_turn()
    ride.finish()


def carry(riders, cid):
    return call(carry_kernel, (), (), (), cid, "carry", (1 << 20, 1 << 20, 0), riders)[1]


def sds(*shape, dtype=BF16):
    return jax.ShapeDtypeStruct(shape, dtype)


FAR = 1e30


def inner_kernel(
    fetch, ride, parent_ref, x_ref, w_ref, b_ref, xg_ref, qw_ref, kv_ref, o_ref, lse_ref, *rest
):
    if fetch:
        full_ref, w_send, w_recv, *rest = rest
    (
        qbuf, qm_ref, m_ref, acc_ref, vt_ref, x_recv, x_right, x_left,
        k1_send, k1_recv, k2_send, k2_recv, kf_send, kf_recv, q_send, q_recv, flag_ref,
    ) = rest
    c = lax.axis_index("ctx")
    mark_path(parent_ref, flag_ref, c)
    t = lax.axis_index("tp")
    f, size = lax.axis_index("fsdp"), lax.axis_size("fsdp")
    barrier = pltpu.get_barrier_semaphore()
    for device in (mate_of(c), across_of(c), 3 - c):
        signal(barrier, {"ctx": device})

    @pl.when(t > 0)
    def _():
        signal(barrier, {"tp": t - 1})

    @pl.when(t < 3)
    def _():
        signal(barrier, {"tp": t + 1})

    if fetch:
        for k in range(1, size):
            signal(barrier, {"fsdp": (f + size - k) % size})
    ends = (t // 3) + (3 - t) // 3
    count = 5 - ends + ride.greet(barrier) + (size - 1 if fetch else 0)
    m_ref[...] = jnp.full_like(m_ref, MASKED)
    acc_ref[...] = jnp.zeros_like(acc_ref)
    vt_ref[:, :, :, 64:80] = jnp.ones((4, 4, 3, 16, 256), BF16)
    ride.ready()
    pl.semaphore_wait(barrier, count)

    def right(src, chunk, step):
        return rcopy(src, xg_ref.at[chunk], x_right.at[step], x_recv.at[chunk], {"tp": t + 1})

    def left(src, chunk, step):
        return rcopy(src, xg_ref.at[chunk], x_left.at[step], x_recv.at[chunk], {"tp": t - 1})

    def arrived(chunk):
        rcopy(xg_ref.at[chunk], xg_ref.at[chunk], x_right.at[0], x_recv.at[chunk], {"tp": t}).wait_recv()

    @pl.when(t < 3)
    def _():
        right(x_ref, t, 0).start()

    @pl.when(t > 0)
    def _():
        left(x_ref, t, 0).start()

    def weight(k):
        device = {"fsdp": (f + k) % size}
        return rcopy(w_ref, full_ref.at[f], w_send.at[k - 1], w_recv.at[k - 1], device)

    if fetch:
        for k in range(1, size):
            weight(k).start()
        full_ref[f] = w_ref[...]
    xg_ref[t] = x_ref[...]
    ride.start()
    if fetch:
        for k in range(1, size):
            weight(k).wait_recv()

    def mate(chunk):
        part = kv_ref.at[c, chunk]
        return rcopy(part, part, k1_send.at[chunk], k1_recv.at[chunk], {"ctx": mate_of(c)})

    def across(chunk):
        part = kv_ref.at[c, chunk]
        return rcopy(part, part, k2_send.at[chunk], k2_recv.at[chunk], {"ctx": across_of(c)})

    def onward(chunk):
        part = kv_ref.at[across_of(c), chunk]
        return rcopy(part, part, kf_send.at[chunk], kf_recv.at[chunk], {"ctx": mate_of(c)})

    def partner(slot):
        return rcopy(qbuf.at[slot], qw_ref.at[2 * slot + 1], q_send.at[slot], q_recv.at[slot], {"ctx": 3 - c})

    def project(step):
        chunk = ordered(t, step)
        w = full_ref[...].reshape(768, 640) if fetch else w_ref[...]
        made = mm(xg_ref[chunk], w) + b_ref[...]
        kv_ref[c, chunk] = made[:, 256:].astype(BF16)
        across(chunk).start()
        mate(chunk).start()
        query = (made[:, :256] * 0.125).astype(BF16)

        @pl.when(chunk % 2 == 0)
        def _():
            qw_ref[chunk] = query

        @pl.when(chunk % 2 == 1)
        def _():
            qbuf[chunk // 2] = query
            partner(chunk // 2).start()

    low = lax.broadcasted_iota(jnp.int32, (256, 128), 1) < 64

    def complete(step):
        chunk = ordered(t, step)
        across(chunk).wait_recv()
        onward(chunk).start()
        mate(chunk).wait_recv()

        @pl.when(chunk % 2 == 1)
        def _():
            partner(chunk // 2).wait_recv()

        pair = qw_ref[chunk, :, 0:128]
        none = jnp.zeros_like(pair)
        qm_ref[0, chunk] = jnp.where(low, pair, none)
        qm_ref[1, chunk] = jnp.where(low, none, pair)
        qm_ref[2, chunk] = qw_ref[chunk, :, 128:256]
        onward(chunk).wait_recv()
        for segment in range(4):
            pair = jnp.transpose(kv_ref[segment, chunk, :, 256:384], (1, 0))
            mixed = jnp.transpose(kv_ref[segment, chunk, :, 128:256], (1, 0))
            for head, rows in enumerate((pair[0:64], pair[64:128], mixed[0:64])):
                vt_ref[segment, chunk, head, 0:64] = rows

    def items(step):
        @pl.loop(step * step, (step + 1) * (step + 1))
        def _(item):
            number = item - step * step
            second = number // (step + 1)
            query_at = ordered_by(t, step + second * (number - 2 * step - 1))
            key_at = ordered_by(t, number + second * (step - number))
            half = query_at % 2

            def visit(segments):
                seen = [flag_ref[half, segment] > 0 for segment in segments]
                far = [jnp.where(one, 0.0, FAR) for one in seen]
                scores, most, made = [], [], []
                for head in range(3):
                    query, at = qm_ref[head, query_at], 128 * (head // 2)
                    rows = [mm_nt(kv_ref[segment, key_at, :, at : at + 128], query) for segment in segments]
                    new = m_ref[query_at, head : head + 1]
                    for one, row in zip(seen, rows):
                        new = jnp.maximum(new, jnp.where(one, jnp.max(row, axis=0, keepdims=True), MASKED))
                    scores.append(rows)
                    most.append(new)
                for head in range(3):
                    total = acc_ref[query_at, head] * jnp.exp(m_ref[query_at, head : head + 1] - most[head])
                    for segment, row, off in zip(segments, scores[head], far):
                        probs = jnp.exp(row - (most[head] + off)).astype(BF16)
                        total += mm(vt_ref[segment, key_at, head], probs)
                    made.append(total)
                for head in range(3):
                    m_ref[query_at, head : head + 1] = most[head]
                    acc_ref[query_at, head] = made[head]

            length = c + 1 + half * (3 - 2 * c)

            @pl.loop(0, length // 2)
            def _(two):
                visit((2 * two, 2 * two + 1))

            @pl.when(length % 2 == 1)
            def _():
                visit((length - 1,))

            if step == 3:
                for n in range(1, len(ride.hops)):
                    pl.when(item == 9 + 2 * n)(functools.partial(ride.one_hop, n))

    project(0)
    for step in range(1, 4):

        @pl.when(t - step >= 0)
        def _():
            arrived(t - step)

            @pl.when(t < 3)
            def _():
                right(xg_ref.at[t - step], t - step, step).start()

        @pl.when(t + step <= 3)
        def _():
            arrived(t + step)

            @pl.when(t > 0)
            def _():
                left(xg_ref.at[t + step], t + step, step).start()

        project(step)
        if step == 2:
            ride.turn()
        if step == 3:
            ride.start_late()
            ride.chain()
            ride.put(xg_ref)
        complete(step - 1)
        items(step - 1)
    complete(3)
    if ride.hops:
        ride.one_hop(0)
    ride.turn()
    ride.chain_turn()
    ride.put(qw_ref, kv_ref)
    items(3)
    for quarter in range(4):
        whole = [acc_ref[quarter, head, 64:65] for head in range(3)]
        parts = [acc_ref[quarter, head, 0:64] / whole[head] for head in range(3)]
        for at, pair in ((0, parts[0:2]), (128, [parts[2], jnp.zeros_like(parts[2])])):
            turned = jnp.transpose(jnp.concatenate(pair, axis=0), (1, 0)).astype(BF16)
            o_ref[quarter, :, at : min(at + 128, 192)] = turned[:, : min(128, 192 - at)]
        for head in range(3):
            lse_ref[quarter, head : head + 1] = m_ref[quarter, head : head + 1] + jnp.log(whole[head])
        lse_ref[quarter, 3:8] = jnp.zeros((5, 256), F32)
    ride.put(o_ref, lse_ref)
    for chunk in range(4):
        mate(chunk).wait_send()
        across(chunk).wait_send()
        onward(chunk).wait_send()
    for slot in range(2):
        partner(slot).wait_send()

    @pl.when(t < 3)
    def _():
        right(x_ref, t, 0).wait_send()

    @pl.when(t > 0)
    def _():
        left(x_ref, t, 0).wait_send()

    for step in (1, 2):

        @pl.when((t - step >= 0) & (t < 3))
        def _():
            right(xg_ref.at[t - step], t - step, step).wait_send()

        @pl.when((t + step <= 3) & (t > 0))
        def _():
            left(xg_ref.at[t + step], t + step, step).wait_send()

    if fetch:
        for k in range(1, size):
            weight(k).wait_send()
    ride.finish()


def inner(x, w, b, parents, cid, riders=(), fetch=False):
    outs = [
        sds(4, 256, 768), sds(4, 256, 256), sds(4, 4, 256, 384), sds(4, 256, 192), sds(4, 8, 256, dtype=F32),
    ]
    scratch = [
        pltpu.VMEM((2, 256, 256), BF16),
        pltpu.VMEM((3, 4, 256, 128), BF16), pltpu.VMEM((4, 8, 256), F32), pltpu.VMEM((4, 3, 80, 256), F32),
        pltpu.VMEM((4, 4, 3, 80, 256), BF16),
        dma(4), dma(3), dma(3),
        dma(4), dma(4), dma(4), dma(4), dma(4), dma(4), dma(2), dma(2), pltpu.SMEM((2, 4), jnp.int32),
    ]
    if fetch:
        size = lax.axis_size("fsdp")
        outs.append(sds(size, *w.shape))
        scratch = [dma(size - 1), dma(size - 1)] + scratch
    cost = (2 * 1024 * 768 * 640 + 5 * 512 * 1024 * 64 * 12, 14 << 20, 5 * 512 * 1024 * 3)
    kernel = functools.partial(inner_kernel, fetch)
    res, ridden = call(kernel, (parents, x, w, b), outs, scratch, cid, "inner", cost, riders, smem=(0,))
    full = res[5].reshape(768, 640) if fetch else w
    xg, qw, kv, o, lse = res[:5]
    return (
        xg.reshape(1024, 768), qw.reshape(1024, 256), kv.reshape(4, 1024, 384),
        o.reshape(1024, 192), lse, full, ridden,
    )


def norm_stats(summed):
    row_mean = jnp.mean(summed, axis=-1, keepdims=True)
    centered = summed - row_mean
    variance = jnp.mean(centered * centered, axis=-1, keepdims=True)
    scale = lax.rsqrt(variance + EPSILON)
    return centered * scale, scale


def norm_back(grad, xhat, scale, gain):
    scaled = grad * gain
    first = jnp.mean(scaled, axis=-1, keepdims=True)
    second = jnp.mean(scaled * xhat, axis=-1, keepdims=True)
    return scale * (scaled - first - xhat * second)


def gelu_both(up):
    phi = 0.5 * (1.0 + lax.erf(up * 0.7071067811865476))
    slope = phi + up * jnp.exp(-0.5 * up * up) * 0.3989422804014327
    return (up * phi).astype(BF16), slope.astype(BF16)


PIECE = 128


def exchange(c, ref, feed, mine_ref, part_ref, send_ref, got_ref, a_send, a_recv, s_send, s_recv, meanwhile):
    mate, across, far = mate_of(c), across_of(c), 3 - c
    pieces = (pl.ds(0, PIECE), pl.ds(PIECE, PIECE))

    def gather(slot, index, p, device):
        part = ref.at[slot, pieces[p]]
        return rcopy(part, part, a_send.at[index, p], a_recv.at[index, p], {"ctx": device})

    def scatter(index, p, device):
        source, target = send_ref.at[index, pieces[p]], got_ref.at[index, pieces[p]]
        return rcopy(source, target, s_send.at[index, p], s_recv.at[index, p], {"ctx": device})

    for p in range(2):
        gather(c, 1, p, across).start()
    for p in range(2):
        gather(c, 0, p, mate).start()
    mine_ref[...] += feed(c, pl.ds(0, 2 * PIECE))
    for p in range(2):
        gather(mate, 0, p, mate).wait_recv()
    send_ref[0] = feed(mate, pl.ds(0, 2 * PIECE)).astype(BF16)
    for p in range(2):
        scatter(0, p, mate).start()

    def take_across(p):
        gather(across, 1, p, across).wait_recv()
        gather(across, 2, p, mate).start()
        part_ref[pieces[p]] = feed(across, pieces[p])

    def take_far(p):
        gather(far, 2, p, mate).wait_recv()
        send_ref[1, pieces[p]] = feed(far, pieces[p]).astype(BF16)
        scatter(1, p, mate).start()

    def join(p):
        scatter(1, p, mate).wait_recv()
        send_ref[2, pieces[p]] = (part_ref[pieces[p]] + got_ref[1, pieces[p]].astype(F32)).astype(BF16)
        scatter(2, p, across).start()

    take_across(0)
    take_far(0)
    take_across(1)
    join(0)
    take_far(1)
    join(1)
    meanwhile()
    for p in range(2):
        scatter(0, p, mate).wait_recv()
        scatter(2, p, across).wait_recv()

    def settle():
        for p in range(2):
            for index in range(3):
                gather(c, index, p, mate).wait_send()
                scatter(index, p, mate).wait_send()

    return mine_ref[...] + got_ref[0].astype(F32) + got_ref[2].astype(F32), settle


def block_kernel(
    ride, o_ref, wo_ref, w1_ref, w2_ref, b1_ref, vec_ref, stream_ref,
    out_ref, low_ref, xhat1_ref, r1_ref, xhat2_ref, r2_ref, xg_ref, act_ref, slope_ref, rows_ref, down_ref,
    w_send, w_recv, mine_ref, part_ref, send_ref, got_ref, o_send, o_recv, a_send, a_recv, s_send, s_recv,
):
    c = lax.axis_index("ctx")
    t = lax.axis_index("tp")
    barrier = pltpu.get_barrier_semaphore()
    for place in range(4):

        @pl.when((t % 2 == 0) & (t != place))
        def _():
            signal(barrier, {"tp": place})

        @pl.when(t % 2 == 1)
        def _():
            signal(barrier, {"ctx": 3 - c, "tp": place})

    signal(barrier, {"ctx": mate_of(c)})
    signal(barrier, {"ctx": across_of(c)})
    f, size = lax.axis_index("fsdp"), lax.axis_size("fsdp")
    for k in range(1, size):
        signal(barrier, {"fsdp": (f + size - k) % size})
    count = 5 + t % 2 + size - 1 + ride.greet(barrier)
    ride.ready()
    pl.semaphore_wait(barrier, count)

    def weight(k):
        device = {"fsdp": (f + k) % size}
        return rcopy(w2_ref, down_ref.at[f], w_send.at[k - 1], w_recv.at[k - 1], device)

    def give(quarter):
        device = {"tp": quarter} if quarter % 2 == 0 else {"ctx": 3 - c, "tp": quarter}
        return rcopy(o_ref.at[quarter], rows_ref.at[t], o_send.at[quarter], o_recv.at[t], device)

    def given(group):
        rcopy(rows_ref.at[group], rows_ref.at[group], o_send.at[0], o_recv.at[group], {"tp": t}).wait_recv()

    for quarter in (3, 2, 1, 0):
        if quarter % 2 == 0:

            @pl.when(t != quarter)
            def _():
                give(quarter).start()

            @pl.when(t == quarter)
            def _():
                rows_ref[quarter] = o_ref[quarter]

        else:
            give(quarter).start()
    for k in range(1, size):
        weight(k).start()
    down_ref[f] = w2_ref[...]
    branch = stream_ref[...] + vec_ref[0:1]
    for group in range(4):

        @pl.when((t % 2 == 1) | (t != group))
        def _():
            given(group)

        branch += mm_nt(rows_ref[group], wo_ref[group])
    ride.start()
    xhat, scale = norm_stats(branch)
    xhat1_ref[...] = xhat
    r1_ref[...] = jnp.broadcast_to(scale, r1_ref.shape)
    normed = xhat * vec_ref[2:3] + vec_ref[3:4]
    xg_ref[c] = normed.astype(BF16)
    mine_ref[...] = normed + vec_ref[1:2]
    for k in range(1, size):
        weight(k).wait_recv()

    def feed(segment, rows):
        up = mm(xg_ref[segment, rows], w1_ref[...]) + b1_ref[...]
        act, slope = gelu_both(up)
        act_ref[segment, rows] = act
        slope_ref[segment, rows] = slope
        return mm_nt(act, down_ref[...].reshape(768, 768))

    def meanwhile():
        ride.turn()
        ride.put(xhat1_ref, r1_ref, xg_ref, act_ref, slope_ref, rows_ref, down_ref)

    summed, settle = exchange(
        c, xg_ref, feed, mine_ref, part_ref, send_ref, got_ref, a_send, a_recv, s_send, s_recv, meanwhile
    )
    xhat, scale = norm_stats(summed)
    xhat2_ref[...] = xhat
    r2_ref[...] = jnp.broadcast_to(scale, r2_ref.shape)
    out = xhat * vec_ref[4:5] + vec_ref[5:6]
    out_ref[...] = out
    low_ref[...] = out.astype(BF16)
    ride.put(out_ref, low_ref, xhat2_ref, r2_ref)
    for quarter in range(4):
        if quarter % 2 == 0:

            @pl.when(t != quarter)
            def _():
                give(quarter).wait_send()

        else:
            give(quarter).wait_send()
    for k in range(1, size):
        weight(k).wait_send()
    settle()
    ride.finish()


def block(o, wo, w1, w2, b1, vecs, stream, cid, riders=()):
    size = lax.axis_size("fsdp")
    f = functools.partial(sds, dtype=F32)
    outs = [
        f(256, 768), sds(256, 768), f(256, 768), f(256, 128), f(256, 768), f(256, 128),
        sds(4, 256, 768), sds(4, 256, 768), sds(4, 256, 768), sds(4, 256, 192), sds(size, *w2.shape),
    ]
    scratch = [
        dma(size - 1), dma(size - 1),
        pltpu.VMEM((256, 768), F32),
        pltpu.VMEM((256, 768), F32),
        pltpu.VMEM((3, 256, 768), BF16),
        pltpu.VMEM((3, 256, 768), BF16),
        dma(4), dma(4), dma(3, 2), dma(3, 2), dma(3, 2), dma(3, 2),
    ]
    cost = (2 * 256 * 768 * 768 + 4 * 1024 * 768 * 768, 16 << 20, 1 << 20)
    operands = (o.reshape(4, 256, 192), wo, w1, w2, b1, vecs, stream)
    res, ridden = call(block_kernel, operands, outs, scratch, cid, "block", cost, riders)
    flat = lambda a: a.reshape(1024, 768)
    return tuple(res[:6]) + (flat(res[6]), flat(res[7]), flat(res[8]), res[9], res[10].reshape(768, 768), ridden)


def block_back_kernel(
    ride, grad_ref, xhat2_ref, r2_ref, xhat1_ref, r1_ref, vec_ref, slope_ref, w1_ref, w2_ref, wo_ref,
    xg_ref, act_ref, rows_ref, back_ref, do_ref, stat_ref, dup_ref, ddown_ref, dout_ref,
    w_send, w_recv, term_ref, all_up_ref, gg_ref, gu_ref, mine_ref, part_ref, send_ref, got_ref, dsend_ref, d_send, d_recv, a_send, a_recv, s_send, s_recv,
):
    c = lax.axis_index("ctx")
    t = lax.axis_index("tp")
    barrier = pltpu.get_barrier_semaphore()
    for place in range(4):
        if place % 2 == 0:

            @pl.when(t != place)
            def _():
                signal(barrier, {"tp": place})

        else:
            signal(barrier, {"ctx": 3 - c, "tp": place})
    signal(barrier, {"ctx": mate_of(c)})
    signal(barrier, {"ctx": across_of(c)})
    f, size = lax.axis_index("fsdp"), lax.axis_size("fsdp")
    depth = dup_ref.shape[0]
    for k in range(1, size):
        signal(barrier, {"fsdp": (f + size - k) % size})
    count = 5 + t % 2 + size - 1 + ride.greet(barrier)
    ride.ready()
    pl.semaphore_wait(barrier, count)

    def row(values):
        return jnp.sum(values, axis=0, keepdims=True)

    grad = grad_ref[...]
    back_two = norm_back(grad, xhat2_ref[...], r2_ref[:, 0:1], vec_ref[4:5])
    g2 = back_two.astype(BF16)
    gg_ref[c] = g2
    mine_ref[...] = back_two
    ride.start()
    stat_ref[1:2] = row(grad * xhat2_ref[...])
    stat_ref[3:4] = row(grad)
    stat_ref[5:6] = row(g2.astype(F32))
    stat_ref[6:8] = jnp.zeros((2, 768), F32)

    def feed(segment, rows):
        gu = (mm(gg_ref[segment, rows], w2_ref[...]) * slope_ref[segment, rows].astype(F32)).astype(BF16)
        gu_ref[segment, rows] = gu
        stat_ref[6:7] += row(gu.astype(F32))
        return mm_nt(gu, w1_ref[...])

    tall = lambda ref: ref[...].reshape(1024, 768)

    def slice_of(place):
        return pl.ds(pl.multiple_of(place * depth, depth), depth)

    def term(k):
        to = (f + k) % size
        return rcopy(
            all_up_ref.at[slice_of(to)], term_ref.at[k - 1], w_send.at[k - 1], w_recv.at[k - 1], {"fsdp": to}
        )

    def meanwhile():
        @pl.loop(0, 3)
        def _(tile):
            cols = pl.ds(pl.multiple_of(tile * 256, 256), 256)
            all_up_ref[cols] = mm_tn(xg_ref[:, cols], tall(gu_ref)).astype(BF16)

        for k in range(1, size):
            term(k).start()

        @pl.loop(0, 3)
        def _(tile):
            cols = pl.ds(pl.multiple_of(tile * 256, 256), 256)
            ddown_ref[cols] = mm_tn(gg_ref[:, :, cols].reshape(1024, 256), act_ref[...]).astype(BF16)

        ride.put(ddown_ref)
        ride.turn()

    grad_normed, settle = exchange(
        c, gg_ref, feed, mine_ref, part_ref, send_ref, got_ref, a_send, a_recv, s_send, s_recv, meanwhile
    )
    back_one = norm_back(grad_normed, xhat1_ref[...], r1_ref[:, 0:1], vec_ref[2:3])
    back_ref[...] = back_one
    g1 = back_one.astype(BF16)

    def give_near(group):
        return rcopy(dsend_ref.at[group], do_ref.at[t], d_send.at[group], d_recv.at[t], {"tp": group})

    def give_far(group):
        return rcopy(dsend_ref.at[group], do_ref.at[t], d_send.at[group], d_recv.at[t], {"ctx": 3 - c, "tp": group})

    for group in range(4):
        dsend_ref[group] = mm(g1, wo_ref[group]).astype(BF16)

        @pl.when((t % 2 == 0) & (t == group))
        def _():
            do_ref[t] = dsend_ref[group]

        @pl.when((t % 2 == 0) & (t != group))
        def _():
            give_near(group).start()

        @pl.when(t % 2 == 1)
        def _():
            give_far(group).start()

    stat_ref[0:1] = row(grad_normed * xhat1_ref[...])
    stat_ref[2:3] = row(grad_normed)
    stat_ref[4:5] = row(g1.astype(F32))
    for group in range(4):
        dout_ref[group] = mm_tn(g1, rows_ref[group]).astype(BF16)
    ride.put(back_ref, stat_ref, dout_ref)
    ride.chain()
    total = all_up_ref[slice_of(f)].astype(F32)
    for k in range(1, size):
        term(k).wait_recv()
        total += term_ref[k - 1].astype(F32)
    dup_ref[...] = total.astype(BF16)
    ride.put(dup_ref)
    for quarter in range(4):

        def taken():
            rcopy(do_ref.at[quarter], do_ref.at[quarter], d_send.at[0], d_recv.at[quarter], {"tp": t}).wait_recv()

        if quarter % 2 == 0:
            pl.when(t != quarter)(taken)
        else:
            taken()
    for group in range(4):

        @pl.when((t % 2 == 1) | (t != group))
        def _():
            give_near(group).wait_send()

    ride.chain_turn()
    for k in range(1, size):
        term(k).wait_send()
    settle()
    ride.finish()


def block_back(grad, xhat2, r2, xhat1, r1, vecs, slope, w1, w2, wo, xg, act, rows, cid, riders=()):
    f = functools.partial(sds, dtype=F32)
    size = lax.axis_size("fsdp")
    depth = 768 // size
    outs = [
        f(256, 768), sds(4, 256, 192), f(8, 768), sds(depth, 768), sds(768, 768), sds(4, 768, 192),
    ]
    scratch = [
        dma(size - 1), dma(size - 1), pltpu.VMEM((size - 1, depth, 768), BF16), pltpu.VMEM((768, 768), BF16),
        pltpu.VMEM((4, 256, 768), BF16),
        pltpu.VMEM((4, 256, 768), BF16),
        pltpu.VMEM((256, 768), F32),
        pltpu.VMEM((256, 768), F32),
        pltpu.VMEM((3, 256, 768), BF16),
        pltpu.VMEM((3, 256, 768), BF16),
        pltpu.VMEM((4, 256, 192), BF16),
        dma(4), dma(4), dma(3, 2), dma(3, 2), dma(3, 2), dma(3, 2),
    ]
    cost = (4 * 256 * 768 * 768 + 8 * 1024 * 768 * 768, 20 << 20, 1 << 10)
    operands = (grad, xhat2, r2, xhat1, r1, vecs, slope.reshape(4, 256, 768), w1, w2, wo, xg, act, rows)
    res, ridden = call(block_back_kernel, operands, outs, scratch, cid, "block_back", cost, riders)
    back, do, stats, d_up, d_down, d_out = res
    return back, do.reshape(1024, 192), stats, d_up, d_down, d_out, ridden


def inner_back_kernel(
    lowest, ride, parent_ref, qw_ref, kv_ref, do_ref, o_ref, lse_ref, w_ref, back_ref, xg_ref, mark_ref,
    grad_ref, low_ref, din_ref, sum_out_ref, mem_ref,
    qm_ref, dm_ref, row_ref, acc_ref, wide_ref, dkv_ref, dqs_ref,
    w_send, w_recv, term_ref, all_in_ref, dq_ref, own_ref, part_ref,
    near_ref, join_ref, sum_ref, far_ref, pass_ref, take_ref,
    q_send, q_recv, n_send, n_recv, j_send, j_recv, f_send, f_recv, p_send, p_recv, flag_ref,
):
    c = lax.axis_index("ctx")
    mark_path(parent_ref, flag_ref, c)
    t = lax.axis_index("tp")
    f, size = lax.axis_index("fsdp"), lax.axis_size("fsdp")
    depth = din_ref.shape[0]
    mate, across, far = mate_of(c), across_of(c), 3 - c
    barrier = pltpu.get_barrier_semaphore()
    for device in (mate, across, far):
        signal(barrier, {"ctx": device})

    @pl.when(t > 0)
    def _():
        signal(barrier, {"tp": t - 1})

    @pl.when(t < 3)
    def _():
        signal(barrier, {"tp": t + 1})

    for k in range(1, size):
        signal(barrier, {"fsdp": (f + size - k) % size})
    ends = (t // 3) + (3 - t) // 3
    count = 5 - ends + size - 1 + ride.greet(barrier)
    ride.ready()

    low = lax.broadcasted_iota(jnp.int32, (1024, 128), 1) < 64
    pair = qw_ref[:, 0:128]
    none = jnp.zeros_like(pair)
    qm_ref[0] = jnp.where(low, pair, none)
    qm_ref[1] = jnp.where(low, none, pair)
    qm_ref[2] = qw_ref[:, 128:256]
    pair = do_ref[:, 0:128]
    dm_ref[0] = jnp.where(low, pair, none)
    dm_ref[1] = jnp.where(low, none, pair)
    dm_ref[2] = jnp.concatenate([do_ref[:, 128:192], none[:, :64]], axis=1)
    product = do_ref[...].astype(F32) * o_ref[...].astype(F32)
    head_row = lax.broadcasted_iota(jnp.int32, (8, 192), 0)
    head_of = lax.broadcasted_iota(jnp.int32, (8, 192), 1) // 64
    delta = lax.dot_general(
        (head_row == head_of).astype(F32), product, (((1,), (1,)), ((), ())),
        precision=lax.Precision.HIGHEST, preferred_element_type=F32,
    )
    for quarter in range(4):
        row_ref[quarter, 0:8] = lse_ref[quarter]
        row_ref[quarter, 8:16] = delta[:, quarter * 256 : (quarter + 1) * 256]
    acc_ref[...] = jnp.zeros_like(acc_ref)
    wide_ref[...] = jnp.zeros_like(wide_ref)
    pl.semaphore_wait(barrier, count)
    ride.start()

    def partner(slot):
        return rcopy(dqs_ref.at[slot], dq_ref.at[2 * slot + 1], q_send.at[slot], q_recv.at[slot], {"ctx": far})

    def near(chunk):
        return rcopy(dkv_ref.at[mate, chunk], near_ref.at[chunk], n_send.at[chunk], n_recv.at[chunk], {"ctx": mate})

    def join(chunk):
        return rcopy(dkv_ref.at[far, chunk], join_ref.at[chunk], j_send.at[chunk], j_recv.at[chunk], {"ctx": mate})

    def cross(chunk):
        return rcopy(sum_ref.at[chunk], far_ref.at[chunk], f_send.at[chunk], f_recv.at[chunk], {"ctx": across})

    pieces = (pl.ds(0, PIECE), pl.ds(PIECE, PIECE))

    def onward(side, chunk, p):
        return rcopy(
            pass_ref.at[chunk, pieces[p]], take_ref.at[side, chunk, pieces[p]],
            p_send.at[chunk, p], p_recv.at[side, chunk, p], {"tp": t - 1 + 2 * side},
        )

    def passed(side, chunk, p):
        part = take_ref.at[side, chunk, pieces[p]]
        rcopy(part, part, p_send.at[0, p], p_recv.at[side, chunk, p], {"tp": t}).wait_recv()

    chunks = [ordered(t, 3 - k) for k in range(4)]
    at_end = (t == 0) | (t == 3)

    def leave(k):
        chunk = chunks[k]
        dkv_ref[:, chunk] = wide_ref[:, chunk].astype(BF16)
        join(chunk).start()
        near(chunk).start()
        query = (acc_ref[chunk].astype(BF16).astype(F32) * 0.125).astype(BF16)

        @pl.when(chunk % 2 == 0)
        def _():
            dq_ref[chunk] = query

        @pl.when(chunk % 2 == 1)
        def _():
            dqs_ref[chunk // 2] = query
            partner(chunk // 2).start()

    def go_across(k):
        chunk = chunks[k]
        join(chunk).wait_recv()
        sum_ref[chunk] = (dkv_ref[across, chunk].astype(F32) + join_ref[chunk].astype(F32)).astype(BF16)
        cross(chunk).start()

    def gather_up(k):
        chunk = chunks[k]
        if k < 3:

            @pl.when(chunk % 2 == 1)
            def _():
                partner(chunk // 2).wait_recv()

        near(chunk).wait_recv()
        cross(chunk).wait_recv()
        own = (
            dkv_ref[c, chunk].astype(F32) + near_ref[chunk].astype(F32) + far_ref[chunk].astype(F32)
        ).astype(BF16)
        own_ref[chunk] = own
        part_ref[chunk] = mm_nt(dq_ref[chunk], w_ref[:, 0:256]) + mm_nt(own, w_ref[:, 256:640])

    def relay(k):
        chunk = chunks[k]

        def move(side, first):
            for p in range(2):

                @pl.when(jnp.logical_not(first))
                def _():
                    passed(side, chunk, p)
                    total = part_ref[chunk, pieces[p]] + take_ref[side, chunk, pieces[p]].astype(F32)
                    pass_ref[chunk, pieces[p]] = total.astype(BF16)

                @pl.when(first)
                def _():
                    pass_ref[chunk, pieces[p]] = part_ref[chunk, pieces[p]].astype(BF16)

                onward(side, chunk, p).start()

        @pl.when(chunk < t)
        def _():
            move(0, t == 3)

        @pl.when(chunk > t)
        def _():
            move(1, t == 0)

    def relay_ends(k):
        pl.when(at_end)(functools.partial(relay, k))

    def relay_inner(k):
        pl.when(jnp.logical_not(at_end))(functools.partial(relay, k))

    low_keys = lax.broadcasted_iota(jnp.int32, (256, 128), 1) < 64

    def one_item(item, done):
        phase = (item + 9) // 16 + (item + 4) // 16 + (item + 1) // 16
        number = item - phase * (8 - phase)
        second = number // (4 - phase)
        query_at = ordered_by(t, 3 - (phase + second * (number - 3 + phase)))
        key_at = ordered_by(t, 3 - (phase + (1 - second) * number))
        half = query_at % 2
        rows = pl.ds(pl.multiple_of(query_at * 256, 256), 256)

        def visit(segments):
            queries = [qm_ref[head, rows] for head in range(3)]
            grads = [dm_ref[head, rows] for head in range(3)]
            made = []
            for segment in segments:
                penalty = jnp.where(flag_ref[half, segment] > 0, 0.0, FAR)
                key_pair = kv_ref[segment, key_at, :, 0:128]
                mixed = kv_ref[segment, key_at, :, 128:256]
                value_pair = kv_ref[segment, key_at, :, 256:384]
                for head in range(3):
                    shift = row_ref[query_at, head : head + 1] + penalty
                    prob = jnp.exp(mm_nt(key_pair if head < 2 else mixed, queries[head]) - shift)
                    grad_prob = mm_nt(value_pair if head < 2 else mixed, grads[head])
                    grad_score = (prob * (grad_prob - row_ref[query_at, 8 + head : 9 + head])).astype(BF16)
                    made.append((prob.astype(BF16), grad_score))
            pair_sum, mixed_sum = 0.0, 0.0
            for number, segment in enumerate(segments):
                (p0, g0), (p1, g1), (p2, g2) = made[3 * number : 3 * number + 3]
                for_keys = mm(g0, queries[0]) + mm(g1, queries[1])
                for_mixed = mm(g2, queries[2]) + mm(p2, grads[2])
                for_values = mm(p0, grads[0]) + mm(p1, grads[1])
                wide_ref[segment, key_at] += jnp.concatenate([for_keys, for_mixed, for_values], axis=1)
                key_pair = kv_ref[segment, key_at, :, 0:128]
                nothing = jnp.zeros_like(key_pair)
                pair_sum += mm_tn(g0, jnp.where(low_keys, key_pair, nothing))
                pair_sum += mm_tn(g1, jnp.where(low_keys, nothing, key_pair))
                mixed_sum += mm_tn(g2, jnp.where(low_keys, nothing, kv_ref[segment, key_at, :, 128:256]))
            acc_ref[query_at] += jnp.concatenate([pair_sum, mixed_sum], axis=1)

        length = c + 1 + half * (3 - 2 * c)

        @pl.loop(0, length // 2)
        def _(two):
            visit((2 * two, 2 * two + 1))

        @pl.when(length % 2 == 1)
        def _():
            visit((length - 1,))

        now = done + length

        def at(place, action, k):
            pl.when(item == place)(functools.partial(action, k))

        def once(amount, action, k):
            pl.when((done < amount) & (now >= amount))(functools.partial(action, k))

        for n in range(len(ride.hops)):
            once(RIDE_HOPS[n], ride.one_hop, n)
        ride.turn_when((done < 14) & (now >= 14))
        for k, place in enumerate((6, 11, 14)):
            at(place, leave, k)
        once(24, go_across, 0)
        once(31, gather_up, 0)
        once(31, relay_ends, 0)
        once(32, go_across, 1)
        once(38, gather_up, 1)
        once(38, relay_ends, 1)
        return now

    lax.fori_loop(0, 16, one_item, 0)
    leave(3)
    go_across(2)
    relay_inner(0)
    go_across(3)
    gather_up(2)
    relay_ends(2)
    relay_inner(1)

    def slice_of(place):
        return pl.ds(pl.multiple_of(place * depth, depth), depth)

    spans = (pl.ds(0, 256), pl.ds(256, 256), pl.ds(512, 128))

    def term(k, span):
        to, cols = (f + k) % size, spans[span]
        return rcopy(
            all_in_ref.at[slice_of(to), cols], term_ref.at[k - 1, :, cols],
            w_send.at[k - 1, span], w_recv.at[k - 1, span], {"fsdp": to},
        )


    @pl.when(t % 2 == 1)
    def _():
        partner(t // 2).wait_recv()

    query = dq_ref[...].reshape(1024, 256)
    for span in range(3):
        if span == 0:
            ride.chain()
        if span == 1:
            relay_inner(2)
            gather_up(3)
            ride.chain_turn()
        own = own_ref[...].reshape(1024, 384)
        made = (query, own[:, 0:256], own[:, 256:384])[span]
        all_in_ref[:, spans[span]] = mm_tn(xg_ref[...], made).astype(BF16)
        for k in range(1, size):
            term(k, span).start()

    sum_out_ref[0:1, 0:256] = jnp.sum(query.astype(F32), axis=0, keepdims=True)
    sum_out_ref[0:1, 256:640] = jnp.sum(own.astype(F32), axis=0, keepdims=True)
    ride.put(sum_out_ref)
    ride.store(1)
    total = all_in_ref[slice_of(f)].astype(F32)
    for k in range(1, size):
        for span in range(3):
            term(k, span).wait_recv()
        total += term_ref[k - 1].astype(F32)
    din_ref[...] = total.astype(BF16)
    ride.put(din_ref)
    ride.store(2)
    grad_ref[...] = part_ref[t] + back_ref[...]

    for side, there in ((0, t < 3), (1, t > 0)):

        @pl.when(there)
        def _():
            for p in range(2):
                passed(side, t, p)
                grad_ref[pieces[p]] += take_ref[side, t, pieces[p]].astype(F32)

    low_ref[...] = grad_ref[...].astype(BF16)
    ride.put(grad_ref, low_ref)
    if lowest:
        mem_ref[...] = lax.dot_general(
            mark_ref[...], grad_ref[...], (((0,), (0,)), ((), ())),
            precision=lax.Precision.HIGHEST, preferred_element_type=F32,
        )
    else:
        mem_ref[...] = jnp.zeros_like(mem_ref)
    ride.put(mem_ref)
    for k in range(1, size):
        for span in range(3):
            term(k, span).wait_send()
    for chunk in range(4):
        join(chunk).wait_send()
        near(chunk).wait_send()
        cross(chunk).wait_send()

        @pl.when(t != chunk)
        def _():
            for p in range(2):
                onward(1, chunk, p).wait_send()

    for slot in range(2):
        partner(slot).wait_send()
    ride.finish()


RIDE_HOPS = (8, 11, 14, 17)


def inner_back(qw, kv, do, o, lse, parents, w, back_one, xg, marks, lowest, cid, riders=()):
    size = lax.axis_size("fsdp")
    depth = 768 // size
    f = functools.partial(sds, dtype=F32)
    outs = [f(256, 768), sds(256, 768), sds(depth, 640), f(8, 640), f(marks.shape[1], 768)]
    scratch = [
        pltpu.VMEM((3, 1024, 128), BF16), pltpu.VMEM((3, 1024, 128), BF16), pltpu.VMEM((4, 16, 256), F32),
        pltpu.VMEM((4, 256, 256), F32), pltpu.VMEM((4, 4, 256, 384), F32), pltpu.VMEM((4, 4, 256, 384), BF16),
        pltpu.VMEM((2, 256, 256), BF16),
        dma(size - 1, 3), dma(size - 1, 3), pltpu.VMEM((size - 1, depth, 640), BF16), pltpu.VMEM((768, 640), BF16),
        pltpu.VMEM((4, 256, 256), BF16), pltpu.VMEM((4, 256, 384), BF16),
        pltpu.VMEM((4, 256, 768), F32),
        pltpu.VMEM((4, 256, 384), BF16), pltpu.VMEM((4, 256, 384), BF16),
        pltpu.VMEM((4, 256, 384), BF16), pltpu.VMEM((4, 256, 384), BF16),
        pltpu.VMEM((4, 256, 768), BF16), pltpu.VMEM((2, 4, 256, 768), BF16),
        dma(2), dma(2), dma(4), dma(4), dma(4), dma(4), dma(4), dma(4), dma(4, 2), dma(2, 4, 2),
        pltpu.SMEM((2, 4), jnp.int32),
    ]
    cost = (5 * 512 * 1024 * 64 * 30 + 4 * 1024 * 768 * 640, 16 << 20, 5 * 512 * 1024 * 3)
    operands = (parents, qw, kv.reshape(4, 4, 256, 384), do, o, lse, w, back_one, xg, marks)
    res, ridden = call(functools.partial(inner_back_kernel, lowest), operands, outs, scratch, cid, "inner_back", cost, riders, smem=(0,))
    return (*res[:3], res[3][0], res[4], ridden)


def joined(query, key, value, gap):
    return jnp.concatenate(
        [
            query[..., :128], gap, query[..., 128:],
            key[..., :128], value[..., 128:], key[..., 128:], value[..., :128],
        ],
        axis=-1,
    )


def parted(grads):
    query = jnp.concatenate([grads[..., :128], grads[..., 192:256]], axis=-1)
    key = jnp.concatenate([grads[..., 256:384], grads[..., 448:512]], axis=-1)
    value = jnp.concatenate([grads[..., 512:640], grads[..., 384:448]], axis=-1)
    return query, key, value


def added(terms, axes=(0,)):
    return jnp.sum(terms.astype(F32), axis=axes)


def low(values):
    return values.astype(BF16)


def shards(
    hidden, cotangent, mem_pos, parents, memory, wq, wk, wv, wo, w1, w2,
    head_bias, ffn_bias, out_bias, norm_gains, norm_shifts,
):
    c = lax.axis_index("ctx")
    t = lax.axis_index("tp")
    size = lax.axis_size("fsdp")
    layers = wq.shape[0]
    share = hidden.shape[0]
    depth = wq.shape[1]
    piece = depth // 4
    positions = t * share + jnp.arange(share, dtype=jnp.int32)
    marks = (mem_pos[0, 0][None, :] == positions[:, None]).astype(F32)
    stream = hidden.astype(F32) + jnp.dot(
        marks, memory, precision=lax.Precision.HIGHEST, preferred_element_type=F32
    )
    ids = jnp.arange(4, dtype=jnp.int32)

    gap = jnp.zeros(wq.shape[:2] + (64,), BF16)
    own_in = joined(wq, wk, wv, gap)
    none = jnp.zeros((layers, 192), F32)
    in_bias = joined(head_bias[:, 0], none, head_bias[:, 1], jnp.zeros((layers, 64), F32))
    down_turned = jnp.swapaxes(w2, 1, 2)
    out_turned = jnp.swapaxes(wo, 1, 2).reshape(layers, 4, piece, 192)
    out_piece = lax.dynamic_index_in_dim(out_turned, c, axis=1, keepdims=False)

    def vectors(n):
        norms = [norm_gains[n, 0], norm_shifts[n, 0], norm_gains[n, 1], norm_shifts[n, 1]]
        return jnp.concatenate([out_bias[n], jnp.stack(norms), jnp.zeros((2, 768), F32)])

    saved, weights = [], []
    rounded = low(stream)
    riders = [plane_gather(out_piece[0], size), ctx_gather(sds(4, size, piece, 192), axis=2, first=0)]
    riders += [flip_gather(w1[0], size).later(), tp_flip(down_turned[0]).later(hopped=True), tp_flip(ffn_bias)]
    xg, qw, kv, o, lse, w_in, got = inner(rounded, own_in[0], in_bias[0][None], parents, 0, riders, fetch=True)
    _, out, w_up, down, units = got
    for n in range(layers):
        last = n == layers - 1
        w_out = out.reshape(4, 768, 192)
        w_up = w_up.reshape(768, 768)
        vecs = vectors(n)
        riders = []
        if not last:
            riders = [
                tp_flip(w1[n + 1]),
                plane_gather(out_piece[n + 1], size), fsdp_gather(own_in[n + 1], size),
            ]
        stream, rounded, xhat1, r1, xhat2, r2, xg2, act, slope, rows, w_down, got = block(
            o, w_out, w_up, down, units[n][None], vecs, stream, 16 * n + 2, riders
        )
        weights.append((w_in, w_up, w_down, w_out, vecs))
        saved.append((xg, qw, kv, o, lse, xhat1, r1, xhat2, r2, xg2, act, slope, rows))
        if not last:
            up, out, w_in = got
            riders = [ctx_gather(out, axis=2), tp_flip(down_turned[n + 1]).later(), fsdp_gather(up, size)]
            xg, qw, kv, o, lse, w_in, (out, down, w_up) = inner(
                rounded, w_in.reshape(768, 640), in_bias[n + 1][None], parents, 16 * n + 16, riders
            )
    output = rounded

    grad = cotangent.astype(F32)
    small, heads = [None] * layers, [None] * layers
    done = [None] * layers
    above = None
    for n in reversed(range(layers)):
        w_in, w_up, w_down, w_out, vecs = weights[n]
        xg, qw, kv, o, lse, xhat1, r1, xhat2, r2, xg2, act, slope, rows = saved[n]
        riders = []
        if above is not None:
            riders = [plane_scatter(above["out"], size), ctx_scatter(above["in"])]
            riders += [ctx_gather(sds(piece, 192), first=0, summed=True)]
            riders += [ctx_gather(sds(piece, 640), first=1, summed=True)]
        back_one, do, small[n], d_up, d_down, d_out, got = block_back(
            grad, xhat2, r2, xhat1, r1, vecs, slope, w_up, w_down, w_out, xg2, act, rows, 16 * n + 3, riders
        )
        quarters = sds(4, depth // 4, 768)
        riders = [
            tp_flip(d_up.reshape(quarters.shape)), scatter_flip(d_down.reshape(size, *quarters.shape)),
            ctx_scatter(d_out.reshape(4, size, 4, piece, 192), axis=2),
            ctx_scatter(quarters, first=0), ctx_scatter(quarters, first=1),
        ]
        riders += [stored_sum(at, riders[at].out) for at in (2, 3, 4)]
        if above is not None:
            done[n + 1] = tuple(got[2:4])
            riders += [ctx_gather(above["up"]), ctx_gather(above["down"])]
        grad, low_grad, d_in, sums, memory_part, got = inner_back(
            qw, kv, do, o, lse, parents, w_in, back_one, xg, marks, n == 0, 16 * n + 4, riders
        )
        if above is not None:
            done[n + 1] = (done[n + 1][1], done[n + 1][0], got[8], got[9])
        d_query_bias, _, d_value_bias = parted(sums)
        heads[n] = jnp.stack([d_query_bias, d_value_bias])
        above = {
            "up": got[6],
            "down": got[7],
            "in": d_in.reshape(4, depth // 4, 640),
            "out": got[5],
        }
    hidden_grad = low_grad
    small = jnp.stack(small)
    place = (ids == t).astype(F32)
    unit = (ids == flipped_place(c, t)).astype(F32)
    head_rows = (jnp.stack(heads)[:, :, None, :] * place[None, None, :, None]).reshape(2 * layers, 768)
    unit_rows = (small[:, 6][:, None, :] * unit[None, :, None]).reshape(4 * layers, 768)
    stat_rows = small[:, :6].reshape(6 * layers, 768)
    filled = 12 * layers + memory_part.shape[0]
    slices = 4 * size
    width = -(-filled // slices)
    rest = jnp.zeros((width * slices - filled, 768), F32)
    sums = jnp.concatenate([stat_rows, unit_rows, head_rows, memory_part, rest])
    sums = sums.reshape(4, size, width, 768)
    riders = [ctx_scatter(above["in"]), plane_scatter(above["out"], size), plane_scatter(sums, size)]
    riders += [ctx_gather(above["up"]).later(), ctx_gather(above["down"]).later()]
    riders += [ctx_gather(sds(piece, 640), first=0, summed=True), ctx_gather(sds(piece, 192), first=1, summed=True)]
    got = carry(riders + [small_sum(sds(width, 768, dtype=F32), size, first=2)], 6)[3:]
    done[0] = (got[2], got[3], got[0], got[1])
    totals = got[4].reshape(width * slices, 768)
    stats = totals[: 6 * layers].reshape(layers, 6, 768)
    at = 6 * layers
    ffn_rows = totals[at : at + 4 * layers].reshape(layers, 4, 768)
    ffn_grad = jnp.sum(ffn_rows * place[None, :, None], axis=1)
    at += 4 * layers
    head_sums = totals[at : at + 2 * layers].reshape(layers, 2, 4, 192)
    head_grad = jnp.sum(head_sums * place[None, None, :, None], axis=2)
    at += 2 * layers
    memory_grad = totals[at : at + memory_part.shape[0]]
    d_in = jnp.stack([part[0].reshape(depth, 640) for part in done]).astype(F32)
    d_out = jnp.stack([jnp.swapaxes(part[1].reshape(depth, 192), 0, 1) for part in done]).astype(F32)
    d_up = jnp.stack([part[2].reshape(depth, 768) for part in done]).astype(F32)
    d_down = jnp.stack([jnp.swapaxes(part[3].reshape(depth, 768), 0, 1) for part in done]).astype(F32)
    return (
        output, hidden_grad, memory_grad, *parted(d_in), d_out, d_up, d_down,
        head_grad, ffn_grad, stats[:, 4:6], stats[:, 0:2], stats[:, 2:4],
    )


def solution(mesh):
    rows = P(("fsdp", "ctx", "tp"), None)
    inner = P(None, "fsdp", "tp")
    outer = P(None, "tp", "fsdp")
    weights = (inner, inner, inner, outer, inner, outer)
    biases = (P(None, None, "tp"), P(None, "tp"), P(), P(), P())
    return jax.shard_map(
        shards,
        mesh=mesh,
        in_specs=(rows, rows, P("fsdp", "ctx", None), P("fsdp", None), P()) + weights + biases,
        out_specs=(rows, rows, P()) + weights + biases,
        check_vma=False,
    )
```
